32 devices in a mesh: fsdp: 8 (over z, y), rep: 4 (over x, core).
Axes of the slice: x: 2, y: 2, z: 4, core: 2. Of those that a mesh axis runs over, the one named last changes fastest.
Arguments:
- tokens: float32 [16384, 768], P(('fsdp', 'rep')), may hold values from -6 to 6
- mask_bits: int32 [16384], P(('fsdp', 'rep')), may hold values from 0 to 1, as said below
- timesteps: int32 [128], P(('fsdp', 'rep')), may hold values from 0 to 999
- cotangent: float32 [16384, 768], P(('fsdp', 'rep')), may hold values from -6 to 6
- w_qkv: float32 [768, 2304], P(('fsdp', 'rep')), may hold values from -0.21875 to 0.21875
- w_out: float32 [768, 768], P(('fsdp', 'rep')), may hold values from -0.625 to 0.625
- w_up: float32 [768, 3072], P(('fsdp', 'rep')), may hold values from -0.21875 to 0.21875
- w_down: float32 [3072, 768], P(('fsdp', 'rep')), may hold values from -0.109375 to 0.109375
- time_table: float32 [768, 1000], P(('fsdp', 'rep')), may hold values from -6 to 6
- b_query: float32 [768], P(('fsdp', 'rep')), may hold values from -3 to 3
- b_value: float32 [768], P(('fsdp', 'rep')), may hold values from -3 to 3
- b_out: float32 [768], P(('fsdp', 'rep')), may hold values from -3 to 3
- b_up: float32 [3072], P(('fsdp', 'rep')), may hold values from -3 to 3
- b_down: float32 [768], P(('fsdp', 'rep')), may hold values from -3 to 3
- gain_attn: float32 [768], P(('fsdp', 'rep')), may hold values from 0.5 to 1.5
- shift_attn: float32 [768], P(('fsdp', 'rep')), may hold values from -2 to 2
- gain_mlp: float32 [768], P(('fsdp', 'rep')), may hold values from 0.5 to 1.5
- shift_mlp: float32 [768], P(('fsdp', 'rep')), may hold values from -2 to 2
- mask_vector: float32 [768], P(('fsdp', 'rep')), may hold values from -5 to 5
Outputs:
- output: float32 [16384, 768], P(('fsdp', 'rep'))
- grad_tokens: float32 [16384, 768], P(('fsdp', 'rep'))
- grad_w_qkv: float32 [768, 2304], P(('fsdp', 'rep'))
- grad_w_out: float32 [768, 768], P(('fsdp', 'rep'))
- grad_w_up: float32 [768, 3072], P(('fsdp', 'rep'))
- grad_w_down: float32 [3072, 768], P(('fsdp', 'rep'))
- grad_time_table: float32 [768, 1000], P(('fsdp', 'rep'))
- grad_b_query: float32 [768], P(('fsdp', 'rep'))
- grad_b_value: float32 [768], P(('fsdp', 'rep'))
- grad_b_out: float32 [768], P(('fsdp', 'rep'))
- grad_b_up: float32 [3072], P(('fsdp', 'rep'))
- grad_b_down: float32 [768], P(('fsdp', 'rep'))
- grad_gain_attn: float32 [768], P(('fsdp', 'rep'))
- grad_shift_attn: float32 [768], P(('fsdp', 'rep'))
- grad_gain_mlp: float32 [768], P(('fsdp', 'rep'))
- grad_shift_mlp: float32 [768], P(('fsdp', 'rep'))
- grad_mask_vector: float32 [768], P(('fsdp', 'rep'))
The draws below stay inside these ranges and needn't reach their ends.
Inputs may be any that keep to these rules, and one draw needn't show every extreme that they name: `mask_bits`: 1 marks an absorbed token; the number of absorbed tokens of a sequence varies widely, from none to all 128.
All inputs are finite; a program needn't handle non-finite values.
Results may differ from the reference program's by a relative error of at most 0.019.
Values may be sent and summed in bfloat16 or wider, within the bound.
No kernel may reach another device: no remote copies, remote signals or barrier semaphores. Data moves between devices by JAX's collectives and lax.ppermute only.
A program may use at most 192 MiB of HBM per device.

```python
import math
import jax
import jax.numpy as jnp
from jax import lax

D = 768
HEADS = 12
HDIM = 64
FF = 3072
TSTEPS = 1000
L = 128
SEQS = 128
TOKENS = 16384


def draw_mask_bits(key, part):
    level_key = jax.random.fold_in(key, 11)
    order_key = jax.random.fold_in(key, 12)
    levels = jax.random.randint(level_key, (SEQS,), 0, 9)
    counts = jnp.minimum(jnp.left_shift(jnp.ones_like(levels), levels) - 1, L)
    order_scores = jax.random.randint(order_key, (SEQS, L), 0, 1 << 20) * L
    order_scores = order_scores + lax.broadcasted_iota(jnp.int32, (SEQS, L), 1)
    ranking = jnp.argsort(jnp.argsort(order_scores, axis=1), axis=1)
    return (ranking < counts[:, None]).astype(jnp.int32).reshape(SEQS * L)


def set_ends(array, rng, least, top_value):
    extent = array.shape
    spot = [jax.random.randint(jax.random.fold_in(rng, axis), (), 0, extent[axis]) for axis in range(len(extent))]
    array = array.at[tuple(spot)].set(least)
    longest = extent.index(max(extent))
    spot[longest] = (spot[longest] + 1) % extent[longest]
    return array.at[tuple(spot)].set(top_value)


def raised(values, rng, source, target, parts, factor):
    def block_of(position):
        return (jnp.arange(values.shape[position]) // (values.shape[position] // parts)).reshape((-1,) + (1,) * (values.ndim - 1 - position))

    first = jax.random.permutation(rng, parts)[block_of(target)]
    far = (block_of(target) + parts // 2) % parts
    return jnp.where((block_of(source) == first) | (block_of(source) == far), factor * values, values)


def steps_of(rng, extent, split, low, largest):
    level, own = 1.0, jax.random.fold_in(rng, 6)
    for position, blocks in split:
        draws = jnp.exp(jax.random.uniform(jax.random.fold_in(own, position), (blocks,), jnp.float32, low / len(split), largest / len(split)))
        level = level * jnp.repeat(draws, extent[position] // blocks).reshape([-1 if axis == position else 1 for axis in range(len(extent))])
    return level


def bell_draw(rng, dims, width, reach, cuts=(), held_as=jnp.bfloat16):
    drawn = width * jax.random.normal(rng, dims, jnp.float32)
    if cuts:
        drawn = drawn * steps_of(rng, dims, cuts, -0.22, 0.18)
    return jnp.clip(drawn, -reach, reach).astype(held_as)


def heavy_noise(stream_key, shape, scale, most, shards, heavy, kind=jnp.bfloat16):
    values = scale * jax.random.normal(stream_key, shape, jnp.float32)
    if shards:
        values = values * steps_of(stream_key, shape, shards, -0.22, 0.18)
    return jnp.clip(raised(values, jax.random.fold_in(stream_key, 3), *heavy), -most, most).astype(kind)


def setup_inputs(seed: int = 0) -> dict:
    streams_of = jax.random.split(jax.random.key(seed), 20)
    tokens = heavy_noise(streams_of[0], (TOKENS, D), 1.0, 6.0, ((0, 32),), (0, 1, 32, 2.75), jnp.float32)
    mask_bits = draw_mask_bits(jax.random.fold_in(streams_of[19], 71), 0)
    timesteps = set_ends(jax.random.randint(streams_of[2], (SEQS,), 0, TSTEPS), jax.random.fold_in(streams_of[2], 1), 0, TSTEPS - 1).astype(jnp.int32)
    cotangent = bell_draw(streams_of[3], (TOKENS, D), 1.0, 6.0, ((0, 32),), jnp.float32)
    w_qkv = bell_draw(streams_of[4], (D, 3 * D), D ** -0.5, 0.21875, ((0, 32),), jnp.float32)
    w_out = bell_draw(streams_of[5], (D, D), (D // 8) ** -0.5, 0.625, ((0, 32),), jnp.float32)
    w_up = bell_draw(streams_of[6], (D, FF), D ** -0.5, 0.21875, ((0, 32),), jnp.float32)
    w_down = bell_draw(streams_of[7], (FF, D), FF ** -0.5, 0.109375, ((0, 32),), jnp.float32)
    time_table = bell_draw(streams_of[8], (D, TSTEPS), 1.0, 6.0, ((0, 32),), jnp.float32)
    b_query = bell_draw(streams_of[9], (D,), 0.5, 3.0, ((0, 32),), jnp.float32)
    b_value = bell_draw(streams_of[10], (D,), 0.5, 3.0, ((0, 32),), jnp.float32)
    b_out = bell_draw(streams_of[11], (D,), 0.5, 3.0, ((0, 32),), jnp.float32)
    b_up = bell_draw(streams_of[12], (FF,), 0.5, 3.0, ((0, 32),), jnp.float32)
    b_down = bell_draw(streams_of[13], (D,), 0.5, 3.0, ((0, 32),), jnp.float32)
    gain_attn = jnp.clip(1.0 + 0.1 * jax.random.normal(streams_of[14], (D,), jnp.float32), 0.5, 1.5)
    shift_attn = bell_draw(streams_of[15], (D,), 0.3, 2.0, ((0, 32),), jnp.float32)
    gain_mlp = jnp.clip(1.0 + 0.1 * jax.random.normal(streams_of[16], (D,), jnp.float32), 0.5, 1.5)
    shift_mlp = bell_draw(streams_of[17], (D,), 0.3, 2.0, ((0, 32),), jnp.float32)
    mask_vector = bell_draw(streams_of[18], (D,), 1.0, 5.0, ((0, 32),), jnp.float32)
    return {"tokens": tokens, "mask_bits": mask_bits, "timesteps": timesteps, "cotangent": cotangent, "w_qkv": w_qkv, "w_out": w_out, "w_up": w_up, "w_down": w_down, "time_table": time_table, "b_query": b_query, "b_value": b_value, "b_out": b_out, "b_up": b_up, "b_down": b_down, "gain_attn": gain_attn, "shift_attn": shift_attn, "gain_mlp": gain_mlp, "shift_mlp": shift_mlp, "mask_vector": mask_vector}


EPSILON = 1e-05
HIGHEST = lax.Precision.HIGHEST

@jax.custom_vjp
def low(v):
    return lax.optimization_barrier(v.astype(jnp.bfloat16)).astype(jnp.float32)

@jax.custom_vjp
def low_back(v):
    return v

def low_keep(v):
    return (low(v), None)

def low_pass(kept, grad):
    return (grad,)

def back_keep(v):
    return (v, None)

def back_low(kept, grad):
    return (low(grad),)
low.defvjp(low_keep, low_pass)
low_back.defvjp(back_keep, back_low)

def layer_norm(values, gain, shift):
    center = values - lax.optimization_barrier(jnp.mean(values, -1, keepdims=True))
    spread = lax.optimization_barrier(jnp.mean(center * center, -1, keepdims=True))
    return center * lax.rsqrt(spread + EPSILON) * gain + shift

def matmul(left, right):
    return jnp.dot(left, right, precision=HIGHEST, preferred_element_type=jnp.float32)

def forward(params, inputs, absorbed, onehot):
    w_qkv, w_out, w_up, w_down, time_table, b_query, b_value, b_out, b_up, b_down, gain_attn, shift_attn, gain_mlp, shift_mlp, mask_vector = [low(item) for item in params]
    seq_count = onehot.shape[0]
    scale = 1.0 / math.sqrt(HDIM)
    table_rows = matmul(onehot, time_table.T)
    start = inputs * (1.0 - absorbed) + absorbed * mask_vector[None, :]
    start = (start.reshape(seq_count, L, D) + table_rows[:, None, :]).reshape(seq_count * L, D)
    normed_one = low(layer_norm(start, gain_attn, shift_attn))
    bias_all = jnp.concatenate([b_query, jnp.zeros_like(b_query), b_value])
    projected = low(low_back(matmul(normed_one, w_qkv) + bias_all))
    queries = projected[:, :D].reshape(seq_count, L, HEADS, HDIM)
    key_rows = projected[:, D:2 * D].reshape(seq_count, L, HEADS, HDIM)
    value_rows = projected[:, 2 * D:].reshape(seq_count, L, HEADS, HDIM)
    scores = low_back(jnp.einsum('sqhd,skhd->shqk', queries, key_rows, precision=HIGHEST) * scale)
    probs = jax.nn.softmax(scores, axis=-1)
    context = jnp.einsum('shqk,skhd->sqhd', low(probs), value_rows, precision=HIGHEST)
    context = low(low_back(context.reshape(seq_count * L, D)))
    middle = start + low_back(matmul(context, w_out) + b_out)
    normed_two = low(layer_norm(middle, gain_mlp, shift_mlp))
    pre_gelu = low_back(matmul(normed_two, w_up) + b_up)
    hidden = low(jax.nn.gelu(pre_gelu))
    return middle + low_back(matmul(hidden, w_down) + b_down)

def reference(tokens, mask_bits, timesteps, cotangent, w_qkv, w_out, w_up, w_down, time_table, b_query, b_value, b_out, b_up, b_down, gain_attn, shift_attn, gain_mlp, shift_mlp, mask_vector):
    params = tuple((item.astype(jnp.float32) for item in (w_qkv, w_out, w_up, w_down, time_table, b_query, b_value, b_out, b_up, b_down, gain_attn, shift_attn, gain_mlp, shift_mlp, mask_vector)))
    group = 32
    groups = SEQS // group
    token_groups = tokens.astype(jnp.float32).reshape(groups, group * L, D)
    absorbed = mask_bits.astype(jnp.float32).reshape(groups, group * L, 1)
    onehot = (timesteps[:, None] == jnp.arange(TSTEPS, dtype=jnp.int32)[None, :]).astype(jnp.float32)
    onehot = onehot.reshape(groups, group, TSTEPS)
    cot_groups = cotangent.astype(jnp.float32).reshape(groups, group * L, D)

    def one_group(totals, pieces):
        token_part, absorbed_part, onehot_part, cot_part = pieces

        def apply(prm, values):
            return forward(prm, values, absorbed_part, onehot_part)
        result, pull = jax.vjp(apply, params, token_part)
        grad_params, grad_inputs = pull(cot_part * absorbed_part)
        totals = jax.tree.map(lambda first, second: first + second, totals, grad_params)
        return (totals, (result, grad_inputs))
    zeros = jax.tree.map(jnp.zeros_like, params)
    totals, (results, grad_inputs) = lax.scan(one_group, zeros, (token_groups, absorbed, onehot, cot_groups))
    return (results.reshape(TOKENS, D), grad_inputs.reshape(TOKENS, D), totals[0], totals[1], totals[2], totals[3], totals[4], totals[5], totals[6], totals[7], totals[8], totals[9], totals[10], totals[11], totals[12], totals[13], totals[14])
```

```python
import functools
import math

import jax
import jax.numpy as jnp
from jax import lax
from jax.sharding import PartitionSpec as P

HDIM = 64
EPSILON = 1e-05
AXES = ("fsdp", "rep")
BF = jnp.bfloat16
F32 = jnp.float32


def layer_norm(values, gain, shift):
    center = values - jnp.mean(values, -1, keepdims=True)
    spread = jnp.mean(center * center, -1, keepdims=True)
    return center * lax.rsqrt(spread + EPSILON) * gain + shift


def product(left, right):
    return jnp.dot(left, right, preferred_element_type=F32)


def left_product(left, right):
    return lax.dot_general(left, right, (((0,), (0,)), ((), ())), preferred_element_type=F32)


def right_product(left, right):
    return lax.dot_general(left, right, (((1,), (1,)), ((), ())), preferred_element_type=F32)


def column_sums(values):
    return jnp.sum(values.astype(F32), 0)


def pick(array, index, axis):
    return lax.dynamic_index_in_dim(array, index, axis, keepdims=False)


def ordered(bit, mine, other, axis):
    return jnp.concatenate(
        [jnp.where(bit == 0, mine, other), jnp.where(bit == 0, other, mine)], axis
    )


def paired(bit, mine, other, axis):
    return jnp.stack([jnp.where(bit == 0, mine, other), jnp.where(bit == 0, other, mine)], axis)


class Tree:
    def __init__(self):
        fsdp, rep = lax.axis_index("fsdp"), lax.axis_index("rep")
        self.z, self.y, self.x, self.core = fsdp // 2, fsdp % 2, rep // 2, rep % 2

    def to_core(self, value):
        return lax.ppermute(value, "rep", [(i, i ^ 1) for i in range(4)])

    def to_x(self, value):
        return lax.ppermute(value, "rep", [(i, i ^ 2) for i in range(4)])

    def to_y(self, value):
        return lax.ppermute(value, "fsdp", [(i, i ^ 1) for i in range(8)])

    def to_z(self, value, step):
        return lax.ppermute(value, "fsdp", [(i, i ^ (2 * step)) for i in range(8)])

    def spread(self, first, second):
        own = jnp.concatenate([first, second], 0)
        cut = first.shape[0]
        held = [own] + [self.to_z(own, step) for step in (1, 2, 3)]
        low, high = self.z % 2 == 1, self.z // 2 == 1

        def along_z(rows):
            out = []
            for place in range(4):
                near = [jnp.where(low, held[(place ^ 1) ^ h], held[place ^ h]) for h in (0, 2)]
                out.append(jnp.where(high, near[1], near[0])[rows])
            return jnp.stack(out)

        first, second = along_z(slice(0, cut)), along_z(slice(cut, None))
        first_got, second_got = self.to_x(first), self.to_y(second)
        first = paired(self.x, first, first_got, 1)
        second = paired(self.y, second, second_got, 1)
        first_got, second_got = self.to_y(first), self.to_x(second)
        first = paired(self.y, first, first_got, 1)
        second = paired(self.x, second, second_got, 2)
        whole = jnp.concatenate([first, second], 3)
        return whole.reshape(-1, own.shape[-1])

    def gather_columns(self, shard):
        mine, other = pick(shard, self.core, 1), pick(shard, 1 - self.core, 1)
        got = self.to_core(other)
        half = self.spread(jnp.where(self.core == 0, mine, got), jnp.where(self.core == 0, got, mine))
        return half, self.to_core(half)

    def gather_rows(self, shard):
        cut = shard.shape[0] // 2
        half = self.spread(shard[:cut], shard[cut:])
        return half, self.to_core(half)

    def collect(self, mine, others, cut):
        got = [self.to_core(other) for other in others]

        def stage(terms, index, axis):
            return sum(pick(term, index, axis).astype(F32) for term in terms)

        def joined(groups, rows, index, axis):
            return jnp.concatenate(
                [stage([term[:, :, :, part] for term in group], index, axis) for group, part in zip(groups, rows)], 2
            )

        groups = [[a, b] for a, b in zip(mine, got)]
        first_rows = [slice(0, cut)] + [slice(None)] * (len(mine) - 1)
        keep = joined(groups, first_rows, self.x, 2)
        keep = keep + self.to_x(joined(groups, first_rows, 1 - self.x, 2).astype(BF))
        first = pick(keep, self.y, 1) + self.to_y(pick(keep, 1 - self.y, 1).astype(BF))
        second_rows = [slice(cut, None)]
        keep = joined(groups[:1], second_rows, self.y, 1)
        keep = keep + self.to_y(joined(groups[:1], second_rows, 1 - self.y, 1).astype(BF))
        second = pick(keep, self.x, 1) + self.to_x(pick(keep, 1 - self.x, 1).astype(BF))
        both = jnp.concatenate([first, second], 1)
        total = pick(both, self.z, 0)
        for step in (1, 2, 3):
            total = total + self.to_z(pick(both, self.z ^ step, 0).astype(BF), step)
        split = first.shape[1]
        return total[:split], total[split:]

    def shaped(self, array):
        return array.reshape(4, 2, 2, -1, array.shape[-1])

    def reduce_columns(self, mine, other, extra=None):
        mine, other = [self.shaped(mine)], [self.shaped(other.astype(BF))]
        cut = mine[0].shape[3] // 2
        if extra is not None:
            mine.append(self.shaped(pick(extra, self.core, 1)))
            other.append(self.shaped(pick(extra, 1 - self.core, 1).astype(BF)))
        first, second = self.collect(mine, other, cut)
        block = first[cut:]
        first = first[:cut]
        keep = jnp.where(self.core == 0, first, second)
        got = self.to_core(jnp.where(self.core == 0, second, first))
        return paired(self.core, keep, got, 1), block

    def reduce_rows(self, mine, other):
        mine, other = self.shaped(mine), self.shaped(other.astype(BF))
        first, second = self.collect([mine], [other], mine.shape[3] // 2)
        return jnp.concatenate([first, second], 0)


class Plain:
    def __init__(self):
        self.core = 0

    def gather_columns(self, shard):
        whole = lax.all_gather(shard, AXES, axis=0, tiled=True)
        return whole[:, 0], whole[:, 1]

    def gather_rows(self, shard):
        whole = lax.all_gather(shard, AXES, axis=0)
        whole = whole.reshape(-1, 2, *shard.shape)
        return whole[:, 0].reshape(-1, shard.shape[1]), whole[:, 1].reshape(-1, shard.shape[1])

    def reduce_columns(self, mine, other, extra=None):
        sums = jnp.stack([mine, other], 1).astype(BF)
        sums = lax.psum_scatter(sums, AXES, scatter_dimension=0, tiled=True).astype(F32)
        if extra is None:
            return sums, None
        extra = extra.reshape(-1, extra.shape[3]).astype(BF)
        return sums, lax.psum_scatter(extra, AXES, scatter_dimension=0, tiled=True).astype(F32)

    def reduce_rows(self, mine, other):
        width = mine.shape[1]
        count = lax.axis_size(AXES)
        sums = jnp.stack([mine.reshape(count // 2, -1, width), other.reshape(count // 2, -1, width)], 1)
        sums = sums.reshape(-1, width).astype(BF)
        return lax.psum_scatter(sums, AXES, scatter_dimension=0, tiled=True).astype(F32)


def body(
    fast,
    tokens,
    mask_bits,
    timesteps,
    cotangent,
    w_qkv,
    w_out,
    w_up,
    w_down,
    time_table,
    b_query,
    b_value,
    b_out,
    b_up,
    b_down,
    gain_attn,
    shift_attn,
    gain_mlp,
    shift_mlp,
    mask_vector,
):
    moves = Tree() if fast else Plain()
    core = moves.core
    count = lax.axis_size(AXES)
    chips = count // 2
    place = lax.axis_index(AXES)
    width = tokens.shape[1]
    part = width // count
    hidden_width = w_up.shape[1]
    hidden_part = hidden_width // count
    seq_count = timesteps.shape[0]
    seq_length = tokens.shape[0] // seq_count
    row_count = tokens.shape[0]
    half = width // 2
    half_heads = half // HDIM
    scale = 1.0 / math.sqrt(HDIM)
    table_cols = time_table.shape[1]
    absorbed = (mask_bits == 1)[:, None]
    absorbed_float = mask_bits.astype(F32)[:, None]

    qkv_shard = w_qkv.astype(BF).reshape(part, 3, 2, half).transpose(0, 2, 1, 3).reshape(part, 2, 3 * half)
    up_shard = (
        w_up.astype(BF)
        .reshape(part, chips, 2, hidden_part)
        .transpose(0, 2, 1, 3)
        .reshape(part, 2, hidden_width // 2)
    )
    qkv_w = moves.gather_columns(qkv_shard)
    out_w = moves.gather_columns(w_out.astype(BF).reshape(part, 2, half))
    up_w = moves.gather_columns(up_shard)
    down_w = moves.gather_rows(w_down.astype(BF))
    out_w = ordered(core, out_w[0], out_w[1], 1)

    small = [b_query, b_value, b_out, b_down, gain_attn, shift_attn, gain_mlp, shift_mlp, mask_vector]
    fixed = len(small)
    up_cols = hidden_part // part
    seq_cols = -(-2 * seq_count // part)
    steps = jnp.concatenate([timesteps // 256, timesteps % 256]).astype(BF)
    steps = jnp.pad(steps, (0, seq_cols * part - 2 * seq_count)).reshape(seq_cols, part)
    small = jnp.concatenate(
        [jnp.stack([item.astype(BF) for item in small]), b_up.astype(BF).reshape(up_cols, part), steps], 0
    )
    small_cols = small.shape[0]
    all_cols = -(-(table_cols + small_cols) // 128) * 128
    small = jnp.pad(small, ((0, all_cols - table_cols - small_cols), (0, 0)))
    table = jnp.concatenate([time_table.astype(BF), small.T], 1)
    table = lax.all_gather(table, AXES, axis=0, tiled=True)
    chosen = jnp.concatenate([timesteps, table_cols + jnp.arange(small_cols, dtype=jnp.int32)])
    chosen = chosen[:, None] == lax.broadcasted_iota(jnp.int32, (seq_count + small_cols, all_cols), 1)
    rows = right_product(chosen.astype(BF), table)
    table_rows = rows[:seq_count]
    rows = rows[seq_count:]
    bias_query, bias_value, bias_out, bias_down, gain_one, shift_one, gain_two, shift_two, mask_row = [
        rows[i] for i in range(fixed)
    ]
    bias_up = rows[fixed : fixed + up_cols].reshape(up_cols, chips, 2, part).transpose(2, 1, 0, 3)
    bias_up = bias_up.reshape(2, hidden_width // 2)
    bias_up = (pick(bias_up, core, 0), pick(bias_up, 1 - core, 0))
    steps = rows[fixed + up_cols :].reshape(seq_cols, count, part).transpose(1, 0, 2).reshape(count, -1)
    steps = steps.astype(jnp.int32)
    steps = (steps[:, :seq_count] * 256 + steps[:, seq_count : 2 * seq_count]).reshape(-1)
    bias_qkv = jnp.stack([bias_query, jnp.zeros_like(bias_query), bias_value]).reshape(3, 2, half)
    bias_qkv = [pick(bias_qkv, index, 1).reshape(-1) for index in (core, 1 - core)]

    start = jnp.where(absorbed, mask_row[None, :], tokens)
    start = (start.reshape(seq_count, seq_length, width) + table_rows[:, None, :]).reshape(row_count, width)
    normed_one = layer_norm(start, gain_one, shift_one).astype(BF)

    def split_heads(block):
        return block.reshape(seq_count, seq_length, half_heads, HDIM)

    def attention(weight, bias):
        projected = (product(normed_one, weight) + bias).astype(BF)
        queries, key_rows, value_rows = [split_heads(projected[:, i * half : (i + 1) * half]) for i in range(3)]
        scores = jnp.einsum("sqhd,skhd->shqk", queries, key_rows, preferred_element_type=F32) * scale
        highest = jnp.max(scores, -1, keepdims=True)
        log_total = highest + jnp.log(jnp.sum(jnp.exp(scores - highest), -1, keepdims=True))
        probs_low = jnp.exp(scores - log_total).astype(BF)
        context = jnp.einsum("shqk,skhd->sqhd", probs_low, value_rows, preferred_element_type=F32)
        return context.reshape(row_count, half).astype(BF), (queries, key_rows, value_rows, log_total)

    context_mine, kept_mine = attention(qkv_w[0], bias_qkv[0])
    context_other, kept_other = attention(qkv_w[1], bias_qkv[1])
    context = ordered(core, context_mine, context_other, 1)
    middle = start + (product(context, out_w) + bias_out)
    normed_two = layer_norm(middle, gain_two, shift_two).astype(BF)
    pre_gelu = [product(normed_two, up_w[i]) + bias_up[i] for i in range(2)]
    hidden = [jax.nn.gelu(pre).astype(BF) for pre in pre_gelu]
    output = middle + (product(hidden[0], down_w[0]) + product(hidden[1], down_w[1]) + bias_down)

    grad_output = cotangent * absorbed_float
    grad_branch = grad_output.astype(BF)
    down_sum = moves.reduce_rows(left_product(hidden[0], grad_branch), left_product(hidden[1], grad_branch))
    grad_b_down = column_sums(grad_branch)
    grad_pre = []
    for i in range(2):
        grad_hidden = right_product(grad_branch, down_w[i])
        _, gelu_pull = jax.vjp(jax.nn.gelu, pre_gelu[i])
        grad_pre.append(gelu_pull(grad_hidden)[0].astype(BF))
    up_sum, _ = moves.reduce_columns(left_product(normed_two, grad_pre[0]), left_product(normed_two, grad_pre[1]))
    grad_b_up = [column_sums(item).reshape(chips, hidden_part) for item in grad_pre]
    grad_normed_two = right_product(grad_pre[0], up_w[0]) + right_product(grad_pre[1], up_w[1])
    _, norm_pull = jax.vjp(layer_norm, middle, gain_two, shift_two)
    back_middle, grad_gain_mlp, grad_shift_mlp = norm_pull(grad_normed_two)
    grad_middle = grad_output + back_middle

    grad_attn = grad_middle.astype(BF)
    grad_halves = [lax.dynamic_slice_in_dim(grad_attn, index * half, half, 1) for index in (core, 1 - core)]
    out_sum, _ = moves.reduce_columns(left_product(context, grad_halves[0]), left_product(context, grad_halves[1]))
    grad_b_out = column_sums(grad_attn)
    grad_context = right_product(grad_attn, out_w).astype(BF)

    def attention_back(kept, grad_half):
        queries, key_rows, value_rows, log_total = kept
        grad_half = split_heads(grad_half)
        scores = jnp.einsum("sqhd,skhd->shqk", queries, key_rows, preferred_element_type=F32) * scale
        probs = jnp.exp(scores - log_total)
        probs_low = probs.astype(BF)
        grad_values = jnp.einsum("shqk,sqhd->skhd", probs_low, grad_half, preferred_element_type=F32)
        grad_probs = jnp.einsum("sqhd,skhd->shqk", grad_half, value_rows, preferred_element_type=F32)
        grad_scores = probs * (grad_probs - jnp.sum(grad_probs * probs, -1, keepdims=True))
        grad_scores = grad_scores.astype(BF)
        grad_queries = jnp.einsum("shqk,skhd->sqhd", grad_scores, key_rows, preferred_element_type=F32) * scale
        grad_keys = jnp.einsum("shqk,sqhd->skhd", grad_scores, queries, preferred_element_type=F32) * scale
        parts = [item.reshape(row_count, half) for item in (grad_queries, grad_keys, grad_values)]
        return jnp.concatenate(parts, 1).astype(BF)

    grad_qkv = [
        attention_back(kept, lax.dynamic_slice_in_dim(grad_context, index * half, half, 1))
        for kept, index in ((kept_mine, core), (kept_other, 1 - core))
    ]
    grad_normed_one = right_product(grad_qkv[0], qkv_w[0]) + right_product(grad_qkv[1], qkv_w[1])
    _, norm_pull = jax.vjp(layer_norm, start, gain_one, shift_one)
    back_start, grad_gain_attn, grad_shift_attn = norm_pull(grad_normed_one)
    grad_start = grad_middle + back_start
    grad_tokens = jnp.where(absorbed, 0.0, grad_start)
    grad_mask_vector = jnp.sum(grad_start * absorbed_float, 0)
    seq_sums = jnp.sum(grad_start.reshape(seq_count, seq_length, width), 1)

    sums = [column_sums(item) for item in grad_qkv]
    grad_b_query = ordered(core, sums[0][:half], sums[1][:half], 0)
    grad_b_value = ordered(core, sums[0][2 * half :], sums[1][2 * half :], 0)
    small = jnp.stack(
        [
            grad_b_query,
            grad_b_value,
            grad_b_out,
            grad_b_down,
            grad_gain_attn,
            grad_shift_attn,
            grad_gain_mlp,
            grad_shift_mlp,
            grad_mask_vector,
        ]
    )
    small = small.reshape(fixed, chips, 2, part).transpose(1, 2, 0, 3).reshape(chips, 2, fixed * part)
    small = jnp.concatenate([small, paired(core, grad_b_up[0], grad_b_up[1], 1)], 2)
    columns = 3 * half
    slot = seq_count * part
    slots = count * slot
    block_rows = 8 * (-(-(slots + columns) // (8 * columns)))
    seq_sums = seq_sums.reshape(seq_count, chips, 2, part).transpose(1, 2, 0, 3).reshape(chips, 2, slot)
    extra = jnp.pad(small, ((0, 0), (0, 0), (0, block_rows * columns - small.shape[2])))
    extra = lax.dynamic_update_slice(extra, seq_sums, (0, 0, columns + place * slot))
    extra = extra.reshape(chips, 2, block_rows, columns)

    qkv_sum, extra = moves.reduce_columns(
        left_product(normed_one, grad_qkv[0]), left_product(normed_one, grad_qkv[1]), extra
    )
    extra = extra.reshape(-1)
    small = extra[: fixed * part].reshape(fixed, part)
    grad_b_up = extra[fixed * part : fixed * part + hidden_part]
    seq_sums = extra[columns : columns + slots].reshape(count * seq_count, part)
    onehot = (
        steps[:, None] == lax.broadcasted_iota(jnp.int32, (count * seq_count, table_cols), 1)
    ).astype(F32)
    grad_time_table = jnp.einsum("sd,sn->dn", seq_sums, onehot, precision=lax.Precision.HIGHEST)
    grad_w_qkv = qkv_sum.reshape(part, 2, 3, half).transpose(0, 2, 1, 3).reshape(part, 3 * width)
    grad_w_out = out_sum.reshape(part, width)
    grad_w_up = up_sum.reshape(part, 2, chips, hidden_part).transpose(0, 2, 1, 3).reshape(part, hidden_width)
    return (
        output,
        grad_tokens,
        grad_w_qkv,
        grad_w_out,
        grad_w_up,
        down_sum,
        grad_time_table,
        small[0],
        small[1],
        small[2],
        grad_b_up,
        small[3],
        small[4],
        small[5],
        small[6],
        small[7],
        small[8],
    )


def solution(mesh):
    matrix, vector = P(AXES, None), P(AXES)
    fast = dict(mesh.shape) == {"fsdp": 8, "rep": 4}
    return jax.shard_map(
        functools.partial(body, fast),
        mesh=mesh,
        in_specs=(matrix, vector, vector) + (matrix,) * 6 + (vector,) * 10,
        out_specs=(matrix,) * 7 + (vector,) * 10,
        check_vma=False,
    )
```

```python
import functools
import math

import jax
import jax.numpy as jnp
from jax import lax
from jax.experimental import pallas as pl
from jax.experimental.pallas import tpu as pltpu
from jax.sharding import PartitionSpec as P

HDIM = 64
EPSILON = 1e-05
AXES = ("fsdp", "rep")
BF = jnp.bfloat16
F32 = jnp.float32
LANES = 128
VMEM_BYTES = 32 << 20
GELU_OUTER = math.sqrt(2.0 / math.pi)
GELU_INNER = 0.044715


def layer_norm(values, gain, shift):
    center = values - jnp.mean(values, -1, keepdims=True)
    spread = jnp.mean(center * center, -1, keepdims=True)
    return center * lax.rsqrt(spread + EPSILON) * gain + shift


def contract(left, right, left_dim, right_dim):
    dims = (((left_dim,), (right_dim,)), ((), ()))
    return lax.dot_general(left, right, dims, preferred_element_type=F32)


def product(left, right):
    return contract(left, right, 1, 0)


def left_product(left, right):
    return contract(left, right, 0, 0)


def right_product(left, right):
    return contract(left, right, 1, 1)


def column_sums(values):
    return jnp.sum(values.astype(F32), 0)


def pick(array, index, axis):
    return lax.dynamic_index_in_dim(array, index, axis, keepdims=False)


def paired(bit, mine, other, axis):
    return jnp.stack([jnp.where(bit == 0, mine, other), jnp.where(bit == 0, other, mine)], axis)


def after(value, *others):
    return lax.optimization_barrier((value, others))[0]


def lane_masks(factor):
    lane = lax.broadcasted_iota(jnp.int32, (1, LANES), 1)
    return [jnp.where((lane < HDIM) == (head == 0), factor, 0.0).astype(BF) for head in (0, 1)]


def softmax(scores):
    powers = jnp.exp(scores - jnp.max(scores, -1, keepdims=True))
    return powers * (1.0 / jnp.sum(powers, -1, keepdims=True))


def attention_kernel(length, scale, rows_ref, query_ref, key_ref, value_ref, bias_ref, qkv_ref, context_ref):
    rows = rows_ref[...]
    for index, weight in enumerate((query_ref, key_ref, value_ref)):
        qkv_ref[index] = (product(rows, weight[...]) + bias_ref[index : index + 1, :]).astype(BF)
    ones, scaled = lane_masks(1.0), lane_masks(scale)

    for sequence in range(rows.shape[0] // length):
        span = slice(sequence * length, (sequence + 1) * length)
        queries, key_rows, value_rows = [qkv_ref[index, span, :] for index in range(3)]
        total = 0.0
        for head in (0, 1):
            probs = softmax(right_product(queries * scaled[head], key_rows)).astype(BF)
            total = total + product(probs, value_rows * ones[head])
        context_ref[span, :] = total.astype(BF)


def attention(rows, weight, bias, length):
    tokens, width = rows.shape
    half = bias.shape[1]
    pairs = half // LANES

    def weight_spec(index):
        return pl.BlockSpec((width, LANES), lambda pair: (0, index * pairs + pair))

    return pl.pallas_call(
        functools.partial(attention_kernel, length, 1.0 / math.sqrt(HDIM)),
        grid=(pairs,),
        in_specs=[
            pl.BlockSpec((tokens, width), lambda pair: (0, 0)),
            weight_spec(0),
            weight_spec(1),
            weight_spec(2),
            pl.BlockSpec((3, LANES), lambda pair: (0, pair)),
        ],
        out_specs=[
            pl.BlockSpec((3, tokens, LANES), lambda pair: (0, 0, pair)),
            pl.BlockSpec((tokens, LANES), lambda pair: (0, pair)),
        ],
        out_shape=[
            jax.ShapeDtypeStruct((3, tokens, half), BF),
            jax.ShapeDtypeStruct((tokens, half), BF),
        ],
        compiler_params=pltpu.CompilerParams(vmem_limit_bytes=VMEM_BYTES),
        cost_estimate=pl.CostEstimate(
            flops=6 * tokens * width * half,
            bytes_accessed=2 * tokens * width + 6 * width * half + 8 * tokens * half,
            transcendentals=2 * tokens * length * pairs,
        ),
        name="attention",
    )(rows, weight, weight, weight, bias)


def attention_back_kernel(length, scale, qkv_ref, grad_ref, rows_ref, grads_ref, weight_ref, sums_ref):
    ones, scaled = lane_masks(1.0), lane_masks(scale)

    for sequence in range(grad_ref.shape[0] // length):
        span = slice(sequence * length, (sequence + 1) * length)
        queries, key_rows, value_rows = [qkv_ref[index, span, :] for index in range(3)]
        grad = grad_ref[span, :]
        grad_queries, grad_keys, grad_values = 0.0, 0.0, 0.0
        for head in (0, 1):
            probs = softmax(right_product(queries * scaled[head], key_rows))
            grad_head = grad * ones[head]
            grad_probs = right_product(grad_head, value_rows)
            grad_scores = probs * (grad_probs - jnp.sum(grad_probs * probs, -1, keepdims=True))
            grad_scores = grad_scores.astype(BF)
            grad_values = grad_values + left_product(probs.astype(BF), grad_head)
            grad_queries = grad_queries + product(grad_scores, key_rows * ones[head])
            grad_keys = grad_keys + left_product(grad_scores, queries * ones[head])
        grads_ref[0, span, :] = (grad_queries * scale).astype(BF)
        grads_ref[1, span, :] = (grad_keys * scale).astype(BF)
        grads_ref[2, span, :] = grad_values.astype(BF)

    rows = rows_ref[...]
    for index in range(3):
        grads = grads_ref[index]
        weight_ref[index] = product(rows, grads).astype(weight_ref.dtype)
        sums_ref[index : index + 1, :] = jnp.sum(grads.astype(F32), 0, keepdims=True)


def attention_back(qkv, grad, rows_across, length, dtype):
    _, tokens, half = qkv.shape
    width = rows_across.shape[0]
    pairs = half // LANES
    return pl.pallas_call(
        functools.partial(attention_back_kernel, length, 1.0 / math.sqrt(HDIM)),
        grid=(pairs,),
        in_specs=[
            pl.BlockSpec((3, tokens, LANES), lambda pair: (0, 0, pair)),
            pl.BlockSpec((tokens, LANES), lambda pair: (0, pair)),
            pl.BlockSpec((width, tokens), lambda pair: (0, 0)),
        ],
        out_specs=[
            pl.BlockSpec((3, tokens, LANES), lambda pair: (0, 0, pair)),
            pl.BlockSpec((3, width, LANES), lambda pair: (0, 0, pair)),
            pl.BlockSpec((3, LANES), lambda pair: (0, pair)),
        ],
        out_shape=[
            jax.ShapeDtypeStruct((3, tokens, half), BF),
            jax.ShapeDtypeStruct((3, width, half), dtype),
            jax.ShapeDtypeStruct((3, half), F32),
        ],
        compiler_params=pltpu.CompilerParams(vmem_limit_bytes=VMEM_BYTES),
        cost_estimate=pl.CostEstimate(
            flops=6 * tokens * width * half,
            bytes_accessed=2 * tokens * width + 12 * width * half + 14 * tokens * half,
            transcendentals=2 * tokens * length * pairs,
        ),
        name="attention_back",
    )(qkv, grad, rows_across)


def feed_kernel(rows_ref, weight_ref, bias_ref, hidden_ref, slope_ref, pre_ref):
    pre_ref[...] = product(rows_ref[...], weight_ref[...])
    step = 32

    def chunk(index, carry):
        span = pl.ds(pl.multiple_of(index * step, step), step)
        pre = pre_ref[span, :] + bias_ref[...]
        square = pre * pre
        bend = jnp.tanh(GELU_OUTER * (pre + GELU_INNER * (square * pre)))
        share = 0.5 * (1.0 + bend)
        hidden_ref[span, :] = (pre * share).astype(BF)
        inner = (0.5 * GELU_OUTER) * pre * (1.0 + (3.0 * GELU_INNER) * square)
        slope_ref[span, :] = share + inner * (1.0 - bend * bend)
        return carry

    lax.fori_loop(0, rows_ref.shape[0] // step, chunk, 0, unroll=2)


def feed(rows, weight, bias, block=512):
    tokens, width = rows.shape
    columns = weight.shape[1]
    block = math.gcd(block, columns)
    out = pl.BlockSpec((tokens, block), lambda step: (0, step))
    return pl.pallas_call(
        feed_kernel,
        grid=(columns // block,),
        in_specs=[
            pl.BlockSpec((tokens, width), lambda step: (0, 0)),
            pl.BlockSpec((width, block), lambda step: (0, step)),
            pl.BlockSpec((1, block), lambda step: (0, step)),
        ],
        out_specs=[out, out],
        out_shape=[
            jax.ShapeDtypeStruct((tokens, columns), BF),
            jax.ShapeDtypeStruct((tokens, columns), F32),
        ],
        scratch_shapes=[pltpu.VMEM((tokens, block), F32)],
        compiler_params=pltpu.CompilerParams(vmem_limit_bytes=VMEM_BYTES),
        cost_estimate=pl.CostEstimate(
            flops=2 * tokens * width * columns,
            bytes_accessed=2 * tokens * width + 2 * width * columns + 6 * tokens * columns,
            transcendentals=tokens * columns,
        ),
        name="feed",
    )(rows, weight, bias)


def feed_back_kernel(grad_ref, weight_ref, slope_ref, rows_ref, pre_ref, sum_ref, up_ref):
    grad = (right_product(grad_ref[...], weight_ref[...]) * slope_ref[...]).astype(BF)
    pre_ref[...] = grad
    sum_ref[...] = jnp.sum(grad.astype(F32), 0, keepdims=True)
    up_ref[...] = product(rows_ref[...], grad).astype(up_ref.dtype)


def feed_back(grad, weight, slope, rows_across, dtype, block=512):
    tokens, width = grad.shape
    columns = weight.shape[0]
    block = math.gcd(block, columns)
    out = pl.BlockSpec((tokens, block), lambda step: (0, step))
    return pl.pallas_call(
        feed_back_kernel,
        grid=(columns // block,),
        in_specs=[
            pl.BlockSpec((tokens, width), lambda step: (0, 0)),
            pl.BlockSpec((block, width), lambda step: (step, 0)),
            out,
            pl.BlockSpec((width, tokens), lambda step: (0, 0)),
        ],
        out_specs=[
            out,
            pl.BlockSpec((1, block), lambda step: (0, step)),
            pl.BlockSpec((width, block), lambda step: (0, step)),
        ],
        out_shape=[
            jax.ShapeDtypeStruct((tokens, columns), BF),
            jax.ShapeDtypeStruct((1, columns), F32),
            jax.ShapeDtypeStruct((width, columns), dtype),
        ],
        compiler_params=pltpu.CompilerParams(vmem_limit_bytes=VMEM_BYTES),
        cost_estimate=pl.CostEstimate(
            flops=4 * tokens * width * columns,
            bytes_accessed=4 * tokens * width + 6 * width * columns + 6 * tokens * columns,
            transcendentals=0,
        ),
        name="feed_back",
    )(grad, weight, slope, rows_across)


class Tree:
    def __init__(self):
        fsdp, rep = lax.axis_index("fsdp"), lax.axis_index("rep")
        self.z, self.y, self.x, self.core = fsdp // 2, fsdp % 2, rep // 2, rep % 2

    def to_core(self, value):
        return lax.ppermute(value, "rep", [(i, i ^ 1) for i in range(4)])

    def to_x(self, value):
        return lax.ppermute(value, "rep", [(i, i ^ 2) for i in range(4)])

    def to_y(self, value):
        return lax.ppermute(value, "fsdp", [(i, i ^ 1) for i in range(8)])

    def to_z(self, value, step):
        return lax.ppermute(value, "fsdp", [(i, i ^ (2 * step)) for i in range(8)])


class Gather:
    def __init__(self, tree, first, second):
        self.tree, self.cut = tree, first.shape[0]
        self.own = jnp.concatenate([first, second], 0)

    @staticmethod
    def columns(tree, shard):
        mine = pick(shard, tree.core, 1)
        got = tree.to_core(pick(shard, 1 - tree.core, 1))
        return Gather(tree, jnp.where(tree.core == 0, mine, got), jnp.where(tree.core == 0, got, mine))

    @staticmethod
    def rows(tree, shard):
        cut = shard.shape[0] // 2
        return Gather(tree, shard[:cut], shard[cut:])

    def along_z(self, *wait):
        tree = self.tree
        own = after(self.own, *wait)
        held = [own] + [tree.to_z(own, step) for step in (1, 2, 3)]
        low, high = tree.z % 2 == 1, tree.z // 2 == 1

        def chosen(rows):
            out = []
            for place in range(4):
                near = [jnp.where(low, held[(place ^ 1) ^ h], held[place ^ h]) for h in (0, 2)]
                out.append(jnp.where(high, near[1], near[0])[rows])
            return jnp.stack(out)

        self.first, self.second = chosen(slice(0, self.cut)), chosen(slice(self.cut, None))
        return self.first, self.second

    def one(self, *wait):
        tree = self.tree
        first, second = after((self.first, self.second), *wait)
        self.first = paired(tree.x, first, tree.to_x(first), 1)
        self.second = paired(tree.y, second, tree.to_y(second), 1)
        return self.first, self.second

    def two(self, *wait):
        tree = self.tree
        first, second = after((self.first, self.second), *wait)
        first = paired(tree.y, first, tree.to_y(first), 1)
        second = paired(tree.x, second, tree.to_x(second), 2)
        half = jnp.concatenate([first, second], 3)
        self.half = half.reshape(-1, half.shape[-1])
        return self.half

    def halves(self):
        return self.half, self.tree.to_core(self.half)


class Reduce:
    def __init__(self, tree, rows):
        self.tree, self.rows = tree, rows
        self.mine, self.got = [], []

    def add(self, mine, other):
        sent = other.astype(BF)
        got = self.tree.to_core(sent)
        self.mine.append(mine)
        self.got.append(got)
        return got

    def one(self):
        tree = self.tree
        shaped = [
            [array.reshape(4, 2, 2, self.rows, -1) for array in (mine, got)] for mine, got in zip(self.mine, self.got)
        ]

        def stage(rows, index, axis):
            sums = [
                pick(mine[:, :, :, rows], index, axis).astype(F32) + pick(got[:, :, :, rows], index, axis).astype(F32)
                for mine, got in shaped
            ]
            return jnp.concatenate(sums, -1)

        upper, lower = slice(0, self.rows // 2), slice(self.rows // 2, None)
        self.first_kept = stage(upper, tree.x, 2)
        self.second_kept = stage(lower, tree.y, 1)
        self.sent = (stage(upper, 1 - tree.x, 2).astype(BF), stage(lower, 1 - tree.y, 1).astype(BF))
        self.got = (tree.to_x(self.sent[0]), tree.to_y(self.sent[1]))

    def two(self):
        tree = self.tree
        first, second = self.first_kept + self.got[0], self.second_kept + self.got[1]
        self.first_kept, self.second_kept = pick(first, tree.y, 1), pick(second, tree.x, 1)
        self.sent = (pick(first, 1 - tree.y, 1).astype(BF), pick(second, 1 - tree.x, 1).astype(BF))
        self.got = (tree.to_y(self.sent[0]), tree.to_x(self.sent[1]))

    def along_z(self):
        tree = self.tree
        both = jnp.concatenate([self.first_kept + self.got[0], self.second_kept + self.got[1]], 1)
        self.first_kept = pick(both, tree.z, 0)
        self.sent = tuple(pick(both, tree.z ^ step, 0).astype(BF) for step in (1, 2, 3))
        self.got = tuple(tree.to_z(sent, step) for sent, step in zip(self.sent, (1, 2, 3)))

    def sums(self):
        return self.first_kept + self.got[0] + self.got[1] + self.got[2]

    def columns(self):
        tree, total = self.tree, self.sums()
        first, second = total[: self.rows // 2], total[self.rows // 2 :]
        keep = jnp.where(tree.core == 0, first, second)
        got = tree.to_core(jnp.where(tree.core == 0, second, first))
        return paired(tree.core, keep, got, 1)


class Whole:
    core = 0

    def __init__(self, rows=None):
        self.mine, self.other = [], []
        self.got, self.sent = (), ()

    @staticmethod
    def columns_of(shard):
        out = Whole()
        whole = lax.all_gather(shard, AXES, axis=0, tiled=True)
        out.half, out.rest = whole[:, 0], whole[:, 1]
        return out

    @staticmethod
    def rows_of(shard):
        out = Whole()
        whole = lax.all_gather(shard, AXES, axis=0)
        whole = whole.reshape(-1, 2, *shard.shape)
        out.half, out.rest = [whole[:, i].reshape(-1, shard.shape[1]) for i in range(2)]
        return out

    def along_z(self, *wait):
        return ()

    def one(self, *wait):
        return ()

    def two(self, *wait):
        return self.half

    def halves(self):
        return self.half, self.rest

    def add(self, mine, other):
        self.mine.append(mine.astype(BF))
        self.other.append(other.astype(BF))
        return mine

    def columns(self):
        parts = [jnp.concatenate(item, 1) for item in (self.mine, self.other)]
        return lax.psum_scatter(jnp.stack(parts, 1), AXES, scatter_dimension=0, tiled=True).astype(F32)

    def sums(self):
        count = lax.axis_size(AXES)
        mine, other = [item[0].reshape(count // 2, -1, item[0].shape[1]) for item in (self.mine, self.other)]
        sums = jnp.stack([mine, other], 1).reshape(-1, mine.shape[-1])
        return lax.psum_scatter(sums, AXES, scatter_dimension=0, tiled=True).astype(F32)


def body(
    fast,
    tokens,
    mask_bits,
    timesteps,
    cotangent,
    w_qkv,
    w_out,
    w_up,
    w_down,
    time_table,
    b_query,
    b_value,
    b_out,
    b_up,
    b_down,
    gain_attn,
    shift_attn,
    gain_mlp,
    shift_mlp,
    mask_vector,
):
    tree = Tree() if fast else Whole()
    gather_columns = functools.partial(Gather.columns, tree) if fast else Whole.columns_of
    gather_rows = functools.partial(Gather.rows, tree) if fast else Whole.rows_of
    reduction = functools.partial(Reduce, tree) if fast else Whole
    core = tree.core
    count = lax.axis_size(AXES)
    chips = count // 2
    place = lax.axis_index(AXES)
    width = tokens.shape[1]
    part = width // count
    hidden_width = w_up.shape[1]
    hidden_part = hidden_width // count
    seq_count = timesteps.shape[0]
    seq_length = tokens.shape[0] // seq_count
    row_count = tokens.shape[0]
    half = width // 2
    table_cols = time_table.shape[1]
    absorbed = (mask_bits == 1)[:, None]
    absorbed_float = mask_bits.astype(F32)[:, None]
    sides = (core, 1 - core)

    small = [b_query, b_value, b_out, b_down, gain_attn, shift_attn, gain_mlp, shift_mlp, mask_vector]
    fixed = len(small)
    up_cols = hidden_part // part
    seq_cols = -(-2 * seq_count // part)
    steps = jnp.concatenate([timesteps // 256, timesteps % 256]).astype(F32)
    steps = jnp.pad(steps, (0, seq_cols * part - 2 * seq_count)).reshape(seq_cols, part)
    small = jnp.concatenate([jnp.stack(small), b_up.reshape(up_cols, part), steps], 0)
    small_cols = small.shape[0]
    all_cols = -(-(table_cols + small_cols) // (2 * LANES)) * (2 * LANES)
    table_half = all_cols // 2
    small = jnp.pad(small, ((0, all_cols - table_cols - small_cols), (0, 0)))
    table = jnp.concatenate([time_table, small.T], 1).astype(BF).reshape(part, 2, table_half)

    qkv = w_qkv.astype(BF).reshape(part, 3, 2, half)
    shard = [qkv[:, 0], qkv[:, 1], qkv[:, 2], w_out.astype(BF).reshape(part, 2, half), table]
    attn_w = gather_columns(jnp.concatenate(shard, 2))
    up_w = gather_columns(
        w_up.astype(BF)
        .reshape(part, chips, 2, hidden_part)
        .transpose(0, 2, 1, 3)
        .reshape(part, 2, hidden_width // 2)
    )
    down_w = gather_rows(w_down.astype(BF))
    attn_z = attn_w.along_z()
    up_z = up_w.along_z(attn_z)
    attn_one = attn_w.one()
    down_z = down_w.along_z(up_z)
    attn_w.two()
    up_one = up_w.one(attn_w.half)
    attn_w = attn_w.halves()
    out_w = jnp.concatenate(
        [
            jnp.where(core == 0, *[w[:, 3 * half : 4 * half] for w in pair])
            for pair in (attn_w, attn_w[::-1])
        ],
        1,
    )

    chosen = jnp.concatenate([timesteps, table_cols + jnp.arange(small_cols, dtype=jnp.int32)])
    rows = 0.0
    for side, weight in zip(sides, attn_w):
        columns = lax.broadcasted_iota(jnp.int32, (seq_count + small_cols, table_half), 1) + side * table_half
        rows = rows + right_product((chosen[:, None] == columns).astype(BF), weight[:, 4 * half :])
    table_rows = rows[:seq_count]
    rows = rows[seq_count:]
    bias_query, bias_value, bias_out, bias_down, gain_one, shift_one, gain_two, shift_two, mask_row = [
        rows[i] for i in range(fixed)
    ]
    bias_up = rows[fixed : fixed + up_cols].reshape(up_cols, chips, 2, part).transpose(2, 1, 0, 3)
    bias_up = bias_up.reshape(2, 1, hidden_width // 2)
    bias_up = [pick(bias_up, side, 0) for side in sides]
    steps = rows[fixed + up_cols :].reshape(seq_cols, count, part).transpose(1, 0, 2).reshape(count, -1)
    steps = steps.astype(jnp.int32)
    steps = (steps[:, :seq_count] * 256 + steps[:, seq_count : 2 * seq_count]).reshape(-1)
    bias_qkv = jnp.stack([bias_query, jnp.zeros_like(bias_query), bias_value]).reshape(3, 2, half)
    bias_qkv = [pick(bias_qkv, side, 1) for side in sides]

    start = jnp.where(absorbed, mask_row[None, :], tokens)
    start = (start.reshape(seq_count, seq_length, width) + table_rows[:, None, :]).reshape(row_count, width)
    normed_one = layer_norm(start, gain_one, shift_one).astype(BF)
    across_one = normed_one.T
    qkv_mine, context_mine = attention(normed_one, attn_w[0], bias_qkv[0], seq_length)
    up_half = up_w.two(context_mine)
    qkv_other, context_other = attention(after(normed_one, up_one), attn_w[1], bias_qkv[1], seq_length)
    context = jnp.concatenate(
        [
            jnp.where(core == 0, context_mine, context_other),
            jnp.where(core == 0, context_other, context_mine),
        ],
        1,
    )
    middle = start + (product(context, out_w) + bias_out)
    down_one = down_w.one(up_half, context_other)
    up_w = up_w.halves()
    normed_two = layer_norm(middle, gain_two, shift_two).astype(BF)
    across_two = normed_two.T
    down_w.two(normed_two)
    hidden, slope = [None, None], [None, None]
    hidden[0], slope[0] = feed(normed_two, up_w[0], bias_up[0])
    hidden[1], slope[1] = feed(after(normed_two, down_one), up_w[1], bias_up[1])
    down_w = down_w.halves()

    grad_output = cotangent * absorbed_float
    grad_branch = grad_output.astype(BF)
    down_sum = reduction(hidden_part)
    down_got = down_sum.add(left_product(hidden[0], grad_branch), left_product(hidden[1], grad_branch))
    grad_b_down = column_sums(grad_branch)
    up_sum = reduction(2 * part)
    grad_pre, grad_b_up, grad_up = [None, None], [None, None], [None, None]
    grad_pre[1], grad_b_up[1], grad_up[1] = feed_back(grad_branch, down_w[1], slope[1], across_two, BF)
    if fast:
        down_sum.one()
    grad_pre[0], grad_b_up[0], grad_up[0] = feed_back(
        after(grad_branch, down_sum.sent), down_w[0], slope[0], across_two, F32
    )
    up_sum.add(grad_up[0], grad_up[1])
    if fast:
        down_sum.two()
    grad_pre = after(grad_pre, down_sum.sent)
    grad_normed_two = right_product(grad_pre[0], up_w[0]) + right_product(grad_pre[1], up_w[1])
    _, norm_pull = jax.vjp(layer_norm, middle, gain_two, shift_two)
    back_middle, grad_gain_mlp, grad_shift_mlp = norm_pull(grad_normed_two)
    grad_middle = grad_output + back_middle

    grad_attn = grad_middle.astype(BF)
    grad_halves = [lax.dynamic_slice_in_dim(grad_attn, side * half, half, 1) for side in sides]
    attn_sum = reduction(2 * part)
    grad_out = [left_product(context, item) for item in grad_halves]
    grad_b_out = column_sums(grad_attn)
    grad_context = right_product(grad_attn, out_w).astype(BF)
    grad_context = [lax.dynamic_slice_in_dim(grad_context, side * half, half, 1) for side in sides]
    if fast:
        down_sum.along_z()
        up_sum.one()
    grads = [None, None]
    grads[1] = attention_back(
        qkv_other, after(grad_context[1], down_sum.sent, up_sum.sent), across_one, seq_length, BF
    )
    if fast:
        up_sum.two()
    grads[0] = attention_back(
        qkv_mine, after(grad_context[0], down_sum.got, up_sum.sent), across_one, seq_length, F32
    )
    grad_qkv, grad_weights, sums = zip(*grads)
    for index in range(3):
        attn_sum.add(grad_weights[0][index], grad_weights[1][index])
    attn_sum.add(grad_out[0], grad_out[1])
    if fast:
        up_sum.along_z()
    grad_qkv = after(grad_qkv, up_sum.sent)
    grad_normed_one = sum(
        right_product(grad_qkv[i][j], attn_w[i][:, j * half : (j + 1) * half]) for i in range(2) for j in range(3)
    )
    _, norm_pull = jax.vjp(layer_norm, start, gain_one, shift_one)
    back_start, grad_gain_attn, grad_shift_attn = norm_pull(grad_normed_one)
    grad_start = grad_middle + back_start
    grad_tokens = jnp.where(absorbed, 0.0, grad_start)
    grad_mask_vector = jnp.sum(grad_start * absorbed_float, 0)
    seq_sums = jnp.sum(grad_start.reshape(seq_count, seq_length, width), 1)

    grad_b_up = paired(core, *[item.reshape(chips, hidden_part) for item in grad_b_up], 1)
    grad_b_up = grad_b_up.reshape(count, up_cols, part).transpose(1, 0, 2).reshape(up_cols, width)
    grad_b_qkv = paired(core, sums[0], sums[1], 1).reshape(3, width)
    small = jnp.stack(
        [
            grad_b_qkv[0],
            grad_b_qkv[2],
            grad_b_out,
            grad_b_down,
            grad_gain_attn,
            grad_shift_attn,
            grad_gain_mlp,
            grad_shift_mlp,
            grad_mask_vector,
        ]
    )
    seqs = count * seq_count
    small = jnp.concatenate([small, grad_b_up], 0)
    blocks = jnp.pad(small, ((0, seqs + LANES - small.shape[0]), (0, 0)))
    blocks = lax.dynamic_update_slice(blocks, seq_sums, (LANES + place * seq_count, 0)).T
    blocks = [blocks[:, :LANES], blocks[:, LANES:]]
    if fast:
        attn_sum.add(jnp.where(core == 0, *blocks), jnp.where(core == 0, *blocks[::-1]))
        attn_sum.one()
        attn_sum.two()
        attn_sum.along_z()
        attn_grad = attn_sum.columns()
        small, seq_sums = attn_grad[:, 0, 4 * half :], attn_grad[:, 1, 4 * half :]
    else:
        attn_grad = attn_sum.columns()
        small, seq_sums = [
            lax.psum_scatter(item.astype(BF), AXES, scatter_dimension=0, tiled=True).astype(F32) for item in blocks
        ]
    small = small[:, : fixed + up_cols].T
    grad_b_up = small[fixed:].reshape(hidden_part)
    onehot = (steps[:, None] == lax.broadcasted_iota(jnp.int32, (seqs, table_cols), 1)).astype(F32)
    grad_time_table = jnp.dot(seq_sums, onehot, precision=lax.Precision.HIGHEST)
    grad_w_qkv = attn_grad[:, :, : 3 * half].reshape(part, 2, 3, half).transpose(0, 2, 1, 3).reshape(part, 3 * width)
    grad_w_out = attn_grad[:, :, 3 * half : 4 * half].reshape(part, width)
    grad_w_up = up_sum.columns().reshape(part, 2, chips, hidden_part).transpose(0, 2, 1, 3)
    grad_w_up = grad_w_up.reshape(part, hidden_width)
    output = middle + (product(hidden[0], down_w[0]) + product(hidden[1], down_w[1]) + bias_down)
    return (
        output,
        grad_tokens,
        grad_w_qkv,
        grad_w_out,
        grad_w_up,
        down_sum.sums(),
        grad_time_table,
        small[0],
        small[1],
        small[2],
        grad_b_up,
        small[3],
        small[4],
        small[5],
        small[6],
        small[7],
        small[8],
    )


def solution(mesh):
    matrix, vector = P(AXES, None), P(AXES)
    fast = dict(mesh.shape) == {"fsdp": 8, "rep": 4}
    return jax.shard_map(
        functools.partial(body, fast),
        mesh=mesh,
        in_specs=(matrix, vector, vector) + (matrix,) * 6 + (vector,) * 10,
        out_specs=(matrix,) * 7 + (vector,) * 10,
        check_vma=False,
    )
```

```python
import functools
import math

import jax
import jax.numpy as jnp
from jax import lax
from jax.experimental import pallas as pl
from jax.experimental.pallas import tpu as pltpu
from jax.sharding import PartitionSpec as P

HDIM = 64
EPSILON = 1e-05
AXES = ("fsdp", "rep")
BF = jnp.bfloat16
F32 = jnp.float32
LANES = 128
VMEM_BYTES = 32 << 20
GELU_OUTER = math.sqrt(2.0 / math.pi)
GELU_INNER = 0.044715


def contract(left, right, left_dim, right_dim):
    dims = (((left_dim,), (right_dim,)), ((), ()))
    return lax.dot_general(left, right, dims, preferred_element_type=F32)


def product(left, right):
    return contract(left, right, 1, 0)


def left_product(left, right):
    return contract(left, right, 0, 0)


def right_product(left, right):
    return contract(left, right, 1, 1)


def pick(array, index, axis):
    return lax.dynamic_index_in_dim(array, index, axis, keepdims=False)


def paired(bit, mine, other, axis):
    return jnp.stack([jnp.where(bit == 0, mine, other), jnp.where(bit == 0, other, mine)], axis)


def after(value, *others):
    return lax.optimization_barrier((value, others))[0]


def lane_masks(factor):
    lane = lax.broadcasted_iota(jnp.int32, (1, LANES), 1)
    return [jnp.where((lane < HDIM) == (head == 0), factor, 0.0).astype(BF) for head in (0, 1)]


def softmax(scores):
    powers = jnp.exp(scores - jnp.max(scores, -1, keepdims=True))
    return powers * (1.0 / jnp.sum(powers, -1, keepdims=True))


def attention_kernel(length, scale, rows_ref, query_ref, key_ref, value_ref, bias_ref, qkv_ref, context_ref):
    rows = rows_ref[...]
    for index, weight in enumerate((query_ref, key_ref, value_ref)):
        qkv_ref[index] = (product(rows, weight[...]) + bias_ref[index : index + 1, :]).astype(BF)
    ones, scaled = lane_masks(1.0), lane_masks(scale)

    for sequence in range(rows.shape[0] // length):
        span = slice(sequence * length, (sequence + 1) * length)
        queries, key_rows, value_rows = [qkv_ref[index, span, :] for index in range(3)]
        total = 0.0
        for head in (0, 1):
            probs = softmax(right_product(queries * scaled[head], key_rows)).astype(BF)
            total = total + product(probs, value_rows * ones[head])
        context_ref[span, :] = total.astype(BF)


def attention(rows, weight, bias, length):
    tokens, width = rows.shape
    half = bias.shape[1]
    pairs = half // LANES

    def weight_spec(index):
        return pl.BlockSpec((width, LANES), lambda pair: (0, index * pairs + pair))

    return pl.pallas_call(
        functools.partial(attention_kernel, length, 1.0 / math.sqrt(HDIM)),
        grid=(pairs,),
        in_specs=[
            pl.BlockSpec((tokens, width), lambda pair: (0, 0)),
            weight_spec(0),
            weight_spec(1),
            weight_spec(2),
            pl.BlockSpec((8, LANES), lambda pair: (0, pair)),
        ],
        out_specs=[
            pl.BlockSpec((3, tokens, LANES), lambda pair: (0, 0, pair)),
            pl.BlockSpec((tokens, LANES), lambda pair: (0, pair)),
        ],
        out_shape=[
            jax.ShapeDtypeStruct((3, tokens, half), BF),
            jax.ShapeDtypeStruct((tokens, half), BF),
        ],
        compiler_params=pltpu.CompilerParams(vmem_limit_bytes=VMEM_BYTES),
        cost_estimate=pl.CostEstimate(
            flops=6 * tokens * width * half,
            bytes_accessed=2 * tokens * width + 6 * width * half + 8 * tokens * half,
            transcendentals=2 * tokens * length * pairs,
        ),
        name="attention",
    )(rows, weight, weight, weight, bias)


def attention_back_kernel(length, scale, qkv_ref, grad_ref, rows_ref, grads_ref, weight_ref, sums_ref):
    ones, scaled = lane_masks(1.0), lane_masks(scale)

    for sequence in range(grad_ref.shape[0] // length):
        span = slice(sequence * length, (sequence + 1) * length)
        queries, key_rows, value_rows = [qkv_ref[index, span, :] for index in range(3)]
        grad = grad_ref[span, :]
        grad_queries, grad_keys, grad_values = 0.0, 0.0, 0.0
        for head in (0, 1):
            probs = softmax(right_product(queries * scaled[head], key_rows))
            grad_head = grad * ones[head]
            grad_probs = right_product(grad_head, value_rows)
            grad_scores = probs * (grad_probs - jnp.sum(grad_probs * probs, -1, keepdims=True))
            grad_scores = grad_scores.astype(BF)
            grad_values = grad_values + left_product(probs.astype(BF), grad_head)
            grad_queries = grad_queries + product(grad_scores, key_rows * ones[head])
            grad_keys = grad_keys + left_product(grad_scores, queries * ones[head])
        grads_ref[0, span, :] = (grad_queries * scale).astype(BF)
        grads_ref[1, span, :] = (grad_keys * scale).astype(BF)
        grads_ref[2, span, :] = grad_values.astype(BF)

    rows = rows_ref[...]
    for index in range(3):
        grads = grads_ref[index]
        weight_ref[index] = product(rows, grads).astype(weight_ref.dtype)
        sums_ref[index : index + 1, :] = jnp.sum(grads.astype(F32), 0, keepdims=True)


def attention_back(qkv, grad, rows_across, length, dtype):
    _, tokens, half = qkv.shape
    width = rows_across.shape[0]
    pairs = half // LANES
    return pl.pallas_call(
        functools.partial(attention_back_kernel, length, 1.0 / math.sqrt(HDIM)),
        grid=(pairs,),
        in_specs=[
            pl.BlockSpec((3, tokens, LANES), lambda pair: (0, 0, pair)),
            pl.BlockSpec((tokens, LANES), lambda pair: (0, pair)),
            pl.BlockSpec((width, tokens), lambda pair: (0, 0)),
        ],
        out_specs=[
            pl.BlockSpec((3, tokens, LANES), lambda pair: (0, 0, pair)),
            pl.BlockSpec((3, width, LANES), lambda pair: (0, 0, pair)),
            pl.BlockSpec((3, LANES), lambda pair: (0, pair)),
        ],
        out_shape=[
            jax.ShapeDtypeStruct((3, tokens, half), BF),
            jax.ShapeDtypeStruct((3, width, half), dtype),
            jax.ShapeDtypeStruct((3, half), F32),
        ],
        compiler_params=pltpu.CompilerParams(vmem_limit_bytes=VMEM_BYTES),
        cost_estimate=pl.CostEstimate(
            flops=6 * tokens * width * half,
            bytes_accessed=2 * tokens * width + 12 * width * half + 14 * tokens * half,
            transcendentals=2 * tokens * length * pairs,
        ),
        name="attention_back",
    )(qkv, grad, rows_across)


def feed_kernel(side, rows_ref, weight_ref, bias_ref, hidden_ref, slope_ref, pre_ref):
    pre_ref[...] = product(rows_ref[...], weight_ref[...])
    step = 32

    def chunk(index, carry):
        span = pl.ds(pl.multiple_of(index * step, step), step)
        pre = pre_ref[span, :] + bias_ref[side : side + 1, :]
        square = pre * pre
        bend = jnp.tanh(GELU_OUTER * (pre + GELU_INNER * (square * pre)))
        share = 0.5 * (1.0 + bend)
        hidden_ref[span, :] = (pre * share).astype(BF)
        inner = (0.5 * GELU_OUTER) * pre * (1.0 + (3.0 * GELU_INNER) * square)
        slope_ref[span, :] = share + inner * (1.0 - bend * bend)
        return carry

    lax.fori_loop(0, rows_ref.shape[0] // step, chunk, 0, unroll=2)


def feed(rows, weight, bias, side, block=512):
    tokens, width = rows.shape
    columns = weight.shape[1]
    block = math.gcd(block, columns)
    out = pl.BlockSpec((tokens, block), lambda step: (0, step))
    return pl.pallas_call(
        functools.partial(feed_kernel, side),
        grid=(columns // block,),
        in_specs=[
            pl.BlockSpec((tokens, width), lambda step: (0, 0)),
            pl.BlockSpec((width, block), lambda step: (0, step)),
            pl.BlockSpec((8, block), lambda step: (0, step)),
        ],
        out_specs=[out, out],
        out_shape=[
            jax.ShapeDtypeStruct((tokens, columns), BF),
            jax.ShapeDtypeStruct((tokens, columns), F32),
        ],
        scratch_shapes=[pltpu.VMEM((tokens, block), F32)],
        compiler_params=pltpu.CompilerParams(vmem_limit_bytes=VMEM_BYTES),
        cost_estimate=pl.CostEstimate(
            flops=2 * tokens * width * columns,
            bytes_accessed=2 * tokens * width + 2 * width * columns + 6 * tokens * columns,
            transcendentals=tokens * columns,
        ),
        name="feed",
    )(rows, weight, bias)


def feed_back_kernel(grad_ref, weight_ref, slope_ref, rows_ref, pre_ref, sum_ref, up_ref):
    grad = (right_product(grad_ref[...], weight_ref[...]) * slope_ref[...]).astype(BF)
    pre_ref[...] = grad
    sum_ref[...] = jnp.sum(grad.astype(F32), 0, keepdims=True)
    up_ref[...] = product(rows_ref[...], grad).astype(up_ref.dtype)


def feed_back(grad, weight, slope, rows_across, dtype, block=512):
    tokens, width = grad.shape
    columns = weight.shape[0]
    block = math.gcd(block, columns)
    out = pl.BlockSpec((tokens, block), lambda step: (0, step))
    return pl.pallas_call(
        feed_back_kernel,
        grid=(columns // block,),
        in_specs=[
            pl.BlockSpec((tokens, width), lambda step: (0, 0)),
            pl.BlockSpec((block, width), lambda step: (step, 0)),
            out,
            pl.BlockSpec((width, tokens), lambda step: (0, 0)),
        ],
        out_specs=[
            out,
            pl.BlockSpec((1, block), lambda step: (0, step)),
            pl.BlockSpec((width, block), lambda step: (0, step)),
        ],
        out_shape=[
            jax.ShapeDtypeStruct((tokens, columns), BF),
            jax.ShapeDtypeStruct((1, columns), F32),
            jax.ShapeDtypeStruct((width, columns), dtype),
        ],
        compiler_params=pltpu.CompilerParams(vmem_limit_bytes=VMEM_BYTES),
        cost_estimate=pl.CostEstimate(
            flops=4 * tokens * width * columns,
            bytes_accessed=4 * tokens * width + 6 * width * columns + 6 * tokens * columns,
            transcendentals=0,
        ),
        name="feed_back",
    )(grad, weight, slope, rows_across)


def chosen_side(core, mine, other):
    return jnp.where(core == 0, mine, other), jnp.where(core == 0, other, mine)


def normalized(values):
    center = values - jnp.mean(values, -1, keepdims=True)
    rate = lax.rsqrt(jnp.mean(center * center, -1, keepdims=True) + EPSILON)
    return center * rate, rate


def start_kernel(
    fixed, up_cols, table_cols, seq_count, parts,
    place_ref, tokens_ref, mask_ref, table_mine_ref, table_other_ref,
    rows_ref, start_ref, normed_ref, across_ref, bias_mine_ref, bias_other_ref, bias_up_ref,
):
    core = place_ref[0]
    step = pl.program_id(0)
    width = tokens_ref.shape[1]
    half = width // 2
    chips, part, hidden_part = parts

    @pl.when(step == 0)
    def _():
        count, columns = rows_ref.shape[0], table_mine_ref.shape[1]
        row = lax.broadcasted_iota(jnp.int32, (count, columns), 0)
        wanted = table_cols + row - seq_count
        for index in range(seq_count):
            wanted = jnp.where(row == index, place_ref[2 + index], wanted)
        column = lax.broadcasted_iota(jnp.int32, (count, columns), 1)
        rows = 0.0
        for side, table in ((core, table_mine_ref), (1 - core, table_other_ref)):
            hit = jnp.where(wanted == column + side * columns, 1.0, 0.0).astype(BF)
            rows = rows + right_product(hit, table[...])
        rows_ref[...] = rows
        for ref, side in ((bias_mine_ref, core), (bias_other_ref, 1 - core)):
            ref[...] = jnp.zeros_like(ref)
            for index in (0, 1):
                line = rows_ref[seq_count + index : seq_count + index + 1, :]
                ref[2 * index : 2 * index + 1, :] = jnp.where(side == 0, line[:, :half], line[:, half:])
        for chip in range(chips):
            for index in range(up_cols):
                line = rows_ref[seq_count + fixed + index : seq_count + fixed + index + 1, :]
                pair = [line[:, (2 * chip + i) * part : (2 * chip + i + 1) * part] for i in range(2)]
                where = slice(chip * hidden_part + index * part, chip * hidden_part + (index + 1) * part)
                bias_up_ref[0:1, where], bias_up_ref[1:2, where] = chosen_side(core, *pair)

    small = seq_count
    mask = mask_ref[...]
    start = jnp.where(mask > 0.0, rows_ref[small + 8 : small + 9, :], tokens_ref[...])
    start = start + rows_ref[pl.ds(step, 1), :]
    start_ref[...] = start
    normed, _ = normalized(start)
    normed = normed * rows_ref[small + 4 : small + 5, :] + rows_ref[small + 5 : small + 6, :]
    normed_ref[...] = normed.astype(BF)
    across_ref[...] = normed.T.astype(BF)


def start_rows(place, tokens, mask, weights, fixed, up_cols, table_cols, small_cols, chips, hidden_part):
    count, width = tokens.shape
    seq_count = place.shape[0] - 2
    length = count // seq_count
    half = width // 2
    row_count = -(-(seq_count + small_cols) // 8) * 8
    table_half = weights[0].shape[1] - 4 * half
    tables = 4 * half // table_half
    table_spec = pl.BlockSpec((width, table_half), lambda step: (0, tables))
    rows_spec = pl.BlockSpec((length, width), lambda step: (step, 0))

    def fixed_spec(*shape):
        return pl.BlockSpec(shape, lambda step: (0,) * len(shape))

    return pl.pallas_call(
        functools.partial(
            start_kernel, fixed, up_cols, table_cols, seq_count, (chips, width // (2 * chips), hidden_part)
        ),
        grid=(seq_count,),
        in_specs=[
            pl.BlockSpec(memory_space=pltpu.SMEM),
            rows_spec,
            pl.BlockSpec((length, 1), lambda step: (step, 0)),
            table_spec,
            table_spec,
        ],
        out_specs=[
            fixed_spec(row_count, width),
            rows_spec,
            rows_spec,
            pl.BlockSpec((width, length), lambda step: (0, step)),
            fixed_spec(8, half),
            fixed_spec(8, half),
            fixed_spec(8, chips * hidden_part),
        ],
        out_shape=[
            jax.ShapeDtypeStruct((row_count, width), F32),
            jax.ShapeDtypeStruct((count, width), F32),
            jax.ShapeDtypeStruct((count, width), BF),
            jax.ShapeDtypeStruct((width, count), BF),
            jax.ShapeDtypeStruct((8, half), F32),
            jax.ShapeDtypeStruct((8, half), F32),
            jax.ShapeDtypeStruct((8, chips * hidden_part), F32),
        ],
        compiler_params=pltpu.CompilerParams(vmem_limit_bytes=VMEM_BYTES),
        cost_estimate=pl.CostEstimate(
            flops=4 * row_count * width * table_half, bytes_accessed=14 * count * width, transcendentals=0
        ),
        name="start_rows",
    )(place, tokens, mask, *weights)


def middle_kernel(
    small, place_ref, context_mine_ref, context_other_ref, out_mine_ref, out_other_ref, start_ref, rows_ref,
    middle_ref, normed_ref, across_ref,
):
    core = place_ref[0]
    half = context_mine_ref.shape[1]
    contexts = chosen_side(core, context_mine_ref[...], context_other_ref[...])
    outs = chosen_side(core, out_mine_ref[...], out_other_ref[...])
    for index, out in enumerate(outs):
        span = slice(index * half, (index + 1) * half)
        total = product(contexts[0], out[:half]) + product(contexts[1], out[half:])
        middle_ref[:, span] = start_ref[:, span] + (total + rows_ref[small + 2 : small + 3, span])
    normed, _ = normalized(middle_ref[...])
    normed = normed * rows_ref[small + 6 : small + 7, :] + rows_ref[small + 7 : small + 8, :]
    normed_ref[...] = normed.astype(BF)
    across_ref[...] = normed.T.astype(BF)


def middle_rows(place, contexts, weights, start, rows, block=256):
    count, width = start.shape
    half = width // 2
    small = place.shape[0] - 2
    block = math.gcd(block, count)
    out_spec = pl.BlockSpec((width, half), lambda step: (0, 3))
    rows_spec = pl.BlockSpec((block, width), lambda step: (step, 0))
    half_spec = pl.BlockSpec((block, half), lambda step: (step, 0))
    return pl.pallas_call(
        functools.partial(middle_kernel, small),
        grid=(count // block,),
        in_specs=[
            pl.BlockSpec(memory_space=pltpu.SMEM),
            half_spec,
            half_spec,
            out_spec,
            out_spec,
            rows_spec,
            pl.BlockSpec(rows.shape, lambda step: (0, 0)),
        ],
        out_specs=[rows_spec, rows_spec, pl.BlockSpec((width, block), lambda step: (0, step))],
        out_shape=[
            jax.ShapeDtypeStruct((count, width), F32),
            jax.ShapeDtypeStruct((count, width), BF),
            jax.ShapeDtypeStruct((width, count), BF),
        ],
        compiler_params=pltpu.CompilerParams(vmem_limit_bytes=VMEM_BYTES),
        cost_estimate=pl.CostEstimate(
            flops=2 * count * width * width, bytes_accessed=14 * count * width + 2 * width * width, transcendentals=0
        ),
        name="middle_rows",
    )(place, *contexts, *weights, start, rows)


def norm_back(values, gain, grad):
    unit, rate = normalized(values)
    scaled = grad * gain
    back = scaled - jnp.mean(scaled, -1, keepdims=True) - unit * jnp.mean(scaled * unit, -1, keepdims=True)
    return rate * back, grad * unit


def middle_back_kernel(
    small, place_ref, pre_mine_ref, pre_other_ref, up_mine_ref, up_other_ref, middle_ref, cotangent_ref, mask_ref,
    rows_ref, context_mine_ref, context_other_ref, out_mine_ref, out_other_ref,
    grad_ref, context_grad_mine_ref, context_grad_other_ref, out_grad_mine_ref, out_grad_other_ref, sums_ref,
    normed_ref, total_ref,
):
    core = place_ref[0]
    step = pl.program_id(0)
    half = context_mine_ref.shape[1]

    @pl.when(step == 0)
    def _():
        sums_ref[...] = jnp.zeros_like(sums_ref)
        total_ref[...] = jnp.zeros_like(total_ref)

    normed_ref[...] = right_product(pre_mine_ref[...], up_mine_ref[...]) + right_product(
        pre_other_ref[...], up_other_ref[...]
    )
    grad = normed_ref[...]
    direct = cotangent_ref[...] * mask_ref[...]
    back, shares = norm_back(middle_ref[...], rows_ref[small + 6 : small + 7, :], grad)
    back = direct + back
    grad_ref[...] = back
    low = back.astype(BF)
    for index, item in enumerate((low.astype(F32), direct.astype(BF).astype(F32), shares, grad)):
        sums_ref[index : index + 1, :] += jnp.sum(item, 0, keepdims=True)
    lows = (low[:, :half], low[:, half:])
    contexts = chosen_side(core, context_mine_ref[...], context_other_ref[...])
    outs = chosen_side(core, out_mine_ref[...], out_other_ref[...])
    context_grads = [
        (right_product(lows[0], outs[0][span]) + right_product(lows[1], outs[1][span])).astype(BF)
        for span in (slice(0, half), slice(half, None))
    ]
    context_grad_mine_ref[...], context_grad_other_ref[...] = chosen_side(core, *context_grads)
    for index, item in enumerate(chosen_side(core, *lows)):
        for side, context in enumerate(contexts):
            total_ref[index, side * half : (side + 1) * half, :] += left_product(context, item)

    @pl.when(step == pl.num_programs(0) - 1)
    def _():
        out_grad_mine_ref[...] = total_ref[0]
        out_grad_other_ref[...] = total_ref[1].astype(BF)


def middle_back(place, grads, ups, middle, cotangent, mask, rows, contexts, weights, block=256):
    count, width = middle.shape
    half = width // 2
    hidden_half = ups[0].shape[1]
    small = place.shape[0] - 2
    block = math.gcd(block, count)

    def over_rows(columns):
        return pl.BlockSpec((block, columns), lambda step: (step, 0))

    def whole(*shape):
        return pl.BlockSpec(shape, lambda step: (0,) * len(shape))

    out_spec = pl.BlockSpec((width, half), lambda step: (0, 3))
    return pl.pallas_call(
        functools.partial(middle_back_kernel, small),
        grid=(count // block,),
        in_specs=[
            pl.BlockSpec(memory_space=pltpu.SMEM),
            over_rows(hidden_half),
            over_rows(hidden_half),
            whole(width, hidden_half),
            whole(width, hidden_half),
            over_rows(width),
            over_rows(width),
            over_rows(1),
            whole(*rows.shape),
            over_rows(half),
            over_rows(half),
            out_spec,
            out_spec,
        ],
        out_specs=[
            over_rows(width),
            over_rows(half),
            over_rows(half),
            whole(width, half),
            whole(width, half),
            whole(8, width),
        ],
        out_shape=[
            jax.ShapeDtypeStruct((count, width), F32),
            jax.ShapeDtypeStruct((count, half), BF),
            jax.ShapeDtypeStruct((count, half), BF),
            jax.ShapeDtypeStruct((width, half), F32),
            jax.ShapeDtypeStruct((width, half), BF),
            jax.ShapeDtypeStruct((8, width), F32),
        ],
        scratch_shapes=[pltpu.VMEM((block, width), F32), pltpu.VMEM((2, width, half), F32)],
        compiler_params=pltpu.CompilerParams(vmem_limit_bytes=VMEM_BYTES),
        cost_estimate=pl.CostEstimate(
            flops=4 * count * width * (hidden_half + width),
            bytes_accessed=4 * count * hidden_half + 4 * width * hidden_half + 16 * count * width,
            transcendentals=0,
        ),
        name="middle_back",
    )(place, *grads, *ups, middle, cotangent, mask, rows, *contexts, *weights)


def start_back_kernel(
    small, length, place_ref, grads_mine_ref, grads_other_ref, weight_mine_ref, weight_other_ref, start_ref, middle_ref,
    mask_ref, rows_ref, sums_ref, sums_mine_ref, sums_other_ref,
    tokens_ref, blocks_ref, lines_ref,
):
    core, place = place_ref[0], place_ref[1]
    step = pl.program_id(0)
    width = start_ref.shape[1]
    half = width // 2
    seqs = start_ref.shape[0] // length

    @pl.when(step == 0)
    def _():
        lines_ref[...] = jnp.zeros_like(lines_ref)
        for index, row in ((0, 0), (1, 2)):
            pair = (sums_mine_ref[row : row + 1, :], sums_other_ref[row : row + 1, :])
            lines_ref[index : index + 1, :half], lines_ref[index : index + 1, half:] = chosen_side(core, *pair)
        lines_ref[2:4, :] = sums_ref[0:2, :]
        lines_ref[6:8, :] = sums_ref[2:4, :]

    grad = 0.0
    for grads, weight in ((grads_mine_ref, weight_mine_ref), (grads_other_ref, weight_other_ref)):
        for index in range(3):
            grad = grad + right_product(grads[index], weight[:, index * half : (index + 1) * half])
    back, shares = norm_back(start_ref[...], rows_ref[small + 4 : small + 5, :], grad)
    back = middle_ref[...] + back
    mask = mask_ref[...]
    tokens_ref[...] = jnp.where(mask > 0.0, 0.0, back)
    for index, item in ((4, shares), (5, grad), (8, back * mask)):
        lines_ref[index : index + 1, :] += jnp.sum(item, 0, keepdims=True)
    for index in range(seqs):
        line = LANES + place * small + step * seqs + index
        lines_ref[pl.ds(line, 1), :] = jnp.sum(back[index * length : (index + 1) * length], 0, keepdims=True)

    @pl.when(step == pl.num_programs(0) - 1)
    def _():
        blocks_ref[...] = lines_ref[...].T


def start_back(place, grads, weights, start, middle, mask, rows, sums, side_sums, seqs, length, block=256):
    count, width = start.shape
    half = width // 2
    small = place.shape[0] - 2
    block = math.gcd(block, count)
    lines = LANES + -(-seqs // LANES) * LANES

    def over_rows(columns):
        return pl.BlockSpec((block, columns), lambda step: (step, 0))

    def whole(*shape):
        return pl.BlockSpec(shape, lambda step: (0,) * len(shape))

    grads_spec = pl.BlockSpec((3, block, half), lambda step: (0, step, 0))
    return pl.pallas_call(
        functools.partial(start_back_kernel, small, length),
        grid=(count // block,),
        in_specs=[
            pl.BlockSpec(memory_space=pltpu.SMEM),
            grads_spec,
            grads_spec,
            whole(width, 3 * half),
            whole(width, 3 * half),
            over_rows(width),
            over_rows(width),
            over_rows(1),
            whole(*rows.shape),
            whole(*sums.shape),
            whole(*side_sums[0].shape),
            whole(*side_sums[1].shape),
        ],
        out_specs=[over_rows(width), whole(width, lines)],
        out_shape=[
            jax.ShapeDtypeStruct((count, width), F32),
            jax.ShapeDtypeStruct((width, lines), F32),
        ],
        scratch_shapes=[pltpu.VMEM((lines, width), F32)],
        compiler_params=pltpu.CompilerParams(vmem_limit_bytes=VMEM_BYTES),
        cost_estimate=pl.CostEstimate(
            flops=4 * count * width * 3 * half,
            bytes_accessed=12 * count * half + 12 * width * half + 12 * count * width,
            transcendentals=0,
        ),
        name="start_back",
    )(place, *grads, *weights, start, middle, mask, rows, sums, *side_sums)


class Tree:
    def __init__(self):
        fsdp, rep = lax.axis_index("fsdp"), lax.axis_index("rep")
        self.z, self.y, self.x, self.core = fsdp // 2, fsdp % 2, rep // 2, rep % 2

    def to_core(self, value):
        return lax.ppermute(value, "rep", [(i, i ^ 1) for i in range(4)])

    def to_x(self, value):
        return lax.ppermute(value, "rep", [(i, i ^ 2) for i in range(4)])

    def to_y(self, value):
        return lax.ppermute(value, "fsdp", [(i, i ^ 1) for i in range(8)])

    def to_z(self, value, step):
        return lax.ppermute(value, "fsdp", [(i, i ^ (2 * step)) for i in range(8)])


class Gather:
    def __init__(self, tree, first, second):
        self.tree, self.cut = tree, first.shape[0]
        self.own = jnp.concatenate([first, second], 0)

    @staticmethod
    def columns(tree, shard):
        mine = pick(shard, tree.core, 1)
        got = tree.to_core(pick(shard, 1 - tree.core, 1))
        return Gather(tree, jnp.where(tree.core == 0, mine, got), jnp.where(tree.core == 0, got, mine))

    @staticmethod
    def rows(tree, shard):
        cut = shard.shape[0] // 2
        return Gather(tree, shard[:cut], shard[cut:])

    def along_z(self, *wait):
        tree = self.tree
        own = after(self.own, *wait)
        held = [own] + [tree.to_z(own, step) for step in (1, 2, 3)]
        low, high = tree.z % 2 == 1, tree.z // 2 == 1

        def chosen(rows):
            out = []
            for place in range(4):
                near = [jnp.where(low, held[(place ^ 1) ^ h], held[place ^ h]) for h in (0, 2)]
                out.append(jnp.where(high, near[1], near[0])[rows])
            return jnp.stack(out)

        self.first, self.second = chosen(slice(0, self.cut)), chosen(slice(self.cut, None))
        return self.first, self.second

    def one(self, *wait):
        tree = self.tree
        first, second = after((self.first, self.second), *wait)
        self.first = paired(tree.x, first, tree.to_x(first), 1)
        self.second = paired(tree.y, second, tree.to_y(second), 1)
        return self.first, self.second

    def two(self, *wait):
        tree = self.tree
        first, second = after((self.first, self.second), *wait)
        first = paired(tree.y, first, tree.to_y(first), 1)
        second = paired(tree.x, second, tree.to_x(second), 2)
        half = jnp.concatenate([first, second], 3)
        self.half = half.reshape(-1, half.shape[-1])
        return self.half

    def halves(self):
        return self.half, self.tree.to_core(self.half)


class Reduce:
    def __init__(self, tree, rows):
        self.tree, self.rows = tree, rows
        self.mine, self.got = [], []

    def add(self, mine, other):
        sent = other.astype(BF)
        got = self.tree.to_core(sent)
        self.mine.append(mine)
        self.got.append(got)
        return got

    def one(self):
        tree = self.tree
        shaped = [
            [array.reshape(4, 2, 2, self.rows, -1) for array in (mine, got)] for mine, got in zip(self.mine, self.got)
        ]

        def stage(rows, index, axis):
            sums = [
                pick(mine[:, :, :, rows], index, axis).astype(F32) + pick(got[:, :, :, rows], index, axis).astype(F32)
                for mine, got in shaped
            ]
            return jnp.concatenate(sums, -1)

        upper, lower = slice(0, self.rows // 2), slice(self.rows // 2, None)
        self.first_kept = stage(upper, tree.x, 2)
        self.second_kept = stage(lower, tree.y, 1)
        self.sent = (stage(upper, 1 - tree.x, 2).astype(BF), stage(lower, 1 - tree.y, 1).astype(BF))
        self.got = (tree.to_x(self.sent[0]), tree.to_y(self.sent[1]))

    def two(self):
        tree = self.tree
        first, second = self.first_kept + self.got[0], self.second_kept + self.got[1]
        self.first_kept, self.second_kept = pick(first, tree.y, 1), pick(second, tree.x, 1)
        self.sent = (pick(first, 1 - tree.y, 1).astype(BF), pick(second, 1 - tree.x, 1).astype(BF))
        self.got = (tree.to_y(self.sent[0]), tree.to_x(self.sent[1]))

    def along_z(self):
        tree = self.tree
        both = jnp.concatenate([self.first_kept + self.got[0], self.second_kept + self.got[1]], 1)
        self.first_kept = pick(both, tree.z, 0)
        self.sent = tuple(pick(both, tree.z ^ step, 0).astype(BF) for step in (1, 2, 3))
        self.got = tuple(tree.to_z(sent, step) for sent, step in zip(self.sent, (1, 2, 3)))

    def sums(self):
        return self.first_kept + self.got[0] + self.got[1] + self.got[2]

    def columns(self):
        tree, total = self.tree, self.sums()
        first, second = total[: self.rows // 2], total[self.rows // 2 :]
        keep = jnp.where(tree.core == 0, first, second)
        got = tree.to_core(jnp.where(tree.core == 0, second, first))
        return paired(tree.core, keep, got, 1)


class Whole:
    core = 0

    def __init__(self, rows=None):
        self.mine, self.other = [], []
        self.got, self.sent = (), ()

    @staticmethod
    def columns_of(shard):
        out = Whole()
        whole = lax.all_gather(shard, AXES, axis=0, tiled=True)
        out.half, out.rest = whole[:, 0], whole[:, 1]
        return out

    @staticmethod
    def rows_of(shard):
        out = Whole()
        whole = lax.all_gather(shard, AXES, axis=0)
        whole = whole.reshape(-1, 2, *shard.shape)
        out.half, out.rest = [whole[:, i].reshape(-1, shard.shape[1]) for i in range(2)]
        return out

    def along_z(self, *wait):
        return ()

    def one(self, *wait):
        return ()

    def two(self, *wait):
        return self.half

    def halves(self):
        return self.half, self.rest

    def add(self, mine, other):
        self.mine.append(mine.astype(BF))
        self.other.append(other.astype(BF))
        return mine

    def columns(self):
        parts = [jnp.concatenate(item, 1) for item in (self.mine, self.other)]
        return lax.psum_scatter(jnp.stack(parts, 1), AXES, scatter_dimension=0, tiled=True).astype(F32)

    def sums(self):
        count = lax.axis_size(AXES)
        mine, other = [item[0].reshape(count // 2, -1, item[0].shape[1]) for item in (self.mine, self.other)]
        sums = jnp.stack([mine, other], 1).reshape(-1, mine.shape[-1])
        return lax.psum_scatter(sums, AXES, scatter_dimension=0, tiled=True).astype(F32)


def body(
    fast,
    tokens,
    mask_bits,
    timesteps,
    cotangent,
    w_qkv,
    w_out,
    w_up,
    w_down,
    time_table,
    b_query,
    b_value,
    b_out,
    b_up,
    b_down,
    gain_attn,
    shift_attn,
    gain_mlp,
    shift_mlp,
    mask_vector,
):
    tree = Tree() if fast else Whole()
    gather_columns = functools.partial(Gather.columns, tree) if fast else Whole.columns_of
    gather_rows = functools.partial(Gather.rows, tree) if fast else Whole.rows_of
    reduction = functools.partial(Reduce, tree) if fast else Whole
    core = tree.core
    count = lax.axis_size(AXES)
    chips = count // 2
    place = lax.axis_index(AXES)
    width = tokens.shape[1]
    part = width // count
    hidden_width = w_up.shape[1]
    hidden_part = hidden_width // count
    seq_count = timesteps.shape[0]
    seq_length = tokens.shape[0] // seq_count
    half = width // 2
    table_cols = time_table.shape[1]
    absorbed = mask_bits.astype(F32)[:, None]

    small = [b_query, b_value, b_out, b_down, gain_attn, shift_attn, gain_mlp, shift_mlp, mask_vector]
    fixed = len(small)
    up_cols = hidden_part // part
    seq_cols = -(-2 * seq_count // part)
    steps = jnp.concatenate([timesteps // 256, timesteps % 256]).astype(F32)
    steps = jnp.pad(steps, (0, seq_cols * part - 2 * seq_count)).reshape(seq_cols, part)
    small = jnp.concatenate([jnp.stack(small), b_up.reshape(up_cols, part), steps], 0)
    small_cols = small.shape[0]
    all_cols = -(-(table_cols + small_cols) // (2 * LANES)) * (2 * LANES)
    table_half = all_cols // 2
    small = jnp.pad(small, ((0, all_cols - table_cols - small_cols), (0, 0)))
    table = jnp.concatenate([time_table, small.T], 1).astype(BF).reshape(part, 2, table_half)

    qkv = w_qkv.astype(BF).reshape(part, 3, 2, half)
    shard = [qkv[:, 0], qkv[:, 1], qkv[:, 2], w_out.astype(BF).reshape(part, 2, half), table]
    attn_w = gather_columns(jnp.concatenate(shard, 2))
    up_w = gather_columns(
        w_up.astype(BF)
        .reshape(part, chips, 2, hidden_part)
        .transpose(0, 2, 1, 3)
        .reshape(part, 2, hidden_width // 2)
    )
    down_w = gather_rows(w_down.astype(BF))
    attn_z = attn_w.along_z()
    up_z = up_w.along_z(attn_z)
    attn_one = attn_w.one()
    down_z = down_w.along_z(up_z)
    attn_w.two()
    up_one = up_w.one(attn_w.half)
    attn_w = attn_w.halves()
    place = jnp.concatenate([jnp.stack([jnp.int32(core), place]), timesteps])
    rows, start, normed_one, across_one, bias_mine, bias_other, bias_up = start_rows(
        place, tokens, absorbed, attn_w, fixed, up_cols, table_cols, small_cols, chips, hidden_part
    )
    steps = rows[seq_count + fixed + up_cols : seq_count + small_cols]
    steps = steps.reshape(seq_cols, count, part).transpose(1, 0, 2).reshape(count, -1).astype(jnp.int32)
    steps = (steps[:, :seq_count] * 256 + steps[:, seq_count : 2 * seq_count]).reshape(-1)

    qkv_mine, context_mine = attention(normed_one, attn_w[0], bias_mine, seq_length)
    up_half = up_w.two(context_mine)
    qkv_other, context_other = attention(after(normed_one, up_one), attn_w[1], bias_other, seq_length)
    contexts = (context_mine, context_other)
    middle, normed_two, across_two = middle_rows(place, contexts, attn_w, start, rows)
    down_one = down_w.one(up_half, context_other)
    up_w = up_w.halves()
    down_w.two(normed_two)
    hidden, slope = [None, None], [None, None]
    hidden[0], slope[0] = feed(normed_two, up_w[0], bias_up, 0)
    hidden[1], slope[1] = feed(after(normed_two, down_one), up_w[1], bias_up, 1)
    down_w = down_w.halves()

    grad_branch = (cotangent * absorbed).astype(BF)
    down_sum = reduction(hidden_part)
    down_got = down_sum.add(left_product(hidden[0], grad_branch), left_product(hidden[1], grad_branch))
    up_sum = reduction(2 * part)
    grad_pre, grad_b_up, grad_up = [None, None], [None, None], [None, None]
    grad_pre[1], grad_b_up[1], grad_up[1] = feed_back(grad_branch, down_w[1], slope[1], across_two, BF)
    if fast:
        down_sum.one()
    grad_pre[0], grad_b_up[0], grad_up[0] = feed_back(
        after(grad_branch, down_sum.sent), down_w[0], slope[0], across_two, F32
    )
    up_sum.add(grad_up[0], grad_up[1])
    if fast:
        down_sum.two()
    grad_pre = after(grad_pre, down_sum.sent)
    grad_middle, *grad_context, grad_out_mine, grad_out_other, middle_sums = middle_back(
        place, grad_pre, up_w, middle, cotangent, absorbed, rows, contexts, attn_w
    )

    attn_sum = reduction(2 * part)
    if fast:
        down_sum.along_z()
        up_sum.one()
    grads = [None, None]
    grads[1] = attention_back(
        qkv_other, after(grad_context[1], down_sum.sent, up_sum.sent), across_one, seq_length, BF
    )
    if fast:
        up_sum.two()
    grads[0] = attention_back(
        qkv_mine, after(grad_context[0], down_sum.got, up_sum.sent), across_one, seq_length, F32
    )
    grad_qkv, grad_weights, sums = zip(*grads)
    for index in range(3):
        attn_sum.add(grad_weights[0][index], grad_weights[1][index])
    attn_sum.add(grad_out_mine, grad_out_other)
    if fast:
        up_sum.along_z()
    grad_qkv = after(grad_qkv, up_sum.sent)
    seqs = count * seq_count
    grad_tokens, blocks = start_back(
        place, grad_qkv, attn_w, start, grad_middle, absorbed, rows, middle_sums, sums, seqs, seq_length
    )

    grad_b_up = paired(core, *[item.reshape(chips, hidden_part) for item in grad_b_up], 1).reshape(count, hidden_part)
    grad_b_up = jnp.pad(grad_b_up[:, None], ((0, 0), (0, part - 1), (LANES - hidden_part, 0)))
    grad_b_up = grad_b_up.reshape(width, LANES)
    blocks = [blocks[:, :LANES] + grad_b_up, blocks[:, LANES:]]
    if fast:
        attn_sum.add(jnp.where(core == 0, *blocks), jnp.where(core == 0, *blocks[::-1]))
        attn_sum.one()
        attn_sum.two()
        attn_sum.along_z()
        attn_grad = attn_sum.columns()
        small, seq_sums = attn_grad[:, 0, 4 * half :], attn_grad[:, 1, 4 * half :]
    else:
        attn_grad = attn_sum.columns()
        small, seq_sums = [
            lax.psum_scatter(item.astype(BF), AXES, scatter_dimension=0, tiled=True).astype(F32) for item in blocks
        ]
    grad_b_up = small[0, LANES - hidden_part :]
    small = small[:, :fixed].T
    onehot = (steps[:, None] == lax.broadcasted_iota(jnp.int32, (seqs, table_cols), 1)).astype(F32)
    grad_time_table = jnp.dot(seq_sums, onehot, precision=lax.Precision.HIGHEST)
    grad_w_qkv = attn_grad[:, :, : 3 * half].reshape(part, 2, 3, half).transpose(0, 2, 1, 3).reshape(part, 3 * width)
    grad_w_out = attn_grad[:, :, 3 * half : 4 * half].reshape(part, width)
    grad_w_up = up_sum.columns().reshape(part, 2, chips, hidden_part).transpose(0, 2, 1, 3)
    grad_w_up = grad_w_up.reshape(part, hidden_width)
    output = middle + (product(hidden[0], down_w[0]) + product(hidden[1], down_w[1]) + rows[seq_count + 3])
    return (
        output,
        grad_tokens,
        grad_w_qkv,
        grad_w_out,
        grad_w_up,
        down_sum.sums(),
        grad_time_table,
        small[0],
        small[1],
        small[2],
        grad_b_up,
        small[3],
        small[4],
        small[5],
        small[6],
        small[7],
        small[8],
    )


def solution(mesh):
    matrix, vector = P(AXES, None), P(AXES)
    fast = dict(mesh.shape) == {"fsdp": 8, "rep": 4}
    return jax.shard_map(
        functools.partial(body, fast),
        mesh=mesh,
        in_specs=(matrix, vector, vector) + (matrix,) * 6 + (vector,) * 10,
        out_specs=(matrix,) * 7 + (vector,) * 10,
        check_vma=False,
    )
```

```python
import functools
import math

import jax
import jax.numpy as jnp
from jax import lax
from jax.experimental import pallas as pl
from jax.experimental.pallas import tpu as pltpu
from jax.sharding import PartitionSpec as P

HDIM = 64
EPSILON = 1e-05
AXES = ("fsdp", "rep")
BF = jnp.bfloat16
F32 = jnp.float32
LANES = 128
VMEM_BYTES = 32 << 20
GELU_OUTER = math.sqrt(2.0 / math.pi)
GELU_INNER = 0.044715


def contract(left, right, left_dim, right_dim):
    dims = (((left_dim,), (right_dim,)), ((), ()))
    return lax.dot_general(left, right, dims, preferred_element_type=F32)


def product(left, right):
    return contract(left, right, 1, 0)


def left_product(left, right):
    return contract(left, right, 0, 0)


def right_product(left, right):
    return contract(left, right, 1, 1)


def pick(array, index, axis):
    return lax.dynamic_index_in_dim(array, index, axis, keepdims=False)


def paired(bit, mine, other, axis):
    return jnp.stack([jnp.where(bit == 0, mine, other), jnp.where(bit == 0, other, mine)], axis)


def after(value, *others):
    return lax.optimization_barrier((value, others))[0]


def lane_masks(factor):
    lane = lax.broadcasted_iota(jnp.int32, (1, LANES), 1)
    return [jnp.where((lane < HDIM) == (head == 0), factor, 0.0).astype(BF) for head in (0, 1)]


def softmax(scores):
    powers = jnp.exp(scores - jnp.max(scores, -1, keepdims=True))
    return powers * (1.0 / jnp.sum(powers, -1, keepdims=True))


def attention_kernel(length, scale, rows_ref, query_ref, key_ref, value_ref, bias_ref, qkv_ref, context_ref):
    rows = rows_ref[...]
    for index, weight in enumerate((query_ref, key_ref, value_ref)):
        qkv_ref[index] = (product(rows, weight[...]) + bias_ref[index : index + 1, :]).astype(BF)
    ones, scaled = lane_masks(1.0), lane_masks(scale)

    for sequence in range(rows.shape[0] // length):
        span = slice(sequence * length, (sequence + 1) * length)
        queries, key_rows, value_rows = [qkv_ref[index, span, :] for index in range(3)]
        total = 0.0
        for head in (0, 1):
            probs = softmax(right_product(queries * scaled[head], key_rows)).astype(BF)
            total = total + product(probs, value_rows * ones[head])
        context_ref[span, :] = total.astype(BF)


def attention(rows, weight, bias, length):
    tokens, width = rows.shape
    half = bias.shape[1]
    pairs = half // LANES

    def weight_spec(index):
        return pl.BlockSpec((width, LANES), lambda pair: (0, index * pairs + pair))

    return pl.pallas_call(
        functools.partial(attention_kernel, length, 1.0 / math.sqrt(HDIM)),
        grid=(pairs,),
        in_specs=[
            pl.BlockSpec((tokens, width), lambda pair: (0, 0)),
            weight_spec(0),
            weight_spec(1),
            weight_spec(2),
            pl.BlockSpec((8, LANES), lambda pair: (0, pair)),
        ],
        out_specs=[
            pl.BlockSpec((3, tokens, LANES), lambda pair: (0, 0, pair)),
            pl.BlockSpec((tokens, LANES), lambda pair: (0, pair)),
        ],
        out_shape=[
            jax.ShapeDtypeStruct((3, tokens, half), BF),
            jax.ShapeDtypeStruct((tokens, half), BF),
        ],
        compiler_params=pltpu.CompilerParams(vmem_limit_bytes=VMEM_BYTES),
        cost_estimate=pl.CostEstimate(
            flops=6 * tokens * width * half,
            bytes_accessed=2 * tokens * width + 6 * width * half + 8 * tokens * half,
            transcendentals=2 * tokens * length * pairs,
        ),
        name="attention",
    )(rows, weight, weight, weight, bias)


def attention_back_kernel(length, scale, qkv_ref, grad_ref, rows_ref, grads_ref, weight_ref, sums_ref):
    ones, scaled = lane_masks(1.0), lane_masks(scale)

    for sequence in range(grad_ref.shape[0] // length):
        span = slice(sequence * length, (sequence + 1) * length)
        queries, key_rows, value_rows = [qkv_ref[index, span, :] for index in range(3)]
        grad = grad_ref[span, :]
        grad_queries, grad_keys, grad_values = 0.0, 0.0, 0.0
        for head in (0, 1):
            probs = softmax(right_product(queries * scaled[head], key_rows))
            grad_head = grad * ones[head]
            grad_probs = right_product(grad_head, value_rows)
            grad_scores = probs * (grad_probs - jnp.sum(grad_probs * probs, -1, keepdims=True))
            grad_scores = grad_scores.astype(BF)
            grad_values = grad_values + left_product(probs.astype(BF), grad_head)
            grad_queries = grad_queries + product(grad_scores, key_rows * ones[head])
            grad_keys = grad_keys + left_product(grad_scores, queries * ones[head])
        grads_ref[0, span, :] = (grad_queries * scale).astype(BF)
        grads_ref[1, span, :] = (grad_keys * scale).astype(BF)
        grads_ref[2, span, :] = grad_values.astype(BF)

    rows = rows_ref[...]
    for index in range(3):
        grads = grads_ref[index]
        weight_ref[index] = product(rows, grads).astype(weight_ref.dtype)
        sums_ref[index : index + 1, :] = jnp.sum(grads.astype(F32), 0, keepdims=True)


def attention_back(qkv, grad, rows_across, length, dtype):
    _, tokens, half = qkv.shape
    width = rows_across.shape[0]
    pairs = half // LANES
    return pl.pallas_call(
        functools.partial(attention_back_kernel, length, 1.0 / math.sqrt(HDIM)),
        grid=(pairs,),
        in_specs=[
            pl.BlockSpec((3, tokens, LANES), lambda pair: (0, 0, pair)),
            pl.BlockSpec((tokens, LANES), lambda pair: (0, pair)),
            pl.BlockSpec((width, tokens), lambda pair: (0, 0)),
        ],
        out_specs=[
            pl.BlockSpec((3, tokens, LANES), lambda pair: (0, 0, pair)),
            pl.BlockSpec((3, width, LANES), lambda pair: (0, 0, pair)),
            pl.BlockSpec((3, LANES), lambda pair: (0, pair)),
        ],
        out_shape=[
            jax.ShapeDtypeStruct((3, tokens, half), BF),
            jax.ShapeDtypeStruct((3, width, half), dtype),
            jax.ShapeDtypeStruct((3, half), F32),
        ],
        compiler_params=pltpu.CompilerParams(vmem_limit_bytes=VMEM_BYTES),
        cost_estimate=pl.CostEstimate(
            flops=6 * tokens * width * half,
            bytes_accessed=2 * tokens * width + 12 * width * half + 14 * tokens * half,
            transcendentals=2 * tokens * length * pairs,
        ),
        name="attention_back",
    )(qkv, grad, rows_across)


def feed_kernel(side, rows_ref, weight_ref, bias_ref, hidden_ref, slope_ref, pre_ref):
    pre_ref[...] = product(rows_ref[...], weight_ref[...])
    step = 32

    def chunk(index, carry):
        span = pl.ds(pl.multiple_of(index * step, step), step)
        pre = pre_ref[span, :] + bias_ref[side : side + 1, :]
        square = pre * pre
        bend = jnp.tanh(GELU_OUTER * (pre + GELU_INNER * (square * pre)))
        share = 0.5 * (1.0 + bend)
        hidden_ref[span, :] = (pre * share).astype(BF)
        inner = (0.5 * GELU_OUTER) * pre * (1.0 + (3.0 * GELU_INNER) * square)
        slope_ref[span, :] = share + inner * (1.0 - bend * bend)
        return carry

    lax.fori_loop(0, rows_ref.shape[0] // step, chunk, 0, unroll=2)


def feed(rows, weight, bias, side, block=512):
    tokens, width = rows.shape
    columns = weight.shape[1]
    block = math.gcd(block, columns)
    out = pl.BlockSpec((tokens, block), lambda step: (0, step))
    return pl.pallas_call(
        functools.partial(feed_kernel, side),
        grid=(columns // block,),
        in_specs=[
            pl.BlockSpec((tokens, width), lambda step: (0, 0)),
            pl.BlockSpec((width, block), lambda step: (0, step)),
            pl.BlockSpec((8, block), lambda step: (0, step)),
        ],
        out_specs=[out, out],
        out_shape=[
            jax.ShapeDtypeStruct((tokens, columns), BF),
            jax.ShapeDtypeStruct((tokens, columns), F32),
        ],
        scratch_shapes=[pltpu.VMEM((tokens, block), F32)],
        compiler_params=pltpu.CompilerParams(vmem_limit_bytes=VMEM_BYTES),
        cost_estimate=pl.CostEstimate(
            flops=2 * tokens * width * columns,
            bytes_accessed=2 * tokens * width + 2 * width * columns + 6 * tokens * columns,
            transcendentals=tokens * columns,
        ),
        name="feed",
    )(rows, weight, bias)


def feed_back_kernel(grad_ref, weight_ref, slope_ref, rows_ref, pre_ref, sum_ref, up_ref):
    grad = (right_product(grad_ref[...], weight_ref[...]) * slope_ref[...]).astype(BF)
    pre_ref[...] = grad
    sum_ref[...] = jnp.sum(grad.astype(F32), 0, keepdims=True)
    up_ref[...] = product(rows_ref[...], grad).astype(up_ref.dtype)


def feed_back(grad, weight, slope, rows_across, dtype, block=512):
    tokens, width = grad.shape
    columns = weight.shape[0]
    block = math.gcd(block, columns)
    out = pl.BlockSpec((tokens, block), lambda step: (0, step))
    return pl.pallas_call(
        feed_back_kernel,
        grid=(columns // block,),
        in_specs=[
            pl.BlockSpec((tokens, width), lambda step: (0, 0)),
            pl.BlockSpec((block, width), lambda step: (step, 0)),
            out,
            pl.BlockSpec((width, tokens), lambda step: (0, 0)),
        ],
        out_specs=[
            out,
            pl.BlockSpec((1, block), lambda step: (0, step)),
            pl.BlockSpec((width, block), lambda step: (0, step)),
        ],
        out_shape=[
            jax.ShapeDtypeStruct((tokens, columns), BF),
            jax.ShapeDtypeStruct((1, columns), F32),
            jax.ShapeDtypeStruct((width, columns), dtype),
        ],
        compiler_params=pltpu.CompilerParams(vmem_limit_bytes=VMEM_BYTES),
        cost_estimate=pl.CostEstimate(
            flops=4 * tokens * width * columns,
            bytes_accessed=4 * tokens * width + 6 * width * columns + 6 * tokens * columns,
            transcendentals=0,
        ),
        name="feed_back",
    )(grad, weight, slope, rows_across)


def chosen_side(core, mine, other):
    return jnp.where(core == 0, mine, other), jnp.where(core == 0, other, mine)


def normalized(values):
    center = values - jnp.mean(values, -1, keepdims=True)
    rate = lax.rsqrt(jnp.mean(center * center, -1, keepdims=True) + EPSILON)
    return center * rate, rate


def start_kernel(
    fixed, up_cols, table_cols, seq_count, parts,
    place_ref, tokens_ref, mask_ref, table_mine_ref, table_other_ref,
    rows_ref, start_ref, normed_ref, across_ref, bias_mine_ref, bias_other_ref, bias_up_ref,
):
    core = place_ref[0]
    step = pl.program_id(0)
    width = tokens_ref.shape[1]
    half = width // 2
    chips, part, hidden_part = parts

    @pl.when(step == 0)
    def _():
        count, columns = rows_ref.shape[0], table_mine_ref.shape[1]
        row = lax.broadcasted_iota(jnp.int32, (count, columns), 0)
        wanted = table_cols + row - seq_count
        for index in range(seq_count):
            wanted = jnp.where(row == index, place_ref[2 + index], wanted)
        column = lax.broadcasted_iota(jnp.int32, (count, columns), 1)
        rows = 0.0
        for side, table in ((core, table_mine_ref), (1 - core, table_other_ref)):
            hit = jnp.where(wanted == column + side * columns, 1.0, 0.0).astype(BF)
            rows = rows + right_product(hit, table[...])
        rows_ref[...] = rows
        for ref, side in ((bias_mine_ref, core), (bias_other_ref, 1 - core)):
            ref[...] = jnp.zeros_like(ref)
            for index in (0, 1):
                line = rows_ref[seq_count + index : seq_count + index + 1, :]
                ref[2 * index : 2 * index + 1, :] = jnp.where(side == 0, line[:, :half], line[:, half:])
        for chip in range(chips):
            for index in range(up_cols):
                line = rows_ref[seq_count + fixed + index : seq_count + fixed + index + 1, :]
                pair = [line[:, (2 * chip + i) * part : (2 * chip + i + 1) * part] for i in range(2)]
                where = slice(chip * hidden_part + index * part, chip * hidden_part + (index + 1) * part)
                bias_up_ref[0:1, where], bias_up_ref[1:2, where] = chosen_side(core, *pair)

    small = seq_count
    mask = mask_ref[...]
    start = jnp.where(mask > 0.0, rows_ref[small + 8 : small + 9, :], tokens_ref[...])
    start = start + rows_ref[pl.ds(step, 1), :]
    start_ref[...] = start
    normed, _ = normalized(start)
    normed = normed * rows_ref[small + 4 : small + 5, :] + rows_ref[small + 5 : small + 6, :]
    normed_ref[...] = normed.astype(BF)
    across_ref[...] = normed.T.astype(BF)


def start_rows(place, tokens, mask, weights, fixed, up_cols, table_cols, small_cols, chips, hidden_part):
    count, width = tokens.shape
    seq_count = place.shape[0] - 2
    length = count // seq_count
    half = width // 2
    row_count = -(-(seq_count + small_cols) // 8) * 8
    table_half = weights[0].shape[1] - 4 * half
    tables = 4 * half // table_half
    table_spec = pl.BlockSpec((width, table_half), lambda step: (0, tables))
    rows_spec = pl.BlockSpec((length, width), lambda step: (step, 0))

    def fixed_spec(*shape):
        return pl.BlockSpec(shape, lambda step: (0,) * len(shape))

    return pl.pallas_call(
        functools.partial(
            start_kernel, fixed, up_cols, table_cols, seq_count, (chips, width // (2 * chips), hidden_part)
        ),
        grid=(seq_count,),
        in_specs=[
            pl.BlockSpec(memory_space=pltpu.SMEM),
            rows_spec,
            pl.BlockSpec((length, 1), lambda step: (step, 0)),
            table_spec,
            table_spec,
        ],
        out_specs=[
            fixed_spec(row_count, width),
            rows_spec,
            rows_spec,
            pl.BlockSpec((width, length), lambda step: (0, step)),
            fixed_spec(8, half),
            fixed_spec(8, half),
            fixed_spec(8, chips * hidden_part),
        ],
        out_shape=[
            jax.ShapeDtypeStruct((row_count, width), F32),
            jax.ShapeDtypeStruct((count, width), F32),
            jax.ShapeDtypeStruct((count, width), BF),
            jax.ShapeDtypeStruct((width, count), BF),
            jax.ShapeDtypeStruct((8, half), F32),
            jax.ShapeDtypeStruct((8, half), F32),
            jax.ShapeDtypeStruct((8, chips * hidden_part), F32),
        ],
        compiler_params=pltpu.CompilerParams(vmem_limit_bytes=VMEM_BYTES),
        cost_estimate=pl.CostEstimate(
            flops=4 * row_count * width * table_half, bytes_accessed=14 * count * width, transcendentals=0
        ),
        name="start_rows",
    )(place, tokens, mask, *weights)


def middle_kernel(
    small, place_ref, context_mine_ref, context_other_ref, out_mine_ref, out_other_ref, start_ref, rows_ref,
    middle_ref, normed_ref, across_ref,
):
    core = place_ref[0]
    half = context_mine_ref.shape[1]
    contexts = chosen_side(core, context_mine_ref[...], context_other_ref[...])
    outs = chosen_side(core, out_mine_ref[...], out_other_ref[...])
    for index, out in enumerate(outs):
        span = slice(index * half, (index + 1) * half)
        total = product(contexts[0], out[:half]) + product(contexts[1], out[half:])
        middle_ref[:, span] = start_ref[:, span] + (total + rows_ref[small + 2 : small + 3, span])
    normed, _ = normalized(middle_ref[...])
    normed = normed * rows_ref[small + 6 : small + 7, :] + rows_ref[small + 7 : small + 8, :]
    normed_ref[...] = normed.astype(BF)
    across_ref[...] = normed.T.astype(BF)


def middle_rows(place, contexts, weights, start, rows, block=256):
    count, width = start.shape
    half = width // 2
    small = place.shape[0] - 2
    block = math.gcd(block, count)
    out_spec = pl.BlockSpec((width, half), lambda step: (0, 3))
    rows_spec = pl.BlockSpec((block, width), lambda step: (step, 0))
    half_spec = pl.BlockSpec((block, half), lambda step: (step, 0))
    return pl.pallas_call(
        functools.partial(middle_kernel, small),
        grid=(count // block,),
        in_specs=[
            pl.BlockSpec(memory_space=pltpu.SMEM),
            half_spec,
            half_spec,
            out_spec,
            out_spec,
            rows_spec,
            pl.BlockSpec(rows.shape, lambda step: (0, 0)),
        ],
        out_specs=[rows_spec, rows_spec, pl.BlockSpec((width, block), lambda step: (0, step))],
        out_shape=[
            jax.ShapeDtypeStruct((count, width), F32),
            jax.ShapeDtypeStruct((count, width), BF),
            jax.ShapeDtypeStruct((width, count), BF),
        ],
        compiler_params=pltpu.CompilerParams(vmem_limit_bytes=VMEM_BYTES),
        cost_estimate=pl.CostEstimate(
            flops=2 * count * width * width, bytes_accessed=14 * count * width + 2 * width * width, transcendentals=0
        ),
        name="middle_rows",
    )(place, *contexts, *weights, start, rows)


def norm_back(values, gain, grad):
    unit, rate = normalized(values)
    scaled = grad * gain
    back = scaled - jnp.mean(scaled, -1, keepdims=True) - unit * jnp.mean(scaled * unit, -1, keepdims=True)
    return rate * back, grad * unit


def middle_back_kernel(
    small, place_ref, pre_mine_ref, pre_other_ref, up_mine_ref, up_other_ref, middle_ref, cotangent_ref, mask_ref,
    rows_ref, context_mine_ref, context_other_ref, out_mine_ref, out_other_ref,
    grad_ref, context_grad_mine_ref, context_grad_other_ref, out_grad_mine_ref, out_grad_other_ref, sums_ref,
    normed_ref, total_ref,
):
    core = place_ref[0]
    step = pl.program_id(0)
    half = context_mine_ref.shape[1]

    @pl.when(step == 0)
    def _():
        sums_ref[...] = jnp.zeros_like(sums_ref)
        total_ref[...] = jnp.zeros_like(total_ref)

    normed_ref[...] = right_product(pre_mine_ref[...], up_mine_ref[...]) + right_product(
        pre_other_ref[...], up_other_ref[...]
    )
    grad = normed_ref[...]
    direct = cotangent_ref[...] * mask_ref[...]
    back, shares = norm_back(middle_ref[...], rows_ref[small + 6 : small + 7, :], grad)
    back = direct + back
    grad_ref[...] = back
    low = back.astype(BF)
    for index, item in enumerate((low.astype(F32), direct.astype(BF).astype(F32), shares, grad)):
        sums_ref[index : index + 1, :] += jnp.sum(item, 0, keepdims=True)
    lows = (low[:, :half], low[:, half:])
    contexts = chosen_side(core, context_mine_ref[...], context_other_ref[...])
    outs = chosen_side(core, out_mine_ref[...], out_other_ref[...])
    context_grads = [
        (right_product(lows[0], outs[0][span]) + right_product(lows[1], outs[1][span])).astype(BF)
        for span in (slice(0, half), slice(half, None))
    ]
    context_grad_mine_ref[...], context_grad_other_ref[...] = chosen_side(core, *context_grads)
    for index, item in enumerate(chosen_side(core, *lows)):
        for side, context in enumerate(contexts):
            total_ref[index, side * half : (side + 1) * half, :] += left_product(context, item)

    @pl.when(step == pl.num_programs(0) - 1)
    def _():
        out_grad_mine_ref[...] = total_ref[0]
        out_grad_other_ref[...] = total_ref[1].astype(BF)


def middle_back(place, grads, ups, middle, cotangent, mask, rows, contexts, weights, block=256):
    count, width = middle.shape
    half = width // 2
    hidden_half = ups[0].shape[1]
    small = place.shape[0] - 2
    block = math.gcd(block, count)

    def over_rows(columns):
        return pl.BlockSpec((block, columns), lambda step: (step, 0))

    def whole(*shape):
        return pl.BlockSpec(shape, lambda step: (0,) * len(shape))

    out_spec = pl.BlockSpec((width, half), lambda step: (0, 3))
    return pl.pallas_call(
        functools.partial(middle_back_kernel, small),
        grid=(count // block,),
        in_specs=[
            pl.BlockSpec(memory_space=pltpu.SMEM),
            over_rows(hidden_half),
            over_rows(hidden_half),
            whole(width, hidden_half),
            whole(width, hidden_half),
            over_rows(width),
            over_rows(width),
            over_rows(1),
            whole(*rows.shape),
            over_rows(half),
            over_rows(half),
            out_spec,
            out_spec,
        ],
        out_specs=[
            over_rows(width),
            over_rows(half),
            over_rows(half),
            whole(width, half),
            whole(width, half),
            whole(8, width),
        ],
        out_shape=[
            jax.ShapeDtypeStruct((count, width), F32),
            jax.ShapeDtypeStruct((count, half), BF),
            jax.ShapeDtypeStruct((count, half), BF),
            jax.ShapeDtypeStruct((width, half), F32),
            jax.ShapeDtypeStruct((width, half), BF),
            jax.ShapeDtypeStruct((8, width), F32),
        ],
        scratch_shapes=[pltpu.VMEM((block, width), F32), pltpu.VMEM((2, width, half), F32)],
        compiler_params=pltpu.CompilerParams(vmem_limit_bytes=VMEM_BYTES),
        cost_estimate=pl.CostEstimate(
            flops=4 * count * width * (hidden_half + width),
            bytes_accessed=4 * count * hidden_half + 4 * width * hidden_half + 16 * count * width,
            transcendentals=0,
        ),
        name="middle_back",
    )(place, *grads, *ups, middle, cotangent, mask, rows, *contexts, *weights)


def start_back_kernel(
    small, length, place_ref, grads_mine_ref, grads_other_ref, weight_mine_ref, weight_other_ref, start_ref, middle_ref,
    mask_ref, rows_ref, sums_ref, sums_mine_ref, sums_other_ref,
    tokens_ref, blocks_ref, lines_ref,
):
    core, place = place_ref[0], place_ref[1]
    step = pl.program_id(0)
    width = start_ref.shape[1]
    half = width // 2
    seqs = start_ref.shape[0] // length

    @pl.when(step == 0)
    def _():
        lines_ref[...] = jnp.zeros_like(lines_ref)
        for index, row in ((0, 0), (1, 2)):
            pair = (sums_mine_ref[row : row + 1, :], sums_other_ref[row : row + 1, :])
            lines_ref[index : index + 1, :half], lines_ref[index : index + 1, half:] = chosen_side(core, *pair)
        lines_ref[2:4, :] = sums_ref[0:2, :]
        lines_ref[6:8, :] = sums_ref[2:4, :]

    grad = 0.0
    for grads, weight in ((grads_mine_ref, weight_mine_ref), (grads_other_ref, weight_other_ref)):
        for index in range(3):
            grad = grad + right_product(grads[index], weight[:, index * half : (index + 1) * half])
    back, shares = norm_back(start_ref[...], rows_ref[small + 4 : small + 5, :], grad)
    back = middle_ref[...] + back
    mask = mask_ref[...]
    tokens_ref[...] = jnp.where(mask > 0.0, 0.0, back)
    for index, item in ((4, shares), (5, grad), (8, back * mask)):
        lines_ref[index : index + 1, :] += jnp.sum(item, 0, keepdims=True)
    for index in range(seqs):
        line = LANES + place * small + step * seqs + index
        lines_ref[pl.ds(line, 1), :] = jnp.sum(back[index * length : (index + 1) * length], 0, keepdims=True)

    @pl.when(step == pl.num_programs(0) - 1)
    def _():
        blocks_ref[...] = lines_ref[...].T


def start_back(place, grads, weights, start, middle, mask, rows, sums, side_sums, seqs, length, block=256):
    count, width = start.shape
    half = width // 2
    small = place.shape[0] - 2
    block = math.gcd(block, count)
    lines = LANES + -(-seqs // LANES) * LANES

    def over_rows(columns):
        return pl.BlockSpec((block, columns), lambda step: (step, 0))

    def whole(*shape):
        return pl.BlockSpec(shape, lambda step: (0,) * len(shape))

    grads_spec = pl.BlockSpec((3, block, half), lambda step: (0, step, 0))
    return pl.pallas_call(
        functools.partial(start_back_kernel, small, length),
        grid=(count // block,),
        in_specs=[
            pl.BlockSpec(memory_space=pltpu.SMEM),
            grads_spec,
            grads_spec,
            whole(width, 3 * half),
            whole(width, 3 * half),
            over_rows(width),
            over_rows(width),
            over_rows(1),
            whole(*rows.shape),
            whole(*sums.shape),
            whole(*side_sums[0].shape),
            whole(*side_sums[1].shape),
        ],
        out_specs=[over_rows(width), whole(width, lines)],
        out_shape=[
            jax.ShapeDtypeStruct((count, width), F32),
            jax.ShapeDtypeStruct((width, lines), F32),
        ],
        scratch_shapes=[pltpu.VMEM((lines, width), F32)],
        compiler_params=pltpu.CompilerParams(vmem_limit_bytes=VMEM_BYTES),
        cost_estimate=pl.CostEstimate(
            flops=4 * count * width * 3 * half,
            bytes_accessed=12 * count * half + 12 * width * half + 12 * count * width,
            transcendentals=0,
        ),
        name="start_back",
    )(place, *grads, *weights, start, middle, mask, rows, sums, *side_sums)


class Tree:
    def __init__(self):
        fsdp, rep = lax.axis_index("fsdp"), lax.axis_index("rep")
        self.z, self.core = fsdp // 2, rep % 2
        x, y = rep // 2, fsdp % 2
        self.near = jnp.where(self.core == 0, x, y)
        self.far = jnp.where(self.core == 0, y, x)
        self.x, self.y = x, y

    def to_core(self, value):
        return lax.ppermute(value, "rep", [(i, i ^ 1) for i in range(4)])

    def to_near(self, value):
        return lax.ppermute(value, AXES, [(i, i ^ (4 if i % 2 else 2)) for i in range(32)])

    def to_far(self, value):
        return lax.ppermute(value, AXES, [(i, i ^ (2 if i % 2 else 4)) for i in range(32)])

    def to_z(self, value, step):
        return lax.ppermute(value, "fsdp", [(i, i ^ (2 * step)) for i in range(8)])


class Gather:
    def __init__(self, tree, own):
        self.tree, self.own = tree, own

    @staticmethod
    def columns(tree, shard):
        mine = pick(shard, tree.core, 1)
        got = tree.to_core(pick(shard, 1 - tree.core, 1))
        return Gather(tree, paired(tree.core, mine, got, 0).reshape(-1, mine.shape[1]))

    @staticmethod
    def rows(tree, shard):
        return Gather(tree, shard)

    def along_z(self, *wait):
        tree = self.tree
        own = after(self.own, *wait)
        held = [own] + [tree.to_z(own, step) for step in (1, 2, 3)]
        low, high = tree.z % 2 == 1, tree.z // 2 == 1
        out = []
        for place in range(4):
            near = [jnp.where(low, held[(place ^ 1) ^ h], held[place ^ h]) for h in (0, 2)]
            out.append(jnp.where(high, near[1], near[0]))
        self.held = jnp.stack(out)
        return self.held

    def one(self, *wait):
        tree = self.tree
        held = after(self.held, *wait)
        self.held = paired(tree.near, held, tree.to_near(held), 1)
        return self.held

    def two(self, *wait):
        tree = self.tree
        held = after(self.held, *wait)
        got = tree.to_far(held)
        same, first = tree.far == 0, tree.core == 0
        lower, upper = jnp.where(same, held, got), jnp.where(same, got, held)
        blocks = [
            lower[:, 0],
            jnp.where(first, lower[:, 1], upper[:, 0]),
            jnp.where(first, upper[:, 0], lower[:, 1]),
            upper[:, 1],
        ]
        self.half = jnp.stack(blocks, 1).reshape(-1, held.shape[-1])
        return self.half

    def halves(self, *wait):
        return self.half, self.tree.to_core(after(self.half, *wait))


class Reduce:
    def __init__(self, tree, rows):
        self.tree, self.rows = tree, rows
        self.terms = []

    def add(self, mine, other):
        got = self.tree.to_core(other.astype(BF))
        self.terms.append([array.reshape(4, 4, self.rows, -1) for array in (mine, got)])
        return got

    def one(self):
        tree = self.tree

        def stage(near):
            places = [jnp.where(tree.core == 0, 2 * far + near, 2 * near + far) for far in (0, 1)]
            sums = [
                jnp.concatenate([sum(pick(term, place, 1).astype(F32) for term in pair) for pair in self.terms], -1)
                for place in places
            ]
            return jnp.stack(sums, 1)

        self.kept, self.sent = stage(tree.near), stage(1 - tree.near).astype(BF)
        self.got = tree.to_near(self.sent)

    def two(self):
        tree = self.tree
        total = self.kept + self.got
        self.kept, self.sent = pick(total, tree.far, 1), pick(total, 1 - tree.far, 1).astype(BF)
        self.got = tree.to_far(self.sent)

    def along_z(self):
        tree = self.tree
        total = self.kept + self.got
        self.kept = pick(total, tree.z, 0)
        self.sent = tuple(pick(total, tree.z ^ step, 0).astype(BF) for step in (1, 2, 3))
        self.got = tuple(tree.to_z(sent, step) for sent, step in zip(self.sent, (1, 2, 3)))

    def sums(self):
        return self.kept + self.got[0] + self.got[1] + self.got[2]

    def columns(self):
        tree, total = self.tree, self.sums()
        rows = total.reshape(2, self.rows // 2, -1)
        keep = pick(rows, tree.core, 0)
        return paired(tree.core, keep, tree.to_core(pick(rows, 1 - tree.core, 0)), 1)


class Whole:
    core = 0

    def __init__(self, rows=None):
        self.mine, self.other = [], []
        self.got, self.sent = (), ()

    @staticmethod
    def columns_of(shard):
        out = Whole()
        whole = lax.all_gather(shard, AXES, axis=0, tiled=True)
        out.half, out.rest = whole[:, 0], whole[:, 1]
        return out

    @staticmethod
    def rows_of(shard):
        out = Whole()
        whole = lax.all_gather(shard, AXES, axis=0)
        whole = whole.reshape(-1, 2, *shard.shape)
        out.half, out.rest = [whole[:, i].reshape(-1, shard.shape[1]) for i in range(2)]
        return out

    def along_z(self, *wait):
        return ()

    def one(self, *wait):
        return ()

    def two(self, *wait):
        return self.half

    def halves(self, *wait):
        return self.half, self.rest

    def add(self, mine, other):
        self.mine.append(mine.astype(BF))
        self.other.append(other.astype(BF))
        return mine

    def columns(self):
        parts = [jnp.concatenate(item, 1) for item in (self.mine, self.other)]
        return lax.psum_scatter(jnp.stack(parts, 1), AXES, scatter_dimension=0, tiled=True).astype(F32)

    def sums(self):
        count = lax.axis_size(AXES)
        mine, other = [item[0].reshape(count // 2, -1, item[0].shape[1]) for item in (self.mine, self.other)]
        sums = jnp.stack([mine, other], 1).reshape(-1, mine.shape[-1])
        return lax.psum_scatter(sums, AXES, scatter_dimension=0, tiled=True).astype(F32)


def body(
    fast,
    tokens,
    mask_bits,
    timesteps,
    cotangent,
    w_qkv,
    w_out,
    w_up,
    w_down,
    time_table,
    b_query,
    b_value,
    b_out,
    b_up,
    b_down,
    gain_attn,
    shift_attn,
    gain_mlp,
    shift_mlp,
    mask_vector,
):
    tree = Tree() if fast else Whole()
    gather_columns = functools.partial(Gather.columns, tree) if fast else Whole.columns_of
    gather_rows = functools.partial(Gather.rows, tree) if fast else Whole.rows_of
    reduction = functools.partial(Reduce, tree) if fast else Whole
    core = tree.core
    count = lax.axis_size(AXES)
    chips = count // 2
    place = lax.axis_index(AXES)
    width = tokens.shape[1]
    part = width // count
    hidden_width = w_up.shape[1]
    hidden_part = hidden_width // count
    seq_count = timesteps.shape[0]
    seq_length = tokens.shape[0] // seq_count
    half = width // 2
    table_cols = time_table.shape[1]
    absorbed = mask_bits.astype(F32)[:, None]

    small = [b_query, b_value, b_out, b_down, gain_attn, shift_attn, gain_mlp, shift_mlp, mask_vector]
    fixed = len(small)
    up_cols = hidden_part // part
    seq_cols = -(-2 * seq_count // part)
    steps = jnp.concatenate([timesteps // 256, timesteps % 256]).astype(F32)
    steps = jnp.pad(steps, (0, seq_cols * part - 2 * seq_count)).reshape(seq_cols, part)
    small = jnp.concatenate([jnp.stack(small), b_up.reshape(up_cols, part), steps], 0)
    small_cols = small.shape[0]
    all_cols = -(-(table_cols + small_cols) // (2 * LANES)) * (2 * LANES)
    table_half = all_cols // 2
    small = jnp.pad(small, ((0, all_cols - table_cols - small_cols), (0, 0)))
    table = jnp.concatenate([time_table, small.T], 1).astype(BF).reshape(part, 2, table_half)

    qkv = w_qkv.astype(BF).reshape(part, 3, 2, half)
    shard = [qkv[:, 0], qkv[:, 1], qkv[:, 2], w_out.astype(BF).reshape(part, 2, half), table]
    attn_w = gather_columns(jnp.concatenate(shard, 2))
    up_w = gather_columns(
        w_up.astype(BF)
        .reshape(part, chips, 2, hidden_part)
        .transpose(0, 2, 1, 3)
        .reshape(part, 2, hidden_width // 2)
    )
    down_w = gather_rows(w_down.astype(BF))
    attn_w.along_z()
    attn_one = attn_w.one()
    up_z = up_w.along_z(attn_one)
    attn_half = attn_w.two()
    attn_w = attn_w.halves(up_z)
    up_one = up_w.one(attn_half)
    down_z = down_w.along_z(attn_half)

    place = jnp.concatenate([jnp.stack([jnp.int32(core), place]), timesteps])
    rows, start, normed_one, across_one, bias_mine, bias_other, bias_up = start_rows(
        place, tokens, absorbed, attn_w, fixed, up_cols, table_cols, small_cols, chips, hidden_part
    )
    steps = rows[seq_count + fixed + up_cols : seq_count + small_cols]
    steps = steps.reshape(seq_cols, count, part).transpose(1, 0, 2).reshape(count, -1).astype(jnp.int32)
    steps = (steps[:, :seq_count] * 256 + steps[:, seq_count : 2 * seq_count]).reshape(-1)

    up_half = up_w.two(normed_one)
    qkv_mine, context_mine = attention(after(normed_one, up_one, down_z), attn_w[0], bias_mine, seq_length)
    down_one = down_w.one(up_half, context_mine)
    up_w = up_w.halves(context_mine)
    qkv_other, context_other = attention(after(normed_one, up_half), attn_w[1], bias_other, seq_length)
    down_half = down_w.two(context_other)
    down_w = down_w.halves()
    contexts = (context_mine, context_other)
    middle, normed_two, across_two = middle_rows(place, contexts, attn_w, after(start, down_one), rows)
    hidden, slope = [None, None], [None, None]
    hidden[0], slope[0] = feed(normed_two, up_w[0], bias_up, 0)
    hidden[1], slope[1] = feed(normed_two, up_w[1], bias_up, 1)

    grad_branch = after((cotangent * absorbed).astype(BF), down_half)
    down_sum = reduction(hidden_part)
    down_got = down_sum.add(left_product(hidden[0], grad_branch), left_product(hidden[1], grad_branch))
    up_sum = reduction(2 * part)
    grad_pre, grad_b_up, grad_up = [None, None], [None, None], [None, None]
    grad_pre[1], grad_b_up[1], grad_up[1] = feed_back(grad_branch, down_w[1], slope[1], across_two, BF)
    if fast:
        down_sum.one()
    grad_pre[0], grad_b_up[0], grad_up[0] = feed_back(
        after(grad_branch, down_sum.sent), down_w[0], slope[0], across_two, F32
    )
    up_sum.add(grad_up[0], grad_up[1])
    if fast:
        down_sum.two()
    grad_pre = after(grad_pre, down_sum.sent)
    grad_middle, *grad_context, grad_out_mine, grad_out_other, middle_sums = middle_back(
        place, grad_pre, up_w, middle, cotangent, absorbed, rows, contexts, attn_w
    )

    attn_sum = reduction(2 * part)
    up_sum.add(grad_out_mine, grad_out_other)
    if fast:
        down_sum.along_z()
        up_sum.one()
    grads = [None, None]
    grads[1] = attention_back(
        qkv_other, after(grad_context[1], down_sum.sent, up_sum.sent), across_one, seq_length, BF
    )
    if fast:
        up_sum.two()
    grads[0] = attention_back(
        qkv_mine, after(grad_context[0], down_sum.got, up_sum.sent), across_one, seq_length, F32
    )
    grad_qkv, grad_weights, sums = zip(*grads)
    for index in range(3):
        attn_sum.add(grad_weights[0][index], grad_weights[1][index])
    if fast:
        up_sum.along_z()
    grad_qkv = after(grad_qkv, up_sum.sent)
    seqs = count * seq_count
    grad_tokens, blocks = start_back(
        place, grad_qkv, attn_w, start, grad_middle, absorbed, rows, middle_sums, sums, seqs, seq_length
    )

    grad_b_up = paired(core, *[item.reshape(chips, hidden_part) for item in grad_b_up], 1).reshape(count, hidden_part)
    grad_b_up = jnp.pad(grad_b_up[:, None], ((0, 0), (0, part - 1), (LANES - hidden_part, 0)))
    grad_b_up = grad_b_up.reshape(width, LANES)
    blocks = [blocks[:, :LANES] + grad_b_up, blocks[:, LANES:]]
    if fast:
        attn_sum.add(jnp.where(core == 0, *blocks), jnp.where(core == 0, *blocks[::-1]))
        attn_sum.one()
        attn_sum.two()
        attn_sum.along_z()
        attn_grad = attn_sum.columns()
        small, seq_sums = attn_grad[:, 0, 3 * half :], attn_grad[:, 1, 3 * half :]
    else:
        attn_grad = attn_sum.columns()
        small, seq_sums = [
            lax.psum_scatter(item.astype(BF), AXES, scatter_dimension=0, tiled=True).astype(F32) for item in blocks
        ]
    grad_b_up = small[0, LANES - hidden_part :]
    small = small[:, :fixed].T
    onehot = (steps[:, None] == lax.broadcasted_iota(jnp.int32, (seqs, table_cols), 1)).astype(F32)
    grad_time_table = jnp.dot(seq_sums, onehot, precision=lax.Precision.HIGHEST)
    grad_w_qkv = attn_grad[:, :, : 3 * half].reshape(part, 2, 3, half).transpose(0, 2, 1, 3).reshape(part, 3 * width)
    up_grad = up_sum.columns()
    grad_w_out = up_grad[:, :, hidden_width // 2 :].reshape(part, width)
    grad_w_up = up_grad[:, :, : hidden_width // 2].reshape(part, 2, chips, hidden_part).transpose(0, 2, 1, 3)
    grad_w_up = grad_w_up.reshape(part, hidden_width)
    hidden = after(hidden, attn_sum.sent)
    output = middle + (product(hidden[0], down_w[0]) + product(hidden[1], down_w[1]) + rows[seq_count + 3])
    return (
        output,
        grad_tokens,
        grad_w_qkv,
        grad_w_out,
        grad_w_up,
        down_sum.sums(),
        grad_time_table,
        small[0],
        small[1],
        small[2],
        grad_b_up,
        small[3],
        small[4],
        small[5],
        small[6],
        small[7],
        small[8],
    )


def solution(mesh):
    matrix, vector = P(AXES, None), P(AXES)
    fast = dict(mesh.shape) == {"fsdp": 8, "rep": 4}
    return jax.shard_map(
        functools.partial(body, fast),
        mesh=mesh,
        in_specs=(matrix, vector, vector) + (matrix,) * 6 + (vector,) * 10,
        out_specs=(matrix,) * 7 + (vector,) * 10,
        check_vma=False,
    )
```

```python
import functools
import math

import jax
import jax.numpy as jnp
from jax import lax
from jax.experimental import pallas as pl
from jax.experimental.pallas import tpu as pltpu
from jax.sharding import PartitionSpec as P

HDIM = 64
EPSILON = 1e-05
AXES = ("fsdp", "rep")
BF = jnp.bfloat16
F32 = jnp.float32
LANES = 128
VMEM_BYTES = 16 << 20
GELU_OUTER = math.sqrt(2.0 / math.pi)
GELU_INNER = 0.044715


def contract(left, right, left_dim, right_dim):
    dims = (((left_dim,), (right_dim,)), ((), ()))
    return lax.dot_general(left, right, dims, preferred_element_type=F32)


def product(left, right):
    return contract(left, right, 1, 0)


def left_product(left, right):
    return contract(left, right, 0, 0)


def right_product(left, right):
    return contract(left, right, 1, 1)


def pick(array, index, axis):
    return lax.dynamic_index_in_dim(array, index, axis, keepdims=False)


def paired(bit, mine, other, axis):
    return jnp.stack([jnp.where(bit == 0, mine, other), jnp.where(bit == 0, other, mine)], axis)


def after(value, *others):
    return lax.optimization_barrier((value, others))[0]


def lane_masks(factor):
    lane = lax.broadcasted_iota(jnp.int32, (1, LANES), 1)
    return [jnp.where((lane < HDIM) == (head == 0), factor, 0.0).astype(BF) for head in (0, 1)]


def softmax(scores):
    powers = jnp.exp(scores - jnp.max(scores, -1, keepdims=True))
    return powers * (1.0 / jnp.sum(powers, -1, keepdims=True))


def attention_kernel(length, scale, rows_ref, query_ref, key_ref, value_ref, bias_ref, qkv_ref, context_ref):
    rows = rows_ref[...]
    for index, weight in enumerate((query_ref, key_ref, value_ref)):
        qkv_ref[index] = (product(rows, weight[...]) + bias_ref[index : index + 1, :]).astype(BF)
    ones, scaled = lane_masks(1.0), lane_masks(scale)

    for sequence in range(rows.shape[0] // length):
        span = slice(sequence * length, (sequence + 1) * length)
        queries, key_rows, value_rows = [qkv_ref[index, span, :] for index in range(3)]
        total = 0.0
        for head in (0, 1):
            probs = softmax(right_product(queries * scaled[head], key_rows)).astype(BF)
            total = total + product(probs, value_rows * ones[head])
        context_ref[span, :] = total.astype(BF)


def attention(rows, weight, bias, length):
    tokens, width = rows.shape
    half = bias.shape[1]
    pairs = half // LANES

    def weight_spec(index):
        return pl.BlockSpec((width, LANES), lambda pair: (0, index * pairs + pair))

    return pl.pallas_call(
        functools.partial(attention_kernel, length, 1.0 / math.sqrt(HDIM)),
        grid=(pairs,),
        in_specs=[
            pl.BlockSpec((tokens, width), lambda pair: (0, 0)),
            weight_spec(0),
            weight_spec(1),
            weight_spec(2),
            pl.BlockSpec((8, LANES), lambda pair: (0, pair)),
        ],
        out_specs=[
            pl.BlockSpec((3, tokens, LANES), lambda pair: (0, 0, pair)),
            pl.BlockSpec((tokens, LANES), lambda pair: (0, pair)),
        ],
        out_shape=[
            jax.ShapeDtypeStruct((3, tokens, half), BF),
            jax.ShapeDtypeStruct((tokens, half), BF),
        ],
        compiler_params=pltpu.CompilerParams(vmem_limit_bytes=VMEM_BYTES),
        cost_estimate=pl.CostEstimate(
            flops=6 * tokens * width * half,
            bytes_accessed=2 * tokens * width + 6 * width * half + 8 * tokens * half,
            transcendentals=2 * tokens * length * pairs,
        ),
        name="attention",
    )(rows, weight, weight, weight, bias)


def attention_back_kernel(length, scale, qkv_ref, grad_ref, rows_ref, grads_ref, weight_ref, sums_ref):
    ones, scaled = lane_masks(1.0), lane_masks(scale)

    for sequence in range(grad_ref.shape[0] // length):
        span = slice(sequence * length, (sequence + 1) * length)
        queries, key_rows, value_rows = [qkv_ref[index, span, :] for index in range(3)]
        grad = grad_ref[span, :]
        grad_queries, grad_keys, grad_values = 0.0, 0.0, 0.0
        for head in (0, 1):
            probs = softmax(right_product(queries * scaled[head], key_rows))
            grad_head = grad * ones[head]
            grad_probs = right_product(grad_head, value_rows)
            grad_scores = probs * (grad_probs - jnp.sum(grad_probs * probs, -1, keepdims=True))
            grad_scores = grad_scores.astype(BF)
            grad_values = grad_values + left_product(probs.astype(BF), grad_head)
            grad_queries = grad_queries + product(grad_scores, key_rows * ones[head])
            grad_keys = grad_keys + left_product(grad_scores, queries * ones[head])
        grads_ref[0, span, :] = (grad_queries * scale).astype(BF)
        grads_ref[1, span, :] = (grad_keys * scale).astype(BF)
        grads_ref[2, span, :] = grad_values.astype(BF)

    rows = rows_ref[...]
    for index in range(3):
        grads = grads_ref[index]
        weight_ref[index] = product(rows, grads).astype(weight_ref.dtype)
        sums_ref[index : index + 1, :] = jnp.sum(grads.astype(F32), 0, keepdims=True)


def attention_back(qkv, grad, rows_across, length, dtype):
    _, tokens, half = qkv.shape
    width = rows_across.shape[0]
    pairs = half // LANES
    return pl.pallas_call(
        functools.partial(attention_back_kernel, length, 1.0 / math.sqrt(HDIM)),
        grid=(pairs,),
        in_specs=[
            pl.BlockSpec((3, tokens, LANES), lambda pair: (0, 0, pair)),
            pl.BlockSpec((tokens, LANES), lambda pair: (0, pair)),
            pl.BlockSpec((width, tokens), lambda pair: (0, 0)),
        ],
        out_specs=[
            pl.BlockSpec((3, tokens, LANES), lambda pair: (0, 0, pair)),
            pl.BlockSpec((3, width, LANES), lambda pair: (0, 0, pair)),
            pl.BlockSpec((3, LANES), lambda pair: (0, pair)),
        ],
        out_shape=[
            jax.ShapeDtypeStruct((3, tokens, half), BF),
            jax.ShapeDtypeStruct((3, width, half), dtype),
            jax.ShapeDtypeStruct((3, half), F32),
        ],
        compiler_params=pltpu.CompilerParams(vmem_limit_bytes=VMEM_BYTES),
        cost_estimate=pl.CostEstimate(
            flops=6 * tokens * width * half,
            bytes_accessed=2 * tokens * width + 12 * width * half + 14 * tokens * half,
            transcendentals=2 * tokens * length * pairs,
        ),
        name="attention_back",
    )(qkv, grad, rows_across)


def feed_kernel(side, rows_ref, weight_ref, bias_ref, hidden_ref, slope_ref, pre_ref):
    pre_ref[...] = product(rows_ref[...], weight_ref[...])
    step = 32

    def chunk(index, carry):
        span = pl.ds(pl.multiple_of(index * step, step), step)
        pre = pre_ref[span, :] + bias_ref[side : side + 1, :]
        square = pre * pre
        bend = jnp.tanh(GELU_OUTER * (pre + GELU_INNER * (square * pre)))
        share = 0.5 * (1.0 + bend)
        hidden_ref[span, :] = (pre * share).astype(BF)
        inner = (0.5 * GELU_OUTER) * pre * (1.0 + (3.0 * GELU_INNER) * square)
        slope_ref[span, :] = share + inner * (1.0 - bend * bend)
        return carry

    lax.fori_loop(0, rows_ref.shape[0] // step, chunk, 0, unroll=2)


def feed(rows, weight, bias, side, block=512):
    tokens, width = rows.shape
    columns = weight.shape[1]
    block = math.gcd(block, columns)
    out = pl.BlockSpec((tokens, block), lambda step: (0, step))
    return pl.pallas_call(
        functools.partial(feed_kernel, side),
        grid=(columns // block,),
        in_specs=[
            pl.BlockSpec((tokens, width), lambda step: (0, 0)),
            pl.BlockSpec((width, block), lambda step: (0, step)),
            pl.BlockSpec((8, block), lambda step: (0, step)),
        ],
        out_specs=[out, out],
        out_shape=[
            jax.ShapeDtypeStruct((tokens, columns), BF),
            jax.ShapeDtypeStruct((tokens, columns), F32),
        ],
        scratch_shapes=[pltpu.VMEM((tokens, block), F32)],
        compiler_params=pltpu.CompilerParams(vmem_limit_bytes=VMEM_BYTES),
        cost_estimate=pl.CostEstimate(
            flops=2 * tokens * width * columns,
            bytes_accessed=2 * tokens * width + 2 * width * columns + 6 * tokens * columns,
            transcendentals=tokens * columns,
        ),
        name="feed",
    )(rows, weight, bias)


def feed_back_kernel(grad_ref, weight_ref, slope_ref, rows_ref, pre_ref, sum_ref, up_ref):
    grad = (right_product(grad_ref[...], weight_ref[...]) * slope_ref[...]).astype(BF)
    pre_ref[...] = grad
    sum_ref[...] = jnp.sum(grad.astype(F32), 0, keepdims=True)
    up_ref[...] = product(rows_ref[...], grad).astype(up_ref.dtype)


def feed_back(grad, weight, slope, rows_across, dtype, block=512):
    tokens, width = grad.shape
    columns = weight.shape[0]
    block = math.gcd(block, columns)
    out = pl.BlockSpec((tokens, block), lambda step: (0, step))
    return pl.pallas_call(
        feed_back_kernel,
        grid=(columns // block,),
        in_specs=[
            pl.BlockSpec((tokens, width), lambda step: (0, 0)),
            pl.BlockSpec((block, width), lambda step: (step, 0)),
            out,
            pl.BlockSpec((width, tokens), lambda step: (0, 0)),
        ],
        out_specs=[
            out,
            pl.BlockSpec((1, block), lambda step: (0, step)),
            pl.BlockSpec((width, block), lambda step: (0, step)),
        ],
        out_shape=[
            jax.ShapeDtypeStruct((tokens, columns), BF),
            jax.ShapeDtypeStruct((1, columns), F32),
            jax.ShapeDtypeStruct((width, columns), dtype),
        ],
        compiler_params=pltpu.CompilerParams(vmem_limit_bytes=VMEM_BYTES),
        cost_estimate=pl.CostEstimate(
            flops=4 * tokens * width * columns,
            bytes_accessed=4 * tokens * width + 6 * width * columns + 6 * tokens * columns,
            transcendentals=0,
        ),
        name="feed_back",
    )(grad, weight, slope, rows_across)


def chosen_side(core, mine, other):
    return jnp.where(core == 0, mine, other), jnp.where(core == 0, other, mine)


def normalized(values):
    center = values - jnp.mean(values, -1, keepdims=True)
    rate = lax.rsqrt(jnp.mean(center * center, -1, keepdims=True) + EPSILON)
    return center * rate, rate


def start_kernel(
    fixed, up_cols, table_cols, seq_count, parts,
    place_ref, tokens_ref, mask_ref, table_mine_ref, table_other_ref,
    rows_ref, start_ref, normed_ref, across_ref, bias_mine_ref, bias_other_ref, bias_up_ref,
):
    core = place_ref[0]
    step = pl.program_id(0)
    width = tokens_ref.shape[1]
    half = width // 2
    chips, part, hidden_part = parts

    @pl.when(step == 0)
    def _():
        count, columns = rows_ref.shape[0], table_mine_ref.shape[1]
        row = lax.broadcasted_iota(jnp.int32, (count, columns), 0)
        wanted = table_cols + row - seq_count
        for index in range(seq_count):
            wanted = jnp.where(row == index, place_ref[2 + index], wanted)
        column = lax.broadcasted_iota(jnp.int32, (count, columns), 1)
        rows = 0.0
        for side, table in ((core, table_mine_ref), (1 - core, table_other_ref)):
            hit = jnp.where(wanted == column + side * columns, 1.0, 0.0).astype(BF)
            rows = rows + right_product(hit, table[...])
        rows_ref[...] = rows
        for ref, side in ((bias_mine_ref, core), (bias_other_ref, 1 - core)):
            ref[...] = jnp.zeros_like(ref)
            for index in (0, 1):
                line = rows_ref[seq_count + index : seq_count + index + 1, :]
                ref[2 * index : 2 * index + 1, :] = jnp.where(side == 0, line[:, :half], line[:, half:])
        for chip in range(chips):
            for index in range(up_cols):
                line = rows_ref[seq_count + fixed + index : seq_count + fixed + index + 1, :]
                pair = [line[:, (2 * chip + i) * part : (2 * chip + i + 1) * part] for i in range(2)]
                where = slice(chip * hidden_part + index * part, chip * hidden_part + (index + 1) * part)
                bias_up_ref[0:1, where], bias_up_ref[1:2, where] = chosen_side(core, *pair)

    small = seq_count
    mask = mask_ref[...]
    start = jnp.where(mask > 0.0, rows_ref[small + 8 : small + 9, :], tokens_ref[...])
    start = start + rows_ref[pl.ds(step, 1), :]
    start_ref[...] = start
    normed, _ = normalized(start)
    normed = normed * rows_ref[small + 4 : small + 5, :] + rows_ref[small + 5 : small + 6, :]
    normed_ref[...] = normed.astype(BF)
    across_ref[...] = normed.T.astype(BF)


def start_rows(place, tokens, mask, weights, fixed, up_cols, table_cols, small_cols, chips, hidden_part):
    count, width = tokens.shape
    seq_count = place.shape[0] - 2
    length = count // seq_count
    half = width // 2
    row_count = -(-(seq_count + small_cols) // 8) * 8
    table_half = weights[0].shape[1] - 4 * half
    tables = 4 * half // table_half
    table_spec = pl.BlockSpec((width, table_half), lambda step: (0, tables))
    rows_spec = pl.BlockSpec((length, width), lambda step: (step, 0))

    def fixed_spec(*shape):
        return pl.BlockSpec(shape, lambda step: (0,) * len(shape))

    return pl.pallas_call(
        functools.partial(
            start_kernel, fixed, up_cols, table_cols, seq_count, (chips, width // (2 * chips), hidden_part)
        ),
        grid=(seq_count,),
        in_specs=[
            pl.BlockSpec(memory_space=pltpu.SMEM),
            rows_spec,
            pl.BlockSpec((length, 1), lambda step: (step, 0)),
            table_spec,
            table_spec,
        ],
        out_specs=[
            fixed_spec(row_count, width),
            rows_spec,
            rows_spec,
            pl.BlockSpec((width, length), lambda step: (0, step)),
            fixed_spec(8, half),
            fixed_spec(8, half),
            fixed_spec(8, chips * hidden_part),
        ],
        out_shape=[
            jax.ShapeDtypeStruct((row_count, width), F32),
            jax.ShapeDtypeStruct((count, width), F32),
            jax.ShapeDtypeStruct((count, width), BF),
            jax.ShapeDtypeStruct((width, count), BF),
            jax.ShapeDtypeStruct((8, half), F32),
            jax.ShapeDtypeStruct((8, half), F32),
            jax.ShapeDtypeStruct((8, chips * hidden_part), F32),
        ],
        compiler_params=pltpu.CompilerParams(vmem_limit_bytes=VMEM_BYTES),
        cost_estimate=pl.CostEstimate(
            flops=4 * row_count * width * table_half, bytes_accessed=14 * count * width, transcendentals=0
        ),
        name="start_rows",
    )(place, tokens, mask, *weights)


def middle_kernel(
    small, place_ref, context_mine_ref, context_other_ref, out_mine_ref, out_other_ref, start_ref, rows_ref,
    middle_ref, normed_ref, across_ref,
):
    core = place_ref[0]
    half = context_mine_ref.shape[1]
    contexts = chosen_side(core, context_mine_ref[...], context_other_ref[...])
    outs = chosen_side(core, out_mine_ref[...], out_other_ref[...])
    for index, out in enumerate(outs):
        span = slice(index * half, (index + 1) * half)
        total = product(contexts[0], out[:half]) + product(contexts[1], out[half:])
        middle_ref[:, span] = start_ref[:, span] + (total + rows_ref[small + 2 : small + 3, span])
    normed, _ = normalized(middle_ref[...])
    normed = normed * rows_ref[small + 6 : small + 7, :] + rows_ref[small + 7 : small + 8, :]
    normed_ref[...] = normed.astype(BF)
    across_ref[...] = normed.T.astype(BF)


def middle_rows(place, contexts, weights, start, rows, block=256):
    count, width = start.shape
    half = width // 2
    small = place.shape[0] - 2
    block = math.gcd(block, count)
    out_spec = pl.BlockSpec((width, half), lambda step: (0, 3))
    rows_spec = pl.BlockSpec((block, width), lambda step: (step, 0))
    half_spec = pl.BlockSpec((block, half), lambda step: (step, 0))
    return pl.pallas_call(
        functools.partial(middle_kernel, small),
        grid=(count // block,),
        in_specs=[
            pl.BlockSpec(memory_space=pltpu.SMEM),
            half_spec,
            half_spec,
            out_spec,
            out_spec,
            rows_spec,
            pl.BlockSpec(rows.shape, lambda step: (0, 0)),
        ],
        out_specs=[rows_spec, rows_spec, pl.BlockSpec((width, block), lambda step: (0, step))],
        out_shape=[
            jax.ShapeDtypeStruct((count, width), F32),
            jax.ShapeDtypeStruct((count, width), BF),
            jax.ShapeDtypeStruct((width, count), BF),
        ],
        compiler_params=pltpu.CompilerParams(vmem_limit_bytes=VMEM_BYTES),
        cost_estimate=pl.CostEstimate(
            flops=2 * count * width * width, bytes_accessed=14 * count * width + 2 * width * width, transcendentals=0
        ),
        name="middle_rows",
    )(place, *contexts, *weights, start, rows)


def norm_back(values, gain, grad):
    unit, rate = normalized(values)
    scaled = grad * gain
    back = scaled - jnp.mean(scaled, -1, keepdims=True) - unit * jnp.mean(scaled * unit, -1, keepdims=True)
    return rate * back, grad * unit


def middle_back_kernel(
    small, place_ref, pre_mine_ref, pre_other_ref, up_mine_ref, up_other_ref, middle_ref, cotangent_ref, mask_ref,
    rows_ref, context_mine_ref, context_other_ref, out_mine_ref, out_other_ref,
    grad_ref, context_grad_mine_ref, context_grad_other_ref, out_grad_mine_ref, out_grad_other_ref, sums_ref,
    normed_ref, total_ref,
):
    core = place_ref[0]
    step = pl.program_id(0)
    half = context_mine_ref.shape[1]

    @pl.when(step == 0)
    def _():
        sums_ref[...] = jnp.zeros_like(sums_ref)
        total_ref[...] = jnp.zeros_like(total_ref)

    normed_ref[...] = right_product(pre_mine_ref[...], up_mine_ref[...]) + right_product(
        pre_other_ref[...], up_other_ref[...]
    )
    grad = normed_ref[...]
    direct = cotangent_ref[...] * mask_ref[...]
    back, shares = norm_back(middle_ref[...], rows_ref[small + 6 : small + 7, :], grad)
    back = direct + back
    grad_ref[...] = back
    low = back.astype(BF)
    for index, item in enumerate((low.astype(F32), direct.astype(BF).astype(F32), shares, grad)):
        sums_ref[index : index + 1, :] += jnp.sum(item, 0, keepdims=True)
    lows = (low[:, :half], low[:, half:])
    contexts = chosen_side(core, context_mine_ref[...], context_other_ref[...])
    outs = chosen_side(core, out_mine_ref[...], out_other_ref[...])
    context_grads = [
        (right_product(lows[0], outs[0][span]) + right_product(lows[1], outs[1][span])).astype(BF)
        for span in (slice(0, half), slice(half, None))
    ]
    context_grad_mine_ref[...], context_grad_other_ref[...] = chosen_side(core, *context_grads)
    for index, item in enumerate(chosen_side(core, *lows)):
        for side, context in enumerate(contexts):
            total_ref[index, side * half : (side + 1) * half, :] += left_product(context, item)

    @pl.when(step == pl.num_programs(0) - 1)
    def _():
        out_grad_mine_ref[...] = total_ref[0]
        out_grad_other_ref[...] = total_ref[1].astype(BF)


def middle_back(place, grads, ups, middle, cotangent, mask, rows, contexts, weights, block=256):
    count, width = middle.shape
    half = width // 2
    hidden_half = ups[0].shape[1]
    small = place.shape[0] - 2
    block = math.gcd(block, count)

    def over_rows(columns):
        return pl.BlockSpec((block, columns), lambda step: (step, 0))

    def whole(*shape):
        return pl.BlockSpec(shape, lambda step: (0,) * len(shape))

    out_spec = pl.BlockSpec((width, half), lambda step: (0, 3))
    return pl.pallas_call(
        functools.partial(middle_back_kernel, small),
        grid=(count // block,),
        in_specs=[
            pl.BlockSpec(memory_space=pltpu.SMEM),
            over_rows(hidden_half),
            over_rows(hidden_half),
            whole(width, hidden_half),
            whole(width, hidden_half),
            over_rows(width),
            over_rows(width),
            over_rows(1),
            whole(*rows.shape),
            over_rows(half),
            over_rows(half),
            out_spec,
            out_spec,
        ],
        out_specs=[
            over_rows(width),
            over_rows(half),
            over_rows(half),
            whole(width, half),
            whole(width, half),
            whole(8, width),
        ],
        out_shape=[
            jax.ShapeDtypeStruct((count, width), F32),
            jax.ShapeDtypeStruct((count, half), BF),
            jax.ShapeDtypeStruct((count, half), BF),
            jax.ShapeDtypeStruct((width, half), F32),
            jax.ShapeDtypeStruct((width, half), BF),
            jax.ShapeDtypeStruct((8, width), F32),
        ],
        scratch_shapes=[pltpu.VMEM((block, width), F32), pltpu.VMEM((2, width, half), F32)],
        compiler_params=pltpu.CompilerParams(vmem_limit_bytes=2 * VMEM_BYTES),
        cost_estimate=pl.CostEstimate(
            flops=4 * count * width * (hidden_half + width),
            bytes_accessed=4 * count * hidden_half + 4 * width * hidden_half + 16 * count * width,
            transcendentals=0,
        ),
        name="middle_back",
    )(place, *grads, *ups, middle, cotangent, mask, rows, *contexts, *weights)


def start_back_kernel(
    small, length, swap, place_ref, grads_mine_ref, grads_other_ref, weight_mine_ref, weight_other_ref, start_ref, middle_ref,
    mask_ref, rows_ref, sums_ref, sums_mine_ref, sums_other_ref, bias_ref,
    tokens_ref, mine_ref, other_ref, lines_ref,
):
    core, place = place_ref[0], place_ref[1]
    step = pl.program_id(0)
    width = start_ref.shape[1]
    half = width // 2
    seqs = start_ref.shape[0] // length

    @pl.when(step == 0)
    def _():
        lines_ref[...] = jnp.zeros_like(lines_ref)
        for index, row in ((0, 0), (1, 2)):
            pair = (sums_mine_ref[row : row + 1, :], sums_other_ref[row : row + 1, :])
            lines_ref[index : index + 1, :half], lines_ref[index : index + 1, half:] = chosen_side(core, *pair)
        lines_ref[2:4, :] = sums_ref[0:2, :]
        lines_ref[6:8, :] = sums_ref[2:4, :]

    grad = 0.0
    for grads, weight in ((grads_mine_ref, weight_mine_ref), (grads_other_ref, weight_other_ref)):
        for index in range(3):
            grad = grad + right_product(grads[index], weight[:, index * half : (index + 1) * half])
    back, shares = norm_back(start_ref[...], rows_ref[small + 4 : small + 5, :], grad)
    back = middle_ref[...] + back
    mask = mask_ref[...]
    tokens_ref[...] = jnp.where(mask > 0.0, 0.0, back)
    for index, item in ((4, shares), (5, grad), (8, back * mask)):
        lines_ref[index : index + 1, :] += jnp.sum(item, 0, keepdims=True)
    for index in range(seqs):
        line = LANES + place * small + step * seqs + index
        lines_ref[pl.ds(line, 1), :] = jnp.sum(back[index * length : (index + 1) * length], 0, keepdims=True)

    @pl.when(step == pl.num_programs(0) - 1)
    def _():
        blocks = (lines_ref[:LANES, :].T + bias_ref[...], lines_ref[LANES:, :].T)
        if swap:
            blocks = chosen_side(core, *blocks)
        mine_ref[...] = blocks[0]
        other_ref[...] = blocks[1].astype(other_ref.dtype)


def start_back(
    place, grads, weights, start, middle, mask, rows, sums, side_sums, bias, seqs, length, swap, block=256
):
    count, width = start.shape
    half = width // 2
    small = place.shape[0] - 2
    block = math.gcd(block, count)
    lines = LANES + -(-seqs // LANES) * LANES

    def over_rows(columns):
        return pl.BlockSpec((block, columns), lambda step: (step, 0))

    def whole(*shape):
        return pl.BlockSpec(shape, lambda step: (0,) * len(shape))

    grads_spec = pl.BlockSpec((3, block, half), lambda step: (0, step, 0))
    return pl.pallas_call(
        functools.partial(start_back_kernel, small, length, swap),
        grid=(count // block,),
        in_specs=[
            pl.BlockSpec(memory_space=pltpu.SMEM),
            grads_spec,
            grads_spec,
            whole(width, 3 * half),
            whole(width, 3 * half),
            over_rows(width),
            over_rows(width),
            over_rows(1),
            whole(*rows.shape),
            whole(*sums.shape),
            whole(*side_sums[0].shape),
            whole(*side_sums[1].shape),
            whole(width, LANES),
        ],
        out_specs=[over_rows(width), whole(width, LANES), whole(width, lines - LANES)],
        out_shape=[
            jax.ShapeDtypeStruct((count, width), F32),
            jax.ShapeDtypeStruct((width, LANES), F32),
            jax.ShapeDtypeStruct((width, lines - LANES), BF if swap else F32),
        ],
        scratch_shapes=[pltpu.VMEM((lines, width), F32)],
        compiler_params=pltpu.CompilerParams(vmem_limit_bytes=VMEM_BYTES),
        cost_estimate=pl.CostEstimate(
            flops=4 * count * width * 3 * half,
            bytes_accessed=12 * count * half + 12 * width * half + 12 * count * width,
            transcendentals=0,
        ),
        name="start_back",
    )(place, *grads, *weights, start, middle, mask, rows, sums, *side_sums, bias)


def shards_kernel(fixed, seq_cols, place_ref, qkv_ref, out_ref, table_ref, *refs):
    small_refs, (mine_ref, other_ref, full_ref) = refs[: fixed + 1], refs[fixed + 1 :]
    core = place_ref[0]
    part, table_cols = table_ref.shape
    half = out_ref.shape[1] // 2
    seq_count = place_ref.shape[0] - 2
    lines = [ref[...] for ref in small_refs[:fixed]]
    up = small_refs[fixed][...]
    lines += [up[:, i : i + part] for i in range(0, up.shape[1], part)]
    lane = lax.broadcasted_iota(jnp.int32, (1, part), 1)
    for row in range(seq_cols):
        line = jnp.zeros((1, part), jnp.int32)
        for index in range(seq_count):
            step = place_ref[2 + index]
            line = jnp.where(lane + row * part == index, step // 256, line)
            line = jnp.where(lane + row * part == seq_count + index, step % 256, line)
        lines.append(line.astype(F32))
    lines = jnp.concatenate(lines, 0).astype(BF)
    square = (part, part)
    unit = lax.broadcasted_iota(jnp.int32, square, 0) == lax.broadcasted_iota(jnp.int32, square, 1)
    full_ref[...] = jnp.zeros_like(full_ref)
    full_ref[:, :table_cols] = table_ref[...]
    full_ref[:, table_cols : table_cols + lines.shape[0]] = right_product(jnp.where(unit, 1.0, 0.0).astype(BF), lines)
    table_half = full_ref.shape[1] // 2

    def halves(ref, top, wide):
        return chosen_side(core, ref[:, top : top + wide], ref[:, top + wide : top + 2 * wide])

    sources = [(qkv_ref, 2 * half * i, half) for i in range(3)] + [(out_ref, 0, half), (full_ref, 0, table_half)]
    left = 0
    for ref, top, wide in sources:
        mine, other = halves(ref, top, wide)
        mine_ref[:, left : left + wide] = mine.astype(BF)
        other_ref[:, left : left + wide] = other.astype(BF)
        left += wide


def attention_shards(place, w_qkv, w_out, table, small, b_up, seq_cols, all_cols):
    part = table.shape[0]
    shape = jax.ShapeDtypeStruct((part, 2 * w_out.shape[1] + all_cols // 2), BF)
    vmem = pl.BlockSpec(memory_space=pltpu.VMEM)
    return pl.pallas_call(
        functools.partial(shards_kernel, len(small), seq_cols),
        in_specs=[pl.BlockSpec(memory_space=pltpu.SMEM)] + [vmem] * (4 + len(small)),
        out_specs=[vmem, vmem],
        out_shape=[shape, shape],
        scratch_shapes=[pltpu.VMEM((part, all_cols), F32)],
        compiler_params=pltpu.CompilerParams(vmem_limit_bytes=VMEM_BYTES),
        cost_estimate=pl.CostEstimate(flops=0, bytes_accessed=24 * part * w_out.shape[1], transcendentals=0),
        name="attention_shards",
    )(place, w_qkv, w_out, table, *[item.reshape(1, -1) for item in small], b_up.reshape(1, -1))


def route_kernel(rows, route_ref, *refs):
    terms, (sent_ref, kept_ref) = refs[:-2], refs[-2:]
    for index in range(2):
        for out, place in ((sent_ref, route_ref[index]), (kept_ref, route_ref[2 + index])):
            span = pl.ds(pl.multiple_of(place * rows, 8), rows)
            left = 0
            for mine, got in zip(terms[::2], terms[1::2]):
                many = [(slice(None),)] if len(mine.shape) == 2 else [(i, slice(None)) for i in range(mine.shape[0])]
                for at in many:
                    where = (*at[:-1], span)
                    total = mine[where].astype(F32) + got[where].astype(F32)
                    out[0, index, :, left : left + total.shape[1]] = total.astype(out.dtype)
                    left += total.shape[1]


def routed(terms, rows, route):
    specs, columns, bytes_read = [], 0, 0
    for array in [item for pair in terms for item in pair]:
        shape = (4 * rows, array.shape[-1])
        if array.ndim == 2:
            specs.append(pl.BlockSpec(shape, lambda z: (z, 0)))
        else:
            specs.append(pl.BlockSpec((array.shape[0], *shape), lambda z: (0, z, 0)))
        bytes_read += array.size * array.dtype.itemsize
        columns += array.size // (16 * rows)
    columns //= 2
    out = pl.BlockSpec((1, 2, rows, columns), lambda z: (z, 0, 0, 0))
    return pl.pallas_call(
        functools.partial(route_kernel, rows),
        grid=(4,),
        in_specs=[pl.BlockSpec(memory_space=pltpu.SMEM)] + specs,
        out_specs=[out, out],
        out_shape=[
            jax.ShapeDtypeStruct((4, 2, rows, columns), BF),
            jax.ShapeDtypeStruct((4, 2, rows, columns), F32),
        ],
        compiler_params=pltpu.CompilerParams(vmem_limit_bytes=VMEM_BYTES),
        cost_estimate=pl.CostEstimate(
            flops=0, bytes_accessed=bytes_read + 48 * rows * columns, transcendentals=0
        ),
        name="routed",
    )(route, *[item for pair in terms for item in pair])


class Tree:
    def __init__(self):
        fsdp, rep = lax.axis_index("fsdp"), lax.axis_index("rep")
        self.z, self.core = fsdp // 2, rep % 2
        x, y = rep // 2, fsdp % 2
        self.near = jnp.where(self.core == 0, x, y)
        self.far = jnp.where(self.core == 0, y, x)
        places = [jnp.where(self.core == 0, 2 * i + near, 2 * near + i) for near in (1 - self.near, self.near) for i in (0, 1)]
        self.route = jnp.stack(places)

    def to_core(self, value):
        return lax.ppermute(value, "rep", [(i, i ^ 1) for i in range(4)])

    def to_near(self, value):
        return lax.ppermute(value, AXES, [(i, i ^ (4 if i % 2 else 2)) for i in range(32)])

    def to_far(self, value):
        return lax.ppermute(value, AXES, [(i, i ^ (2 if i % 2 else 4)) for i in range(32)])

    def to_z(self, value, step):
        return lax.ppermute(value, "fsdp", [(i, i ^ (2 * step)) for i in range(8)])


class Gather:
    def __init__(self, tree, own):
        self.tree, self.own = tree, own

    @staticmethod
    def columns(tree, mine, other):
        got = tree.to_core(other)
        return Gather(tree, paired(tree.core, mine, got, 0).reshape(-1, mine.shape[1]))

    @staticmethod
    def rows(tree, shard):
        return Gather(tree, shard)

    def along_z(self, *wait):
        own = after(self.own, *wait)
        self.got = [self.tree.to_z(own, step) for step in (1, 2, 3)]
        self.held = own
        return self.got

    def one(self, *wait):
        tree = self.tree
        held = after([self.held, *self.got], *wait)
        low, high = tree.z % 2 == 1, tree.z // 2 == 1
        out = []
        for place in range(4):
            near = [jnp.where(low, held[(place ^ 1) ^ h], held[place ^ h]) for h in (0, 2)]
            out.append(jnp.where(high, near[1], near[0]))
        self.held = jnp.stack(out)
        self.got = tree.to_near(self.held)
        return self.got

    def two(self, *wait):
        tree = self.tree
        held, got = after((self.held, self.got), *wait)
        self.held = paired(tree.near, held, got, 1)
        self.got = tree.to_far(self.held)
        return self.got

    def halves(self, *wait):
        tree = self.tree
        held, got = after((self.held, self.got), *wait)
        same, first = tree.far == 0, tree.core == 0
        lower, upper = jnp.where(same, held, got), jnp.where(same, got, held)
        blocks = [
            lower[:, 0],
            jnp.where(first, lower[:, 1], upper[:, 0]),
            jnp.where(first, upper[:, 0], lower[:, 1]),
            upper[:, 1],
        ]
        half = jnp.stack(blocks, 1).reshape(-1, held.shape[-1])
        return half, tree.to_core(half)


class Reduce:
    def __init__(self, tree, rows):
        self.tree, self.rows = tree, rows
        self.terms = []

    def add(self, mine, other):
        got = self.tree.to_core(other.astype(BF))
        self.terms.append((mine, got))
        return got

    def one(self, *wait):
        self.sent, self.kept = routed(after(self.terms, *wait), self.rows, self.tree.route)
        self.got = self.tree.to_near(self.sent)

    def two(self, *wait):
        tree = self.tree
        kept, got = after((self.kept, self.got), *wait)
        total = kept + got
        self.kept, self.sent = pick(total, tree.far, 1), pick(total, 1 - tree.far, 1).astype(BF)
        self.got = tree.to_far(self.sent)

    def along_z(self, *others):
        tree = self.tree
        total = jnp.concatenate([item.kept + item.got for item in (self, *others)], -1)
        self.kept = pick(total, tree.z, 0)
        self.sent = tuple(pick(total, tree.z ^ step, 0).astype(BF) for step in (1, 2, 3))
        self.got = tuple(tree.to_z(sent, step) for sent, step in zip(self.sent, (1, 2, 3)))

    def sums(self, *wait):
        kept, got = after((self.kept, self.got), *wait)
        return kept + got[0] + got[1] + got[2]

    def columns(self, *wait):
        tree, total = self.tree, self.sums(*wait)
        rows = total.reshape(2, self.rows // 2, -1)
        keep = pick(rows, tree.core, 0)
        return paired(tree.core, keep, tree.to_core(pick(rows, 1 - tree.core, 0)), 1)


class Whole:
    core = 0

    def __init__(self, rows=None):
        self.mine, self.other = [], []
        self.got, self.sent = (), ()

    @staticmethod
    def columns_of(mine, other):
        out = Whole()
        whole = lax.all_gather(jnp.stack([mine, other], 1), AXES, axis=0, tiled=True)
        out.half, out.rest = whole[:, 0], whole[:, 1]
        return out

    @staticmethod
    def rows_of(shard):
        out = Whole()
        whole = lax.all_gather(shard, AXES, axis=0)
        whole = whole.reshape(-1, 2, *shard.shape)
        out.half, out.rest = [whole[:, i].reshape(-1, shard.shape[1]) for i in range(2)]
        return out

    def along_z(self, *wait):
        return ()

    def one(self, *wait):
        return ()

    def two(self, *wait):
        return ()

    def halves(self, *wait):
        return self.half, self.rest

    def add(self, mine, other):
        self.mine.append(mine.astype(BF))
        self.other.append(other.astype(BF))
        return mine

    def columns(self):
        def flat(items):
            return jnp.concatenate([part for item in items for part in (item if item.ndim == 3 else [item])], 1)

        parts = [flat(item) for item in (self.mine, self.other)]
        return lax.psum_scatter(jnp.stack(parts, 1), AXES, scatter_dimension=0, tiled=True).astype(F32)

    def sums(self):
        count = lax.axis_size(AXES)
        mine, other = [item[0].reshape(count // 2, -1, item[0].shape[1]) for item in (self.mine, self.other)]
        sums = jnp.stack([mine, other], 1).reshape(-1, mine.shape[-1])
        return lax.psum_scatter(sums, AXES, scatter_dimension=0, tiled=True).astype(F32)


def body(
    fast,
    tokens,
    mask_bits,
    timesteps,
    cotangent,
    w_qkv,
    w_out,
    w_up,
    w_down,
    time_table,
    b_query,
    b_value,
    b_out,
    b_up,
    b_down,
    gain_attn,
    shift_attn,
    gain_mlp,
    shift_mlp,
    mask_vector,
):
    tree = Tree() if fast else Whole()
    gather_columns = functools.partial(Gather.columns, tree) if fast else Whole.columns_of
    gather_rows = functools.partial(Gather.rows, tree) if fast else Whole.rows_of
    reduction = functools.partial(Reduce, tree) if fast else Whole
    core = tree.core
    count = lax.axis_size(AXES)
    chips = count // 2
    place = lax.axis_index(AXES)
    width = tokens.shape[1]
    part = width // count
    hidden_width = w_up.shape[1]
    hidden_part = hidden_width // count
    seq_count = timesteps.shape[0]
    seq_length = tokens.shape[0] // seq_count
    half = width // 2
    table_cols = time_table.shape[1]
    absorbed = mask_bits.astype(F32)[:, None]

    small = [b_query, b_value, b_out, b_down, gain_attn, shift_attn, gain_mlp, shift_mlp, mask_vector]
    fixed = len(small)
    up_cols = hidden_part // part
    seq_cols = -(-2 * seq_count // part)
    small_cols = fixed + up_cols + seq_cols
    all_cols = -(-(table_cols + small_cols) // (2 * LANES)) * (2 * LANES)
    place = jnp.concatenate([jnp.stack([jnp.int32(core), place]), timesteps])

    attn_w = gather_columns(*attention_shards(place, w_qkv, w_out, time_table, small, b_up, seq_cols, all_cols))
    up_shard = w_up.astype(BF).reshape(part, chips, 2, hidden_part).transpose(2, 0, 1, 3)
    up_shard = up_shard.reshape(2, part, hidden_width // 2)
    up_w = gather_columns(*[pick(up_shard, side, 0) for side in (core, 1 - core)])
    down_w = gather_rows(w_down.astype(BF))
    attn_w.along_z()
    attn_one = attn_w.one()
    up_z = up_w.along_z(attn_one)
    attn_two = attn_w.two()
    up_one = up_w.one(attn_two)
    attn_w = attn_w.halves(up_z)
    down_z = down_w.along_z(attn_two)

    rows, start, normed_one, across_one, bias_mine, bias_other, bias_up = start_rows(
        place, tokens, absorbed, attn_w, fixed, up_cols, table_cols, small_cols, chips, hidden_part
    )
    steps = rows[seq_count + fixed + up_cols : seq_count + small_cols]
    steps = steps.reshape(seq_cols, count, part).transpose(1, 0, 2).reshape(count, -1).astype(jnp.int32)
    steps = (steps[:, :seq_count] * 256 + steps[:, seq_count : 2 * seq_count]).reshape(-1)

    up_two = up_w.two(normed_one)
    qkv_mine, context_mine = attention(after(normed_one, up_one), attn_w[0], bias_mine, seq_length)
    down_one = down_w.one(up_two, context_mine)
    up_w = up_w.halves(context_mine)
    qkv_other, context_other = attention(after(normed_one, up_two), attn_w[1], bias_other, seq_length)
    down_two = down_w.two(context_other)
    contexts = (context_mine, context_other)
    middle, normed_two, across_two = middle_rows(place, contexts, attn_w, after(start, down_one), rows)
    hidden, slope = [None, None], [None, None]
    hidden[0], slope[0] = feed(normed_two, up_w[0], bias_up, 0)
    down_w = down_w.halves(hidden[0])
    hidden[1], slope[1] = feed(after(normed_two, down_two), up_w[1], bias_up, 1)

    grad_branch = (cotangent * absorbed).astype(BF)
    down_sum = reduction(hidden_part)
    down_sum.add(left_product(hidden[0], grad_branch), left_product(hidden[1], grad_branch))
    up_sum = reduction(2 * part)
    grad_pre, grad_b_up, grad_up = [None, None], [None, None], [None, None]
    if fast:
        down_sum.one()
    grad_pre[1], grad_b_up[1], grad_up[1] = feed_back(
        after(grad_branch, down_sum.sent), down_w[1], slope[1], across_two, BF
    )
    grad_pre[0], grad_b_up[0], grad_up[0] = feed_back(grad_branch, down_w[0], slope[0], across_two, F32)
    up_sum.add(grad_up[0], grad_up[1])
    if fast:
        down_sum.two(grad_pre[0])
    grad_pre = after(grad_pre, down_sum.sent)
    grad_middle, *grad_context, grad_out_mine, grad_out_other, middle_sums = middle_back(
        place, grad_pre, up_w, middle, cotangent, absorbed, rows, contexts, attn_w
    )

    attn_sum = reduction(2 * part)
    up_sum.add(grad_out_mine, grad_out_other)
    if fast:
        up_sum.one(down_sum.got)
        down_sum.along_z()
    grads = [None, None]
    grads[1] = attention_back(
        qkv_other, after(grad_context[1], down_sum.sent, up_sum.sent), across_one, seq_length, BF
    )
    if fast:
        up_sum.two(down_sum.got, grads[1])
    grads[0] = attention_back(qkv_mine, after(grad_context[0], up_sum.sent), across_one, seq_length, F32)
    grad_qkv, grad_weights, sums = zip(*grads)
    attn_sum.add(grad_weights[0], grad_weights[1])
    if fast:
        attn_sum.one(up_sum.got)
        up_sum.along_z()
    grad_qkv = after(grad_qkv, up_sum.sent, attn_sum.sent)
    grad_b_up = paired(core, *[item.reshape(chips, hidden_part) for item in grad_b_up], 1).reshape(count, hidden_part)
    grad_b_up = jnp.pad(grad_b_up[:, None], ((0, 0), (0, part - 1), (LANES - hidden_part, 0)))
    seqs = count * seq_count
    grad_tokens, *blocks = start_back(
        place, grad_qkv, attn_w, start, grad_middle, absorbed, rows, middle_sums, sums,
        grad_b_up.reshape(width, LANES), seqs, seq_length, fast,
    )
    if fast:
        attn_sum.two(grad_tokens)
        extra_sum = reduction(2 * part)
        extra_sum.add(*blocks)
        extra_sum.one()
        extra_sum.two(attn_sum.sent)
        attn_sum.along_z(extra_sum)
        hidden = after(hidden, attn_sum.sent)
    output = middle + (product(hidden[0], down_w[0]) + product(hidden[1], down_w[1]) + rows[seq_count + 3])
    if fast:
        attn_grad = attn_sum.columns(output)
        small, seq_sums = attn_grad[:, 0, 3 * half :], attn_grad[:, 1, 3 * half :]
    else:
        attn_grad = attn_sum.columns()
        small, seq_sums = [
            lax.psum_scatter(item.astype(BF), AXES, scatter_dimension=0, tiled=True).astype(F32) for item in blocks
        ]
    grad_b_up = small[0, LANES - hidden_part :]
    small = small[:, :fixed].T
    onehot = (steps[:, None] == lax.broadcasted_iota(jnp.int32, (seqs, table_cols), 1)).astype(F32)
    grad_time_table = jnp.dot(seq_sums, onehot, precision=lax.Precision.HIGHEST)
    grad_w_qkv = attn_grad[:, :, : 3 * half].reshape(part, 2, 3, half).transpose(0, 2, 1, 3).reshape(part, 3 * width)
    up_grad = up_sum.columns()
    grad_w_out = up_grad[:, :, hidden_width // 2 :].reshape(part, width)
    grad_w_up = up_grad[:, :, : hidden_width // 2].reshape(part, 2, chips, hidden_part).transpose(0, 2, 1, 3)
    grad_w_up = grad_w_up.reshape(part, hidden_width)
    return (
        output,
        grad_tokens,
        grad_w_qkv,
        grad_w_out,
        grad_w_up,
        down_sum.sums(),
        grad_time_table,
        small[0],
        small[1],
        small[2],
        grad_b_up,
        small[3],
        small[4],
        small[5],
        small[6],
        small[7],
        small[8],
    )


def solution(mesh):
    matrix, vector = P(AXES, None), P(AXES)
    fast = dict(mesh.shape) == {"fsdp": 8, "rep": 4}
    return jax.shard_map(
        functools.partial(body, fast),
        mesh=mesh,
        in_specs=(matrix, vector, vector) + (matrix,) * 6 + (vector,) * 10,
        out_specs=(matrix,) * 7 + (vector,) * 10,
        check_vma=False,
    )
```

```python
import functools
import math

import jax
import jax.numpy as jnp
from jax import lax
from jax.experimental import pallas as pl
from jax.experimental.pallas import tpu as pltpu
from jax.sharding import PartitionSpec as P

HDIM = 64
EPSILON = 1e-05
AXES = ("fsdp", "rep")
BF = jnp.bfloat16
F32 = jnp.float32
LANES = 128
VMEM_BYTES = 16 << 20
GELU_OUTER = math.sqrt(2.0 / math.pi)
GELU_INNER = 0.044715


def contract(left, right, left_dim, right_dim):
    dims = (((left_dim,), (right_dim,)), ((), ()))
    return lax.dot_general(left, right, dims, preferred_element_type=F32)


def product(left, right):
    return contract(left, right, 1, 0)


def left_product(left, right):
    return contract(left, right, 0, 0)


def right_product(left, right):
    return contract(left, right, 1, 1)


def pick(array, index, axis):
    return lax.dynamic_index_in_dim(array, index, axis, keepdims=False)


def paired(bit, mine, other, axis):
    return jnp.stack([jnp.where(bit == 0, mine, other), jnp.where(bit == 0, other, mine)], axis)


def in_hbm(value):
    return pltpu.with_memory_space_constraint(value, pltpu.HBM)


def after(value, *others):
    return lax.optimization_barrier((value, others))[0]


def lane_masks(factor):
    lane = lax.broadcasted_iota(jnp.int32, (1, LANES), 1)
    return [jnp.where((lane < HDIM) == (head == 0), factor, 0.0).astype(BF) for head in (0, 1)]


def softmax(scores):
    powers = jnp.exp(scores - jnp.max(scores, -1, keepdims=True))
    return powers * (1.0 / jnp.sum(powers, -1, keepdims=True))


def attention_kernel(length, scale, rows_ref, query_ref, key_ref, value_ref, bias_ref, qkv_ref, context_ref):
    rows = rows_ref[...]
    for index, weight in enumerate((query_ref, key_ref, value_ref)):
        qkv_ref[index] = (product(rows, weight[...]) + bias_ref[index : index + 1, :]).astype(BF)
    ones, scaled = lane_masks(1.0), lane_masks(scale)

    for sequence in range(rows.shape[0] // length):
        span = slice(sequence * length, (sequence + 1) * length)
        queries, key_rows, value_rows = [qkv_ref[index, span, :] for index in range(3)]
        total = 0.0
        for head in (0, 1):
            probs = softmax(right_product(queries * scaled[head], key_rows)).astype(BF)
            total = total + product(probs, value_rows * ones[head])
        context_ref[span, :] = total.astype(BF)


def attention(rows, weight, bias, length):
    tokens, width = rows.shape
    half = bias.shape[1]
    pairs = half // LANES

    def weight_spec(index):
        return pl.BlockSpec((width, LANES), lambda pair: (0, index * pairs + pair))

    return pl.pallas_call(
        functools.partial(attention_kernel, length, 1.0 / math.sqrt(HDIM)),
        grid=(pairs,),
        in_specs=[
            pl.BlockSpec((tokens, width), lambda pair: (0, 0)),
            weight_spec(0),
            weight_spec(1),
            weight_spec(2),
            pl.BlockSpec((8, LANES), lambda pair: (0, pair)),
        ],
        out_specs=[
            pl.BlockSpec((3, tokens, LANES), lambda pair: (0, 0, pair)),
            pl.BlockSpec((tokens, LANES), lambda pair: (0, pair)),
        ],
        out_shape=[
            pltpu.HBM((3, tokens, half), BF),
            jax.ShapeDtypeStruct((tokens, half), BF),
        ],
        compiler_params=pltpu.CompilerParams(vmem_limit_bytes=VMEM_BYTES),
        cost_estimate=pl.CostEstimate(
            flops=6 * tokens * width * half,
            bytes_accessed=2 * tokens * width + 6 * width * half + 8 * tokens * half,
            transcendentals=2 * tokens * length * pairs,
        ),
        name="attention",
    )(rows, weight, weight, weight, bias)


def attention_back_kernel(length, scale, qkv_ref, grad_ref, rows_ref, grads_ref, weight_ref, sums_ref):
    ones, scaled = lane_masks(1.0), lane_masks(scale)

    for sequence in range(grad_ref.shape[0] // length):
        span = slice(sequence * length, (sequence + 1) * length)
        queries, key_rows, value_rows = [qkv_ref[index, span, :] for index in range(3)]
        grad = grad_ref[span, :]
        grad_queries, grad_keys, grad_values = 0.0, 0.0, 0.0
        for head in (0, 1):
            probs = softmax(right_product(queries * scaled[head], key_rows))
            grad_head = grad * ones[head]
            grad_probs = right_product(grad_head, value_rows)
            grad_scores = probs * (grad_probs - jnp.sum(grad_probs * probs, -1, keepdims=True))
            grad_scores = grad_scores.astype(BF)
            grad_values = grad_values + left_product(probs.astype(BF), grad_head)
            grad_queries = grad_queries + product(grad_scores, key_rows * ones[head])
            grad_keys = grad_keys + left_product(grad_scores, queries * ones[head])
        grads_ref[0, span, :] = (grad_queries * scale).astype(BF)
        grads_ref[1, span, :] = (grad_keys * scale).astype(BF)
        grads_ref[2, span, :] = grad_values.astype(BF)

    rows = rows_ref[...]
    for index in range(3):
        grads = grads_ref[index]
        weight_ref[index] = product(rows, grads).astype(weight_ref.dtype)
        sums_ref[index : index + 1, :] = jnp.sum(grads.astype(F32), 0, keepdims=True)


def attention_back(qkv, grad, rows_across, length, dtype):
    _, tokens, half = qkv.shape
    width = rows_across.shape[0]
    pairs = half // LANES
    return pl.pallas_call(
        functools.partial(attention_back_kernel, length, 1.0 / math.sqrt(HDIM)),
        grid=(pairs,),
        in_specs=[
            pl.BlockSpec((3, tokens, LANES), lambda pair: (0, 0, pair)),
            pl.BlockSpec((tokens, LANES), lambda pair: (0, pair)),
            pl.BlockSpec((width, tokens), lambda pair: (0, 0)),
        ],
        out_specs=[
            pl.BlockSpec((3, tokens, LANES), lambda pair: (0, 0, pair)),
            pl.BlockSpec((3, width, LANES), lambda pair: (0, 0, pair)),
            pl.BlockSpec((3, LANES), lambda pair: (0, pair)),
        ],
        out_shape=[
            pltpu.HBM((3, tokens, half), BF),
            jax.ShapeDtypeStruct((3, width, half), dtype),
            jax.ShapeDtypeStruct((3, half), F32),
        ],
        compiler_params=pltpu.CompilerParams(vmem_limit_bytes=VMEM_BYTES),
        cost_estimate=pl.CostEstimate(
            flops=6 * tokens * width * half,
            bytes_accessed=2 * tokens * width + 12 * width * half + 14 * tokens * half,
            transcendentals=2 * tokens * length * pairs,
        ),
        name="attention_back",
    )(in_hbm(qkv), in_hbm(grad), in_hbm(rows_across))


def feed_kernel(side, rows_ref, weight_ref, bias_ref, hidden_ref, slope_ref, pre_ref):
    pre_ref[...] = product(rows_ref[...], weight_ref[...])
    step = 32

    def chunk(index, carry):
        span = pl.ds(pl.multiple_of(index * step, step), step)
        pre = pre_ref[span, :] + bias_ref[side : side + 1, :]
        square = pre * pre
        bend = jnp.tanh(GELU_OUTER * (pre + GELU_INNER * (square * pre)))
        share = 0.5 * (1.0 + bend)
        hidden_ref[span, :] = (pre * share).astype(BF)
        inner = (0.5 * GELU_OUTER) * pre * (1.0 + (3.0 * GELU_INNER) * square)
        slope_ref[span, :] = share + inner * (1.0 - bend * bend)
        return carry

    lax.fori_loop(0, rows_ref.shape[0] // step, chunk, 0, unroll=2)


def feed(rows, weight, bias, side, block=512):
    tokens, width = rows.shape
    columns = weight.shape[1]
    block = math.gcd(block, columns)
    out = pl.BlockSpec((tokens, block), lambda step: (0, step))
    return pl.pallas_call(
        functools.partial(feed_kernel, side),
        grid=(columns // block,),
        in_specs=[
            pl.BlockSpec((tokens, width), lambda step: (0, 0)),
            pl.BlockSpec((width, block), lambda step: (0, step)),
            pl.BlockSpec((8, block), lambda step: (0, step)),
        ],
        out_specs=[out, out],
        out_shape=[
            pltpu.HBM((tokens, columns), BF),
            pltpu.HBM((tokens, columns), F32),
        ],
        scratch_shapes=[pltpu.VMEM((tokens, block), F32)],
        compiler_params=pltpu.CompilerParams(vmem_limit_bytes=VMEM_BYTES),
        cost_estimate=pl.CostEstimate(
            flops=2 * tokens * width * columns,
            bytes_accessed=2 * tokens * width + 2 * width * columns + 6 * tokens * columns,
            transcendentals=tokens * columns,
        ),
        name="feed",
    )(rows, weight, bias)


def feed_back_kernel(grad_ref, weight_ref, slope_ref, rows_ref, pre_ref, sum_ref, up_ref):
    grad = (right_product(grad_ref[...], weight_ref[...]) * slope_ref[...]).astype(BF)
    pre_ref[...] = grad
    sum_ref[...] = jnp.sum(grad.astype(F32), 0, keepdims=True)
    up_ref[...] = product(rows_ref[...], grad).astype(up_ref.dtype)


def feed_back(grad, weight, slope, rows_across, dtype, block=512):
    tokens, width = grad.shape
    columns = weight.shape[0]
    block = math.gcd(block, columns)
    out = pl.BlockSpec((tokens, block), lambda step: (0, step))
    return pl.pallas_call(
        feed_back_kernel,
        grid=(columns // block,),
        in_specs=[
            pl.BlockSpec((tokens, width), lambda step: (0, 0)),
            pl.BlockSpec((block, width), lambda step: (step, 0)),
            out,
            pl.BlockSpec((width, tokens), lambda step: (0, 0)),
        ],
        out_specs=[
            out,
            pl.BlockSpec((1, block), lambda step: (0, step)),
            pl.BlockSpec((width, block), lambda step: (0, step)),
        ],
        out_shape=[
            pltpu.HBM((tokens, columns), BF),
            jax.ShapeDtypeStruct((1, columns), F32),
            jax.ShapeDtypeStruct((width, columns), dtype),
        ],
        compiler_params=pltpu.CompilerParams(vmem_limit_bytes=VMEM_BYTES),
        cost_estimate=pl.CostEstimate(
            flops=4 * tokens * width * columns,
            bytes_accessed=4 * tokens * width + 6 * width * columns + 6 * tokens * columns,
            transcendentals=0,
        ),
        name="feed_back",
    )(in_hbm(grad), in_hbm(weight), in_hbm(slope), in_hbm(rows_across))


def chosen_side(core, mine, other):
    return jnp.where(core == 0, mine, other), jnp.where(core == 0, other, mine)


def normalized(values):
    center = values - jnp.mean(values, -1, keepdims=True)
    rate = lax.rsqrt(jnp.mean(center * center, -1, keepdims=True) + EPSILON)
    return center * rate, rate


def start_kernel(
    fixed, up_cols, table_cols, seq_count, parts,
    place_ref, tokens_ref, mask_ref, table_mine_ref, table_other_ref,
    rows_ref, start_ref, normed_ref, across_ref, bias_mine_ref, bias_other_ref, bias_up_ref,
):
    core = place_ref[0]
    step = pl.program_id(0)
    width = tokens_ref.shape[1]
    half = width // 2
    chips, part, hidden_part = parts

    @pl.when(step == 0)
    def _():
        count, columns = rows_ref.shape[0], table_mine_ref.shape[1]
        row = lax.broadcasted_iota(jnp.int32, (count, columns), 0)
        wanted = table_cols + row - seq_count
        for index in range(seq_count):
            wanted = jnp.where(row == index, place_ref[2 + index], wanted)
        column = lax.broadcasted_iota(jnp.int32, (count, columns), 1)
        rows = 0.0
        for side, table in ((core, table_mine_ref), (1 - core, table_other_ref)):
            hit = jnp.where(wanted == column + side * columns, 1.0, 0.0).astype(BF)
            rows = rows + right_product(hit, table[...])
        rows_ref[...] = rows
        for ref, side in ((bias_mine_ref, core), (bias_other_ref, 1 - core)):
            ref[...] = jnp.zeros_like(ref)
            for index in (0, 1):
                line = rows_ref[seq_count + index : seq_count + index + 1, :]
                ref[2 * index : 2 * index + 1, :] = jnp.where(side == 0, line[:, :half], line[:, half:])
        for chip in range(chips):
            for index in range(up_cols):
                line = rows_ref[seq_count + fixed + index : seq_count + fixed + index + 1, :]
                pair = [line[:, (2 * chip + i) * part : (2 * chip + i + 1) * part] for i in range(2)]
                where = slice(chip * hidden_part + index * part, chip * hidden_part + (index + 1) * part)
                bias_up_ref[0:1, where], bias_up_ref[1:2, where] = chosen_side(core, *pair)

    small = seq_count
    mask = mask_ref[...]
    start = jnp.where(mask > 0.0, rows_ref[small + 8 : small + 9, :], tokens_ref[...])
    start = start + rows_ref[pl.ds(step, 1), :]
    start_ref[...] = start
    normed, _ = normalized(start)
    normed = normed * rows_ref[small + 4 : small + 5, :] + rows_ref[small + 5 : small + 6, :]
    normed_ref[...] = normed.astype(BF)
    across_ref[...] = normed.T.astype(BF)


def start_rows(place, tokens, mask, weights, fixed, up_cols, table_cols, small_cols, chips, hidden_part):
    count, width = tokens.shape
    seq_count = place.shape[0] - 2
    length = count // seq_count
    half = width // 2
    row_count = -(-(seq_count + small_cols) // 8) * 8
    table_half = weights[0].shape[1] - 4 * half
    tables = 4 * half // table_half
    table_spec = pl.BlockSpec((width, table_half), lambda step: (0, tables))
    rows_spec = pl.BlockSpec((length, width), lambda step: (step, 0))

    def fixed_spec(*shape):
        return pl.BlockSpec(shape, lambda step: (0,) * len(shape))

    return pl.pallas_call(
        functools.partial(
            start_kernel, fixed, up_cols, table_cols, seq_count, (chips, width // (2 * chips), hidden_part)
        ),
        grid=(seq_count,),
        in_specs=[
            pl.BlockSpec(memory_space=pltpu.SMEM),
            rows_spec,
            pl.BlockSpec((length, 1), lambda step: (step, 0)),
            table_spec,
            table_spec,
        ],
        out_specs=[
            fixed_spec(row_count, width),
            rows_spec,
            rows_spec,
            pl.BlockSpec((width, length), lambda step: (0, step)),
            fixed_spec(8, half),
            fixed_spec(8, half),
            fixed_spec(8, chips * hidden_part),
        ],
        out_shape=[
            jax.ShapeDtypeStruct((row_count, width), F32),
            pltpu.HBM((count, width), F32),
            jax.ShapeDtypeStruct((count, width), BF),
            pltpu.HBM((width, count), BF),
            jax.ShapeDtypeStruct((8, half), F32),
            jax.ShapeDtypeStruct((8, half), F32),
            jax.ShapeDtypeStruct((8, chips * hidden_part), F32),
        ],
        compiler_params=pltpu.CompilerParams(vmem_limit_bytes=VMEM_BYTES),
        cost_estimate=pl.CostEstimate(
            flops=4 * row_count * width * table_half, bytes_accessed=14 * count * width, transcendentals=0
        ),
        name="start_rows",
    )(place, in_hbm(tokens), mask, *weights)


def middle_kernel(
    small, place_ref, context_mine_ref, context_other_ref, out_mine_ref, out_other_ref, start_ref, rows_ref,
    middle_ref, normed_ref, across_ref,
):
    core = place_ref[0]
    half = context_mine_ref.shape[1]
    contexts = chosen_side(core, context_mine_ref[...], context_other_ref[...])
    outs = chosen_side(core, out_mine_ref[...], out_other_ref[...])
    for index, out in enumerate(outs):
        span = slice(index * half, (index + 1) * half)
        total = product(contexts[0], out[:half]) + product(contexts[1], out[half:])
        middle_ref[:, span] = start_ref[:, span] + (total + rows_ref[small + 2 : small + 3, span])
    normed, _ = normalized(middle_ref[...])
    normed = normed * rows_ref[small + 6 : small + 7, :] + rows_ref[small + 7 : small + 8, :]
    normed_ref[...] = normed.astype(BF)
    across_ref[...] = normed.T.astype(BF)


def middle_rows(place, contexts, weights, start, rows, block=256):
    count, width = start.shape
    half = width // 2
    small = place.shape[0] - 2
    block = math.gcd(block, count)
    out_spec = pl.BlockSpec((width, half), lambda step: (0, 3))
    rows_spec = pl.BlockSpec((block, width), lambda step: (step, 0))
    half_spec = pl.BlockSpec((block, half), lambda step: (step, 0))
    return pl.pallas_call(
        functools.partial(middle_kernel, small),
        grid=(count // block,),
        in_specs=[
            pl.BlockSpec(memory_space=pltpu.SMEM),
            half_spec,
            half_spec,
            out_spec,
            out_spec,
            rows_spec,
            pl.BlockSpec(rows.shape, lambda step: (0, 0)),
        ],
        out_specs=[rows_spec, rows_spec, pl.BlockSpec((width, block), lambda step: (0, step))],
        out_shape=[
            pltpu.HBM((count, width), F32),
            jax.ShapeDtypeStruct((count, width), BF),
            pltpu.HBM((width, count), BF),
        ],
        compiler_params=pltpu.CompilerParams(vmem_limit_bytes=VMEM_BYTES),
        cost_estimate=pl.CostEstimate(
            flops=2 * count * width * width, bytes_accessed=14 * count * width + 2 * width * width, transcendentals=0
        ),
        name="middle_rows",
    )(place, *contexts, *weights, start, rows)


def norm_back(values, gain, grad):
    unit, rate = normalized(values)
    scaled = grad * gain
    back = scaled - jnp.mean(scaled, -1, keepdims=True) - unit * jnp.mean(scaled * unit, -1, keepdims=True)
    return rate * back, grad * unit


def middle_back_kernel(
    small, place_ref, pre_mine_ref, pre_other_ref, up_mine_ref, up_other_ref, middle_ref, cotangent_ref, mask_ref,
    rows_ref, context_mine_ref, context_other_ref, out_mine_ref, out_other_ref,
    grad_ref, context_grad_mine_ref, context_grad_other_ref, out_grad_mine_ref, out_grad_other_ref, sums_ref,
    normed_ref, total_ref,
):
    core = place_ref[0]
    step = pl.program_id(0)
    half = context_mine_ref.shape[1]

    @pl.when(step == 0)
    def _():
        sums_ref[...] = jnp.zeros_like(sums_ref)
        total_ref[...] = jnp.zeros_like(total_ref)

    normed_ref[...] = right_product(pre_mine_ref[...], up_mine_ref[...]) + right_product(
        pre_other_ref[...], up_other_ref[...]
    )
    grad = normed_ref[...]
    direct = cotangent_ref[...] * mask_ref[...]
    back, shares = norm_back(middle_ref[...], rows_ref[small + 6 : small + 7, :], grad)
    back = direct + back
    grad_ref[...] = back
    low = back.astype(BF)
    for index, item in enumerate((low.astype(F32), direct.astype(BF).astype(F32), shares, grad)):
        sums_ref[index : index + 1, :] += jnp.sum(item, 0, keepdims=True)
    lows = (low[:, :half], low[:, half:])
    contexts = chosen_side(core, context_mine_ref[...], context_other_ref[...])
    outs = chosen_side(core, out_mine_ref[...], out_other_ref[...])
    context_grads = [
        (right_product(lows[0], outs[0][span]) + right_product(lows[1], outs[1][span])).astype(BF)
        for span in (slice(0, half), slice(half, None))
    ]
    context_grad_mine_ref[...], context_grad_other_ref[...] = chosen_side(core, *context_grads)
    for index, item in enumerate(chosen_side(core, *lows)):
        for side, context in enumerate(contexts):
            total_ref[index, side * half : (side + 1) * half, :] += left_product(context, item)

    @pl.when(step == pl.num_programs(0) - 1)
    def _():
        out_grad_mine_ref[...] = total_ref[0]
        out_grad_other_ref[...] = total_ref[1].astype(BF)


def middle_back(place, grads, ups, middle, cotangent, mask, rows, contexts, weights, block=256):
    count, width = middle.shape
    half = width // 2
    hidden_half = ups[0].shape[1]
    small = place.shape[0] - 2
    block = math.gcd(block, count)

    def over_rows(columns):
        return pl.BlockSpec((block, columns), lambda step: (step, 0))

    def whole(*shape):
        return pl.BlockSpec(shape, lambda step: (0,) * len(shape))

    out_spec = pl.BlockSpec((width, half), lambda step: (0, 3))
    return pl.pallas_call(
        functools.partial(middle_back_kernel, small),
        grid=(count // block,),
        in_specs=[
            pl.BlockSpec(memory_space=pltpu.SMEM),
            over_rows(hidden_half),
            over_rows(hidden_half),
            whole(width, hidden_half),
            whole(width, hidden_half),
            over_rows(width),
            over_rows(width),
            over_rows(1),
            whole(*rows.shape),
            over_rows(half),
            over_rows(half),
            out_spec,
            out_spec,
        ],
        out_specs=[
            over_rows(width),
            over_rows(half),
            over_rows(half),
            whole(width, half),
            whole(width, half),
            whole(8, width),
        ],
        out_shape=[
            jax.ShapeDtypeStruct((count, width), F32),
            jax.ShapeDtypeStruct((count, half), BF),
            jax.ShapeDtypeStruct((count, half), BF),
            jax.ShapeDtypeStruct((width, half), F32),
            jax.ShapeDtypeStruct((width, half), BF),
            jax.ShapeDtypeStruct((8, width), F32),
        ],
        scratch_shapes=[pltpu.VMEM((block, width), F32), pltpu.VMEM((2, width, half), F32)],
        compiler_params=pltpu.CompilerParams(vmem_limit_bytes=2 * VMEM_BYTES),
        cost_estimate=pl.CostEstimate(
            flops=4 * count * width * (hidden_half + width),
            bytes_accessed=4 * count * hidden_half + 4 * width * hidden_half + 16 * count * width,
            transcendentals=0,
        ),
        name="middle_back",
    )(place, *grads, *ups, middle, cotangent, mask, rows, *contexts, *weights)


def start_back_kernel(
    small, length, swap, place_ref, grads_mine_ref, grads_other_ref, weight_mine_ref, weight_other_ref, start_ref, middle_ref,
    mask_ref, rows_ref, sums_ref, sums_mine_ref, sums_other_ref, bias_ref,
    tokens_ref, mine_ref, other_ref, lines_ref,
):
    core, place = place_ref[0], place_ref[1]
    step = pl.program_id(0)
    width = start_ref.shape[1]
    half = width // 2
    seqs = start_ref.shape[0] // length

    @pl.when(step == 0)
    def _():
        lines_ref[...] = jnp.zeros_like(lines_ref)
        for index, row in ((0, 0), (1, 2)):
            pair = (sums_mine_ref[row : row + 1, :], sums_other_ref[row : row + 1, :])
            lines_ref[index : index + 1, :half], lines_ref[index : index + 1, half:] = chosen_side(core, *pair)
        lines_ref[2:4, :] = sums_ref[0:2, :]
        lines_ref[6:8, :] = sums_ref[2:4, :]

    grad = 0.0
    for grads, weight in ((grads_mine_ref, weight_mine_ref), (grads_other_ref, weight_other_ref)):
        for index in range(3):
            grad = grad + right_product(grads[index], weight[:, index * half : (index + 1) * half])
    back, shares = norm_back(start_ref[...], rows_ref[small + 4 : small + 5, :], grad)
    back = middle_ref[...] + back
    mask = mask_ref[...]
    tokens_ref[...] = jnp.where(mask > 0.0, 0.0, back)
    for index, item in ((4, shares), (5, grad), (8, back * mask)):
        lines_ref[index : index + 1, :] += jnp.sum(item, 0, keepdims=True)
    for index in range(seqs):
        line = LANES + place * small + step * seqs + index
        lines_ref[pl.ds(line, 1), :] = jnp.sum(back[index * length : (index + 1) * length], 0, keepdims=True)

    @pl.when(step == pl.num_programs(0) - 1)
    def _():
        blocks = (lines_ref[:LANES, :].T + bias_ref[...], lines_ref[LANES:, :].T)
        if swap:
            blocks = chosen_side(core, *blocks)
        mine_ref[...] = blocks[0]
        other_ref[...] = blocks[1].astype(other_ref.dtype)


def start_back(
    place, grads, weights, start, middle, mask, rows, sums, side_sums, bias, seqs, length, swap, block=256
):
    count, width = start.shape
    half = width // 2
    small = place.shape[0] - 2
    block = math.gcd(block, count)
    lines = LANES + -(-seqs // LANES) * LANES

    def over_rows(columns):
        return pl.BlockSpec((block, columns), lambda step: (step, 0))

    def whole(*shape):
        return pl.BlockSpec(shape, lambda step: (0,) * len(shape))

    grads_spec = pl.BlockSpec((3, block, half), lambda step: (0, step, 0))
    return pl.pallas_call(
        functools.partial(start_back_kernel, small, length, swap),
        grid=(count // block,),
        in_specs=[
            pl.BlockSpec(memory_space=pltpu.SMEM),
            grads_spec,
            grads_spec,
            whole(width, 3 * half),
            whole(width, 3 * half),
            over_rows(width),
            over_rows(width),
            over_rows(1),
            whole(*rows.shape),
            whole(*sums.shape),
            whole(*side_sums[0].shape),
            whole(*side_sums[1].shape),
            whole(width, LANES),
        ],
        out_specs=[over_rows(width), whole(width, LANES), whole(width, lines - LANES)],
        out_shape=[
            jax.ShapeDtypeStruct((count, width), F32),
            jax.ShapeDtypeStruct((width, LANES), F32),
            jax.ShapeDtypeStruct((width, lines - LANES), BF if swap else F32),
        ],
        scratch_shapes=[pltpu.VMEM((lines, width), F32)],
        compiler_params=pltpu.CompilerParams(vmem_limit_bytes=VMEM_BYTES),
        cost_estimate=pl.CostEstimate(
            flops=0, bytes_accessed=1024, transcendentals=0
        ),
        name="start_back",
    )(place, *grads, *weights, start, middle, mask, rows, sums, *side_sums, bias)


def shards_kernel(fixed, seq_cols, place_ref, qkv_ref, out_ref, table_ref, *refs):
    small_refs, (mine_ref, other_ref, full_ref) = refs[: fixed + 1], refs[fixed + 1 :]
    core = place_ref[0]
    part, table_cols = table_ref.shape
    half = out_ref.shape[1] // 2
    seq_count = place_ref.shape[0] - 2
    lines = [ref[...] for ref in small_refs[:fixed]]
    up = small_refs[fixed][...]
    lines += [up[:, i : i + part] for i in range(0, up.shape[1], part)]
    lane = lax.broadcasted_iota(jnp.int32, (1, part), 1)
    for row in range(seq_cols):
        line = jnp.zeros((1, part), jnp.int32)
        for index in range(seq_count):
            step = place_ref[2 + index]
            line = jnp.where(lane + row * part == index, step // 256, line)
            line = jnp.where(lane + row * part == seq_count + index, step % 256, line)
        lines.append(line.astype(F32))
    lines = jnp.concatenate(lines, 0).astype(BF)
    square = (part, part)
    unit = lax.broadcasted_iota(jnp.int32, square, 0) == lax.broadcasted_iota(jnp.int32, square, 1)
    full_ref[...] = jnp.zeros_like(full_ref)
    full_ref[:, :table_cols] = table_ref[...]
    full_ref[:, table_cols : table_cols + lines.shape[0]] = right_product(jnp.where(unit, 1.0, 0.0).astype(BF), lines)
    table_half = full_ref.shape[1] // 2

    def halves(ref, top, wide):
        return chosen_side(core, ref[:, top : top + wide], ref[:, top + wide : top + 2 * wide])

    sources = [(qkv_ref, 2 * half * i, half) for i in range(3)] + [(out_ref, 0, half), (full_ref, 0, table_half)]
    left = 0
    for ref, top, wide in sources:
        mine, other = halves(ref, top, wide)
        mine_ref[:, left : left + wide] = mine.astype(BF)
        other_ref[:, left : left + wide] = other.astype(BF)
        left += wide


def attention_shards(place, w_qkv, w_out, table, small, b_up, seq_cols, all_cols):
    part = table.shape[0]
    shape = jax.ShapeDtypeStruct((part, 2 * w_out.shape[1] + all_cols // 2), BF)
    vmem = pl.BlockSpec(memory_space=pltpu.VMEM)
    return pl.pallas_call(
        functools.partial(shards_kernel, len(small), seq_cols),
        in_specs=[pl.BlockSpec(memory_space=pltpu.SMEM)] + [vmem] * (4 + len(small)),
        out_specs=[vmem, vmem],
        out_shape=[shape, shape],
        scratch_shapes=[pltpu.VMEM((part, all_cols), F32)],
        compiler_params=pltpu.CompilerParams(vmem_limit_bytes=60 << 20),
        cost_estimate=pl.CostEstimate(flops=0, bytes_accessed=24 * part * w_out.shape[1], transcendentals=0),
        name="attention_shards",
    )(place, w_qkv, w_out, table, *[item.reshape(1, -1) for item in small], b_up.reshape(1, -1))


def route_kernel(rows, route_ref, *refs):
    terms, (sent_ref, kept_ref) = refs[:-2], refs[-2:]
    for index in range(2):
        for out, place in ((sent_ref, route_ref[index]), (kept_ref, route_ref[2 + index])):
            span = pl.ds(pl.multiple_of(place * rows, 8), rows)
            left = 0
            for mine, got in zip(terms[::2], terms[1::2]):
                many = [(slice(None),)] if len(mine.shape) == 2 else [(i, slice(None)) for i in range(mine.shape[0])]
                for at in many:
                    where = (*at[:-1], span)
                    total = mine[where].astype(F32) + got[where].astype(F32)
                    out[0, index, :, left : left + total.shape[1]] = total.astype(out.dtype)
                    left += total.shape[1]


def routed(terms, rows, route):
    specs, columns, bytes_read = [], 0, 0
    for array in [item for pair in terms for item in pair]:
        shape = (4 * rows, array.shape[-1])
        if array.ndim == 2:
            specs.append(pl.BlockSpec(shape, lambda z: (z, 0)))
        else:
            specs.append(pl.BlockSpec((array.shape[0], *shape), lambda z: (0, z, 0)))
        bytes_read += array.size * array.dtype.itemsize
        columns += array.size // (16 * rows)
    columns //= 2
    out = pl.BlockSpec((1, 2, rows, columns), lambda z: (z, 0, 0, 0))
    return pl.pallas_call(
        functools.partial(route_kernel, rows),
        grid=(4,),
        in_specs=[pl.BlockSpec(memory_space=pltpu.SMEM)] + specs,
        out_specs=[out, out],
        out_shape=[
            jax.ShapeDtypeStruct((4, 2, rows, columns), BF),
            pltpu.HBM((4, 2, rows, columns), F32),
        ],
        compiler_params=pltpu.CompilerParams(vmem_limit_bytes=VMEM_BYTES),
        cost_estimate=pl.CostEstimate(
            flops=0, bytes_accessed=bytes_read + 48 * rows * columns, transcendentals=0
        ),
        name="routed",
    )(route, *[item for pair in terms for item in pair])


class Tree:
    def __init__(self):
        fsdp, rep = lax.axis_index("fsdp"), lax.axis_index("rep")
        self.z, self.core = fsdp // 2, rep % 2
        x, y = rep // 2, fsdp % 2
        self.near = jnp.where(self.core == 0, x, y)
        self.far = jnp.where(self.core == 0, y, x)
        places = [jnp.where(self.core == 0, 2 * i + near, 2 * near + i) for near in (1 - self.near, self.near) for i in (0, 1)]
        self.route = jnp.stack(places)

    def to_core(self, value):
        return lax.ppermute(value, "rep", [(i, i ^ 1) for i in range(4)])

    def to_near(self, value):
        return lax.ppermute(value, AXES, [(i, i ^ (4 if i % 2 else 2)) for i in range(32)])

    def to_far(self, value):
        return lax.ppermute(value, AXES, [(i, i ^ (2 if i % 2 else 4)) for i in range(32)])

    def to_z(self, value, step):
        return lax.ppermute(value, "fsdp", [(i, i ^ (2 * step)) for i in range(8)])


class Gather:
    def __init__(self, tree, own):
        self.tree, self.own = tree, own

    @staticmethod
    def columns(tree, mine, other):
        got = tree.to_core(other)
        return Gather(tree, paired(tree.core, mine, got, 0).reshape(-1, mine.shape[1]))

    @staticmethod
    def rows(tree, shard):
        return Gather(tree, shard)

    def along_z(self, *wait):
        own = after(self.own, *wait)
        one, three, two = [self.tree.to_z(own, step) for step in (1, 3, 2)]
        self.held, self.got = own, [one, two, three]
        return self.got

    def one(self, *wait):
        tree = self.tree
        held = after([self.held, *self.got], *wait)
        low, high = tree.z % 2 == 1, tree.z // 2 == 1
        out = []
        for place in range(4):
            near = [jnp.where(low, held[(place ^ 1) ^ h], held[place ^ h]) for h in (0, 2)]
            out.append(jnp.where(high, near[1], near[0]))
        self.held = jnp.stack(out)
        self.got = tree.to_near(self.held)
        return self.got

    def two(self, *wait):
        tree = self.tree
        held, got = after((self.held, self.got), *wait)
        self.held = paired(tree.near, held, got, 1)
        self.got = tree.to_far(self.held)
        return self.got

    def halves(self, *wait):
        tree = self.tree
        held, got = after((self.held, self.got), *wait)
        same, first = tree.far == 0, tree.core == 0
        lower, upper = jnp.where(same, held, got), jnp.where(same, got, held)
        blocks = [
            lower[:, 0],
            jnp.where(first, lower[:, 1], upper[:, 0]),
            jnp.where(first, upper[:, 0], lower[:, 1]),
            upper[:, 1],
        ]
        half = jnp.stack(blocks, 1).reshape(-1, held.shape[-1])
        return half, tree.to_core(half)


class Reduce:
    def __init__(self, tree, rows):
        self.tree, self.rows = tree, rows
        self.terms = []

    def add(self, mine, other):
        got = self.tree.to_core(other.astype(BF))
        self.terms.append((mine, got))
        return got

    def one(self, *wait):
        self.sent, self.kept = routed(after(self.terms, *wait), self.rows, self.tree.route)
        self.got = self.tree.to_near(self.sent)

    def two(self, *wait):
        tree = self.tree
        kept, got = after((self.kept, self.got), *wait)
        total = kept + got
        self.kept, self.sent = pick(total, tree.far, 1), pick(total, 1 - tree.far, 1).astype(BF)
        self.got = tree.to_far(self.sent)

    def along_z(self, *others):
        tree = self.tree
        total = jnp.concatenate([item.kept + item.got for item in (self, *others)], -1)
        self.kept = pick(total, tree.z, 0)
        self.sent = tuple(pick(total, tree.z ^ step, 0).astype(BF) for step in (1, 2, 3))
        self.got = tuple(tree.to_z(sent, step) for sent, step in zip(self.sent, (1, 2, 3)))

    def sums(self, *wait):
        kept, got = after((self.kept, self.got), *wait)
        return kept + got[0] + got[1] + got[2]

    def columns(self, *wait):
        tree, total = self.tree, self.sums(*wait)
        rows = total.reshape(2, self.rows // 2, -1)
        keep = pick(rows, tree.core, 0)
        return paired(tree.core, keep, tree.to_core(pick(rows, 1 - tree.core, 0)), 1)


class Whole:
    core = 0

    def __init__(self, rows=None):
        self.mine, self.other = [], []
        self.got, self.sent = (), ()

    @staticmethod
    def columns_of(mine, other):
        out = Whole()
        whole = lax.all_gather(jnp.stack([mine, other], 1), AXES, axis=0, tiled=True)
        out.half, out.rest = whole[:, 0], whole[:, 1]
        return out

    @staticmethod
    def rows_of(shard):
        out = Whole()
        whole = lax.all_gather(shard, AXES, axis=0)
        whole = whole.reshape(-1, 2, *shard.shape)
        out.half, out.rest = [whole[:, i].reshape(-1, shard.shape[1]) for i in range(2)]
        return out

    def along_z(self, *wait):
        return []

    def one(self, *wait):
        return ()

    def two(self, *wait):
        return ()

    def halves(self, *wait):
        return self.half, self.rest

    def add(self, mine, other):
        self.mine.append(mine.astype(BF))
        self.other.append(other.astype(BF))
        return mine

    def columns(self, *wait):
        def flat(items):
            return jnp.concatenate([part for item in items for part in (item if item.ndim == 3 else [item])], 1)

        parts = [flat(item) for item in (self.mine, self.other)]
        return lax.psum_scatter(jnp.stack(parts, 1), AXES, scatter_dimension=0, tiled=True).astype(F32)

    def sums(self, *wait):
        count = lax.axis_size(AXES)
        mine, other = [item[0].reshape(count // 2, -1, item[0].shape[1]) for item in (self.mine, self.other)]
        sums = jnp.stack([mine, other], 1).reshape(-1, mine.shape[-1])
        return lax.psum_scatter(sums, AXES, scatter_dimension=0, tiled=True).astype(F32)


def body(
    fast,
    tokens,
    mask_bits,
    timesteps,
    cotangent,
    w_qkv,
    w_out,
    w_up,
    w_down,
    time_table,
    b_query,
    b_value,
    b_out,
    b_up,
    b_down,
    gain_attn,
    shift_attn,
    gain_mlp,
    shift_mlp,
    mask_vector,
):
    tree = Tree() if fast else Whole()
    gather_columns = functools.partial(Gather.columns, tree) if fast else Whole.columns_of
    gather_rows = functools.partial(Gather.rows, tree) if fast else Whole.rows_of
    reduction = functools.partial(Reduce, tree) if fast else Whole
    core = tree.core
    count = lax.axis_size(AXES)
    chips = count // 2
    place = lax.axis_index(AXES)
    width = tokens.shape[1]
    part = width // count
    hidden_width = w_up.shape[1]
    hidden_part = hidden_width // count
    seq_count = timesteps.shape[0]
    seq_length = tokens.shape[0] // seq_count
    half = width // 2
    table_cols = time_table.shape[1]
    absorbed = mask_bits.astype(F32)[:, None]

    small = [b_query, b_value, b_out, b_down, gain_attn, shift_attn, gain_mlp, shift_mlp, mask_vector]
    fixed = len(small)
    up_cols = hidden_part // part
    seq_cols = -(-2 * seq_count // part)
    small_cols = fixed + up_cols + seq_cols
    all_cols = -(-(table_cols + small_cols) // (2 * LANES)) * (2 * LANES)
    place = jnp.concatenate([jnp.stack([jnp.int32(core), place]), timesteps])

    attn_w = gather_columns(*attention_shards(place, w_qkv, w_out, time_table, small, b_up, seq_cols, all_cols))
    up_shard = w_up.astype(BF).reshape(part, chips, 2, hidden_part).transpose(2, 0, 1, 3)
    up_shard = up_shard.reshape(2, part, hidden_width // 2)
    up_w = gather_columns(*[pick(up_shard, side, 0) for side in (core, 1 - core)])
    down_w = gather_rows(w_down.astype(BF))
    attn_w.along_z()
    up_z = up_w.along_z()
    attn_one = attn_w.one()
    attn_two = attn_w.two(up_z[::2])
    up_one = up_w.one(attn_two)
    attn_w = attn_w.halves(up_z)
    down_z = down_w.along_z(attn_two)

    rows, start, normed_one, across_one, bias_mine, bias_other, bias_up = start_rows(
        place, tokens, absorbed, attn_w, fixed, up_cols, table_cols, small_cols, chips, hidden_part
    )
    up_two = up_w.two(normed_one)
    qkv_mine, context_mine = attention(after(normed_one, up_one), attn_w[0], bias_mine, seq_length)
    down_one = down_w.one(up_two, context_mine)
    up_w = up_w.halves(context_mine)
    qkv_other, context_other = attention(after(normed_one, up_two), attn_w[1], bias_other, seq_length)
    down_two = down_w.two(context_other)
    contexts = (context_mine, context_other)
    middle, normed_two, across_two = middle_rows(place, contexts, attn_w, after(start, down_one), rows)
    hidden, slope = [None, None], [None, None]
    hidden[0], slope[0] = feed(normed_two, up_w[0], bias_up, 0)
    down_w = down_w.halves(hidden[0])
    hidden[1], slope[1] = feed(after(normed_two, down_two), up_w[1], bias_up, 1)

    grad_branch = (cotangent * absorbed).astype(BF)
    down_sum = reduction(hidden_part)
    down_sum.add(left_product(hidden[0], grad_branch), left_product(hidden[1], grad_branch))
    up_sum = reduction(2 * part)
    grad_pre, grad_b_up, grad_up = [None, None], [None, None], [None, None]
    if fast:
        down_sum.one()
    grad_pre[1], grad_b_up[1], grad_up[1] = feed_back(
        after(grad_branch, down_sum.sent), down_w[1], slope[1], across_two, BF
    )
    grad_pre[0], grad_b_up[0], grad_up[0] = feed_back(grad_branch, down_w[0], slope[0], across_two, F32)
    up_sum.add(grad_up[0], grad_up[1])
    if fast:
        down_sum.two(grad_pre[0])
    grad_pre = after(grad_pre, down_sum.sent)
    grad_middle, *grad_context, grad_out_mine, grad_out_other, middle_sums = middle_back(
        place, grad_pre, up_w, middle, cotangent, absorbed, rows, contexts, attn_w
    )

    attn_sum = reduction(2 * part)
    up_sum.add(grad_out_mine, grad_out_other)
    if fast:
        up_sum.one(down_sum.got)
        down_sum.along_z()
    grads = [None, None]
    grads[1] = attention_back(
        qkv_other, after(grad_context[1], down_sum.sent, up_sum.sent), across_one, seq_length, BF
    )
    if fast:
        up_sum.two(down_sum.got, grads[1])
    grads[0] = attention_back(qkv_mine, after(grad_context[0], up_sum.sent), across_one, seq_length, F32)
    grad_qkv, grad_weights, sums = zip(*grads)
    attn_sum.add(grad_weights[0], grad_weights[1])
    if fast:
        attn_sum.one(up_sum.got)
        up_sum.along_z()
    grad_qkv = after(grad_qkv, up_sum.sent, attn_sum.sent)
    grad_b_up = paired(core, *[item.reshape(chips, hidden_part) for item in grad_b_up], 1).reshape(count, hidden_part)
    grad_b_up = jnp.pad(grad_b_up[:, None], ((0, 0), (0, part - 1), (LANES - hidden_part, 0)))
    seqs = count * seq_count
    grad_tokens, *blocks = start_back(
        place, grad_qkv, attn_w, start, grad_middle, absorbed, rows, middle_sums, sums,
        grad_b_up.reshape(width, LANES), seqs, seq_length, fast,
    )
    if fast:
        attn_sum.two(grad_tokens)
        extra_sum = reduction(2 * part)
        extra_sum.add(*blocks)
        extra_sum.one()
        extra_sum.two(attn_sum.sent, up_sum.got)
        attn_sum.along_z(extra_sum)
        hidden, rows = after((hidden, rows), attn_sum.sent)
    output = middle + (product(hidden[0], down_w[0]) + product(hidden[1], down_w[1]) + rows[seq_count + 3])
    if fast:
        attn_grad = attn_sum.columns(output)
        small, seq_sums = attn_grad[:, 0, 3 * half :], attn_grad[:, 1, 3 * half :]
    else:
        attn_grad = attn_sum.columns()
        small, seq_sums = [
            lax.psum_scatter(item.astype(BF), AXES, scatter_dimension=0, tiled=True).astype(F32) for item in blocks
        ]
    steps = rows[seq_count + fixed + up_cols : seq_count + small_cols]
    steps = steps.reshape(seq_cols, count, part).transpose(1, 0, 2).reshape(count, -1).astype(jnp.int32)
    steps = (steps[:, :seq_count] * 256 + steps[:, seq_count : 2 * seq_count]).reshape(-1)
    grad_b_up = small[0, LANES - hidden_part :]
    small = small[:, :fixed].T
    onehot = (steps[:, None] == lax.broadcasted_iota(jnp.int32, (seqs, table_cols), 1)).astype(F32)
    grad_time_table = jnp.dot(seq_sums, onehot, precision=lax.Precision.HIGHEST)
    grad_w_qkv = attn_grad[:, :, : 3 * half].reshape(part, 2, 3, half).transpose(0, 2, 1, 3).reshape(part, 3 * width)
    up_grad = up_sum.columns(extra_sum.sent if fast else ())
    grad_w_out = up_grad[:, :, hidden_width // 2 :].reshape(part, width)
    grad_w_up = up_grad[:, :, : hidden_width // 2].reshape(part, 2, chips, hidden_part).transpose(0, 2, 1, 3)
    grad_w_up = grad_w_up.reshape(part, hidden_width)
    return (
        output,
        grad_tokens,
        grad_w_qkv,
        grad_w_out,
        grad_w_up,
        down_sum.sums(extra_sum.sent if fast else ()),
        grad_time_table,
        small[0],
        small[1],
        small[2],
        grad_b_up,
        small[3],
        small[4],
        small[5],
        small[6],
        small[7],
        small[8],
    )


def solution(mesh):
    matrix, vector = P(AXES, None), P(AXES)
    fast = dict(mesh.shape) == {"fsdp": 8, "rep": 4}
    return jax.shard_map(
        functools.partial(body, fast),
        mesh=mesh,
        in_specs=(matrix, vector, vector) + (matrix,) * 6 + (vector,) * 10,
        out_specs=(matrix,) * 7 + (vector,) * 10,
        check_vma=False,
    )
```

```python
import functools
import math

import jax
import jax.numpy as jnp
from jax import lax
from jax.experimental import pallas as pl
from jax.experimental.pallas import tpu as pltpu
from jax.sharding import PartitionSpec as P

HDIM = 64
EPSILON = 1e-05
AXES = ("fsdp", "rep")
BF = jnp.bfloat16
F32 = jnp.float32
LANES = 128
VMEM_BYTES = 16 << 20
GELU_OUTER = math.sqrt(2.0 / math.pi)
GELU_INNER = 0.044715


def contract(left, right, left_dim, right_dim):
    dims = (((left_dim,), (right_dim,)), ((), ()))
    return lax.dot_general(left, right, dims, preferred_element_type=F32)


def product(left, right):
    return contract(left, right, 1, 0)


def left_product(left, right):
    return contract(left, right, 0, 0)


def right_product(left, right):
    return contract(left, right, 1, 1)


def pick(array, index, axis):
    return lax.dynamic_index_in_dim(array, index, axis, keepdims=False)


def paired(bit, mine, other, axis):
    return jnp.stack([jnp.where(bit == 0, mine, other), jnp.where(bit == 0, other, mine)], axis)


def in_hbm(value):
    return pltpu.with_memory_space_constraint(value, pltpu.HBM)


def after(value, *others):
    return lax.optimization_barrier((value, others))[0]


def lane_masks(factor):
    lane = lax.broadcasted_iota(jnp.int32, (1, LANES), 1)
    return [jnp.where((lane < HDIM) == (head == 0), factor, 0.0).astype(BF) for head in (0, 1)]


def stacked(values, masks):
    return jnp.concatenate([values * masks[0], values * masks[1]], 0)


def unstacked(values):
    rows = values.shape[0] // 2
    lane = lax.broadcasted_iota(jnp.int32, (1, LANES), 1)
    return jnp.where(lane < HDIM, values[:rows], values[rows:])


def softmax_down(scores):
    powers = jnp.exp(scores - jnp.max(scores, 0, keepdims=True))
    return powers * (1.0 / jnp.sum(powers, 0, keepdims=True))


def attention_kernel(length, scale, rows_ref, query_ref, key_ref, value_ref, bias_ref, qkv_ref, context_ref):
    weight = jnp.concatenate([query_ref[...], key_ref[...], value_ref[...]], 1)
    projected = product(rows_ref[...], weight)
    for index in range(3):
        part = projected[:, index * LANES : (index + 1) * LANES]
        qkv_ref[index] = (part + bias_ref[index : index + 1, :]).astype(BF)
    scaled = lane_masks(scale)

    for sequence in range(rows_ref.shape[0] // length):
        span = slice(sequence * length, (sequence + 1) * length)
        queries, key_rows, value_rows = [qkv_ref[index, span, :] for index in range(3)]
        probs = softmax_down(right_product(key_rows, stacked(queries, scaled))).astype(BF)
        context_ref[span, :] = unstacked(left_product(probs, value_rows)).astype(BF)


def attention(rows, weight, bias, length):
    tokens, width = rows.shape
    half = bias.shape[1]
    pairs = half // LANES

    def weight_spec(index):
        return pl.BlockSpec((width, LANES), lambda pair: (0, index * pairs + pair))

    return pl.pallas_call(
        functools.partial(attention_kernel, length, 1.0 / math.sqrt(HDIM)),
        grid=(pairs,),
        in_specs=[
            pl.BlockSpec((tokens, width), lambda pair: (0, 0)),
            weight_spec(0),
            weight_spec(1),
            weight_spec(2),
            pl.BlockSpec((8, LANES), lambda pair: (0, pair)),
        ],
        out_specs=[
            pl.BlockSpec((3, tokens, LANES), lambda pair: (0, 0, pair)),
            pl.BlockSpec((tokens, LANES), lambda pair: (0, pair)),
        ],
        out_shape=[
            pltpu.HBM((3, tokens, half), BF),
            jax.ShapeDtypeStruct((tokens, half), BF),
        ],
        compiler_params=pltpu.CompilerParams(vmem_limit_bytes=VMEM_BYTES),
        cost_estimate=pl.CostEstimate(
            flops=6 * tokens * width * half,
            bytes_accessed=2 * tokens * width + 6 * width * half + 8 * tokens * half,
            transcendentals=2 * tokens * length * pairs,
        ),
        name="attention",
    )(rows, weight, weight, weight, bias)


def attention_back_kernel(length, scale, qkv_ref, grad_ref, rows_ref, grads_ref, weight_ref, sums_ref):
    ones, scaled = lane_masks(1.0), lane_masks(scale)

    for sequence in range(grad_ref.shape[0] // length):
        span = slice(sequence * length, (sequence + 1) * length)
        queries, key_rows, value_rows = [qkv_ref[index, span, :] for index in range(3)]
        queries, grad = stacked(queries, scaled), stacked(grad_ref[span, :], ones)
        probs = softmax_down(right_product(key_rows, queries))
        grad_probs = right_product(value_rows, grad)
        grad_scores = probs * (grad_probs - jnp.sum(grad_probs * probs, 0, keepdims=True))
        grad_scores = grad_scores.astype(BF)
        grad_queries = unstacked(left_product(grad_scores, key_rows)) * scale
        grads_ref[0, span, :] = grad_queries.astype(BF)
        grads_ref[1, span, :] = product(grad_scores, queries).astype(BF)
        grads_ref[2, span, :] = product(probs.astype(BF), grad).astype(BF)

    grads = jnp.concatenate([grads_ref[index] for index in range(3)], 1)
    weight = product(rows_ref[...], grads)
    for index in range(3):
        weight_ref[index] = weight[:, index * LANES : (index + 1) * LANES].astype(weight_ref.dtype)
        sums_ref[index : index + 1, :] = jnp.sum(grads_ref[index].astype(F32), 0, keepdims=True)


def attention_back(qkv, grad, rows_across, length, dtype):
    _, tokens, half = qkv.shape
    width = rows_across.shape[0]
    pairs = half // LANES
    return pl.pallas_call(
        functools.partial(attention_back_kernel, length, 1.0 / math.sqrt(HDIM)),
        grid=(pairs,),
        in_specs=[
            pl.BlockSpec((3, tokens, LANES), lambda pair: (0, 0, pair)),
            pl.BlockSpec((tokens, LANES), lambda pair: (0, pair)),
            pl.BlockSpec((width, tokens), lambda pair: (0, 0)),
        ],
        out_specs=[
            pl.BlockSpec((3, tokens, LANES), lambda pair: (0, 0, pair)),
            pl.BlockSpec((3, width, LANES), lambda pair: (0, 0, pair)),
            pl.BlockSpec((3, LANES), lambda pair: (0, pair)),
        ],
        out_shape=[
            pltpu.HBM((3, tokens, half), BF),
            jax.ShapeDtypeStruct((3, width, half), dtype),
            jax.ShapeDtypeStruct((3, half), F32),
        ],
        compiler_params=pltpu.CompilerParams(vmem_limit_bytes=VMEM_BYTES),
        cost_estimate=pl.CostEstimate(
            flops=6 * tokens * width * half,
            bytes_accessed=2 * tokens * width + 12 * width * half + 14 * tokens * half,
            transcendentals=2 * tokens * length * pairs,
        ),
        name="attention_back",
    )(in_hbm(qkv), in_hbm(grad), in_hbm(rows_across))


def feed_kernel(side, rows_ref, weight_ref, bias_ref, hidden_ref, slope_ref, pre_ref):
    pre_ref[...] = product(rows_ref[...], weight_ref[...])
    step = 32

    def chunk(index, carry):
        span = pl.ds(pl.multiple_of(index * step, step), step)
        pre = pre_ref[span, :] + bias_ref[side : side + 1, :]
        square = pre * pre
        bend = jnp.tanh(GELU_OUTER * (pre + GELU_INNER * (square * pre)))
        share = 0.5 * (1.0 + bend)
        hidden_ref[span, :] = (pre * share).astype(BF)
        inner = (0.5 * GELU_OUTER) * pre * (1.0 + (3.0 * GELU_INNER) * square)
        slope_ref[span, :] = share + inner * (1.0 - bend * bend)
        return carry

    lax.fori_loop(0, rows_ref.shape[0] // step, chunk, 0, unroll=2)


def feed(rows, weight, bias, side, block=512):
    tokens, width = rows.shape
    columns = weight.shape[1]
    block = math.gcd(block, columns)
    out = pl.BlockSpec((tokens, block), lambda step: (0, step))
    return pl.pallas_call(
        functools.partial(feed_kernel, side),
        grid=(columns // block,),
        in_specs=[
            pl.BlockSpec((tokens, width), lambda step: (0, 0)),
            pl.BlockSpec((width, block), lambda step: (0, step)),
            pl.BlockSpec((8, block), lambda step: (0, step)),
        ],
        out_specs=[out, out],
        out_shape=[
            pltpu.HBM((tokens, columns), BF),
            pltpu.HBM((tokens, columns), F32),
        ],
        scratch_shapes=[pltpu.VMEM((tokens, block), F32)],
        compiler_params=pltpu.CompilerParams(vmem_limit_bytes=VMEM_BYTES),
        cost_estimate=pl.CostEstimate(
            flops=2 * tokens * width * columns,
            bytes_accessed=2 * tokens * width + 2 * width * columns + 6 * tokens * columns,
            transcendentals=tokens * columns,
        ),
        name="feed",
    )(rows, weight, bias)


def feed_back_kernel(grad_ref, weight_ref, slope_ref, rows_ref, pre_ref, sum_ref, up_ref):
    grad = (right_product(grad_ref[...], weight_ref[...]) * slope_ref[...]).astype(BF)
    pre_ref[...] = grad
    sum_ref[...] = jnp.sum(grad.astype(F32), 0, keepdims=True)
    up_ref[...] = product(rows_ref[...], grad).astype(up_ref.dtype)


def feed_back(grad, weight, slope, rows_across, dtype, block=768):
    tokens, width = grad.shape
    columns = weight.shape[0]
    block = math.gcd(block, columns)
    out = pl.BlockSpec((tokens, block), lambda step: (0, step))
    return pl.pallas_call(
        feed_back_kernel,
        grid=(columns // block,),
        in_specs=[
            pl.BlockSpec((tokens, width), lambda step: (0, 0)),
            pl.BlockSpec((block, width), lambda step: (step, 0)),
            out,
            pl.BlockSpec((width, tokens), lambda step: (0, 0)),
        ],
        out_specs=[
            out,
            pl.BlockSpec((1, block), lambda step: (0, step)),
            pl.BlockSpec((width, block), lambda step: (0, step)),
        ],
        out_shape=[
            pltpu.HBM((tokens, columns), BF),
            jax.ShapeDtypeStruct((1, columns), F32),
            jax.ShapeDtypeStruct((width, columns), dtype),
        ],
        compiler_params=pltpu.CompilerParams(vmem_limit_bytes=VMEM_BYTES),
        cost_estimate=pl.CostEstimate(
            flops=4 * tokens * width * columns,
            bytes_accessed=4 * tokens * width + 6 * width * columns + 6 * tokens * columns,
            transcendentals=0,
        ),
        name="feed_back",
    )(in_hbm(grad), in_hbm(weight), in_hbm(slope), in_hbm(rows_across))


def chosen_side(core, mine, other):
    return jnp.where(core == 0, mine, other), jnp.where(core == 0, other, mine)


def normalized(values):
    center = values - jnp.mean(values, -1, keepdims=True)
    rate = lax.rsqrt(jnp.mean(center * center, -1, keepdims=True) + EPSILON)
    return center * rate, rate


def start_kernel(
    fixed, up_cols, table_cols, seq_count, parts,
    place_ref, tokens_ref, mask_ref, table_mine_ref, table_other_ref,
    rows_ref, start_ref, normed_ref, across_ref, bias_mine_ref, bias_other_ref, bias_up_ref,
):
    core = place_ref[0]
    step = pl.program_id(0)
    width = tokens_ref.shape[1]
    half = width // 2
    chips, part, hidden_part = parts

    @pl.when(step == 0)
    def _():
        count, columns = rows_ref.shape[0], table_mine_ref.shape[1]
        row = lax.broadcasted_iota(jnp.int32, (count, columns), 0)
        wanted = table_cols + row - seq_count
        for index in range(seq_count):
            wanted = jnp.where(row == index, place_ref[2 + index], wanted)
        column = lax.broadcasted_iota(jnp.int32, (count, columns), 1)
        rows = 0.0
        for side, table in ((core, table_mine_ref), (1 - core, table_other_ref)):
            hit = jnp.where(wanted == column + side * columns, 1.0, 0.0).astype(BF)
            rows = rows + right_product(hit, table[...])
        rows_ref[...] = rows
        for ref, side in ((bias_mine_ref, core), (bias_other_ref, 1 - core)):
            ref[...] = jnp.zeros_like(ref)
            for index in (0, 1):
                line = rows_ref[seq_count + index : seq_count + index + 1, :]
                ref[2 * index : 2 * index + 1, :] = jnp.where(side == 0, line[:, :half], line[:, half:])
        for chip in range(chips):
            for index in range(up_cols):
                line = rows_ref[seq_count + fixed + index : seq_count + fixed + index + 1, :]
                pair = [line[:, (2 * chip + i) * part : (2 * chip + i + 1) * part] for i in range(2)]
                where = slice(chip * hidden_part + index * part, chip * hidden_part + (index + 1) * part)
                bias_up_ref[0:1, where], bias_up_ref[1:2, where] = chosen_side(core, *pair)

    small = seq_count
    mask = mask_ref[...]
    start = jnp.where(mask > 0.0, rows_ref[small + 8 : small + 9, :], tokens_ref[...])
    start = start + rows_ref[pl.ds(step, 1), :]
    start_ref[...] = start
    normed, _ = normalized(start)
    normed = normed * rows_ref[small + 4 : small + 5, :] + rows_ref[small + 5 : small + 6, :]
    normed_ref[...] = normed.astype(BF)
    across_ref[...] = normed.T.astype(BF)


def start_rows(place, tokens, mask, weights, fixed, up_cols, table_cols, small_cols, chips, hidden_part):
    count, width = tokens.shape
    seq_count = place.shape[0] - 2
    length = count // seq_count
    half = width // 2
    row_count = -(-(seq_count + small_cols) // 8) * 8
    table_half = weights[0].shape[1] - 4 * half
    tables = 4 * half // table_half
    table_spec = pl.BlockSpec((width, table_half), lambda step: (0, tables))
    rows_spec = pl.BlockSpec((length, width), lambda step: (step, 0))

    def fixed_spec(*shape):
        return pl.BlockSpec(shape, lambda step: (0,) * len(shape))

    return pl.pallas_call(
        functools.partial(
            start_kernel, fixed, up_cols, table_cols, seq_count, (chips, width // (2 * chips), hidden_part)
        ),
        grid=(seq_count,),
        in_specs=[
            pl.BlockSpec(memory_space=pltpu.SMEM),
            rows_spec,
            pl.BlockSpec((length, 1), lambda step: (step, 0)),
            table_spec,
            table_spec,
        ],
        out_specs=[
            fixed_spec(row_count, width),
            rows_spec,
            rows_spec,
            pl.BlockSpec((width, length), lambda step: (0, step)),
            fixed_spec(8, half),
            fixed_spec(8, half),
            fixed_spec(8, chips * hidden_part),
        ],
        out_shape=[
            jax.ShapeDtypeStruct((row_count, width), F32),
            pltpu.HBM((count, width), F32),
            jax.ShapeDtypeStruct((count, width), BF),
            pltpu.HBM((width, count), BF),
            jax.ShapeDtypeStruct((8, half), F32),
            jax.ShapeDtypeStruct((8, half), F32),
            jax.ShapeDtypeStruct((8, chips * hidden_part), F32),
        ],
        compiler_params=pltpu.CompilerParams(vmem_limit_bytes=VMEM_BYTES),
        cost_estimate=pl.CostEstimate(
            flops=4 * row_count * width * table_half, bytes_accessed=14 * count * width, transcendentals=0
        ),
        name="start_rows",
    )(place, in_hbm(tokens), mask, *weights)


def middle_kernel(
    small, place_ref, context_mine_ref, context_other_ref, out_mine_ref, out_other_ref, start_ref, rows_ref,
    middle_ref, normed_ref, across_ref,
):
    core = place_ref[0]
    half = context_mine_ref.shape[1]
    contexts = chosen_side(core, context_mine_ref[...], context_other_ref[...])
    outs = chosen_side(core, out_mine_ref[...], out_other_ref[...])
    for index, out in enumerate(outs):
        span = slice(index * half, (index + 1) * half)
        total = product(contexts[0], out[:half]) + product(contexts[1], out[half:])
        middle_ref[:, span] = start_ref[:, span] + (total + rows_ref[small + 2 : small + 3, span])
    normed, _ = normalized(middle_ref[...])
    normed = normed * rows_ref[small + 6 : small + 7, :] + rows_ref[small + 7 : small + 8, :]
    normed_ref[...] = normed.astype(BF)
    across_ref[...] = normed.T.astype(BF)


def middle_rows(place, contexts, weights, start, rows, block=256):
    count, width = start.shape
    half = width // 2
    small = place.shape[0] - 2
    block = math.gcd(block, count)
    out_spec = pl.BlockSpec((width, half), lambda step: (0, 3))
    rows_spec = pl.BlockSpec((block, width), lambda step: (step, 0))
    half_spec = pl.BlockSpec((block, half), lambda step: (step, 0))
    return pl.pallas_call(
        functools.partial(middle_kernel, small),
        grid=(count // block,),
        in_specs=[
            pl.BlockSpec(memory_space=pltpu.SMEM),
            half_spec,
            half_spec,
            out_spec,
            out_spec,
            rows_spec,
            pl.BlockSpec(rows.shape, lambda step: (0, 0)),
        ],
        out_specs=[rows_spec, rows_spec, pl.BlockSpec((width, block), lambda step: (0, step))],
        out_shape=[
            pltpu.HBM((count, width), F32),
            jax.ShapeDtypeStruct((count, width), BF),
            pltpu.HBM((width, count), BF),
        ],
        compiler_params=pltpu.CompilerParams(vmem_limit_bytes=VMEM_BYTES),
        cost_estimate=pl.CostEstimate(
            flops=2 * count * width * width, bytes_accessed=14 * count * width + 2 * width * width, transcendentals=0
        ),
        name="middle_rows",
    )(place, *contexts, *weights, start, rows)


def norm_back(values, gain, grad):
    unit, rate = normalized(values)
    scaled = grad * gain
    back = scaled - jnp.mean(scaled, -1, keepdims=True) - unit * jnp.mean(scaled * unit, -1, keepdims=True)
    return rate * back, grad * unit


def middle_back_kernel(
    small, place_ref, pre_mine_ref, pre_other_ref, up_mine_ref, up_other_ref, middle_ref, cotangent_ref, mask_ref,
    rows_ref, context_mine_ref, context_other_ref, out_mine_ref, out_other_ref,
    grad_ref, context_grad_mine_ref, context_grad_other_ref, out_grad_mine_ref, out_grad_other_ref, sums_ref,
    normed_ref, total_ref,
):
    core = place_ref[0]
    step = pl.program_id(0)
    half = context_mine_ref.shape[1]

    @pl.when(step == 0)
    def _():
        sums_ref[...] = jnp.zeros_like(sums_ref)
        total_ref[...] = jnp.zeros_like(total_ref)

    normed_ref[...] = right_product(pre_mine_ref[...], up_mine_ref[...]) + right_product(
        pre_other_ref[...], up_other_ref[...]
    )
    grad = normed_ref[...]
    direct = cotangent_ref[...] * mask_ref[...]
    back, shares = norm_back(middle_ref[...], rows_ref[small + 6 : small + 7, :], grad)
    back = direct + back
    grad_ref[...] = back
    low = back.astype(BF)
    for index, item in enumerate((low.astype(F32), direct.astype(BF).astype(F32), shares, grad)):
        sums_ref[index : index + 1, :] += jnp.sum(item, 0, keepdims=True)
    lows = (low[:, :half], low[:, half:])
    contexts = chosen_side(core, context_mine_ref[...], context_other_ref[...])
    outs = chosen_side(core, out_mine_ref[...], out_other_ref[...])
    context_grads = [
        (right_product(lows[0], outs[0][span]) + right_product(lows[1], outs[1][span])).astype(BF)
        for span in (slice(0, half), slice(half, None))
    ]
    context_grad_mine_ref[...], context_grad_other_ref[...] = chosen_side(core, *context_grads)
    for index, item in enumerate(chosen_side(core, *lows)):
        for side, context in enumerate(contexts):
            total_ref[index, side * half : (side + 1) * half, :] += left_product(context, item)

    @pl.when(step == pl.num_programs(0) - 1)
    def _():
        out_grad_mine_ref[...] = total_ref[0]
        out_grad_other_ref[...] = total_ref[1].astype(BF)


def middle_back(place, grads, ups, middle, cotangent, mask, rows, contexts, weights, block=512):
    count, width = middle.shape
    half = width // 2
    hidden_half = ups[0].shape[1]
    small = place.shape[0] - 2
    block = math.gcd(block, count)

    def over_rows(columns):
        return pl.BlockSpec((block, columns), lambda step: (step, 0))

    def whole(*shape):
        return pl.BlockSpec(shape, lambda step: (0,) * len(shape))

    out_spec = pl.BlockSpec((width, half), lambda step: (0, 3))
    return pl.pallas_call(
        functools.partial(middle_back_kernel, small),
        grid=(count // block,),
        in_specs=[
            pl.BlockSpec(memory_space=pltpu.SMEM),
            over_rows(hidden_half),
            over_rows(hidden_half),
            whole(width, hidden_half),
            whole(width, hidden_half),
            over_rows(width),
            over_rows(width),
            over_rows(1),
            whole(*rows.shape),
            over_rows(half),
            over_rows(half),
            out_spec,
            out_spec,
        ],
        out_specs=[
            over_rows(width),
            over_rows(half),
            over_rows(half),
            whole(width, half),
            whole(width, half),
            whole(8, width),
        ],
        out_shape=[
            jax.ShapeDtypeStruct((count, width), F32),
            jax.ShapeDtypeStruct((count, half), BF),
            jax.ShapeDtypeStruct((count, half), BF),
            jax.ShapeDtypeStruct((width, half), F32),
            jax.ShapeDtypeStruct((width, half), BF),
            jax.ShapeDtypeStruct((8, width), F32),
        ],
        scratch_shapes=[pltpu.VMEM((block, width), F32), pltpu.VMEM((2, width, half), F32)],
        compiler_params=pltpu.CompilerParams(vmem_limit_bytes=2 * VMEM_BYTES),
        cost_estimate=pl.CostEstimate(
            flops=4 * count * width * (hidden_half + width),
            bytes_accessed=4 * count * hidden_half + 4 * width * hidden_half + 16 * count * width,
            transcendentals=0,
        ),
        name="middle_back",
    )(place, *grads, *ups, middle, cotangent, mask, rows, *contexts, *weights)


def start_back_kernel(
    small, length, swap, place_ref, grads_mine_ref, grads_other_ref, weight_mine_ref, weight_other_ref, start_ref, middle_ref,
    mask_ref, rows_ref, sums_ref, sums_mine_ref, sums_other_ref, bias_ref,
    tokens_ref, mine_ref, other_ref, lines_ref,
):
    core, place = place_ref[0], place_ref[1]
    step = pl.program_id(0)
    width = start_ref.shape[1]
    half = width // 2
    seqs = start_ref.shape[0] // length

    @pl.when(step == 0)
    def _():
        lines_ref[...] = jnp.zeros_like(lines_ref)
        for index, row in ((0, 0), (1, 2)):
            pair = (sums_mine_ref[row : row + 1, :], sums_other_ref[row : row + 1, :])
            lines_ref[index : index + 1, :half], lines_ref[index : index + 1, half:] = chosen_side(core, *pair)
        lines_ref[2:4, :] = sums_ref[0:2, :]
        lines_ref[6:8, :] = sums_ref[2:4, :]

    grad = 0.0
    for grads, weight in ((grads_mine_ref, weight_mine_ref), (grads_other_ref, weight_other_ref)):
        for index in range(3):
            grad = grad + right_product(grads[index], weight[:, index * half : (index + 1) * half])
    back, shares = norm_back(start_ref[...], rows_ref[small + 4 : small + 5, :], grad)
    back = middle_ref[...] + back
    mask = mask_ref[...]
    tokens_ref[...] = jnp.where(mask > 0.0, 0.0, back)
    for index, item in ((4, shares), (5, grad), (8, back * mask)):
        lines_ref[index : index + 1, :] += jnp.sum(item, 0, keepdims=True)
    for index in range(seqs):
        line = LANES + place * small + step * seqs + index
        lines_ref[pl.ds(line, 1), :] = jnp.sum(back[index * length : (index + 1) * length], 0, keepdims=True)

    @pl.when(step == pl.num_programs(0) - 1)
    def _():
        blocks = (lines_ref[:LANES, :].T + bias_ref[...], lines_ref[LANES:, :].T)
        if swap:
            blocks = chosen_side(core, *blocks)
        mine_ref[...] = blocks[0]
        other_ref[...] = blocks[1].astype(other_ref.dtype)


def start_back(
    place, grads, weights, start, middle, mask, rows, sums, side_sums, bias, seqs, length, swap, block=256
):
    count, width = start.shape
    half = width // 2
    small = place.shape[0] - 2
    block = math.gcd(block, count)
    lines = LANES + -(-seqs // LANES) * LANES

    def over_rows(columns):
        return pl.BlockSpec((block, columns), lambda step: (step, 0))

    def whole(*shape):
        return pl.BlockSpec(shape, lambda step: (0,) * len(shape))

    grads_spec = pl.BlockSpec((3, block, half), lambda step: (0, step, 0))
    return pl.pallas_call(
        functools.partial(start_back_kernel, small, length, swap),
        grid=(count // block,),
        in_specs=[
            pl.BlockSpec(memory_space=pltpu.SMEM),
            grads_spec,
            grads_spec,
            whole(width, 3 * half),
            whole(width, 3 * half),
            over_rows(width),
            over_rows(width),
            over_rows(1),
            whole(*rows.shape),
            whole(*sums.shape),
            whole(*side_sums[0].shape),
            whole(*side_sums[1].shape),
            whole(width, LANES),
        ],
        out_specs=[over_rows(width), whole(width, LANES), whole(width, lines - LANES)],
        out_shape=[
            jax.ShapeDtypeStruct((count, width), F32),
            jax.ShapeDtypeStruct((width, LANES), F32),
            jax.ShapeDtypeStruct((width, lines - LANES), BF if swap else F32),
        ],
        scratch_shapes=[pltpu.VMEM((lines, width), F32)],
        compiler_params=pltpu.CompilerParams(vmem_limit_bytes=VMEM_BYTES),
        cost_estimate=pl.CostEstimate(
            flops=0, bytes_accessed=1024, transcendentals=0
        ),
        name="start_back",
    )(place, *grads, *weights, start, middle, mask, rows, sums, *side_sums, bias)


def shards_kernel(fixed, seq_cols, place_ref, qkv_ref, out_ref, table_ref, *refs):
    small_refs, (mine_ref, other_ref, full_ref) = refs[: fixed + 1], refs[fixed + 1 :]
    core = place_ref[0]
    part, table_cols = table_ref.shape
    half = out_ref.shape[1] // 2
    seq_count = place_ref.shape[0] - 2
    lines = [ref[...] for ref in small_refs[:fixed]]
    up = small_refs[fixed][...]
    lines += [up[:, i : i + part] for i in range(0, up.shape[1], part)]
    lane = lax.broadcasted_iota(jnp.int32, (1, part), 1)
    for row in range(seq_cols):
        line = jnp.zeros((1, part), jnp.int32)
        for index in range(seq_count):
            step = place_ref[2 + index]
            line = jnp.where(lane + row * part == index, step // 256, line)
            line = jnp.where(lane + row * part == seq_count + index, step % 256, line)
        lines.append(line.astype(F32))
    lines = jnp.concatenate(lines, 0).astype(BF)
    square = (part, part)
    unit = lax.broadcasted_iota(jnp.int32, square, 0) == lax.broadcasted_iota(jnp.int32, square, 1)
    full_ref[...] = jnp.zeros_like(full_ref)
    full_ref[:, :table_cols] = table_ref[...]
    full_ref[:, table_cols : table_cols + lines.shape[0]] = right_product(jnp.where(unit, 1.0, 0.0).astype(BF), lines)
    table_half = full_ref.shape[1] // 2

    def halves(ref, top, wide):
        return chosen_side(core, ref[:, top : top + wide], ref[:, top + wide : top + 2 * wide])

    sources = [(qkv_ref, 2 * half * i, half) for i in range(3)] + [(out_ref, 0, half), (full_ref, 0, table_half)]
    left = 0
    for ref, top, wide in sources:
        mine, other = halves(ref, top, wide)
        mine_ref[:, left : left + wide] = mine.astype(BF)
        other_ref[:, left : left + wide] = other.astype(BF)
        left += wide


def attention_shards(place, w_qkv, w_out, table, small, b_up, seq_cols, all_cols):
    part = table.shape[0]
    shape = jax.ShapeDtypeStruct((part, 2 * w_out.shape[1] + all_cols // 2), BF)
    vmem = pl.BlockSpec(memory_space=pltpu.VMEM)
    return pl.pallas_call(
        functools.partial(shards_kernel, len(small), seq_cols),
        in_specs=[pl.BlockSpec(memory_space=pltpu.SMEM)] + [vmem] * (4 + len(small)),
        out_specs=[vmem, vmem],
        out_shape=[shape, shape],
        scratch_shapes=[pltpu.VMEM((part, all_cols), F32)],
        compiler_params=pltpu.CompilerParams(vmem_limit_bytes=60 << 20),
        cost_estimate=pl.CostEstimate(flops=0, bytes_accessed=24 * part * w_out.shape[1], transcendentals=0),
        name="attention_shards",
    )(place, w_qkv, w_out, table, *[item.reshape(1, -1) for item in small], b_up.reshape(1, -1))


def route_kernel(rows, route_ref, *refs):
    terms, (sent_ref, kept_ref) = refs[:-2], refs[-2:]
    for index in range(2):
        for out, place in ((sent_ref, route_ref[index]), (kept_ref, route_ref[2 + index])):
            span = pl.ds(pl.multiple_of(place * rows, 8), rows)
            left = 0
            for mine, got in zip(terms[::2], terms[1::2]):
                many = [(slice(None),)] if len(mine.shape) == 2 else [(i, slice(None)) for i in range(mine.shape[0])]
                for at in many:
                    where = (*at[:-1], span)
                    total = mine[where].astype(F32) + got[where].astype(F32)
                    out[0, index, :, left : left + total.shape[1]] = total.astype(out.dtype)
                    left += total.shape[1]


def routed(terms, rows, route):
    specs, columns, bytes_read = [], 0, 0
    for array in [item for pair in terms for item in pair]:
        shape = (4 * rows, array.shape[-1])
        if array.ndim == 2:
            specs.append(pl.BlockSpec(shape, lambda z: (z, 0)))
        else:
            specs.append(pl.BlockSpec((array.shape[0], *shape), lambda z: (0, z, 0)))
        bytes_read += array.size * array.dtype.itemsize
        columns += array.size // (16 * rows)
    columns //= 2
    out = pl.BlockSpec((1, 2, rows, columns), lambda z: (z, 0, 0, 0))
    return pl.pallas_call(
        functools.partial(route_kernel, rows),
        grid=(4,),
        in_specs=[pl.BlockSpec(memory_space=pltpu.SMEM)] + specs,
        out_specs=[out, out],
        out_shape=[
            jax.ShapeDtypeStruct((4, 2, rows, columns), BF),
            pltpu.HBM((4, 2, rows, columns), F32),
        ],
        compiler_params=pltpu.CompilerParams(vmem_limit_bytes=VMEM_BYTES),
        cost_estimate=pl.CostEstimate(
            flops=0, bytes_accessed=bytes_read + 48 * rows * columns, transcendentals=0
        ),
        name="routed",
    )(route, *[item for pair in terms for item in pair])


class Tree:
    def __init__(self):
        fsdp, rep = lax.axis_index("fsdp"), lax.axis_index("rep")
        self.z, self.core = fsdp // 2, rep % 2
        x, y = rep // 2, fsdp % 2
        self.near = jnp.where(self.core == 0, x, y)
        self.far = jnp.where(self.core == 0, y, x)
        places = [jnp.where(self.core == 0, 2 * i + near, 2 * near + i) for near in (1 - self.near, self.near) for i in (0, 1)]
        self.route = jnp.stack(places)

    def to_core(self, value):
        return lax.ppermute(value, "rep", [(i, i ^ 1) for i in range(4)])

    def to_near(self, value):
        return lax.ppermute(value, AXES, [(i, i ^ (4 if i % 2 else 2)) for i in range(32)])

    def to_far(self, value):
        return lax.ppermute(value, AXES, [(i, i ^ (2 if i % 2 else 4)) for i in range(32)])

    def to_z(self, value, step):
        return lax.ppermute(value, "fsdp", [(i, i ^ (2 * step)) for i in range(8)])


class Gather:
    def __init__(self, tree, own):
        self.tree, self.own = tree, own

    @staticmethod
    def columns(tree, mine, other):
        got = tree.to_core(other)
        return Gather(tree, paired(tree.core, mine, got, 0).reshape(-1, mine.shape[1]))

    @staticmethod
    def rows(tree, shard):
        return Gather(tree, shard)

    def along_z(self, *wait):
        own = after(self.own, *wait)
        one, three, two = [self.tree.to_z(own, step) for step in (1, 3, 2)]
        self.held, self.got = own, [one, two, three]
        return self.got

    def one(self, *wait):
        tree = self.tree
        held = after([self.held, *self.got], *wait)
        low, high = tree.z % 2 == 1, tree.z // 2 == 1
        out = []
        for place in range(4):
            near = [jnp.where(low, held[(place ^ 1) ^ h], held[place ^ h]) for h in (0, 2)]
            out.append(jnp.where(high, near[1], near[0]))
        self.held = jnp.stack(out)
        self.got = tree.to_near(self.held)
        return self.got

    def two(self, *wait):
        tree = self.tree
        held, got = after((self.held, self.got), *wait)
        self.held = paired(tree.near, held, got, 1)
        self.got = tree.to_far(self.held)
        return self.got

    def halves(self, *wait):
        tree = self.tree
        held, got = after((self.held, self.got), *wait)
        same, first = tree.far == 0, tree.core == 0
        lower, upper = jnp.where(same, held, got), jnp.where(same, got, held)
        blocks = [
            lower[:, 0],
            jnp.where(first, lower[:, 1], upper[:, 0]),
            jnp.where(first, upper[:, 0], lower[:, 1]),
            upper[:, 1],
        ]
        half = jnp.stack(blocks, 1).reshape(-1, held.shape[-1])
        return half, tree.to_core(half)


class Reduce:
    def __init__(self, tree, rows):
        self.tree, self.rows = tree, rows
        self.terms = []

    def add(self, mine, other):
        got = self.tree.to_core(other.astype(BF))
        self.terms.append((mine, got))
        return got

    def one(self, *wait):
        self.sent, self.kept = routed(after(self.terms, *wait), self.rows, self.tree.route)
        self.got = self.tree.to_near(self.sent)

    def two(self, *wait):
        tree = self.tree
        kept, got = after((self.kept, self.got), *wait)
        total = kept + got
        self.kept, self.sent = pick(total, tree.far, 1), pick(total, 1 - tree.far, 1).astype(BF)
        self.got = tree.to_far(self.sent)

    def along_z(self, *others):
        tree = self.tree
        total = jnp.concatenate([item.kept + item.got for item in (self, *others)], -1)
        self.kept = pick(total, tree.z, 0)
        self.sent = tuple(pick(total, tree.z ^ step, 0).astype(BF) for step in (1, 2, 3))
        self.got = tuple(tree.to_z(sent, step) for sent, step in zip(self.sent, (1, 2, 3)))

    def sums(self, *wait):
        kept, got = after((self.kept, self.got), *wait)
        return kept + got[0] + got[1] + got[2]

    def columns(self, *wait):
        tree, total = self.tree, self.sums(*wait)
        rows = total.reshape(2, self.rows // 2, -1)
        keep = pick(rows, tree.core, 0)
        return paired(tree.core, keep, tree.to_core(pick(rows, 1 - tree.core, 0)), 1)


class Whole:
    core = 0

    def __init__(self, rows=None):
        self.mine, self.other = [], []
        self.got, self.sent = (), ()

    @staticmethod
    def columns_of(mine, other):
        out = Whole()
        whole = lax.all_gather(jnp.stack([mine, other], 1), AXES, axis=0, tiled=True)
        out.half, out.rest = whole[:, 0], whole[:, 1]
        return out

    @staticmethod
    def rows_of(shard):
        out = Whole()
        whole = lax.all_gather(shard, AXES, axis=0)
        whole = whole.reshape(-1, 2, *shard.shape)
        out.half, out.rest = [whole[:, i].reshape(-1, shard.shape[1]) for i in range(2)]
        return out

    def along_z(self, *wait):
        return []

    def one(self, *wait):
        return ()

    def two(self, *wait):
        return ()

    def halves(self, *wait):
        return self.half, self.rest

    def add(self, mine, other):
        self.mine.append(mine.astype(BF))
        self.other.append(other.astype(BF))
        return mine

    def columns(self, *wait):
        def flat(items):
            return jnp.concatenate([part for item in items for part in (item if item.ndim == 3 else [item])], 1)

        parts = [flat(item) for item in (self.mine, self.other)]
        return lax.psum_scatter(jnp.stack(parts, 1), AXES, scatter_dimension=0, tiled=True).astype(F32)

    def sums(self, *wait):
        count = lax.axis_size(AXES)
        mine, other = [item[0].reshape(count // 2, -1, item[0].shape[1]) for item in (self.mine, self.other)]
        sums = jnp.stack([mine, other], 1).reshape(-1, mine.shape[-1])
        return lax.psum_scatter(sums, AXES, scatter_dimension=0, tiled=True).astype(F32)


def body(
    fast,
    tokens,
    mask_bits,
    timesteps,
    cotangent,
    w_qkv,
    w_out,
    w_up,
    w_down,
    time_table,
    b_query,
    b_value,
    b_out,
    b_up,
    b_down,
    gain_attn,
    shift_attn,
    gain_mlp,
    shift_mlp,
    mask_vector,
):
    tree = Tree() if fast else Whole()
    gather_columns = functools.partial(Gather.columns, tree) if fast else Whole.columns_of
    gather_rows = functools.partial(Gather.rows, tree) if fast else Whole.rows_of
    reduction = functools.partial(Reduce, tree) if fast else Whole
    core = tree.core
    count = lax.axis_size(AXES)
    chips = count // 2
    place = lax.axis_index(AXES)
    width = tokens.shape[1]
    part = width // count
    hidden_width = w_up.shape[1]
    hidden_part = hidden_width // count
    seq_count = timesteps.shape[0]
    seq_length = tokens.shape[0] // seq_count
    half = width // 2
    table_cols = time_table.shape[1]
    absorbed = mask_bits.astype(F32)[:, None]

    small = [b_query, b_value, b_out, b_down, gain_attn, shift_attn, gain_mlp, shift_mlp, mask_vector]
    fixed = len(small)
    up_cols = hidden_part // part
    seq_cols = -(-2 * seq_count // part)
    small_cols = fixed + up_cols + seq_cols
    all_cols = -(-(table_cols + small_cols) // (2 * LANES)) * (2 * LANES)
    place = jnp.concatenate([jnp.stack([jnp.int32(core), place]), timesteps])

    attn_w = gather_columns(*attention_shards(place, w_qkv, w_out, time_table, small, b_up, seq_cols, all_cols))
    up_shard = w_up.astype(BF).reshape(part, chips, 2, hidden_part).transpose(2, 0, 1, 3)
    up_shard = up_shard.reshape(2, part, hidden_width // 2)
    up_w = gather_columns(*[pick(up_shard, side, 0) for side in (core, 1 - core)])
    down_w = gather_rows(w_down.astype(BF))
    attn_w.along_z()
    up_z = up_w.along_z()
    attn_one = attn_w.one()
    attn_two = attn_w.two(up_z[::2])
    up_one = up_w.one(attn_two)
    attn_w = attn_w.halves(up_z)
    down_z = down_w.along_z(attn_two)

    rows, start, normed_one, across_one, bias_mine, bias_other, bias_up = start_rows(
        place, tokens, absorbed, attn_w, fixed, up_cols, table_cols, small_cols, chips, hidden_part
    )
    up_two = up_w.two(normed_one)
    qkv_mine, context_mine = attention(after(normed_one, up_one), attn_w[0], bias_mine, seq_length)
    down_one = down_w.one(up_two, context_mine)
    up_w = up_w.halves(context_mine)
    qkv_other, context_other = attention(after(normed_one, up_two), attn_w[1], bias_other, seq_length)
    down_two = down_w.two(context_other)
    contexts = (context_mine, context_other)
    middle, normed_two, across_two = middle_rows(place, contexts, attn_w, after(start, down_one), rows)
    hidden, slope = [None, None], [None, None]
    hidden[0], slope[0] = feed(normed_two, up_w[0], bias_up, 0)
    down_w = down_w.halves(hidden[0])
    hidden[1], slope[1] = feed(after(normed_two, down_two), up_w[1], bias_up, 1)

    grad_branch = (cotangent * absorbed).astype(BF)
    down_sum = reduction(hidden_part)
    down_sum.add(left_product(hidden[0], grad_branch), left_product(hidden[1], grad_branch))
    up_sum = reduction(2 * part)
    grad_pre, grad_b_up, grad_up = [None, None], [None, None], [None, None]
    if fast:
        down_sum.one()
    grad_pre[1], grad_b_up[1], grad_up[1] = feed_back(
        after(grad_branch, down_sum.sent), down_w[1], slope[1], across_two, BF
    )
    grad_pre[0], grad_b_up[0], grad_up[0] = feed_back(grad_branch, down_w[0], slope[0], across_two, F32)
    up_sum.add(grad_up[0], grad_up[1])
    if fast:
        down_sum.two(grad_pre[0])
    grad_pre = after(grad_pre, down_sum.sent)
    grad_middle, *grad_context, grad_out_mine, grad_out_other, middle_sums = middle_back(
        place, grad_pre, up_w, middle, cotangent, absorbed, rows, contexts, attn_w
    )

    attn_sum = reduction(2 * part)
    up_sum.add(grad_out_mine, grad_out_other)
    if fast:
        up_sum.one(down_sum.got)
        down_sum.along_z()
    grads = [None, None]
    grads[1] = attention_back(
        qkv_other, after(grad_context[1], down_sum.sent, up_sum.sent), across_one, seq_length, BF
    )
    if fast:
        up_sum.two(down_sum.got, grads[1])
    grads[0] = attention_back(qkv_mine, after(grad_context[0], up_sum.sent), across_one, seq_length, F32)
    grad_qkv, grad_weights, sums = zip(*grads)
    attn_sum.add(grad_weights[0], grad_weights[1])
    if fast:
        attn_sum.one(up_sum.got)
        up_sum.along_z()
    grad_qkv = after(grad_qkv, up_sum.sent, attn_sum.sent)
    grad_b_up = paired(core, *[item.reshape(chips, hidden_part) for item in grad_b_up], 1).reshape(count, hidden_part)
    grad_b_up = jnp.pad(grad_b_up[:, None], ((0, 0), (0, part - 1), (LANES - hidden_part, 0)))
    seqs = count * seq_count
    grad_tokens, *blocks = start_back(
        place, grad_qkv, attn_w, start, grad_middle, absorbed, rows, middle_sums, sums,
        grad_b_up.reshape(width, LANES), seqs, seq_length, fast,
    )
    if fast:
        attn_sum.two(grad_tokens)
        extra_sum = reduction(2 * part)
        extra_sum.add(*blocks)
        extra_sum.one()
        extra_sum.two(attn_sum.sent, up_sum.got)
        attn_sum.along_z(extra_sum)
        hidden, rows = after((hidden, rows), attn_sum.sent)
    output = middle + (product(hidden[0], down_w[0]) + product(hidden[1], down_w[1]) + rows[seq_count + 3])
    if fast:
        attn_grad = attn_sum.columns(output)
        small, seq_sums = attn_grad[:, 0, 3 * half :], attn_grad[:, 1, 3 * half :]
    else:
        attn_grad = attn_sum.columns()
        small, seq_sums = [
            lax.psum_scatter(item.astype(BF), AXES, scatter_dimension=0, tiled=True).astype(F32) for item in blocks
        ]
    steps = rows[seq_count + fixed + up_cols : seq_count + small_cols]
    steps = steps.reshape(seq_cols, count, part).transpose(1, 0, 2).reshape(count, -1).astype(jnp.int32)
    steps = (steps[:, :seq_count] * 256 + steps[:, seq_count : 2 * seq_count]).reshape(-1)
    grad_b_up = small[0, LANES - hidden_part :]
    small = small[:, :fixed].T
    onehot = (steps[:, None] == lax.broadcasted_iota(jnp.int32, (seqs, table_cols), 1)).astype(F32)
    grad_time_table = jnp.dot(seq_sums, onehot, precision=lax.Precision.HIGHEST)
    grad_w_qkv = attn_grad[:, :, : 3 * half].reshape(part, 2, 3, half).transpose(0, 2, 1, 3).reshape(part, 3 * width)
    up_grad = up_sum.columns(extra_sum.sent if fast else ())
    grad_w_out = up_grad[:, :, hidden_width // 2 :].reshape(part, width)
    grad_w_up = up_grad[:, :, : hidden_width // 2].reshape(part, 2, chips, hidden_part).transpose(0, 2, 1, 3)
    grad_w_up = grad_w_up.reshape(part, hidden_width)
    return (
        output,
        grad_tokens,
        grad_w_qkv,
        grad_w_out,
        grad_w_up,
        down_sum.sums(extra_sum.sent if fast else ()),
        grad_time_table,
        small[0],
        small[1],
        small[2],
        grad_b_up,
        small[3],
        small[4],
        small[5],
        small[6],
        small[7],
        small[8],
    )


def solution(mesh):
    matrix, vector = P(AXES, None), P(AXES)
    fast = dict(mesh.shape) == {"fsdp": 8, "rep": 4}
    return jax.shard_map(
        functools.partial(body, fast),
        mesh=mesh,
        in_specs=(matrix, vector, vector) + (matrix,) * 6 + (vector,) * 10,
        out_specs=(matrix,) * 7 + (vector,) * 10,
        check_vma=False,
    )
```

```python
import functools
import math

import jax
import jax.numpy as jnp
from jax import lax
from jax.experimental import pallas as pl
from jax.experimental.pallas import tpu as pltpu
from jax.sharding import PartitionSpec as P

HDIM = 64
EPSILON = 1e-05
AXES = ("fsdp", "rep")
BF = jnp.bfloat16
F32 = jnp.float32
LANES = 128
VMEM_BYTES = 18 << 20
GELU_OUTER = math.sqrt(2.0 / math.pi)
GELU_INNER = 0.044715


def contract(left, right, left_dim, right_dim):
    dims = (((left_dim,), (right_dim,)), ((), ()))
    return lax.dot_general(left, right, dims, preferred_element_type=F32)


def product(left, right):
    return contract(left, right, 1, 0)


def left_product(left, right):
    return contract(left, right, 0, 0)


def right_product(left, right):
    return contract(left, right, 1, 1)


def pick(array, index, axis):
    return lax.dynamic_index_in_dim(array, index, axis, keepdims=False)


def paired(bit, mine, other, axis):
    return jnp.stack([jnp.where(bit == 0, mine, other), jnp.where(bit == 0, other, mine)], axis)


def in_hbm(value):
    return pltpu.with_memory_space_constraint(value, pltpu.HBM)


def after(value, *others):
    return lax.optimization_barrier((value, others))[0]


def lane_masks(factor):
    lane = lax.broadcasted_iota(jnp.int32, (1, LANES), 1)
    return [jnp.where((lane < HDIM) == (head == 0), factor, 0.0).astype(BF) for head in (0, 1)]


def stacked(values, masks):
    return jnp.concatenate([values * masks[0], values * masks[1]], 0)


def unstacked(values):
    rows = values.shape[0] // 2
    lane = lax.broadcasted_iota(jnp.int32, (1, LANES), 1)
    return jnp.where(lane < HDIM, values[:rows], values[rows:])


def softmax_down(scores):
    powers = jnp.exp(scores - jnp.max(scores, 0, keepdims=True))
    return powers * (1.0 / jnp.sum(powers, 0, keepdims=True))


def attention_kernel(length, scale, rows_ref, query_ref, key_ref, value_ref, bias_ref, qkv_ref, context_ref):
    weight = jnp.concatenate([query_ref[...], key_ref[...], value_ref[...]], 1)
    projected = product(rows_ref[...], weight)
    for index in range(3):
        part = projected[:, index * LANES : (index + 1) * LANES]
        qkv_ref[index] = (part + bias_ref[index : index + 1, :]).astype(BF)
    scaled = lane_masks(scale)

    for sequence in range(rows_ref.shape[0] // length):
        span = slice(sequence * length, (sequence + 1) * length)
        queries, key_rows, value_rows = [qkv_ref[index, span, :] for index in range(3)]
        probs = softmax_down(right_product(key_rows, stacked(queries, scaled))).astype(BF)
        context_ref[span, :] = unstacked(left_product(probs, value_rows)).astype(BF)


def attention(rows, weight, bias, length):
    tokens, width = rows.shape
    half = bias.shape[1]
    pairs = half // LANES

    def weight_spec(index):
        return pl.BlockSpec((width, LANES), lambda pair: (0, index * pairs + pair))

    return pl.pallas_call(
        functools.partial(attention_kernel, length, 1.0 / math.sqrt(HDIM)),
        grid=(pairs,),
        in_specs=[
            pl.BlockSpec((tokens, width), lambda pair: (0, 0)),
            weight_spec(0),
            weight_spec(1),
            weight_spec(2),
            pl.BlockSpec((8, LANES), lambda pair: (0, pair)),
        ],
        out_specs=[
            pl.BlockSpec((3, tokens, LANES), lambda pair: (0, 0, pair)),
            pl.BlockSpec((tokens, LANES), lambda pair: (0, pair)),
        ],
        out_shape=[
            pltpu.HBM((3, tokens, half), BF),
            jax.ShapeDtypeStruct((tokens, half), BF),
        ],
        compiler_params=pltpu.CompilerParams(vmem_limit_bytes=VMEM_BYTES),
        cost_estimate=pl.CostEstimate(
            flops=6 * tokens * width * half,
            bytes_accessed=2 * tokens * width + 6 * width * half + 8 * tokens * half,
            transcendentals=2 * tokens * length * pairs,
        ),
        name="attention",
    )(rows, weight, weight, weight, bias)


def attention_back_kernel(length, scale, qkv_ref, grad_ref, rows_ref, grads_ref, weight_ref, sums_ref):
    ones, scaled = lane_masks(1.0), lane_masks(scale)

    for sequence in range(grad_ref.shape[0] // length):
        span = slice(sequence * length, (sequence + 1) * length)
        queries, key_rows, value_rows = [qkv_ref[index, span, :] for index in range(3)]
        queries, grad = stacked(queries, scaled), stacked(grad_ref[span, :], ones)
        probs = softmax_down(right_product(key_rows, queries))
        grad_probs = right_product(value_rows, grad)
        grad_scores = probs * (grad_probs - jnp.sum(grad_probs * probs, 0, keepdims=True))
        grad_scores = grad_scores.astype(BF)
        grad_queries = unstacked(left_product(grad_scores, key_rows)) * scale
        grads_ref[0, span, :] = grad_queries.astype(BF)
        grads_ref[1, span, :] = product(grad_scores, queries).astype(BF)
        grads_ref[2, span, :] = product(probs.astype(BF), grad).astype(BF)

    grads = jnp.concatenate([grads_ref[index] for index in range(3)], 1)
    weight = product(rows_ref[...], grads)
    for index in range(3):
        weight_ref[index] = weight[:, index * LANES : (index + 1) * LANES].astype(weight_ref.dtype)
        sums_ref[index : index + 1, :] = jnp.sum(grads_ref[index].astype(F32), 0, keepdims=True)


def attention_back(qkv, grad, rows_across, length, dtype):
    _, tokens, half = qkv.shape
    width = rows_across.shape[0]
    pairs = half // LANES
    return pl.pallas_call(
        functools.partial(attention_back_kernel, length, 1.0 / math.sqrt(HDIM)),
        grid=(pairs,),
        in_specs=[
            pl.BlockSpec((3, tokens, LANES), lambda pair: (0, 0, pair)),
            pl.BlockSpec((tokens, LANES), lambda pair: (0, pair)),
            pl.BlockSpec((width, tokens), lambda pair: (0, 0)),
        ],
        out_specs=[
            pl.BlockSpec((3, tokens, LANES), lambda pair: (0, 0, pair)),
            pl.BlockSpec((3, width, LANES), lambda pair: (0, 0, pair)),
            pl.BlockSpec((3, LANES), lambda pair: (0, pair)),
        ],
        out_shape=[
            pltpu.HBM((3, tokens, half), BF),
            jax.ShapeDtypeStruct((3, width, half), dtype),
            jax.ShapeDtypeStruct((3, half), F32),
        ],
        compiler_params=pltpu.CompilerParams(vmem_limit_bytes=VMEM_BYTES),
        cost_estimate=pl.CostEstimate(
            flops=6 * tokens * width * half,
            bytes_accessed=2 * tokens * width + 12 * width * half + 14 * tokens * half,
            transcendentals=2 * tokens * length * pairs,
        ),
        name="attention_back",
    )(in_hbm(qkv), in_hbm(grad), in_hbm(rows_across))


def feed_kernel(side, rows_ref, weight_ref, bias_ref, hidden_ref, slope_ref, pre_ref):
    pre_ref[...] = product(rows_ref[...], weight_ref[...])
    step = 32

    def chunk(index, carry):
        span = pl.ds(pl.multiple_of(index * step, step), step)
        pre = pre_ref[span, :] + bias_ref[side : side + 1, :]
        square = pre * pre
        bend = jnp.tanh(GELU_OUTER * (pre + GELU_INNER * (square * pre)))
        share = 0.5 * (1.0 + bend)
        hidden_ref[span, :] = (pre * share).astype(BF)
        inner = (0.5 * GELU_OUTER) * pre * (1.0 + (3.0 * GELU_INNER) * square)
        slope_ref[span, :] = share + inner * (1.0 - bend * bend)
        return carry

    lax.fori_loop(0, rows_ref.shape[0] // step, chunk, 0, unroll=2)


def feed(rows, weight, bias, side, block=512):
    tokens, width = rows.shape
    columns = weight.shape[1]
    block = math.gcd(block, columns)
    out = pl.BlockSpec((tokens, block), lambda step: (0, step))
    return pl.pallas_call(
        functools.partial(feed_kernel, side),
        grid=(columns // block,),
        in_specs=[
            pl.BlockSpec((tokens, width), lambda step: (0, 0)),
            pl.BlockSpec((width, block), lambda step: (0, step)),
            pl.BlockSpec((8, block), lambda step: (0, step)),
        ],
        out_specs=[out, out],
        out_shape=[
            pltpu.HBM((tokens, columns), BF),
            pltpu.HBM((tokens, columns), F32),
        ],
        scratch_shapes=[pltpu.VMEM((tokens, block), F32)],
        compiler_params=pltpu.CompilerParams(vmem_limit_bytes=VMEM_BYTES),
        cost_estimate=pl.CostEstimate(
            flops=2 * tokens * width * columns,
            bytes_accessed=2 * tokens * width + 2 * width * columns + 6 * tokens * columns,
            transcendentals=tokens * columns,
        ),
        name="feed",
    )(rows, weight, bias)


def feed_back_kernel(grad_ref, weight_ref, slope_ref, rows_ref, pre_ref, sum_ref, up_ref):
    grad = (right_product(grad_ref[...], weight_ref[...]) * slope_ref[...]).astype(BF)
    pre_ref[...] = grad
    sum_ref[...] = jnp.sum(grad.astype(F32), 0, keepdims=True)
    up_ref[...] = product(rows_ref[...], grad).astype(up_ref.dtype)


def feed_back(grad, weight, slope, rows_across, dtype, block=768):
    tokens, width = grad.shape
    columns = weight.shape[0]
    block = math.gcd(block, columns)
    out = pl.BlockSpec((tokens, block), lambda step: (0, step))
    return pl.pallas_call(
        feed_back_kernel,
        grid=(columns // block,),
        in_specs=[
            pl.BlockSpec((tokens, width), lambda step: (0, 0)),
            pl.BlockSpec((block, width), lambda step: (step, 0)),
            out,
            pl.BlockSpec((width, tokens), lambda step: (0, 0)),
        ],
        out_specs=[
            out,
            pl.BlockSpec((1, block), lambda step: (0, step)),
            pl.BlockSpec((width, block), lambda step: (0, step)),
        ],
        out_shape=[
            pltpu.HBM((tokens, columns), BF),
            jax.ShapeDtypeStruct((1, columns), F32),
            jax.ShapeDtypeStruct((width, columns), dtype),
        ],
        compiler_params=pltpu.CompilerParams(vmem_limit_bytes=VMEM_BYTES),
        cost_estimate=pl.CostEstimate(
            flops=4 * tokens * width * columns,
            bytes_accessed=4 * tokens * width + 6 * width * columns + 6 * tokens * columns,
            transcendentals=0,
        ),
        name="feed_back",
    )(in_hbm(grad), in_hbm(weight), in_hbm(slope), in_hbm(rows_across))


def chosen_side(core, mine, other):
    return jnp.where(core == 0, mine, other), jnp.where(core == 0, other, mine)


def normalized(values):
    center = values - jnp.mean(values, -1, keepdims=True)
    rate = lax.rsqrt(jnp.mean(center * center, -1, keepdims=True) + EPSILON)
    return center * rate, rate


def start_kernel(
    fixed, up_cols, table_cols, seq_count, parts,
    place_ref, tokens_ref, mask_ref, table_mine_ref, table_other_ref,
    rows_ref, start_ref, normed_ref, across_ref, bias_mine_ref, bias_other_ref, bias_up_ref,
):
    core = place_ref[0]
    step = pl.program_id(0)
    width = tokens_ref.shape[1]
    half = width // 2
    chips, part, hidden_part = parts

    @pl.when(step == 0)
    def _():
        count, columns = rows_ref.shape[0], table_mine_ref.shape[1]
        row = lax.broadcasted_iota(jnp.int32, (count, columns), 0)
        wanted = table_cols + row - seq_count
        for index in range(seq_count):
            wanted = jnp.where(row == index, place_ref[2 + index], wanted)
        column = lax.broadcasted_iota(jnp.int32, (count, columns), 1)
        rows = 0.0
        for side, table in ((core, table_mine_ref), (1 - core, table_other_ref)):
            hit = jnp.where(wanted == column + side * columns, 1.0, 0.0).astype(BF)
            rows = rows + right_product(hit, table[...])
        rows_ref[...] = rows
        for ref, side in ((bias_mine_ref, core), (bias_other_ref, 1 - core)):
            ref[...] = jnp.zeros_like(ref)
            for index in (0, 1):
                line = rows_ref[seq_count + index : seq_count + index + 1, :]
                ref[2 * index : 2 * index + 1, :] = jnp.where(side == 0, line[:, :half], line[:, half:])
        for chip in range(chips):
            for index in range(up_cols):
                line = rows_ref[seq_count + fixed + index : seq_count + fixed + index + 1, :]
                pair = [line[:, (2 * chip + i) * part : (2 * chip + i + 1) * part] for i in range(2)]
                where = slice(chip * hidden_part + index * part, chip * hidden_part + (index + 1) * part)
                bias_up_ref[0:1, where], bias_up_ref[1:2, where] = chosen_side(core, *pair)

    small = seq_count
    mask = mask_ref[...]
    start = jnp.where(mask > 0.0, rows_ref[small + 8 : small + 9, :], tokens_ref[...])
    start = start + rows_ref[pl.ds(step, 1), :]
    start_ref[...] = start
    normed, _ = normalized(start)
    normed = normed * rows_ref[small + 4 : small + 5, :] + rows_ref[small + 5 : small + 6, :]
    normed_ref[...] = normed.astype(BF)
    across_ref[...] = normed.T.astype(BF)


def start_rows(place, tokens, mask, weights, fixed, up_cols, table_cols, small_cols, chips, hidden_part):
    count, width = tokens.shape
    seq_count = place.shape[0] - 2
    length = count // seq_count
    half = width // 2
    row_count = -(-(seq_count + small_cols) // 8) * 8
    table_half = weights[0].shape[1] - 4 * half
    tables = 4 * half // table_half
    table_spec = pl.BlockSpec((width, table_half), lambda step: (0, tables))
    rows_spec = pl.BlockSpec((length, width), lambda step: (step, 0))

    def fixed_spec(*shape):
        return pl.BlockSpec(shape, lambda step: (0,) * len(shape))

    return pl.pallas_call(
        functools.partial(
            start_kernel, fixed, up_cols, table_cols, seq_count, (chips, width // (2 * chips), hidden_part)
        ),
        grid=(seq_count,),
        in_specs=[
            pl.BlockSpec(memory_space=pltpu.SMEM),
            rows_spec,
            pl.BlockSpec((length, 1), lambda step: (step, 0)),
            table_spec,
            table_spec,
        ],
        out_specs=[
            fixed_spec(row_count, width),
            rows_spec,
            rows_spec,
            pl.BlockSpec((width, length), lambda step: (0, step)),
            fixed_spec(8, half),
            fixed_spec(8, half),
            fixed_spec(8, chips * hidden_part),
        ],
        out_shape=[
            jax.ShapeDtypeStruct((row_count, width), F32),
            pltpu.HBM((count, width), F32),
            jax.ShapeDtypeStruct((count, width), BF),
            pltpu.HBM((width, count), BF),
            jax.ShapeDtypeStruct((8, half), F32),
            jax.ShapeDtypeStruct((8, half), F32),
            jax.ShapeDtypeStruct((8, chips * hidden_part), F32),
        ],
        compiler_params=pltpu.CompilerParams(vmem_limit_bytes=VMEM_BYTES),
        cost_estimate=pl.CostEstimate(
            flops=4 * row_count * width * table_half, bytes_accessed=14 * count * width, transcendentals=0
        ),
        name="start_rows",
    )(place, in_hbm(tokens), mask, *weights)


def middle_kernel(
    small, place_ref, context_mine_ref, context_other_ref, out_mine_ref, out_other_ref, start_ref, rows_ref,
    middle_ref, normed_ref, across_ref,
):
    core = place_ref[0]
    half = context_mine_ref.shape[1]
    contexts = chosen_side(core, context_mine_ref[...], context_other_ref[...])
    outs = chosen_side(core, out_mine_ref[...], out_other_ref[...])
    for index, out in enumerate(outs):
        span = slice(index * half, (index + 1) * half)
        total = product(contexts[0], out[:half]) + product(contexts[1], out[half:])
        middle_ref[:, span] = start_ref[:, span] + (total + rows_ref[small + 2 : small + 3, span])
    normed, _ = normalized(middle_ref[...])
    normed = normed * rows_ref[small + 6 : small + 7, :] + rows_ref[small + 7 : small + 8, :]
    normed_ref[...] = normed.astype(BF)
    across_ref[...] = normed.T.astype(BF)


def middle_rows(place, contexts, weights, start, rows, block=256):
    count, width = start.shape
    half = width // 2
    small = place.shape[0] - 2
    block = math.gcd(block, count)
    out_spec = pl.BlockSpec((width, half), lambda step: (0, 3))
    rows_spec = pl.BlockSpec((block, width), lambda step: (step, 0))
    half_spec = pl.BlockSpec((block, half), lambda step: (step, 0))
    return pl.pallas_call(
        functools.partial(middle_kernel, small),
        grid=(count // block,),
        in_specs=[
            pl.BlockSpec(memory_space=pltpu.SMEM),
            half_spec,
            half_spec,
            out_spec,
            out_spec,
            rows_spec,
            pl.BlockSpec(rows.shape, lambda step: (0, 0)),
        ],
        out_specs=[rows_spec, rows_spec, pl.BlockSpec((width, block), lambda step: (0, step))],
        out_shape=[
            pltpu.HBM((count, width), F32),
            jax.ShapeDtypeStruct((count, width), BF),
            pltpu.HBM((width, count), BF),
        ],
        compiler_params=pltpu.CompilerParams(vmem_limit_bytes=VMEM_BYTES),
        cost_estimate=pl.CostEstimate(
            flops=2 * count * width * width, bytes_accessed=14 * count * width + 2 * width * width, transcendentals=0
        ),
        name="middle_rows",
    )(place, *contexts, *weights, start, rows)


def norm_back(values, gain, grad):
    unit, rate = normalized(values)
    scaled = grad * gain
    back = scaled - jnp.mean(scaled, -1, keepdims=True) - unit * jnp.mean(scaled * unit, -1, keepdims=True)
    return rate * back, grad * unit


def middle_back_kernel(
    small, place_ref, pre_mine_ref, pre_other_ref, up_mine_ref, up_other_ref, middle_ref, cotangent_ref, mask_ref,
    rows_ref, context_mine_ref, context_other_ref, out_mine_ref, out_other_ref,
    grad_ref, context_grad_mine_ref, context_grad_other_ref, out_grad_mine_ref, out_grad_other_ref, sums_ref,
    normed_ref, total_ref,
):
    core = place_ref[0]
    step = pl.program_id(0)
    half = context_mine_ref.shape[1]

    @pl.when(step == 0)
    def _():
        sums_ref[...] = jnp.zeros_like(sums_ref)
        total_ref[...] = jnp.zeros_like(total_ref)

    normed_ref[...] = right_product(pre_mine_ref[...], up_mine_ref[...]) + right_product(
        pre_other_ref[...], up_other_ref[...]
    )
    grad = normed_ref[...]
    direct = cotangent_ref[...] * mask_ref[...]
    back, shares = norm_back(middle_ref[...], rows_ref[small + 6 : small + 7, :], grad)
    back = direct + back
    grad_ref[...] = back
    low = back.astype(BF)
    for index, item in enumerate((low.astype(F32), direct.astype(BF).astype(F32), shares, grad)):
        sums_ref[index : index + 1, :] += jnp.sum(item, 0, keepdims=True)
    lows = (low[:, :half], low[:, half:])
    contexts = chosen_side(core, context_mine_ref[...], context_other_ref[...])
    outs = chosen_side(core, out_mine_ref[...], out_other_ref[...])
    context_grads = [
        (right_product(lows[0], outs[0][span]) + right_product(lows[1], outs[1][span])).astype(BF)
        for span in (slice(0, half), slice(half, None))
    ]
    context_grad_mine_ref[...], context_grad_other_ref[...] = chosen_side(core, *context_grads)
    for index, item in enumerate(chosen_side(core, *lows)):
        for side, context in enumerate(contexts):
            total_ref[index, side * half : (side + 1) * half, :] += left_product(context, item)

    @pl.when(step == pl.num_programs(0) - 1)
    def _():
        out_grad_mine_ref[...] = total_ref[0]
        out_grad_other_ref[...] = total_ref[1].astype(BF)


def middle_back(place, grads, ups, middle, cotangent, mask, rows, contexts, weights, block=512):
    count, width = middle.shape
    half = width // 2
    hidden_half = ups[0].shape[1]
    small = place.shape[0] - 2
    block = math.gcd(block, count)

    def over_rows(columns):
        return pl.BlockSpec((block, columns), lambda step: (step, 0))

    def whole(*shape):
        return pl.BlockSpec(shape, lambda step: (0,) * len(shape))

    out_spec = pl.BlockSpec((width, half), lambda step: (0, 3))
    return pl.pallas_call(
        functools.partial(middle_back_kernel, small),
        grid=(count // block,),
        in_specs=[
            pl.BlockSpec(memory_space=pltpu.SMEM),
            over_rows(hidden_half),
            over_rows(hidden_half),
            whole(width, hidden_half),
            whole(width, hidden_half),
            over_rows(width),
            over_rows(width),
            over_rows(1),
            whole(*rows.shape),
            over_rows(half),
            over_rows(half),
            out_spec,
            out_spec,
        ],
        out_specs=[
            over_rows(width),
            over_rows(half),
            over_rows(half),
            whole(width, half),
            whole(width, half),
            whole(8, width),
        ],
        out_shape=[
            jax.ShapeDtypeStruct((count, width), F32),
            jax.ShapeDtypeStruct((count, half), BF),
            jax.ShapeDtypeStruct((count, half), BF),
            jax.ShapeDtypeStruct((width, half), F32),
            jax.ShapeDtypeStruct((width, half), BF),
            jax.ShapeDtypeStruct((8, width), F32),
        ],
        scratch_shapes=[pltpu.VMEM((block, width), F32), pltpu.VMEM((2, width, half), F32)],
        compiler_params=pltpu.CompilerParams(vmem_limit_bytes=2 * VMEM_BYTES),
        cost_estimate=pl.CostEstimate(
            flops=4 * count * width * (hidden_half + width),
            bytes_accessed=4 * count * hidden_half + 4 * width * hidden_half + 16 * count * width,
            transcendentals=0,
        ),
        name="middle_back",
    )(place, *grads, *ups, middle, cotangent, mask, rows, *contexts, *weights)


def start_back_kernel(
    small, length, swap, place_ref, grads_mine_ref, grads_other_ref, weight_mine_ref, weight_other_ref, start_ref, middle_ref,
    mask_ref, rows_ref, sums_ref, sums_mine_ref, sums_other_ref, bias_ref,
    tokens_ref, mine_ref, other_ref, lines_ref,
):
    core, place = place_ref[0], place_ref[1]
    step = pl.program_id(0)
    width = start_ref.shape[1]
    half = width // 2
    seqs = start_ref.shape[0] // length

    @pl.when(step == 0)
    def _():
        lines_ref[...] = jnp.zeros_like(lines_ref)
        for index, row in ((0, 0), (1, 2)):
            pair = (sums_mine_ref[row : row + 1, :], sums_other_ref[row : row + 1, :])
            lines_ref[index : index + 1, :half], lines_ref[index : index + 1, half:] = chosen_side(core, *pair)
        lines_ref[2:4, :] = sums_ref[0:2, :]
        lines_ref[6:8, :] = sums_ref[2:4, :]

    grad = 0.0
    for grads, weight in ((grads_mine_ref, weight_mine_ref), (grads_other_ref, weight_other_ref)):
        for index in range(3):
            grad = grad + right_product(grads[index], weight[:, index * half : (index + 1) * half])
    back, shares = norm_back(start_ref[...], rows_ref[small + 4 : small + 5, :], grad)
    back = middle_ref[...] + back
    mask = mask_ref[...]
    tokens_ref[...] = jnp.where(mask > 0.0, 0.0, back)
    for index, item in ((4, shares), (5, grad), (8, back * mask)):
        lines_ref[index : index + 1, :] += jnp.sum(item, 0, keepdims=True)
    for index in range(seqs):
        line = LANES + place * small + step * seqs + index
        lines_ref[pl.ds(line, 1), :] = jnp.sum(back[index * length : (index + 1) * length], 0, keepdims=True)

    @pl.when(step == pl.num_programs(0) - 1)
    def _():
        blocks = (lines_ref[:LANES, :].T + bias_ref[...], lines_ref[LANES:, :].T)
        if swap:
            blocks = chosen_side(core, *blocks)
        mine_ref[...] = blocks[0]
        other_ref[...] = blocks[1].astype(other_ref.dtype)


def start_back(
    place, grads, weights, start, middle, mask, rows, sums, side_sums, bias, seqs, length, swap, block=256
):
    count, width = start.shape
    half = width // 2
    small = place.shape[0] - 2
    block = math.gcd(block, count)
    lines = LANES + -(-seqs // LANES) * LANES

    def over_rows(columns):
        return pl.BlockSpec((block, columns), lambda step: (step, 0))

    def whole(*shape):
        return pl.BlockSpec(shape, lambda step: (0,) * len(shape))

    grads_spec = pl.BlockSpec((3, block, half), lambda step: (0, step, 0))
    return pl.pallas_call(
        functools.partial(start_back_kernel, small, length, swap),
        grid=(count // block,),
        in_specs=[
            pl.BlockSpec(memory_space=pltpu.SMEM),
            grads_spec,
            grads_spec,
            whole(width, 3 * half),
            whole(width, 3 * half),
            over_rows(width),
            over_rows(width),
            over_rows(1),
            whole(*rows.shape),
            whole(*sums.shape),
            whole(*side_sums[0].shape),
            whole(*side_sums[1].shape),
            whole(width, LANES),
        ],
        out_specs=[over_rows(width), whole(width, LANES), whole(width, lines - LANES)],
        out_shape=[
            jax.ShapeDtypeStruct((count, width), F32),
            jax.ShapeDtypeStruct((width, LANES), F32),
            jax.ShapeDtypeStruct((width, lines - LANES), BF if swap else F32),
        ],
        scratch_shapes=[pltpu.VMEM((lines, width), F32)],
        compiler_params=pltpu.CompilerParams(vmem_limit_bytes=VMEM_BYTES),
        cost_estimate=pl.CostEstimate(
            flops=0, bytes_accessed=1024, transcendentals=0
        ),
        name="start_back",
    )(place, *grads, *weights, start, middle, mask, rows, sums, *side_sums, bias)


def shards_kernel(fixed, seq_cols, core_ref, steps_ref, qkv_ref, out_ref, table_ref, *refs):
    small_refs, (mine_ref, other_ref, full_ref) = refs[: fixed + 1], refs[fixed + 1 :]
    core = core_ref[0]
    part, table_cols = table_ref.shape
    half = out_ref.shape[1] // 2
    seq_count = steps_ref.shape[0]
    lines = [ref[...] for ref in small_refs[:fixed]]
    up = small_refs[fixed][...]
    lines += [up[:, i : i + part] for i in range(0, up.shape[1], part)]
    lane = lax.broadcasted_iota(jnp.int32, (1, part), 1)
    for row in range(seq_cols):
        line = jnp.zeros((1, part), jnp.int32)
        for index in range(seq_count):
            step = steps_ref[index]
            line = jnp.where(lane + row * part == index, step // 256, line)
            line = jnp.where(lane + row * part == seq_count + index, step % 256, line)
        lines.append(line.astype(F32))
    lines = jnp.concatenate(lines, 0).astype(BF)
    square = (part, part)
    unit = lax.broadcasted_iota(jnp.int32, square, 0) == lax.broadcasted_iota(jnp.int32, square, 1)
    full_ref[...] = jnp.zeros_like(full_ref)
    full_ref[:, :table_cols] = table_ref[...]
    full_ref[:, table_cols : table_cols + lines.shape[0]] = right_product(jnp.where(unit, 1.0, 0.0).astype(BF), lines)
    table_half = full_ref.shape[1] // 2

    def halves(ref, top, wide):
        return chosen_side(core, ref[:, top : top + wide], ref[:, top + wide : top + 2 * wide])

    sources = [(qkv_ref, 2 * half * i, half) for i in range(3)] + [(out_ref, 0, half), (full_ref, 0, table_half)]
    left = 0
    for ref, top, wide in sources:
        mine, other = halves(ref, top, wide)
        mine_ref[:, left : left + wide] = mine.astype(BF)
        other_ref[:, left : left + wide] = other.astype(BF)
        left += wide


def attention_shards(core, timesteps, w_qkv, w_out, table, small, b_up, seq_cols, all_cols):
    part = table.shape[0]
    shape = jax.ShapeDtypeStruct((part, 2 * w_out.shape[1] + all_cols // 2), BF)
    vmem = pl.BlockSpec(memory_space=pltpu.VMEM)
    return pl.pallas_call(
        functools.partial(shards_kernel, len(small), seq_cols),
        in_specs=[pl.BlockSpec(memory_space=pltpu.SMEM)] * 2 + [vmem] * (4 + len(small)),
        out_specs=[vmem, vmem],
        out_shape=[shape, shape],
        scratch_shapes=[pltpu.VMEM((part, all_cols), F32)],
        compiler_params=pltpu.CompilerParams(vmem_limit_bytes=60 << 20),
        cost_estimate=pl.CostEstimate(flops=0, bytes_accessed=24 * part * w_out.shape[1], transcendentals=0),
        name="attention_shards",
    )(core, timesteps, w_qkv, w_out, table, *[item.reshape(1, -1) for item in small], b_up.reshape(1, -1))


def route_kernel(rows, route_ref, *refs):
    terms, (sent_ref, kept_ref) = refs[:-2], refs[-2:]
    for index in range(2):
        for out, place in ((sent_ref, route_ref[index]), (kept_ref, route_ref[2 + index])):
            span = pl.ds(pl.multiple_of(place * rows, 8), rows)
            left = 0
            for mine, got in zip(terms[::2], terms[1::2]):
                many = [(slice(None),)] if len(mine.shape) == 2 else [(i, slice(None)) for i in range(mine.shape[0])]
                for at in many:
                    where = (*at[:-1], span)
                    total = mine[where].astype(F32) + got[where].astype(F32)
                    out[0, index, :, left : left + total.shape[1]] = total.astype(out.dtype)
                    left += total.shape[1]


def routed(terms, rows, route):
    specs, columns, bytes_read = [], 0, 0
    for array in [item for pair in terms for item in pair]:
        shape = (4 * rows, array.shape[-1])
        if array.ndim == 2:
            specs.append(pl.BlockSpec(shape, lambda z: (z, 0)))
        else:
            specs.append(pl.BlockSpec((array.shape[0], *shape), lambda z: (0, z, 0)))
        bytes_read += array.size * array.dtype.itemsize
        columns += array.size // (16 * rows)
    columns //= 2
    out = pl.BlockSpec((1, 2, rows, columns), lambda z: (z, 0, 0, 0))
    return pl.pallas_call(
        functools.partial(route_kernel, rows),
        grid=(4,),
        in_specs=[pl.BlockSpec(memory_space=pltpu.SMEM)] + specs,
        out_specs=[out, out],
        out_shape=[
            jax.ShapeDtypeStruct((4, 2, rows, columns), BF),
            pltpu.HBM((4, 2, rows, columns), F32),
        ],
        compiler_params=pltpu.CompilerParams(vmem_limit_bytes=VMEM_BYTES),
        cost_estimate=pl.CostEstimate(
            flops=0, bytes_accessed=bytes_read + 48 * rows * columns, transcendentals=0
        ),
        name="routed",
    )(route, *[item for pair in terms for item in pair])


class Tree:
    def __init__(self):
        fsdp, rep = lax.axis_index("fsdp"), lax.axis_index("rep")
        self.z, self.core = fsdp // 2, rep % 2
        x, y = rep // 2, fsdp % 2
        self.near = jnp.where(self.core == 0, x, y)
        self.far = jnp.where(self.core == 0, y, x)
        places = [jnp.where(self.core == 0, 2 * i + near, 2 * near + i) for near in (1 - self.near, self.near) for i in (0, 1)]
        self.route = jnp.stack(places)

    def to_core(self, value):
        return lax.ppermute(value, "rep", [(i, i ^ 1) for i in range(4)])

    def to_near(self, value):
        return lax.ppermute(value, AXES, [(i, i ^ (4 if i % 2 else 2)) for i in range(32)])

    def to_far(self, value):
        return lax.ppermute(value, AXES, [(i, i ^ (2 if i % 2 else 4)) for i in range(32)])

    def to_z(self, value, step):
        return lax.ppermute(value, "fsdp", [(i, i ^ (2 * step)) for i in range(8)])


class Gather:
    def __init__(self, tree, own):
        self.tree, self.own = tree, own

    @staticmethod
    def columns(tree, mine, other):
        got = tree.to_core(other)
        return Gather(tree, paired(tree.core, mine, got, 0).reshape(-1, mine.shape[1]))

    @staticmethod
    def rows(tree, shard):
        return Gather(tree, shard)

    def along_z(self, *wait):
        own = after(self.own, *wait)
        one, three, two = [self.tree.to_z(own, step) for step in (1, 3, 2)]
        self.held, self.got = own, [one, two, three]
        return self.got

    def one(self, *wait):
        tree = self.tree
        held = after([self.held, *self.got], *wait)
        low, high = tree.z % 2 == 1, tree.z // 2 == 1
        out = []
        for place in range(4):
            near = [jnp.where(low, held[(place ^ 1) ^ h], held[place ^ h]) for h in (0, 2)]
            out.append(jnp.where(high, near[1], near[0]))
        self.held = jnp.stack(out)
        self.got = tree.to_near(self.held)
        return self.got

    def two(self, *wait):
        tree = self.tree
        held, got = after((self.held, self.got), *wait)
        self.held = paired(tree.near, held, got, 1)
        self.got = tree.to_far(self.held)
        return self.got

    def halves(self, *wait):
        tree = self.tree
        held, got = after((self.held, self.got), *wait)
        same, first = tree.far == 0, tree.core == 0
        lower, upper = jnp.where(same, held, got), jnp.where(same, got, held)
        blocks = [
            lower[:, 0],
            jnp.where(first, lower[:, 1], upper[:, 0]),
            jnp.where(first, upper[:, 0], lower[:, 1]),
            upper[:, 1],
        ]
        half = jnp.stack(blocks, 1).reshape(-1, held.shape[-1])
        return half, tree.to_core(half)


class Reduce:
    def __init__(self, tree, rows):
        self.tree, self.rows = tree, rows
        self.terms = []

    def add(self, mine, other):
        got = self.tree.to_core(other.astype(BF))
        self.terms.append((mine, got))
        return got

    def one(self, *wait):
        self.sent, self.kept = routed(after(self.terms, *wait), self.rows, self.tree.route)
        self.got = self.tree.to_near(self.sent)

    def two(self, *wait, apart=False):
        tree = self.tree
        kept, got = after((self.kept, self.got), *wait)
        if apart:
            self.sent = (pick(kept, 1 - tree.far, 1) + pick(got, 1 - tree.far, 1)).astype(BF)
            self.kept = pick(kept, tree.far, 1) + pick(got, tree.far, 1)
            self.got = tree.to_far(self.sent)
            return
        total = kept + got
        self.kept, self.sent = pick(total, tree.far, 1), pick(total, 1 - tree.far, 1).astype(BF)
        self.got = tree.to_far(self.sent)

    def along_z(self, *others):
        tree = self.tree
        total = jnp.concatenate([item.kept + item.got for item in (self, *others)], -1)
        self.kept = pick(total, tree.z, 0)
        self.sent = tuple(pick(total, tree.z ^ step, 0).astype(BF) for step in (1, 2, 3))
        self.got = tuple(tree.to_z(sent, step) for sent, step in zip(self.sent, (1, 2, 3)))

    def sums(self, *wait):
        kept, got = after((self.kept, self.got), *wait)
        return kept + got[0] + got[1] + got[2]

    def columns(self, *wait):
        tree, total = self.tree, self.sums(*wait)
        rows = total.reshape(2, self.rows // 2, -1)
        keep = pick(rows, tree.core, 0)
        return paired(tree.core, keep, tree.to_core(pick(rows, 1 - tree.core, 0)), 1)


class Whole:
    core = 0

    def __init__(self, rows=None):
        self.mine, self.other = [], []
        self.got, self.sent = (), ()

    @staticmethod
    def columns_of(mine, other):
        out = Whole()
        whole = lax.all_gather(jnp.stack([mine, other], 1), AXES, axis=0, tiled=True)
        out.half, out.rest = whole[:, 0], whole[:, 1]
        return out

    @staticmethod
    def rows_of(shard):
        out = Whole()
        whole = lax.all_gather(shard, AXES, axis=0)
        whole = whole.reshape(-1, 2, *shard.shape)
        out.half, out.rest = [whole[:, i].reshape(-1, shard.shape[1]) for i in range(2)]
        return out

    def along_z(self, *wait):
        return []

    def one(self, *wait):
        return ()

    def two(self, *wait):
        return ()

    def halves(self, *wait):
        return self.half, self.rest

    def add(self, mine, other):
        self.mine.append(mine.astype(BF))
        self.other.append(other.astype(BF))
        return mine

    def columns(self, *wait):
        def flat(items):
            return jnp.concatenate([part for item in items for part in (item if item.ndim == 3 else [item])], 1)

        parts = [flat(item) for item in (self.mine, self.other)]
        return lax.psum_scatter(jnp.stack(parts, 1), AXES, scatter_dimension=0, tiled=True).astype(F32)

    def sums(self, *wait):
        count = lax.axis_size(AXES)
        mine, other = [item[0].reshape(count // 2, -1, item[0].shape[1]) for item in (self.mine, self.other)]
        sums = jnp.stack([mine, other], 1).reshape(-1, mine.shape[-1])
        return lax.psum_scatter(sums, AXES, scatter_dimension=0, tiled=True).astype(F32)


def body(
    fast,
    tokens,
    mask_bits,
    timesteps,
    cotangent,
    w_qkv,
    w_out,
    w_up,
    w_down,
    time_table,
    b_query,
    b_value,
    b_out,
    b_up,
    b_down,
    gain_attn,
    shift_attn,
    gain_mlp,
    shift_mlp,
    mask_vector,
):
    tree = Tree() if fast else Whole()
    gather_columns = functools.partial(Gather.columns, tree) if fast else Whole.columns_of
    gather_rows = functools.partial(Gather.rows, tree) if fast else Whole.rows_of
    reduction = functools.partial(Reduce, tree) if fast else Whole
    core = tree.core
    count = lax.axis_size(AXES)
    chips = count // 2
    place = lax.axis_index(AXES)
    width = tokens.shape[1]
    part = width // count
    hidden_width = w_up.shape[1]
    hidden_part = hidden_width // count
    seq_count = timesteps.shape[0]
    seq_length = tokens.shape[0] // seq_count
    half = width // 2
    table_cols = time_table.shape[1]
    absorbed = mask_bits.astype(F32)[:, None]

    small = [b_query, b_value, b_out, b_down, gain_attn, shift_attn, gain_mlp, shift_mlp, mask_vector]
    fixed = len(small)
    up_cols = hidden_part // part
    seq_cols = -(-2 * seq_count // part)
    small_cols = fixed + up_cols + seq_cols
    all_cols = -(-(table_cols + small_cols) // (2 * LANES)) * (2 * LANES)
    place = jnp.concatenate([jnp.stack([jnp.int32(core), place]), timesteps])

    shards = attention_shards(
        jnp.full((1,), core, jnp.int32), timesteps, w_qkv, w_out, time_table, small, b_up, seq_cols, all_cols
    )
    attn_w = gather_columns(*shards)
    up_shard = w_up.astype(BF).reshape(part, chips, 2, hidden_part).transpose(2, 0, 1, 3)
    up_shard = up_shard.reshape(2, part, hidden_width // 2)
    up_w = gather_columns(*[pick(up_shard, side, 0) for side in (core, 1 - core)])
    down_w = gather_rows(w_down.astype(BF))
    attn_w.along_z()
    up_z = up_w.along_z()
    attn_one = attn_w.one()
    attn_two = attn_w.two(up_z[::2])
    up_one = up_w.one(attn_two)
    attn_w = attn_w.halves(up_z)
    down_z = down_w.along_z(attn_two)

    rows, start, normed_one, across_one, bias_mine, bias_other, bias_up = start_rows(
        place, tokens, absorbed, attn_w, fixed, up_cols, table_cols, small_cols, chips, hidden_part
    )
    up_two = up_w.two(normed_one)
    qkv_mine, context_mine = attention(after(normed_one, up_one), attn_w[0], bias_mine, seq_length)
    down_one = down_w.one(up_two, context_mine)
    up_w = up_w.halves(context_mine)
    qkv_other, context_other = attention(after(normed_one, up_two), attn_w[1], bias_other, seq_length)
    down_two = down_w.two()
    contexts = (context_mine, context_other)
    middle, normed_two, across_two = middle_rows(place, contexts, attn_w, after(start, down_one), rows)
    hidden, slope = [None, None], [None, None]
    hidden[0], slope[0] = feed(normed_two, up_w[0], bias_up, 0)
    down_w = down_w.halves(hidden[0])
    hidden[1], slope[1] = feed(after(normed_two, down_two), up_w[1], bias_up, 1)

    grad_branch = (cotangent * absorbed).astype(BF)
    down_sum = reduction(hidden_part)
    down_sum.add(left_product(hidden[0], grad_branch), left_product(hidden[1], grad_branch))
    up_sum = reduction(2 * part)
    grad_pre, grad_b_up, grad_up = [None, None], [None, None], [None, None]
    if fast:
        down_sum.one()
    grad_pre[1], grad_b_up[1], grad_up[1] = feed_back(
        grad_branch, down_w[1], slope[1], across_two, BF
    )
    grad_pre[0], grad_b_up[0], grad_up[0] = feed_back(grad_branch, down_w[0], slope[0], across_two, F32)
    up_sum.add(grad_up[0], grad_up[1])
    if fast:
        down_sum.two(grad_pre[1])
    grad_pre = after(grad_pre, down_sum.sent)
    grad_middle, *grad_context, grad_out_mine, grad_out_other, middle_sums = middle_back(
        place, grad_pre, up_w, middle, cotangent, absorbed, rows, contexts, attn_w
    )

    attn_sum = reduction(2 * part)
    up_sum.add(grad_out_mine, grad_out_other)
    if fast:
        up_sum.one(down_sum.got)
        down_sum.along_z()
    grads = [None, None]
    grads[1] = attention_back(
        qkv_other, after(grad_context[1], down_sum.sent, up_sum.sent), across_one, seq_length, BF
    )
    if fast:
        up_sum.two(down_sum.got, grads[1])
    grads[0] = attention_back(qkv_mine, after(grad_context[0], up_sum.sent), across_one, seq_length, F32)
    grad_qkv, grad_weights, sums = zip(*grads)
    attn_sum.add(grad_weights[0], grad_weights[1])
    if fast:
        attn_sum.one()
        up_sum.along_z()
    grad_qkv = after(grad_qkv, up_sum.sent, attn_sum.sent)
    grad_b_up = paired(core, *[item.reshape(chips, hidden_part) for item in grad_b_up], 1).reshape(count, hidden_part)
    grad_b_up = jnp.pad(grad_b_up[:, None], ((0, 0), (0, part - 1), (LANES - hidden_part, 0)))
    seqs = count * seq_count
    grad_tokens, *blocks = start_back(
        place, grad_qkv, attn_w, start, grad_middle, absorbed, rows, middle_sums, sums,
        grad_b_up.reshape(width, LANES), seqs, seq_length, fast,
    )
    if fast:
        attn_sum.two()
        extra_sum = reduction(2 * part)
        extra_sum.add(*blocks)
        extra_sum.one()
        extra_sum.two(attn_sum.sent, up_sum.got)
        attn_sum.along_z(extra_sum)
        hidden, rows = after((hidden, rows), attn_sum.sent)
    output = middle + (product(hidden[0], down_w[0]) + product(hidden[1], down_w[1]) + rows[seq_count + 3])
    if fast:
        attn_grad = attn_sum.columns(output)
        small, seq_sums = attn_grad[:, 0, 3 * half :], attn_grad[:, 1, 3 * half :]
    else:
        attn_grad = attn_sum.columns()
        small, seq_sums = [
            lax.psum_scatter(item.astype(BF), AXES, scatter_dimension=0, tiled=True).astype(F32) for item in blocks
        ]
    steps = rows[seq_count + fixed + up_cols : seq_count + small_cols]
    steps = steps.reshape(seq_cols, count, part).transpose(1, 0, 2).reshape(count, -1).astype(jnp.int32)
    steps = (steps[:, :seq_count] * 256 + steps[:, seq_count : 2 * seq_count]).reshape(-1)
    grad_b_up = small[0, LANES - hidden_part :]
    small = small[:, :fixed].T
    onehot = (steps[:, None] == lax.broadcasted_iota(jnp.int32, (seqs, table_cols), 1)).astype(F32)
    grad_time_table = jnp.dot(seq_sums, onehot, precision=lax.Precision.HIGHEST)
    grad_w_qkv = attn_grad[:, :, : 3 * half].reshape(part, 2, 3, half).transpose(0, 2, 1, 3).reshape(part, 3 * width)
    up_grad = up_sum.columns(extra_sum.sent if fast else ())
    grad_w_out = up_grad[:, :, hidden_width // 2 :].reshape(part, width)
    grad_w_up = up_grad[:, :, : hidden_width // 2].reshape(part, 2, chips, hidden_part).transpose(0, 2, 1, 3)
    grad_w_up = grad_w_up.reshape(part, hidden_width)
    return (
        output,
        grad_tokens,
        grad_w_qkv,
        grad_w_out,
        grad_w_up,
        down_sum.sums(extra_sum.sent if fast else ()),
        grad_time_table,
        small[0],
        small[1],
        small[2],
        grad_b_up,
        small[3],
        small[4],
        small[5],
        small[6],
        small[7],
        small[8],
    )


def solution(mesh):
    matrix, vector = P(AXES, None), P(AXES)
    fast = dict(mesh.shape) == {"fsdp": 8, "rep": 4}
    return jax.shard_map(
        functools.partial(body, fast),
        mesh=mesh,
        in_specs=(matrix, vector, vector) + (matrix,) * 6 + (vector,) * 10,
        out_specs=(matrix,) * 7 + (vector,) * 10,
        check_vma=False,
    )
```

```python
import functools
import math

import jax
import jax.numpy as jnp
from jax import lax
from jax.experimental import pallas as pl
from jax.experimental.pallas import tpu as pltpu
from jax.sharding import PartitionSpec as P

HDIM = 64
EPSILON = 1e-05
AXES = ("fsdp", "rep")
BF = jnp.bfloat16
F32 = jnp.float32
LANES = 128
VMEM_BYTES = 18 << 20
GELU_OUTER = math.sqrt(2.0 / math.pi)
GELU_INNER = 0.044715


def contract(left, right, left_dim, right_dim):
    dims = (((left_dim,), (right_dim,)), ((), ()))
    return lax.dot_general(left, right, dims, preferred_element_type=F32)


def product(left, right):
    return contract(left, right, 1, 0)


def left_product(left, right):
    return contract(left, right, 0, 0)


def right_product(left, right):
    return contract(left, right, 1, 1)


def pick(array, index, axis):
    return lax.dynamic_index_in_dim(array, index, axis, keepdims=False)


def paired(bit, mine, other, axis):
    return jnp.stack([jnp.where(bit == 0, mine, other), jnp.where(bit == 0, other, mine)], axis)


def in_hbm(value):
    return pltpu.with_memory_space_constraint(value, pltpu.HBM)


def after(value, *others):
    return lax.optimization_barrier((value, others))[0]


def lane_masks(factor):
    lane = lax.broadcasted_iota(jnp.int32, (1, LANES), 1)
    return [jnp.where((lane < HDIM) == (head == 0), factor, 0.0).astype(BF) for head in (0, 1)]


def stacked(values, masks):
    return jnp.concatenate([values * masks[0], values * masks[1]], 0)


def unstacked(values):
    rows = values.shape[0] // 2
    lane = lax.broadcasted_iota(jnp.int32, (1, LANES), 1)
    return jnp.where(lane < HDIM, values[:rows], values[rows:])


def softmax_down(scores):
    powers = jnp.exp(scores - jnp.max(scores, 0, keepdims=True))
    return powers * (1.0 / jnp.sum(powers, 0, keepdims=True))


def attention_kernel(length, scale, rows_ref, query_ref, key_ref, value_ref, bias_ref, qkv_ref, context_ref):
    weight = jnp.concatenate([query_ref[...], key_ref[...], value_ref[...]], 1)
    projected = product(rows_ref[...], weight)
    for index in range(3):
        part = projected[:, index * LANES : (index + 1) * LANES]
        qkv_ref[index] = (part + bias_ref[index : index + 1, :]).astype(BF)
    scaled = lane_masks(scale)

    for sequence in range(rows_ref.shape[0] // length):
        span = slice(sequence * length, (sequence + 1) * length)
        queries, key_rows, value_rows = [qkv_ref[index, span, :] for index in range(3)]
        probs = softmax_down(right_product(key_rows, stacked(queries, scaled))).astype(BF)
        context_ref[span, :] = unstacked(left_product(probs, value_rows)).astype(BF)


def attention(rows, weight, bias, length):
    tokens, width = rows.shape
    half = bias.shape[1]
    pairs = half // LANES

    def weight_spec(index):
        return pl.BlockSpec((width, LANES), lambda pair: (0, index * pairs + pair))

    return pl.pallas_call(
        functools.partial(attention_kernel, length, 1.0 / math.sqrt(HDIM)),
        grid=(pairs,),
        in_specs=[
            pl.BlockSpec((tokens, width), lambda pair: (0, 0)),
            weight_spec(0),
            weight_spec(1),
            weight_spec(2),
            pl.BlockSpec((8, LANES), lambda pair: (0, pair)),
        ],
        out_specs=[
            pl.BlockSpec((3, tokens, LANES), lambda pair: (0, 0, pair)),
            pl.BlockSpec((tokens, LANES), lambda pair: (0, pair)),
        ],
        out_shape=[
            pltpu.HBM((3, tokens, half), BF),
            jax.ShapeDtypeStruct((tokens, half), BF),
        ],
        compiler_params=pltpu.CompilerParams(vmem_limit_bytes=VMEM_BYTES),
        cost_estimate=pl.CostEstimate(
            flops=6 * tokens * width * half,
            bytes_accessed=2 * tokens * width + 6 * width * half + 8 * tokens * half,
            transcendentals=2 * tokens * length * pairs,
        ),
        name="attention",
    )(rows, weight, weight, weight, bias)


def attention_back_kernel(length, scale, qkv_ref, grad_ref, rows_ref, grads_ref, weight_ref, sums_ref):
    ones, scaled = lane_masks(1.0), lane_masks(scale)

    for sequence in range(grad_ref.shape[0] // length):
        span = slice(sequence * length, (sequence + 1) * length)
        queries, key_rows, value_rows = [qkv_ref[index, span, :] for index in range(3)]
        queries, grad = stacked(queries, scaled), stacked(grad_ref[span, :], ones)
        probs = softmax_down(right_product(key_rows, queries))
        grad_probs = right_product(value_rows, grad)
        grad_scores = probs * (grad_probs - jnp.sum(grad_probs * probs, 0, keepdims=True))
        grad_scores = grad_scores.astype(BF)
        grad_queries = unstacked(left_product(grad_scores, key_rows)) * scale
        grads_ref[0, span, :] = grad_queries.astype(BF)
        grads_ref[1, span, :] = product(grad_scores, queries).astype(BF)
        grads_ref[2, span, :] = product(probs.astype(BF), grad).astype(BF)

    grads = jnp.concatenate([grads_ref[index] for index in range(3)], 1)
    weight = product(rows_ref[...], grads)
    for index in range(3):
        weight_ref[index] = weight[:, index * LANES : (index + 1) * LANES].astype(weight_ref.dtype)
        sums_ref[index : index + 1, :] = jnp.sum(grads_ref[index].astype(F32), 0, keepdims=True)


def attention_back(qkv, grad, rows_across, length, dtype):
    _, tokens, half = qkv.shape
    width = rows_across.shape[0]
    pairs = half // LANES
    return pl.pallas_call(
        functools.partial(attention_back_kernel, length, 1.0 / math.sqrt(HDIM)),
        grid=(pairs,),
        in_specs=[
            pl.BlockSpec((3, tokens, LANES), lambda pair: (0, 0, pair)),
            pl.BlockSpec((tokens, LANES), lambda pair: (0, pair)),
            pl.BlockSpec((width, tokens), lambda pair: (0, 0)),
        ],
        out_specs=[
            pl.BlockSpec((3, tokens, LANES), lambda pair: (0, 0, pair)),
            pl.BlockSpec((3, width, LANES), lambda pair: (0, 0, pair)),
            pl.BlockSpec((3, LANES), lambda pair: (0, pair)),
        ],
        out_shape=[
            pltpu.HBM((3, tokens, half), BF),
            jax.ShapeDtypeStruct((3, width, half), dtype),
            jax.ShapeDtypeStruct((3, half), F32),
        ],
        compiler_params=pltpu.CompilerParams(vmem_limit_bytes=VMEM_BYTES),
        cost_estimate=pl.CostEstimate(
            flops=6 * tokens * width * half,
            bytes_accessed=2 * tokens * width + 12 * width * half + 14 * tokens * half,
            transcendentals=2 * tokens * length * pairs,
        ),
        name="attention_back",
    )(in_hbm(qkv), in_hbm(grad), in_hbm(rows_across))


def feed_kernel(side, rows_ref, weight_ref, bias_ref, hidden_ref, slope_ref, pre_ref):
    pre_ref[...] = product(rows_ref[...], weight_ref[...])
    step = 32

    def chunk(index, carry):
        span = pl.ds(pl.multiple_of(index * step, step), step)
        pre = pre_ref[span, :] + bias_ref[side : side + 1, :]
        square = pre * pre
        bend = jnp.tanh(GELU_OUTER * (pre + GELU_INNER * (square * pre)))
        share = 0.5 * (1.0 + bend)
        hidden_ref[span, :] = (pre * share).astype(BF)
        inner = (0.5 * GELU_OUTER) * pre * (1.0 + (3.0 * GELU_INNER) * square)
        slope_ref[span, :] = share + inner * (1.0 - bend * bend)
        return carry

    lax.fori_loop(0, rows_ref.shape[0] // step, chunk, 0, unroll=2)


def feed(rows, weight, bias, side, block=512):
    tokens, width = rows.shape
    columns = weight.shape[1]
    block = math.gcd(block, columns)
    out = pl.BlockSpec((tokens, block), lambda step: (0, step))
    return pl.pallas_call(
        functools.partial(feed_kernel, side),
        grid=(columns // block,),
        in_specs=[
            pl.BlockSpec((tokens, width), lambda step: (0, 0)),
            pl.BlockSpec((width, block), lambda step: (0, step)),
            pl.BlockSpec((8, block), lambda step: (0, step)),
        ],
        out_specs=[out, out],
        out_shape=[
            pltpu.HBM((tokens, columns), BF),
            pltpu.HBM((tokens, columns), F32),
        ],
        scratch_shapes=[pltpu.VMEM((tokens, block), F32)],
        compiler_params=pltpu.CompilerParams(vmem_limit_bytes=VMEM_BYTES),
        cost_estimate=pl.CostEstimate(
            flops=2 * tokens * width * columns,
            bytes_accessed=2 * tokens * width + 2 * width * columns + 6 * tokens * columns,
            transcendentals=tokens * columns,
        ),
        name="feed",
    )(rows, weight, bias)


def feed_back_kernel(grad_ref, weight_ref, slope_ref, rows_ref, pre_ref, sum_ref, up_ref):
    grad = (right_product(grad_ref[...], weight_ref[...]) * slope_ref[...]).astype(BF)
    pre_ref[...] = grad
    sum_ref[...] = jnp.sum(grad.astype(F32), 0, keepdims=True)
    up_ref[...] = product(rows_ref[...], grad).astype(up_ref.dtype)


def feed_back(grad, weight, slope, rows_across, dtype, block=768):
    tokens, width = grad.shape
    columns = weight.shape[0]
    block = math.gcd(block, columns)
    out = pl.BlockSpec((tokens, block), lambda step: (0, step))
    return pl.pallas_call(
        feed_back_kernel,
        grid=(columns // block,),
        in_specs=[
            pl.BlockSpec((tokens, width), lambda step: (0, 0)),
            pl.BlockSpec((block, width), lambda step: (step, 0)),
            out,
            pl.BlockSpec((width, tokens), lambda step: (0, 0)),
        ],
        out_specs=[
            out,
            pl.BlockSpec((1, block), lambda step: (0, step)),
            pl.BlockSpec((width, block), lambda step: (0, step)),
        ],
        out_shape=[
            pltpu.HBM((tokens, columns), BF),
            jax.ShapeDtypeStruct((1, columns), F32),
            jax.ShapeDtypeStruct((width, columns), dtype),
        ],
        compiler_params=pltpu.CompilerParams(vmem_limit_bytes=VMEM_BYTES),
        cost_estimate=pl.CostEstimate(
            flops=4 * tokens * width * columns,
            bytes_accessed=4 * tokens * width + 6 * width * columns + 6 * tokens * columns,
            transcendentals=0,
        ),
        name="feed_back",
    )(in_hbm(grad), in_hbm(weight), in_hbm(slope), in_hbm(rows_across))


def chosen_side(core, mine, other):
    return jnp.where(core == 0, mine, other), jnp.where(core == 0, other, mine)


def normalized(values):
    center = values - jnp.mean(values, -1, keepdims=True)
    rate = lax.rsqrt(jnp.mean(center * center, -1, keepdims=True) + EPSILON)
    return center * rate, rate


def start_kernel(
    fixed, up_cols, table_cols, seq_count, parts,
    place_ref, tokens_ref, mask_ref, table_mine_ref, table_other_ref,
    rows_ref, start_ref, normed_ref, across_ref, bias_mine_ref, bias_other_ref, bias_up_ref,
):
    core = place_ref[0]
    step = pl.program_id(0)
    width = tokens_ref.shape[1]
    half = width // 2
    chips, part, hidden_part = parts

    @pl.when(step == 0)
    def _():
        count, columns = rows_ref.shape[0], table_mine_ref.shape[1]
        row = lax.broadcasted_iota(jnp.int32, (count, columns), 0)
        wanted = table_cols + row - seq_count
        for index in range(seq_count):
            wanted = jnp.where(row == index, place_ref[2 + index], wanted)
        column = lax.broadcasted_iota(jnp.int32, (count, columns), 1)
        rows = 0.0
        for side, table in ((core, table_mine_ref), (1 - core, table_other_ref)):
            hit = jnp.where(wanted == column + side * columns, 1.0, 0.0).astype(BF)
            rows = rows + right_product(hit, table[...])
        rows_ref[...] = rows
        for ref, side in ((bias_mine_ref, core), (bias_other_ref, 1 - core)):
            ref[...] = jnp.zeros_like(ref)
            for index in (0, 1):
                line = rows_ref[seq_count + index : seq_count + index + 1, :]
                ref[2 * index : 2 * index + 1, :] = jnp.where(side == 0, line[:, :half], line[:, half:])
        for chip in range(chips):
            for index in range(up_cols):
                line = rows_ref[seq_count + fixed + index : seq_count + fixed + index + 1, :]
                pair = [line[:, (2 * chip + i) * part : (2 * chip + i + 1) * part] for i in range(2)]
                where = slice(chip * hidden_part + index * part, chip * hidden_part + (index + 1) * part)
                bias_up_ref[0:1, where], bias_up_ref[1:2, where] = chosen_side(core, *pair)

    small = seq_count
    mask = mask_ref[...]
    start = jnp.where(mask > 0.0, rows_ref[small + 8 : small + 9, :], tokens_ref[...])
    start = start + rows_ref[pl.ds(step, 1), :]
    start_ref[...] = start
    normed, _ = normalized(start)
    normed = normed * rows_ref[small + 4 : small + 5, :] + rows_ref[small + 5 : small + 6, :]
    normed_ref[...] = normed.astype(BF)
    across_ref[...] = normed.T.astype(BF)


def start_rows(place, tokens, mask, weights, fixed, up_cols, table_cols, small_cols, chips, hidden_part):
    count, width = tokens.shape
    seq_count = place.shape[0] - 2
    length = count // seq_count
    half = width // 2
    row_count = -(-(seq_count + small_cols) // 8) * 8
    table_half = weights[0].shape[1] - 4 * half
    tables = 4 * half // table_half
    table_spec = pl.BlockSpec((width, table_half), lambda step: (0, tables))
    rows_spec = pl.BlockSpec((length, width), lambda step: (step, 0))

    def fixed_spec(*shape):
        return pl.BlockSpec(shape, lambda step: (0,) * len(shape))

    return pl.pallas_call(
        functools.partial(
            start_kernel, fixed, up_cols, table_cols, seq_count, (chips, width // (2 * chips), hidden_part)
        ),
        grid=(seq_count,),
        in_specs=[
            pl.BlockSpec(memory_space=pltpu.SMEM),
            rows_spec,
            pl.BlockSpec((length, 1), lambda step: (step, 0)),
            table_spec,
            table_spec,
        ],
        out_specs=[
            fixed_spec(row_count, width),
            rows_spec,
            rows_spec,
            pl.BlockSpec((width, length), lambda step: (0, step)),
            fixed_spec(8, half),
            fixed_spec(8, half),
            fixed_spec(8, chips * hidden_part),
        ],
        out_shape=[
            jax.ShapeDtypeStruct((row_count, width), F32),
            pltpu.HBM((count, width), F32),
            jax.ShapeDtypeStruct((count, width), BF),
            pltpu.HBM((width, count), BF),
            jax.ShapeDtypeStruct((8, half), F32),
            jax.ShapeDtypeStruct((8, half), F32),
            jax.ShapeDtypeStruct((8, chips * hidden_part), F32),
        ],
        compiler_params=pltpu.CompilerParams(vmem_limit_bytes=VMEM_BYTES),
        cost_estimate=pl.CostEstimate(
            flops=4 * row_count * width * table_half, bytes_accessed=14 * count * width, transcendentals=0
        ),
        name="start_rows",
    )(place, in_hbm(tokens), mask, *weights)


def middle_kernel(
    small, place_ref, context_mine_ref, context_other_ref, out_mine_ref, out_other_ref, start_ref, rows_ref,
    middle_ref, normed_ref, across_ref,
):
    core = place_ref[0]
    half = context_mine_ref.shape[1]
    contexts = chosen_side(core, context_mine_ref[...], context_other_ref[...])
    outs = chosen_side(core, out_mine_ref[...], out_other_ref[...])
    for index, out in enumerate(outs):
        span = slice(index * half, (index + 1) * half)
        total = product(contexts[0], out[:half]) + product(contexts[1], out[half:])
        middle_ref[:, span] = start_ref[:, span] + (total + rows_ref[small + 2 : small + 3, span])
    normed, _ = normalized(middle_ref[...])
    normed = normed * rows_ref[small + 6 : small + 7, :] + rows_ref[small + 7 : small + 8, :]
    normed_ref[...] = normed.astype(BF)
    across_ref[...] = normed.T.astype(BF)


def middle_rows(place, contexts, weights, start, rows, block=256):
    count, width = start.shape
    half = width // 2
    small = place.shape[0] - 2
    block = math.gcd(block, count)
    out_spec = pl.BlockSpec((width, half), lambda step: (0, 3))
    rows_spec = pl.BlockSpec((block, width), lambda step: (step, 0))
    half_spec = pl.BlockSpec((block, half), lambda step: (step, 0))
    return pl.pallas_call(
        functools.partial(middle_kernel, small),
        grid=(count // block,),
        in_specs=[
            pl.BlockSpec(memory_space=pltpu.SMEM),
            half_spec,
            half_spec,
            out_spec,
            out_spec,
            rows_spec,
            pl.BlockSpec(rows.shape, lambda step: (0, 0)),
        ],
        out_specs=[rows_spec, rows_spec, pl.BlockSpec((width, block), lambda step: (0, step))],
        out_shape=[
            pltpu.HBM((count, width), F32),
            jax.ShapeDtypeStruct((count, width), BF),
            pltpu.HBM((width, count), BF),
        ],
        compiler_params=pltpu.CompilerParams(vmem_limit_bytes=VMEM_BYTES),
        cost_estimate=pl.CostEstimate(
            flops=2 * count * width * width, bytes_accessed=14 * count * width + 2 * width * width, transcendentals=0
        ),
        name="middle_rows",
    )(place, *contexts, *weights, start, rows)


def norm_back(values, gain, grad):
    unit, rate = normalized(values)
    scaled = grad * gain
    back = scaled - jnp.mean(scaled, -1, keepdims=True) - unit * jnp.mean(scaled * unit, -1, keepdims=True)
    return rate * back, grad * unit


def middle_back_kernel(
    small, place_ref, pre_mine_ref, pre_other_ref, up_mine_ref, up_other_ref, middle_ref, cotangent_ref, mask_ref,
    rows_ref, context_mine_ref, context_other_ref, out_mine_ref, out_other_ref,
    grad_ref, context_grad_mine_ref, context_grad_other_ref, out_grad_mine_ref, out_grad_other_ref, sums_ref,
    normed_ref, total_ref,
):
    core = place_ref[0]
    step = pl.program_id(0)
    half = context_mine_ref.shape[1]

    @pl.when(step == 0)
    def _():
        sums_ref[...] = jnp.zeros_like(sums_ref)
        total_ref[...] = jnp.zeros_like(total_ref)

    normed_ref[...] = right_product(pre_mine_ref[...], up_mine_ref[...]) + right_product(
        pre_other_ref[...], up_other_ref[...]
    )
    grad = normed_ref[...]
    direct = cotangent_ref[...] * mask_ref[...]
    back, shares = norm_back(middle_ref[...], rows_ref[small + 6 : small + 7, :], grad)
    back = direct + back
    grad_ref[...] = back
    low = back.astype(BF)
    for index, item in enumerate((low.astype(F32), direct.astype(BF).astype(F32), shares, grad)):
        sums_ref[index : index + 1, :] += jnp.sum(item, 0, keepdims=True)
    lows = (low[:, :half], low[:, half:])
    contexts = chosen_side(core, context_mine_ref[...], context_other_ref[...])
    outs = chosen_side(core, out_mine_ref[...], out_other_ref[...])
    context_grads = [
        (right_product(lows[0], outs[0][span]) + right_product(lows[1], outs[1][span])).astype(BF)
        for span in (slice(0, half), slice(half, None))
    ]
    context_grad_mine_ref[...], context_grad_other_ref[...] = chosen_side(core, *context_grads)
    for index, item in enumerate(chosen_side(core, *lows)):
        for side, context in enumerate(contexts):
            total_ref[index, side * half : (side + 1) * half, :] += left_product(context, item)

    @pl.when(step == pl.num_programs(0) - 1)
    def _():
        out_grad_mine_ref[...] = total_ref[0]
        out_grad_other_ref[...] = total_ref[1].astype(BF)


def middle_back(place, grads, ups, middle, cotangent, mask, rows, contexts, weights, block=512):
    count, width = middle.shape
    half = width // 2
    hidden_half = ups[0].shape[1]
    small = place.shape[0] - 2
    block = math.gcd(block, count)

    def over_rows(columns):
        return pl.BlockSpec((block, columns), lambda step: (step, 0))

    def whole(*shape):
        return pl.BlockSpec(shape, lambda step: (0,) * len(shape))

    out_spec = pl.BlockSpec((width, half), lambda step: (0, 3))
    return pl.pallas_call(
        functools.partial(middle_back_kernel, small),
        grid=(count // block,),
        in_specs=[
            pl.BlockSpec(memory_space=pltpu.SMEM),
            over_rows(hidden_half),
            over_rows(hidden_half),
            whole(width, hidden_half),
            whole(width, hidden_half),
            over_rows(width),
            over_rows(width),
            over_rows(1),
            whole(*rows.shape),
            over_rows(half),
            over_rows(half),
            out_spec,
            out_spec,
        ],
        out_specs=[
            over_rows(width),
            over_rows(half),
            over_rows(half),
            whole(width, half),
            whole(width, half),
            whole(8, width),
        ],
        out_shape=[
            jax.ShapeDtypeStruct((count, width), F32),
            jax.ShapeDtypeStruct((count, half), BF),
            jax.ShapeDtypeStruct((count, half), BF),
            jax.ShapeDtypeStruct((width, half), F32),
            jax.ShapeDtypeStruct((width, half), BF),
            jax.ShapeDtypeStruct((8, width), F32),
        ],
        scratch_shapes=[pltpu.VMEM((block, width), F32), pltpu.VMEM((2, width, half), F32)],
        compiler_params=pltpu.CompilerParams(vmem_limit_bytes=2 * VMEM_BYTES),
        cost_estimate=pl.CostEstimate(
            flops=4 * count * width * (hidden_half + width),
            bytes_accessed=4 * count * hidden_half + 4 * width * hidden_half + 16 * count * width,
            transcendentals=0,
        ),
        name="middle_back",
    )(place, *grads, *ups, middle, cotangent, mask, rows, *contexts, *weights)


def start_back_kernel(
    small, length, swap, place_ref, grads_mine_ref, grads_other_ref, weight_mine_ref, weight_other_ref, start_ref, middle_ref,
    mask_ref, rows_ref, sums_ref, sums_mine_ref, sums_other_ref, bias_ref,
    tokens_ref, mine_ref, other_ref, lines_ref,
):
    core, place = place_ref[0], place_ref[1]
    step = pl.program_id(0)
    width = start_ref.shape[1]
    half = width // 2
    seqs = start_ref.shape[0] // length

    @pl.when(step == 0)
    def _():
        lines_ref[...] = jnp.zeros_like(lines_ref)
        for index, row in ((0, 0), (1, 2)):
            pair = (sums_mine_ref[row : row + 1, :], sums_other_ref[row : row + 1, :])
            lines_ref[index : index + 1, :half], lines_ref[index : index + 1, half:] = chosen_side(core, *pair)
        lines_ref[2:4, :] = sums_ref[0:2, :]
        lines_ref[6:8, :] = sums_ref[2:4, :]

    grad = 0.0
    for grads, weight in ((grads_mine_ref, weight_mine_ref), (grads_other_ref, weight_other_ref)):
        for index in range(3):
            grad = grad + right_product(grads[index], weight[:, index * half : (index + 1) * half])
    back, shares = norm_back(start_ref[...], rows_ref[small + 4 : small + 5, :], grad)
    back = middle_ref[...] + back
    mask = mask_ref[...]
    tokens_ref[...] = jnp.where(mask > 0.0, 0.0, back)
    for index, item in ((4, shares), (5, grad), (8, back * mask)):
        lines_ref[index : index + 1, :] += jnp.sum(item, 0, keepdims=True)
    for index in range(seqs):
        line = LANES + place * small + step * seqs + index
        lines_ref[pl.ds(line, 1), :] = jnp.sum(back[index * length : (index + 1) * length], 0, keepdims=True)

    @pl.when(step == pl.num_programs(0) - 1)
    def _():
        blocks = (lines_ref[:LANES, :].T + bias_ref[...], lines_ref[LANES:, :].T)
        if swap:
            blocks = chosen_side(core, *blocks)
        mine_ref[...] = blocks[0]
        other_ref[...] = blocks[1].astype(other_ref.dtype)


def start_back(
    place, grads, weights, start, middle, mask, rows, sums, side_sums, bias, seqs, length, swap, block=256
):
    count, width = start.shape
    half = width // 2
    small = place.shape[0] - 2
    block = math.gcd(block, count)
    lines = LANES + -(-seqs // LANES) * LANES

    def over_rows(columns):
        return pl.BlockSpec((block, columns), lambda step: (step, 0))

    def whole(*shape):
        return pl.BlockSpec(shape, lambda step: (0,) * len(shape))

    grads_spec = pl.BlockSpec((3, block, half), lambda step: (0, step, 0))
    return pl.pallas_call(
        functools.partial(start_back_kernel, small, length, swap),
        grid=(count // block,),
        in_specs=[
            pl.BlockSpec(memory_space=pltpu.SMEM),
            grads_spec,
            grads_spec,
            whole(width, 3 * half),
            whole(width, 3 * half),
            over_rows(width),
            over_rows(width),
            over_rows(1),
            whole(*rows.shape),
            whole(*sums.shape),
            whole(*side_sums[0].shape),
            whole(*side_sums[1].shape),
            whole(width, LANES),
        ],
        out_specs=[over_rows(width), whole(width, LANES), whole(width, lines - LANES)],
        out_shape=[
            jax.ShapeDtypeStruct((count, width), F32),
            jax.ShapeDtypeStruct((width, LANES), F32),
            jax.ShapeDtypeStruct((width, lines - LANES), BF if swap else F32),
        ],
        scratch_shapes=[pltpu.VMEM((lines, width), F32)],
        compiler_params=pltpu.CompilerParams(vmem_limit_bytes=VMEM_BYTES),
        cost_estimate=pl.CostEstimate(
            flops=0, bytes_accessed=1024, transcendentals=0
        ),
        name="start_back",
    )(place, *grads, *weights, start, middle, mask, rows, sums, *side_sums, bias)


def shards_kernel(fixed, seq_cols, core_ref, steps_ref, qkv_ref, out_ref, table_ref, *refs):
    small_refs, (mine_ref, other_ref, full_ref) = refs[: fixed + 1], refs[fixed + 1 :]
    core = core_ref[0]
    part, table_cols = table_ref.shape
    half = out_ref.shape[1] // 2
    seq_count = steps_ref.shape[0]
    lines = [ref[...] for ref in small_refs[:fixed]]
    up = small_refs[fixed][...]
    lines += [up[:, i : i + part] for i in range(0, up.shape[1], part)]
    lane = lax.broadcasted_iota(jnp.int32, (1, part), 1)
    for row in range(seq_cols):
        line = jnp.zeros((1, part), jnp.int32)
        for index in range(seq_count):
            step = steps_ref[index]
            line = jnp.where(lane + row * part == index, step // 256, line)
            line = jnp.where(lane + row * part == seq_count + index, step % 256, line)
        lines.append(line.astype(F32))
    lines = jnp.concatenate(lines, 0).astype(BF)
    square = (part, part)
    unit = lax.broadcasted_iota(jnp.int32, square, 0) == lax.broadcasted_iota(jnp.int32, square, 1)
    full_ref[...] = jnp.zeros_like(full_ref)
    full_ref[:, :table_cols] = table_ref[...]
    full_ref[:, table_cols : table_cols + lines.shape[0]] = right_product(jnp.where(unit, 1.0, 0.0).astype(BF), lines)
    table_half = full_ref.shape[1] // 2

    def halves(ref, top, wide):
        return chosen_side(core, ref[:, top : top + wide], ref[:, top + wide : top + 2 * wide])

    sources = [(qkv_ref, 2 * half * i, half) for i in range(3)] + [(out_ref, 0, half), (full_ref, 0, table_half)]
    left = 0
    for ref, top, wide in sources:
        mine, other = halves(ref, top, wide)
        mine_ref[:, left : left + wide] = mine.astype(BF)
        other_ref[:, left : left + wide] = other.astype(BF)
        left += wide


def attention_shards(core, timesteps, w_qkv, w_out, table, small, b_up, seq_cols, all_cols):
    part = table.shape[0]
    shape = jax.ShapeDtypeStruct((part, 2 * w_out.shape[1] + all_cols // 2), BF)
    vmem = pl.BlockSpec(memory_space=pltpu.VMEM)
    return pl.pallas_call(
        functools.partial(shards_kernel, len(small), seq_cols),
        in_specs=[pl.BlockSpec(memory_space=pltpu.SMEM)] * 2 + [vmem] * (4 + len(small)),
        out_specs=[vmem, vmem],
        out_shape=[shape, shape],
        scratch_shapes=[pltpu.VMEM((part, all_cols), F32)],
        compiler_params=pltpu.CompilerParams(vmem_limit_bytes=60 << 20),
        cost_estimate=pl.CostEstimate(flops=0, bytes_accessed=24 * part * w_out.shape[1], transcendentals=0),
        name="attention_shards",
    )(core, timesteps, w_qkv, w_out, table, *[item.reshape(1, -1) for item in small], b_up.reshape(1, -1))


def route_kernel(rows, route_ref, *refs):
    terms, (sent_ref, kept_ref) = refs[:-2], refs[-2:]
    for index in range(2):
        for out, place in ((sent_ref, route_ref[index]), (kept_ref, route_ref[2 + index])):
            span = pl.ds(pl.multiple_of(place * rows, 8), rows)
            left = 0
            for mine, got in zip(terms[::2], terms[1::2]):
                many = [(slice(None),)] if len(mine.shape) == 2 else [(i, slice(None)) for i in range(mine.shape[0])]
                for at in many:
                    where = (*at[:-1], span)
                    total = mine[where].astype(F32) + got[where].astype(F32)
                    out[0, index, :, left : left + total.shape[1]] = total.astype(out.dtype)
                    left += total.shape[1]


def routed(terms, rows, route):
    specs, columns, bytes_read = [], 0, 0
    for array in [item for pair in terms for item in pair]:
        shape = (4 * rows, array.shape[-1])
        if array.ndim == 2:
            specs.append(pl.BlockSpec(shape, lambda z: (z, 0)))
        else:
            specs.append(pl.BlockSpec((array.shape[0], *shape), lambda z: (0, z, 0)))
        bytes_read += array.size * array.dtype.itemsize
        columns += array.size // (16 * rows)
    columns //= 2
    out = pl.BlockSpec((1, 2, rows, columns), lambda z: (z, 0, 0, 0))
    return pl.pallas_call(
        functools.partial(route_kernel, rows),
        grid=(4,),
        in_specs=[pl.BlockSpec(memory_space=pltpu.SMEM)] + specs,
        out_specs=[out, out],
        out_shape=[
            jax.ShapeDtypeStruct((4, 2, rows, columns), BF),
            pltpu.HBM((4, 2, rows, columns), F32),
        ],
        compiler_params=pltpu.CompilerParams(vmem_limit_bytes=VMEM_BYTES),
        cost_estimate=pl.CostEstimate(
            flops=0, bytes_accessed=bytes_read + 48 * rows * columns, transcendentals=0
        ),
        name="routed",
    )(route, *[item for pair in terms for item in pair])


class Tree:
    def __init__(self):
        fsdp, rep = lax.axis_index("fsdp"), lax.axis_index("rep")
        self.z, self.core = fsdp // 2, rep % 2
        x, y = rep // 2, fsdp % 2
        self.near = jnp.where(self.core == 0, x, y)
        self.far = jnp.where(self.core == 0, y, x)
        places = [jnp.where(self.core == 0, 2 * i + near, 2 * near + i) for near in (1 - self.near, self.near) for i in (0, 1)]
        self.route = jnp.stack(places)

    def to_core(self, value):
        return lax.ppermute(value, "rep", [(i, i ^ 1) for i in range(4)])

    def to_near(self, value):
        return lax.ppermute(value, AXES, [(i, i ^ (4 if i % 2 else 2)) for i in range(32)])

    def to_far(self, value):
        return lax.ppermute(value, AXES, [(i, i ^ (2 if i % 2 else 4)) for i in range(32)])

    def to_z(self, value, step):
        return lax.ppermute(value, "fsdp", [(i, i ^ (2 * step)) for i in range(8)])


class Gather:
    def __init__(self, tree, own):
        self.tree, self.own = tree, own

    @staticmethod
    def columns(tree, mine, other):
        got = tree.to_core(other)
        return Gather(tree, paired(tree.core, mine, got, 0).reshape(-1, mine.shape[1]))

    @staticmethod
    def rows(tree, shard):
        return Gather(tree, shard)

    def along_z(self, *wait):
        own = after(self.own, *wait)
        one, three, two = [self.tree.to_z(own, step) for step in (1, 3, 2)]
        self.held, self.got = own, [one, two, three]
        return self.got

    def one(self, *wait):
        tree = self.tree
        held = after([self.held, *self.got], *wait)
        low, high = tree.z % 2 == 1, tree.z // 2 == 1
        out = []
        for place in range(4):
            near = [jnp.where(low, held[(place ^ 1) ^ h], held[place ^ h]) for h in (0, 2)]
            out.append(jnp.where(high, near[1], near[0]))
        self.held = jnp.stack(out)
        self.got = tree.to_near(self.held)
        return self.got

    def two(self, *wait):
        tree = self.tree
        held, got = after((self.held, self.got), *wait)
        self.held = paired(tree.near, held, got, 1)
        self.got = tree.to_far(self.held)
        return self.got

    def halves(self, *wait):
        tree = self.tree
        held, got = after((self.held, self.got), *wait)
        same, first = tree.far == 0, tree.core == 0
        lower, upper = jnp.where(same, held, got), jnp.where(same, got, held)
        blocks = [
            lower[:, 0],
            jnp.where(first, lower[:, 1], upper[:, 0]),
            jnp.where(first, upper[:, 0], lower[:, 1]),
            upper[:, 1],
        ]
        half = jnp.stack(blocks, 1).reshape(-1, held.shape[-1])
        return half, tree.to_core(half)


class Reduce:
    def __init__(self, tree, rows):
        self.tree, self.rows = tree, rows
        self.terms = []

    def add(self, mine, other):
        got = self.tree.to_core(other.astype(BF))
        self.terms.append((mine, got))
        return got

    def one(self, *wait):
        self.sent, self.kept = routed(after(self.terms, *wait), self.rows, self.tree.route)
        self.got = self.tree.to_near(self.sent)

    def two(self, *wait, apart=False):
        tree = self.tree
        kept, got = after((self.kept, self.got), *wait)
        if apart:
            self.sent = (pick(kept, 1 - tree.far, 1) + pick(got, 1 - tree.far, 1)).astype(BF)
            self.kept = pick(kept, tree.far, 1) + pick(got, tree.far, 1)
            self.got = tree.to_far(self.sent)
            return
        total = kept + got
        self.kept, self.sent = pick(total, tree.far, 1), pick(total, 1 - tree.far, 1).astype(BF)
        self.got = tree.to_far(self.sent)

    def along_z(self, *others):
        tree = self.tree
        total = jnp.concatenate([item.kept + item.got for item in (self, *others)], -1)
        self.kept = pick(total, tree.z, 0)
        self.sent = tuple(pick(total, tree.z ^ step, 0).astype(BF) for step in (1, 2, 3))
        self.got = tuple(tree.to_z(sent, step) for sent, step in zip(self.sent, (1, 2, 3)))

    def sums(self, *wait):
        kept, got = after((self.kept, self.got), *wait)
        return kept + got[0] + got[1] + got[2]

    def columns(self, *wait):
        tree, total = self.tree, self.sums(*wait)
        rows = total.reshape(2, self.rows // 2, -1)
        keep = pick(rows, tree.core, 0)
        return paired(tree.core, keep, tree.to_core(pick(rows, 1 - tree.core, 0)), 1)


class Whole:
    core = 0

    def __init__(self, rows=None):
        self.mine, self.other = [], []
        self.got, self.sent = (), ()

    @staticmethod
    def columns_of(mine, other):
        out = Whole()
        whole = lax.all_gather(jnp.stack([mine, other], 1), AXES, axis=0, tiled=True)
        out.half, out.rest = whole[:, 0], whole[:, 1]
        return out

    @staticmethod
    def rows_of(shard):
        out = Whole()
        whole = lax.all_gather(shard, AXES, axis=0)
        whole = whole.reshape(-1, 2, *shard.shape)
        out.half, out.rest = [whole[:, i].reshape(-1, shard.shape[1]) for i in range(2)]
        return out

    def along_z(self, *wait):
        return []

    def one(self, *wait):
        return ()

    def two(self, *wait):
        return ()

    def halves(self, *wait):
        return self.half, self.rest

    def add(self, mine, other):
        self.mine.append(mine.astype(BF))
        self.other.append(other.astype(BF))
        return mine

    def columns(self, *wait):
        def flat(items):
            return jnp.concatenate([part for item in items for part in (item if item.ndim == 3 else [item])], 1)

        parts = [flat(item) for item in (self.mine, self.other)]
        return lax.psum_scatter(jnp.stack(parts, 1), AXES, scatter_dimension=0, tiled=True).astype(F32)

    def sums(self, *wait):
        count = lax.axis_size(AXES)
        mine, other = [item[0].reshape(count // 2, -1, item[0].shape[1]) for item in (self.mine, self.other)]
        sums = jnp.stack([mine, other], 1).reshape(-1, mine.shape[-1])
        return lax.psum_scatter(sums, AXES, scatter_dimension=0, tiled=True).astype(F32)


def body(
    fast,
    tokens,
    mask_bits,
    timesteps,
    cotangent,
    w_qkv,
    w_out,
    w_up,
    w_down,
    time_table,
    b_query,
    b_value,
    b_out,
    b_up,
    b_down,
    gain_attn,
    shift_attn,
    gain_mlp,
    shift_mlp,
    mask_vector,
):
    tree = Tree() if fast else Whole()
    gather_columns = functools.partial(Gather.columns, tree) if fast else Whole.columns_of
    gather_rows = functools.partial(Gather.rows, tree) if fast else Whole.rows_of
    reduction = functools.partial(Reduce, tree) if fast else Whole
    core = tree.core
    count = lax.axis_size(AXES)
    chips = count // 2
    place = lax.axis_index(AXES)
    width = tokens.shape[1]
    part = width // count
    hidden_width = w_up.shape[1]
    hidden_part = hidden_width // count
    seq_count = timesteps.shape[0]
    seq_length = tokens.shape[0] // seq_count
    half = width // 2
    table_cols = time_table.shape[1]
    absorbed = mask_bits.astype(F32)[:, None]

    small = [b_query, b_value, b_out, b_down, gain_attn, shift_attn, gain_mlp, shift_mlp, mask_vector]
    fixed = len(small)
    up_cols = hidden_part // part
    seq_cols = -(-2 * seq_count // part)
    small_cols = fixed + up_cols + seq_cols
    all_cols = -(-(table_cols + small_cols) // (2 * LANES)) * (2 * LANES)
    place = jnp.concatenate([jnp.stack([jnp.int32(core), place]), timesteps])

    shards = attention_shards(
        jnp.full((1,), core, jnp.int32), timesteps, w_qkv, w_out, time_table, small, b_up, seq_cols, all_cols
    )
    attn_w = gather_columns(*shards)
    up_shard = w_up.astype(BF).reshape(part, chips, 2, hidden_part).transpose(2, 0, 1, 3)
    up_shard = up_shard.reshape(2, part, hidden_width // 2)
    up_w = gather_columns(*[pick(up_shard, side, 0) for side in (core, 1 - core)])
    down_w = gather_rows(w_down.astype(BF))
    attn_w.along_z()
    up_z = up_w.along_z()
    attn_one = attn_w.one()
    attn_two = attn_w.two(up_z[::2])
    up_one = up_w.one(attn_two)
    attn_w = attn_w.halves(up_z)
    down_z = down_w.along_z(attn_two)

    rows, start, normed_one, across_one, bias_mine, bias_other, bias_up = start_rows(
        place, tokens, absorbed, attn_w, fixed, up_cols, table_cols, small_cols, chips, hidden_part
    )
    up_two = up_w.two(normed_one)
    qkv_mine, context_mine = attention(after(normed_one, up_one), attn_w[0], bias_mine, seq_length)
    down_one = down_w.one(up_two, context_mine)
    up_w = up_w.halves(context_mine)
    qkv_other, context_other = attention(after(normed_one, up_two), attn_w[1], bias_other, seq_length)
    down_two = down_w.two()
    contexts = (context_mine, context_other)
    middle, normed_two, across_two = middle_rows(place, contexts, attn_w, after(start, down_one), rows)
    hidden, slope = [None, None], [None, None]
    hidden[0], slope[0] = feed(normed_two, up_w[0], bias_up, 0)
    down_w = down_w.halves(hidden[0])
    hidden[1], slope[1] = feed(after(normed_two, down_two), up_w[1], bias_up, 1)

    grad_branch = (cotangent * absorbed).astype(BF)
    down_sum = reduction(hidden_part)
    down_sum.add(left_product(hidden[0], grad_branch), left_product(hidden[1], grad_branch))
    up_sum = reduction(2 * part)
    grad_pre, grad_b_up, grad_up = [None, None], [None, None], [None, None]
    if fast:
        down_sum.one()
    grad_pre[1], grad_b_up[1], grad_up[1] = feed_back(
        grad_branch, down_w[1], slope[1], across_two, BF
    )
    grad_pre[0], grad_b_up[0], grad_up[0] = feed_back(grad_branch, down_w[0], slope[0], across_two, F32)
    up_sum.add(grad_up[0], grad_up[1])
    if fast:
        down_sum.two(grad_pre[1])
    grad_pre = after(grad_pre, down_sum.sent)
    grad_middle, *grad_context, grad_out_mine, grad_out_other, middle_sums = middle_back(
        place, grad_pre, up_w, middle, cotangent, absorbed, rows, contexts, attn_w
    )

    attn_sum = reduction(2 * part)
    up_sum.add(grad_out_mine, grad_out_other)
    if fast:
        up_sum.one(down_sum.got)
        down_sum.along_z()
    grads = [None, None]
    grads[1] = attention_back(
        qkv_other, after(grad_context[1], down_sum.sent, up_sum.sent), across_one, seq_length, BF
    )
    if fast:
        up_sum.two(down_sum.got, grads[1])
    grads[0] = attention_back(qkv_mine, after(grad_context[0], up_sum.sent), across_one, seq_length, F32)
    grad_qkv, grad_weights, sums = zip(*grads)
    attn_sum.add(grad_weights[0], grad_weights[1])
    if fast:
        attn_sum.one()
        up_sum.along_z()
    grad_qkv = after(grad_qkv, up_sum.sent, attn_sum.sent)
    grad_b_up = paired(core, *[item.reshape(chips, hidden_part) for item in grad_b_up], 1).reshape(count, hidden_part)
    grad_b_up = jnp.pad(grad_b_up[:, None], ((0, 0), (0, part - 1), (LANES - hidden_part, 0)))
    seqs = count * seq_count
    grad_tokens, *blocks = start_back(
        place, grad_qkv, attn_w, start, grad_middle, absorbed, rows, middle_sums, sums,
        grad_b_up.reshape(width, LANES), seqs, seq_length, fast,
    )
    if fast:
        attn_sum.two()
        extra_sum = reduction(2 * part)
        extra_sum.add(*blocks)
        extra_sum.one()
        extra_sum.two(attn_sum.sent)
        attn_sum.along_z(extra_sum)
        hidden, rows = after((hidden, rows), attn_sum.sent)
    output = middle + (product(hidden[0], down_w[0]) + product(hidden[1], down_w[1]) + rows[seq_count + 3])
    if fast:
        attn_grad = attn_sum.columns(output)
        small, seq_sums = attn_grad[:, 0, 3 * half :], attn_grad[:, 1, 3 * half :]
    else:
        attn_grad = attn_sum.columns()
        small, seq_sums = [
            lax.psum_scatter(item.astype(BF), AXES, scatter_dimension=0, tiled=True).astype(F32) for item in blocks
        ]
    steps = rows[seq_count + fixed + up_cols : seq_count + small_cols]
    steps = steps.reshape(seq_cols, count, part).transpose(1, 0, 2).reshape(count, -1).astype(jnp.int32)
    steps = (steps[:, :seq_count] * 256 + steps[:, seq_count : 2 * seq_count]).reshape(-1)
    grad_b_up = small[0, LANES - hidden_part :]
    small = small[:, :fixed].T
    onehot = (steps[:, None] == lax.broadcasted_iota(jnp.int32, (seqs, table_cols), 1)).astype(F32)
    grad_time_table = jnp.dot(seq_sums, onehot, precision=lax.Precision.HIGHEST)
    grad_w_qkv = attn_grad[:, :, : 3 * half].reshape(part, 2, 3, half).transpose(0, 2, 1, 3).reshape(part, 3 * width)
    up_grad = up_sum.columns(extra_sum.sent if fast else ())
    grad_w_out = up_grad[:, :, hidden_width // 2 :].reshape(part, width)
    grad_w_up = up_grad[:, :, : hidden_width // 2].reshape(part, 2, chips, hidden_part).transpose(0, 2, 1, 3)
    grad_w_up = grad_w_up.reshape(part, hidden_width)
    return (
        output,
        grad_tokens,
        grad_w_qkv,
        grad_w_out,
        grad_w_up,
        down_sum.sums(extra_sum.sent if fast else ()),
        grad_time_table,
        small[0],
        small[1],
        small[2],
        grad_b_up,
        small[3],
        small[4],
        small[5],
        small[6],
        small[7],
        small[8],
    )


def solution(mesh):
    matrix, vector = P(AXES, None), P(AXES)
    fast = dict(mesh.shape) == {"fsdp": 8, "rep": 4}
    return jax.shard_map(
        functools.partial(body, fast),
        mesh=mesh,
        in_specs=(matrix, vector, vector) + (matrix,) * 6 + (vector,) * 10,
        out_specs=(matrix,) * 7 + (vector,) * 10,
        check_vma=False,
    )
```

```python
import functools
import math

import jax
import jax.numpy as jnp
from jax import lax
from jax.experimental import pallas as pl
from jax.experimental.pallas import tpu as pltpu
from jax.sharding import PartitionSpec as P

HDIM = 64
EPSILON = 1e-05
AXES = ("fsdp", "rep")
BF = jnp.bfloat16
F32 = jnp.float32
LANES = 128
VMEM_BYTES = 18 << 20
GELU_OUTER = math.sqrt(2.0 / math.pi)
GELU_INNER = 0.044715


def contract(left, right, left_dim, right_dim):
    dims = (((left_dim,), (right_dim,)), ((), ()))
    return lax.dot_general(left, right, dims, preferred_element_type=F32)


def product(left, right):
    return contract(left, right, 1, 0)


def left_product(left, right):
    return contract(left, right, 0, 0)


def right_product(left, right):
    return contract(left, right, 1, 1)


def pick(array, index, axis):
    return lax.dynamic_index_in_dim(array, index, axis, keepdims=False)


def paired(bit, mine, other, axis):
    return jnp.stack([jnp.where(bit == 0, mine, other), jnp.where(bit == 0, other, mine)], axis)


def in_hbm(value):
    return pltpu.with_memory_space_constraint(value, pltpu.HBM)


def after(value, *others):
    return lax.optimization_barrier((value, others))[0]


def lane_masks(factor):
    lane = lax.broadcasted_iota(jnp.int32, (1, LANES), 1)
    return [jnp.where((lane < HDIM) == (head == 0), factor, 0.0).astype(BF) for head in (0, 1)]


def stacked(values, masks):
    return jnp.concatenate([values * masks[0], values * masks[1]], 0)


def unstacked(values):
    rows = values.shape[0] // 2
    lane = lax.broadcasted_iota(jnp.int32, (1, LANES), 1)
    return jnp.where(lane < HDIM, values[:rows], values[rows:])


def softmax_down(scores):
    powers = jnp.exp(scores - jnp.max(scores, 0, keepdims=True))
    return powers * (1.0 / jnp.sum(powers, 0, keepdims=True))


def attention_kernel(length, scale, rows_ref, query_ref, key_ref, value_ref, bias_ref, qkv_ref, context_ref):
    weight = jnp.concatenate([query_ref[...], key_ref[...], value_ref[...]], 1)
    projected = product(rows_ref[...], weight)
    for index in range(3):
        part = projected[:, index * LANES : (index + 1) * LANES]
        qkv_ref[index] = (part + bias_ref[index : index + 1, :]).astype(BF)
    scaled = lane_masks(scale)

    for sequence in range(rows_ref.shape[0] // length):
        span = slice(sequence * length, (sequence + 1) * length)
        queries, key_rows, value_rows = [qkv_ref[index, span, :] for index in range(3)]
        probs = softmax_down(right_product(key_rows, stacked(queries, scaled))).astype(BF)
        context_ref[span, :] = unstacked(left_product(probs, value_rows)).astype(BF)


def attention(rows, weight, bias, length):
    tokens, width = rows.shape
    half = bias.shape[1]
    pairs = half // LANES

    def weight_spec(index):
        return pl.BlockSpec((width, LANES), lambda pair: (0, index * pairs + pair))

    return pl.pallas_call(
        functools.partial(attention_kernel, length, 1.0 / math.sqrt(HDIM)),
        grid=(pairs,),
        in_specs=[
            pl.BlockSpec((tokens, width), lambda pair: (0, 0)),
            weight_spec(0),
            weight_spec(1),
            weight_spec(2),
            pl.BlockSpec((8, LANES), lambda pair: (0, pair)),
        ],
        out_specs=[
            pl.BlockSpec((3, tokens, LANES), lambda pair: (0, 0, pair)),
            pl.BlockSpec((tokens, LANES), lambda pair: (0, pair)),
        ],
        out_shape=[
            pltpu.HBM((3, tokens, half), BF),
            jax.ShapeDtypeStruct((tokens, half), BF),
        ],
        compiler_params=pltpu.CompilerParams(vmem_limit_bytes=VMEM_BYTES),
        cost_estimate=pl.CostEstimate(
            flops=6 * tokens * width * half,
            bytes_accessed=2 * tokens * width + 6 * width * half + 8 * tokens * half,
            transcendentals=2 * tokens * length * pairs,
        ),
        name="attention",
    )(rows, weight, weight, weight, bias)


def attention_back_kernel(length, scale, qkv_ref, grad_ref, rows_ref, grads_ref, weight_ref, sums_ref):
    ones, scaled = lane_masks(1.0), lane_masks(scale)

    for sequence in range(grad_ref.shape[0] // length):
        span = slice(sequence * length, (sequence + 1) * length)
        queries, key_rows, value_rows = [qkv_ref[index, span, :] for index in range(3)]
        queries, grad = stacked(queries, scaled), stacked(grad_ref[span, :], ones)
        probs = softmax_down(right_product(key_rows, queries))
        grad_probs = right_product(value_rows, grad)
        grad_scores = probs * (grad_probs - jnp.sum(grad_probs * probs, 0, keepdims=True))
        grad_scores = grad_scores.astype(BF)
        grad_queries = unstacked(left_product(grad_scores, key_rows)) * scale
        grads_ref[0, span, :] = grad_queries.astype(BF)
        grads_ref[1, span, :] = product(grad_scores, queries).astype(BF)
        grads_ref[2, span, :] = product(probs.astype(BF), grad).astype(BF)

    grads = jnp.concatenate([grads_ref[index] for index in range(3)], 1)
    weight = product(rows_ref[...], grads)
    for index in range(3):
        weight_ref[index] = weight[:, index * LANES : (index + 1) * LANES].astype(weight_ref.dtype)
        sums_ref[index : index + 1, :] = jnp.sum(grads_ref[index].astype(F32), 0, keepdims=True)


def attention_back(qkv, grad, rows_across, length, dtype):
    _, tokens, half = qkv.shape
    width = rows_across.shape[0]
    pairs = half // LANES
    return pl.pallas_call(
        functools.partial(attention_back_kernel, length, 1.0 / math.sqrt(HDIM)),
        grid=(pairs,),
        in_specs=[
            pl.BlockSpec((3, tokens, LANES), lambda pair: (0, 0, pair)),
            pl.BlockSpec((tokens, LANES), lambda pair: (0, pair)),
            pl.BlockSpec((width, tokens), lambda pair: (0, 0)),
        ],
        out_specs=[
            pl.BlockSpec((3, tokens, LANES), lambda pair: (0, 0, pair)),
            pl.BlockSpec((3, width, LANES), lambda pair: (0, 0, pair)),
            pl.BlockSpec((3, LANES), lambda pair: (0, pair)),
        ],
        out_shape=[
            pltpu.HBM((3, tokens, half), BF),
            jax.ShapeDtypeStruct((3, width, half), dtype),
            jax.ShapeDtypeStruct((3, half), F32),
        ],
        compiler_params=pltpu.CompilerParams(vmem_limit_bytes=VMEM_BYTES),
        cost_estimate=pl.CostEstimate(
            flops=6 * tokens * width * half,
            bytes_accessed=2 * tokens * width + 12 * width * half + 14 * tokens * half,
            transcendentals=2 * tokens * length * pairs,
        ),
        name="attention_back",
    )(in_hbm(qkv), in_hbm(grad), in_hbm(rows_across))


def feed_kernel(side, rows_ref, weight_ref, bias_ref, hidden_ref, slope_ref, pre_ref):
    pre_ref[...] = product(rows_ref[...], weight_ref[...])
    step = 32

    def chunk(index, carry):
        span = pl.ds(pl.multiple_of(index * step, step), step)
        pre = pre_ref[span, :] + bias_ref[side : side + 1, :]
        square = pre * pre
        bend = jnp.tanh(GELU_OUTER * (pre + GELU_INNER * (square * pre)))
        share = 0.5 * (1.0 + bend)
        hidden_ref[span, :] = (pre * share).astype(BF)
        inner = (0.5 * GELU_OUTER) * pre * (1.0 + (3.0 * GELU_INNER) * square)
        slope_ref[span, :] = share + inner * (1.0 - bend * bend)
        return carry

    lax.fori_loop(0, rows_ref.shape[0] // step, chunk, 0, unroll=2)


def feed(rows, weight, bias, side, block=512):
    tokens, width = rows.shape
    columns = weight.shape[1]
    block = math.gcd(block, columns)
    out = pl.BlockSpec((tokens, block), lambda step: (0, step))
    return pl.pallas_call(
        functools.partial(feed_kernel, side),
        grid=(columns // block,),
        in_specs=[
            pl.BlockSpec((tokens, width), lambda step: (0, 0)),
            pl.BlockSpec((width, block), lambda step: (0, step)),
            pl.BlockSpec((8, block), lambda step: (0, step)),
        ],
        out_specs=[out, out],
        out_shape=[
            pltpu.HBM((tokens, columns), BF),
            pltpu.HBM((tokens, columns), F32),
        ],
        scratch_shapes=[pltpu.VMEM((tokens, block), F32)],
        compiler_params=pltpu.CompilerParams(vmem_limit_bytes=VMEM_BYTES),
        cost_estimate=pl.CostEstimate(
            flops=2 * tokens * width * columns,
            bytes_accessed=2 * tokens * width + 2 * width * columns + 6 * tokens * columns,
            transcendentals=tokens * columns,
        ),
        name="feed",
    )(rows, weight, bias)


def feed_back_kernel(grad_ref, weight_ref, slope_ref, rows_ref, pre_ref, sum_ref, up_ref):
    grad = (right_product(grad_ref[...], weight_ref[...]) * slope_ref[...]).astype(BF)
    pre_ref[...] = grad
    sum_ref[...] = jnp.sum(grad.astype(F32), 0, keepdims=True)
    up_ref[...] = product(rows_ref[...], grad).astype(up_ref.dtype)


def feed_back(grad, weight, slope, rows_across, dtype, block=768):
    tokens, width = grad.shape
    columns = weight.shape[0]
    block = math.gcd(block, columns)
    out = pl.BlockSpec((tokens, block), lambda step: (0, step))
    return pl.pallas_call(
        feed_back_kernel,
        grid=(columns // block,),
        in_specs=[
            pl.BlockSpec((tokens, width), lambda step: (0, 0)),
            pl.BlockSpec((block, width), lambda step: (step, 0)),
            out,
            pl.BlockSpec((width, tokens), lambda step: (0, 0)),
        ],
        out_specs=[
            out,
            pl.BlockSpec((1, block), lambda step: (0, step)),
            pl.BlockSpec((width, block), lambda step: (0, step)),
        ],
        out_shape=[
            pltpu.HBM((tokens, columns), BF),
            jax.ShapeDtypeStruct((1, columns), F32),
            jax.ShapeDtypeStruct((width, columns), dtype),
        ],
        compiler_params=pltpu.CompilerParams(vmem_limit_bytes=VMEM_BYTES),
        cost_estimate=pl.CostEstimate(
            flops=4 * tokens * width * columns,
            bytes_accessed=4 * tokens * width + 6 * width * columns + 6 * tokens * columns,
            transcendentals=0,
        ),
        name="feed_back",
    )(in_hbm(grad), in_hbm(weight), in_hbm(slope), in_hbm(rows_across))


def chosen_side(core, mine, other):
    return jnp.where(core == 0, mine, other), jnp.where(core == 0, other, mine)


def normalized(values):
    center = values - jnp.mean(values, -1, keepdims=True)
    rate = lax.rsqrt(jnp.mean(center * center, -1, keepdims=True) + EPSILON)
    return center * rate, rate


def start_kernel(
    fixed, up_cols, table_cols, seq_count, parts,
    place_ref, tokens_ref, mask_ref, table_mine_ref, table_other_ref,
    rows_ref, start_ref, normed_ref, across_ref, bias_mine_ref, bias_other_ref, bias_up_ref,
):
    core = place_ref[0]
    step = pl.program_id(0)
    width = tokens_ref.shape[1]
    half = width // 2
    chips, part, hidden_part = parts

    @pl.when(step == 0)
    def _():
        count, columns = rows_ref.shape[0], table_mine_ref.shape[1]
        row = lax.broadcasted_iota(jnp.int32, (count, columns), 0)
        wanted = table_cols + row - seq_count
        for index in range(seq_count):
            wanted = jnp.where(row == index, place_ref[2 + index], wanted)
        column = lax.broadcasted_iota(jnp.int32, (count, columns), 1)
        rows = 0.0
        for side, table in ((core, table_mine_ref), (1 - core, table_other_ref)):
            hit = jnp.where(wanted == column + side * columns, 1.0, 0.0).astype(BF)
            rows = rows + right_product(hit, table[...])
        rows_ref[...] = rows
        for ref, side in ((bias_mine_ref, core), (bias_other_ref, 1 - core)):
            ref[...] = jnp.zeros_like(ref)
            for index in (0, 1):
                line = rows_ref[seq_count + index : seq_count + index + 1, :]
                ref[2 * index : 2 * index + 1, :] = jnp.where(side == 0, line[:, :half], line[:, half:])
        for chip in range(chips):
            for index in range(up_cols):
                line = rows_ref[seq_count + fixed + index : seq_count + fixed + index + 1, :]
                pair = [line[:, (2 * chip + i) * part : (2 * chip + i + 1) * part] for i in range(2)]
                where = slice(chip * hidden_part + index * part, chip * hidden_part + (index + 1) * part)
                bias_up_ref[0:1, where], bias_up_ref[1:2, where] = chosen_side(core, *pair)

    small = seq_count
    mask = mask_ref[...]
    start = jnp.where(mask > 0.0, rows_ref[small + 8 : small + 9, :], tokens_ref[...])
    start = start + rows_ref[pl.ds(step, 1), :]
    start_ref[...] = start
    normed, _ = normalized(start)
    normed = normed * rows_ref[small + 4 : small + 5, :] + rows_ref[small + 5 : small + 6, :]
    normed_ref[...] = normed.astype(BF)
    across_ref[...] = normed.T.astype(BF)


def start_rows(place, tokens, mask, weights, fixed, up_cols, table_cols, small_cols, chips, hidden_part):
    count, width = tokens.shape
    seq_count = place.shape[0] - 2
    length = count // seq_count
    half = width // 2
    row_count = -(-(seq_count + small_cols) // 8) * 8
    table_half = weights[0].shape[1] - 4 * half
    tables = 4 * half // table_half
    table_spec = pl.BlockSpec((width, table_half), lambda step: (0, tables))
    rows_spec = pl.BlockSpec((length, width), lambda step: (step, 0))

    def fixed_spec(*shape):
        return pl.BlockSpec(shape, lambda step: (0,) * len(shape))

    return pl.pallas_call(
        functools.partial(
            start_kernel, fixed, up_cols, table_cols, seq_count, (chips, width // (2 * chips), hidden_part)
        ),
        grid=(seq_count,),
        in_specs=[
            pl.BlockSpec(memory_space=pltpu.SMEM),
            rows_spec,
            pl.BlockSpec((length, 1), lambda step: (step, 0)),
            table_spec,
            table_spec,
        ],
        out_specs=[
            fixed_spec(row_count, width),
            rows_spec,
            rows_spec,
            pl.BlockSpec((width, length), lambda step: (0, step)),
            fixed_spec(8, half),
            fixed_spec(8, half),
            fixed_spec(8, chips * hidden_part),
        ],
        out_shape=[
            jax.ShapeDtypeStruct((row_count, width), F32),
            pltpu.HBM((count, width), F32),
            jax.ShapeDtypeStruct((count, width), BF),
            pltpu.HBM((width, count), BF),
            jax.ShapeDtypeStruct((8, half), F32),
            jax.ShapeDtypeStruct((8, half), F32),
            jax.ShapeDtypeStruct((8, chips * hidden_part), F32),
        ],
        compiler_params=pltpu.CompilerParams(vmem_limit_bytes=VMEM_BYTES),
        cost_estimate=pl.CostEstimate(
            flops=4 * row_count * width * table_half, bytes_accessed=14 * count * width, transcendentals=0
        ),
        name="start_rows",
    )(place, in_hbm(tokens), mask, *weights)


def middle_kernel(
    small, place_ref, context_mine_ref, context_other_ref, out_mine_ref, out_other_ref, start_ref, rows_ref,
    middle_ref, normed_ref, across_ref,
):
    core = place_ref[0]
    half = context_mine_ref.shape[1]
    contexts = chosen_side(core, context_mine_ref[...], context_other_ref[...])
    outs = chosen_side(core, out_mine_ref[...], out_other_ref[...])
    for index, out in enumerate(outs):
        span = slice(index * half, (index + 1) * half)
        total = product(contexts[0], out[:half]) + product(contexts[1], out[half:])
        middle_ref[:, span] = start_ref[:, span] + (total + rows_ref[small + 2 : small + 3, span])
    normed, _ = normalized(middle_ref[...])
    normed = normed * rows_ref[small + 6 : small + 7, :] + rows_ref[small + 7 : small + 8, :]
    normed_ref[...] = normed.astype(BF)
    across_ref[...] = normed.T.astype(BF)


def middle_rows(place, contexts, weights, start, rows, block=256):
    count, width = start.shape
    half = width // 2
    small = place.shape[0] - 2
    block = math.gcd(block, count)
    out_spec = pl.BlockSpec((width, half), lambda step: (0, 3))
    rows_spec = pl.BlockSpec((block, width), lambda step: (step, 0))
    half_spec = pl.BlockSpec((block, half), lambda step: (step, 0))
    return pl.pallas_call(
        functools.partial(middle_kernel, small),
        grid=(count // block,),
        in_specs=[
            pl.BlockSpec(memory_space=pltpu.SMEM),
            half_spec,
            half_spec,
            out_spec,
            out_spec,
            rows_spec,
            pl.BlockSpec(rows.shape, lambda step: (0, 0)),
        ],
        out_specs=[rows_spec, rows_spec, pl.BlockSpec((width, block), lambda step: (0, step))],
        out_shape=[
            pltpu.HBM((count, width), F32),
            jax.ShapeDtypeStruct((count, width), BF),
            pltpu.HBM((width, count), BF),
        ],
        compiler_params=pltpu.CompilerParams(vmem_limit_bytes=VMEM_BYTES),
        cost_estimate=pl.CostEstimate(
            flops=2 * count * width * width, bytes_accessed=14 * count * width + 2 * width * width, transcendentals=0
        ),
        name="middle_rows",
    )(place, *contexts, *weights, start, rows)


def norm_back(values, gain, grad):
    unit, rate = normalized(values)
    scaled = grad * gain
    back = scaled - jnp.mean(scaled, -1, keepdims=True) - unit * jnp.mean(scaled * unit, -1, keepdims=True)
    return rate * back, grad * unit


def middle_back_kernel(
    small, place_ref, pre_mine_ref, pre_other_ref, up_mine_ref, up_other_ref, middle_ref, cotangent_ref, mask_ref,
    rows_ref, context_mine_ref, context_other_ref, out_mine_ref, out_other_ref,
    grad_ref, context_grad_mine_ref, context_grad_other_ref, out_grad_mine_ref, out_grad_other_ref, sums_ref,
    normed_ref, total_ref,
):
    core = place_ref[0]
    step = pl.program_id(0)
    half = context_mine_ref.shape[1]

    @pl.when(step == 0)
    def _():
        sums_ref[...] = jnp.zeros_like(sums_ref)
        total_ref[...] = jnp.zeros_like(total_ref)

    normed_ref[...] = right_product(pre_mine_ref[...], up_mine_ref[...]) + right_product(
        pre_other_ref[...], up_other_ref[...]
    )
    grad = normed_ref[...]
    direct = cotangent_ref[...] * mask_ref[...]
    back, shares = norm_back(middle_ref[...], rows_ref[small + 6 : small + 7, :], grad)
    back = direct + back
    grad_ref[...] = back
    low = back.astype(BF)
    for index, item in enumerate((low.astype(F32), direct.astype(BF).astype(F32), shares, grad)):
        sums_ref[index : index + 1, :] += jnp.sum(item, 0, keepdims=True)
    lows = (low[:, :half], low[:, half:])
    contexts = chosen_side(core, context_mine_ref[...], context_other_ref[...])
    outs = chosen_side(core, out_mine_ref[...], out_other_ref[...])
    context_grads = [
        (right_product(lows[0], outs[0][span]) + right_product(lows[1], outs[1][span])).astype(BF)
        for span in (slice(0, half), slice(half, None))
    ]
    context_grad_mine_ref[...], context_grad_other_ref[...] = chosen_side(core, *context_grads)
    for index, item in enumerate(chosen_side(core, *lows)):
        for side, context in enumerate(contexts):
            total_ref[index, side * half : (side + 1) * half, :] += left_product(context, item)

    @pl.when(step == pl.num_programs(0) - 1)
    def _():
        out_grad_mine_ref[...] = total_ref[0]
        out_grad_other_ref[...] = total_ref[1].astype(BF)


def middle_back(place, grads, ups, middle, cotangent, mask, rows, contexts, weights, block=512):
    count, width = middle.shape
    half = width // 2
    hidden_half = ups[0].shape[1]
    small = place.shape[0] - 2
    block = math.gcd(block, count)

    def over_rows(columns):
        return pl.BlockSpec((block, columns), lambda step: (step, 0))

    def whole(*shape):
        return pl.BlockSpec(shape, lambda step: (0,) * len(shape))

    out_spec = pl.BlockSpec((width, half), lambda step: (0, 3))
    return pl.pallas_call(
        functools.partial(middle_back_kernel, small),
        grid=(count // block,),
        in_specs=[
            pl.BlockSpec(memory_space=pltpu.SMEM),
            over_rows(hidden_half),
            over_rows(hidden_half),
            whole(width, hidden_half),
            whole(width, hidden_half),
            over_rows(width),
            over_rows(width),
            over_rows(1),
            whole(*rows.shape),
            over_rows(half),
            over_rows(half),
            out_spec,
            out_spec,
        ],
        out_specs=[
            over_rows(width),
            over_rows(half),
            over_rows(half),
            whole(width, half),
            whole(width, half),
            whole(8, width),
        ],
        out_shape=[
            jax.ShapeDtypeStruct((count, width), F32),
            jax.ShapeDtypeStruct((count, half), BF),
            jax.ShapeDtypeStruct((count, half), BF),
            jax.ShapeDtypeStruct((width, half), F32),
            jax.ShapeDtypeStruct((width, half), BF),
            jax.ShapeDtypeStruct((8, width), F32),
        ],
        scratch_shapes=[pltpu.VMEM((block, width), F32), pltpu.VMEM((2, width, half), F32)],
        compiler_params=pltpu.CompilerParams(vmem_limit_bytes=2 * VMEM_BYTES),
        cost_estimate=pl.CostEstimate(
            flops=4 * count * width * (hidden_half + width),
            bytes_accessed=4 * count * hidden_half + 4 * width * hidden_half + 16 * count * width,
            transcendentals=0,
        ),
        name="middle_back",
    )(place, *grads, *ups, middle, cotangent, mask, rows, *contexts, *weights)


def start_back_kernel(
    small, length, swap, place_ref, grads_mine_ref, grads_other_ref, weight_mine_ref, weight_other_ref, start_ref, middle_ref,
    mask_ref, rows_ref, sums_ref, sums_mine_ref, sums_other_ref, bias_ref,
    tokens_ref, mine_ref, other_ref, lines_ref,
):
    core, place = place_ref[0], place_ref[1]
    step = pl.program_id(0)
    width = start_ref.shape[1]
    half = width // 2
    seqs = start_ref.shape[0] // length

    @pl.when(step == 0)
    def _():
        lines_ref[...] = jnp.zeros_like(lines_ref)
        for index, row in ((0, 0), (1, 2)):
            pair = (sums_mine_ref[row : row + 1, :], sums_other_ref[row : row + 1, :])
            lines_ref[index : index + 1, :half], lines_ref[index : index + 1, half:] = chosen_side(core, *pair)
        lines_ref[2:4, :] = sums_ref[0:2, :]
        lines_ref[6:8, :] = sums_ref[2:4, :]

    grad = 0.0
    for grads, weight in ((grads_mine_ref, weight_mine_ref), (grads_other_ref, weight_other_ref)):
        for index in range(3):
            grad = grad + right_product(grads[index], weight[:, index * half : (index + 1) * half])
    back, shares = norm_back(start_ref[...], rows_ref[small + 4 : small + 5, :], grad)
    back = middle_ref[...] + back
    mask = mask_ref[...]
    tokens_ref[...] = jnp.where(mask > 0.0, 0.0, back)
    for index, item in ((4, shares), (5, grad), (8, back * mask)):
        lines_ref[index : index + 1, :] += jnp.sum(item, 0, keepdims=True)
    for index in range(seqs):
        line = LANES + place * small + step * seqs + index
        lines_ref[pl.ds(line, 1), :] = jnp.sum(back[index * length : (index + 1) * length], 0, keepdims=True)

    @pl.when(step == pl.num_programs(0) - 1)
    def _():
        blocks = (lines_ref[:LANES, :].T + bias_ref[...], lines_ref[LANES:, :].T)
        if swap:
            blocks = chosen_side(core, *blocks)
        mine_ref[...] = blocks[0]
        other_ref[...] = blocks[1].astype(other_ref.dtype)


def start_back(
    place, grads, weights, start, middle, mask, rows, sums, side_sums, bias, seqs, length, swap, block=256
):
    count, width = start.shape
    half = width // 2
    small = place.shape[0] - 2
    block = math.gcd(block, count)
    lines = LANES + -(-seqs // LANES) * LANES

    def over_rows(columns):
        return pl.BlockSpec((block, columns), lambda step: (step, 0))

    def whole(*shape):
        return pl.BlockSpec(shape, lambda step: (0,) * len(shape))

    grads_spec = pl.BlockSpec((3, block, half), lambda step: (0, step, 0))
    return pl.pallas_call(
        functools.partial(start_back_kernel, small, length, swap),
        grid=(count // block,),
        in_specs=[
            pl.BlockSpec(memory_space=pltpu.SMEM),
            grads_spec,
            grads_spec,
            whole(width, 3 * half),
            whole(width, 3 * half),
            over_rows(width),
            over_rows(width),
            over_rows(1),
            whole(*rows.shape),
            whole(*sums.shape),
            whole(*side_sums[0].shape),
            whole(*side_sums[1].shape),
            whole(width, LANES),
        ],
        out_specs=[over_rows(width), whole(width, LANES), whole(width, lines - LANES)],
        out_shape=[
            jax.ShapeDtypeStruct((count, width), F32),
            jax.ShapeDtypeStruct((width, LANES), F32),
            jax.ShapeDtypeStruct((width, lines - LANES), BF if swap else F32),
        ],
        scratch_shapes=[pltpu.VMEM((lines, width), F32)],
        compiler_params=pltpu.CompilerParams(vmem_limit_bytes=VMEM_BYTES),
        cost_estimate=pl.CostEstimate(
            flops=0, bytes_accessed=1024, transcendentals=0
        ),
        name="start_back",
    )(place, *grads, *weights, start, middle, mask, rows, sums, *side_sums, bias)


def shards_kernel(fixed, seq_cols, core_ref, steps_ref, qkv_ref, out_ref, table_ref, *refs):
    small_refs, (mine_ref, other_ref, full_ref) = refs[: fixed + 1], refs[fixed + 1 :]
    core = core_ref[0]
    part, table_cols = table_ref.shape
    half = out_ref.shape[1] // 2
    seq_count = steps_ref.shape[0]
    lines = [ref[...] for ref in small_refs[:fixed]]
    up = small_refs[fixed][...]
    lines += [up[:, i : i + part] for i in range(0, up.shape[1], part)]
    lane = lax.broadcasted_iota(jnp.int32, (1, part), 1)
    for row in range(seq_cols):
        line = jnp.zeros((1, part), jnp.int32)
        for index in range(seq_count):
            step = steps_ref[index]
            line = jnp.where(lane + row * part == index, step // 256, line)
            line = jnp.where(lane + row * part == seq_count + index, step % 256, line)
        lines.append(line.astype(F32))
    lines = jnp.concatenate(lines, 0).astype(BF)
    square = (part, part)
    unit = lax.broadcasted_iota(jnp.int32, square, 0) == lax.broadcasted_iota(jnp.int32, square, 1)
    full_ref[...] = jnp.zeros_like(full_ref)
    full_ref[:, :table_cols] = table_ref[...]
    full_ref[:, table_cols : table_cols + lines.shape[0]] = right_product(jnp.where(unit, 1.0, 0.0).astype(BF), lines)
    table_half = full_ref.shape[1] // 2

    def halves(ref, top, wide):
        return chosen_side(core, ref[:, top : top + wide], ref[:, top + wide : top + 2 * wide])

    sources = [(qkv_ref, 2 * half * i, half) for i in range(3)] + [(out_ref, 0, half), (full_ref, 0, table_half)]
    left = 0
    for ref, top, wide in sources:
        mine, other = halves(ref, top, wide)
        mine_ref[:, left : left + wide] = mine.astype(BF)
        other_ref[:, left : left + wide] = other.astype(BF)
        left += wide


def attention_shards(core, timesteps, w_qkv, w_out, table, small, b_up, seq_cols, all_cols):
    part = table.shape[0]
    shape = jax.ShapeDtypeStruct((part, 2 * w_out.shape[1] + all_cols // 2), BF)
    vmem = pl.BlockSpec(memory_space=pltpu.VMEM)
    return pl.pallas_call(
        functools.partial(shards_kernel, len(small), seq_cols),
        in_specs=[pl.BlockSpec(memory_space=pltpu.SMEM)] * 2 + [vmem] * (4 + len(small)),
        out_specs=[vmem, vmem],
        out_shape=[shape, shape],
        scratch_shapes=[pltpu.VMEM((part, all_cols), F32)],
        compiler_params=pltpu.CompilerParams(vmem_limit_bytes=60 << 20),
        cost_estimate=pl.CostEstimate(flops=0, bytes_accessed=24 * part * w_out.shape[1], transcendentals=0),
        name="attention_shards",
    )(core, timesteps, w_qkv, w_out, table, *[item.reshape(1, -1) for item in small], b_up.reshape(1, -1))


def route_kernel(rows, route_ref, *refs):
    terms, (sent_ref, kept_ref) = refs[:-2], refs[-2:]
    for index in range(2):
        for out, place in ((sent_ref, route_ref[index]), (kept_ref, route_ref[2 + index])):
            span = pl.ds(pl.multiple_of(place * rows, 8), rows)
            left = 0
            for mine, got in zip(terms[::2], terms[1::2]):
                many = [(slice(None),)] if len(mine.shape) == 2 else [(i, slice(None)) for i in range(mine.shape[0])]
                for at in many:
                    where = (*at[:-1], span)
                    total = mine[where].astype(F32) + got[where].astype(F32)
                    out[0, index, :, left : left + total.shape[1]] = total.astype(out.dtype)
                    left += total.shape[1]


def routed(terms, rows, route):
    specs, columns, bytes_read = [], 0, 0
    for array in [item for pair in terms for item in pair]:
        shape = (4 * rows, array.shape[-1])
        if array.ndim == 2:
            specs.append(pl.BlockSpec(shape, lambda z: (z, 0)))
        else:
            specs.append(pl.BlockSpec((array.shape[0], *shape), lambda z: (0, z, 0)))
        bytes_read += array.size * array.dtype.itemsize
        columns += array.size // (16 * rows)
    columns //= 2
    out = pl.BlockSpec((1, 2, rows, columns), lambda z: (z, 0, 0, 0))
    return pl.pallas_call(
        functools.partial(route_kernel, rows),
        grid=(4,),
        in_specs=[pl.BlockSpec(memory_space=pltpu.SMEM)] + specs,
        out_specs=[out, out],
        out_shape=[
            jax.ShapeDtypeStruct((4, 2, rows, columns), BF),
            pltpu.HBM((4, 2, rows, columns), F32),
        ],
        compiler_params=pltpu.CompilerParams(vmem_limit_bytes=VMEM_BYTES),
        cost_estimate=pl.CostEstimate(
            flops=0, bytes_accessed=bytes_read + 48 * rows * columns, transcendentals=0
        ),
        name="routed",
    )(route, *[item for pair in terms for item in pair])


class Tree:
    def __init__(self):
        fsdp, rep = lax.axis_index("fsdp"), lax.axis_index("rep")
        self.z, self.core = fsdp // 2, rep % 2
        x, y = rep // 2, fsdp % 2
        self.near = jnp.where(self.core == 0, x, y)
        self.far = jnp.where(self.core == 0, y, x)
        places = [jnp.where(self.core == 0, 2 * i + near, 2 * near + i) for near in (1 - self.near, self.near) for i in (0, 1)]
        self.route = jnp.stack(places)

    def to_core(self, value):
        return lax.ppermute(value, "rep", [(i, i ^ 1) for i in range(4)])

    def to_near(self, value):
        return lax.ppermute(value, AXES, [(i, i ^ (4 if i % 2 else 2)) for i in range(32)])

    def to_far(self, value):
        return lax.ppermute(value, AXES, [(i, i ^ (2 if i % 2 else 4)) for i in range(32)])

    def to_z(self, value, step):
        return lax.ppermute(value, "fsdp", [(i, i ^ (2 * step)) for i in range(8)])


class Gather:
    def __init__(self, tree, own):
        self.tree, self.own = tree, own

    @staticmethod
    def columns(tree, mine, other):
        got = tree.to_core(other)
        return Gather(tree, paired(tree.core, mine, got, 0).reshape(-1, mine.shape[1]))

    @staticmethod
    def rows(tree, shard):
        return Gather(tree, shard)

    def along_z(self, *wait):
        own = after(self.own, *wait)
        one, three, two = [self.tree.to_z(own, step) for step in (1, 3, 2)]
        self.held, self.got = own, [one, two, three]
        return self.got

    def one(self, *wait):
        tree = self.tree
        held = after([self.held, *self.got], *wait)
        low, high = tree.z % 2 == 1, tree.z // 2 == 1
        out = []
        for place in range(4):
            near = [jnp.where(low, held[(place ^ 1) ^ h], held[place ^ h]) for h in (0, 2)]
            out.append(jnp.where(high, near[1], near[0]))
        self.held = jnp.stack(out)
        self.got = tree.to_near(self.held)
        return self.got

    def two(self, *wait):
        tree = self.tree
        held, got = after((self.held, self.got), *wait)
        self.held = paired(tree.near, held, got, 1)
        self.got = tree.to_far(self.held)
        return self.got

    def halves(self, *wait):
        tree = self.tree
        held, got = after((self.held, self.got), *wait)
        same, first = tree.far == 0, tree.core == 0
        lower, upper = jnp.where(same, held, got), jnp.where(same, got, held)
        blocks = [
            lower[:, 0],
            jnp.where(first, lower[:, 1], upper[:, 0]),
            jnp.where(first, upper[:, 0], lower[:, 1]),
            upper[:, 1],
        ]
        half = jnp.stack(blocks, 1).reshape(-1, held.shape[-1])
        return half, tree.to_core(half)


class Reduce:
    def __init__(self, tree, rows):
        self.tree, self.rows = tree, rows
        self.terms = []

    def add(self, mine, other):
        got = self.tree.to_core(other.astype(BF))
        self.terms.append((mine, got))
        return got

    def one(self, *wait):
        self.sent, self.kept = routed(after(self.terms, *wait), self.rows, self.tree.route)
        self.got = self.tree.to_near(self.sent)

    def two(self, *wait, apart=False):
        tree = self.tree
        kept, got = after((self.kept, self.got), *wait)
        if apart:
            self.sent = (pick(kept, 1 - tree.far, 1) + pick(got, 1 - tree.far, 1)).astype(BF)
            self.kept = pick(kept, tree.far, 1) + pick(got, tree.far, 1)
            self.got = tree.to_far(self.sent)
            return
        total = kept + got
        self.kept, self.sent = pick(total, tree.far, 1), pick(total, 1 - tree.far, 1).astype(BF)
        self.got = tree.to_far(self.sent)

    def along_z(self, *others):
        tree = self.tree
        total = jnp.concatenate([item.kept + item.got for item in (self, *others)], -1)
        self.kept = pick(total, tree.z, 0)
        self.sent = tuple(pick(total, tree.z ^ step, 0).astype(BF) for step in (1, 2, 3))
        self.got = tuple(tree.to_z(sent, step) for sent, step in zip(self.sent, (1, 2, 3)))

    def sums(self, *wait):
        kept, got = after((self.kept, self.got), *wait)
        return kept + got[0] + got[1] + got[2]

    def columns(self, *wait):
        tree, total = self.tree, self.sums(*wait)
        rows = total.reshape(2, self.rows // 2, -1)
        keep = pick(rows, tree.core, 0)
        return paired(tree.core, keep, tree.to_core(pick(rows, 1 - tree.core, 0)), 1)


class Whole:
    core = 0

    def __init__(self, rows=None):
        self.mine, self.other = [], []
        self.got, self.sent = (), ()

    @staticmethod
    def columns_of(mine, other):
        out = Whole()
        whole = lax.all_gather(jnp.stack([mine, other], 1), AXES, axis=0, tiled=True)
        out.half, out.rest = whole[:, 0], whole[:, 1]
        return out

    @staticmethod
    def rows_of(shard):
        out = Whole()
        whole = lax.all_gather(shard, AXES, axis=0)
        whole = whole.reshape(-1, 2, *shard.shape)
        out.half, out.rest = [whole[:, i].reshape(-1, shard.shape[1]) for i in range(2)]
        return out

    def along_z(self, *wait):
        return []

    def one(self, *wait):
        return ()

    def two(self, *wait):
        return ()

    def halves(self, *wait):
        return self.half, self.rest

    def add(self, mine, other):
        self.mine.append(mine.astype(BF))
        self.other.append(other.astype(BF))
        return mine

    def columns(self, *wait):
        def flat(items):
            return jnp.concatenate([part for item in items for part in (item if item.ndim == 3 else [item])], 1)

        parts = [flat(item) for item in (self.mine, self.other)]
        return lax.psum_scatter(jnp.stack(parts, 1), AXES, scatter_dimension=0, tiled=True).astype(F32)

    def sums(self, *wait):
        count = lax.axis_size(AXES)
        mine, other = [item[0].reshape(count // 2, -1, item[0].shape[1]) for item in (self.mine, self.other)]
        sums = jnp.stack([mine, other], 1).reshape(-1, mine.shape[-1])
        return lax.psum_scatter(sums, AXES, scatter_dimension=0, tiled=True).astype(F32)


def body(
    fast,
    tokens,
    mask_bits,
    timesteps,
    cotangent,
    w_qkv,
    w_out,
    w_up,
    w_down,
    time_table,
    b_query,
    b_value,
    b_out,
    b_up,
    b_down,
    gain_attn,
    shift_attn,
    gain_mlp,
    shift_mlp,
    mask_vector,
):
    tree = Tree() if fast else Whole()
    gather_columns = functools.partial(Gather.columns, tree) if fast else Whole.columns_of
    gather_rows = functools.partial(Gather.rows, tree) if fast else Whole.rows_of
    reduction = functools.partial(Reduce, tree) if fast else Whole
    core = tree.core
    count = lax.axis_size(AXES)
    chips = count // 2
    place = lax.axis_index(AXES)
    width = tokens.shape[1]
    part = width // count
    hidden_width = w_up.shape[1]
    hidden_part = hidden_width // count
    seq_count = timesteps.shape[0]
    seq_length = tokens.shape[0] // seq_count
    half = width // 2
    table_cols = time_table.shape[1]
    absorbed = mask_bits.astype(F32)[:, None]

    small = [b_query, b_value, b_out, b_down, gain_attn, shift_attn, gain_mlp, shift_mlp, mask_vector]
    fixed = len(small)
    up_cols = hidden_part // part
    seq_cols = -(-2 * seq_count // part)
    small_cols = fixed + up_cols + seq_cols
    all_cols = -(-(table_cols + small_cols) // (2 * LANES)) * (2 * LANES)
    place = jnp.concatenate([jnp.stack([jnp.int32(core), place]), timesteps])

    shards = attention_shards(
        jnp.full((1,), core, jnp.int32), timesteps, w_qkv, w_out, time_table, small, b_up, seq_cols, all_cols
    )
    attn_w = gather_columns(*shards)
    up_shard = w_up.astype(BF).reshape(part, chips, 2, hidden_part).transpose(2, 0, 1, 3)
    up_shard = up_shard.reshape(2, part, hidden_width // 2)
    up_w = gather_columns(*[pick(up_shard, side, 0) for side in (core, 1 - core)])
    down_w = gather_rows(w_down.astype(BF))
    attn_w.along_z()
    up_z = up_w.along_z()
    attn_one = attn_w.one()
    attn_two = attn_w.two(up_z[::2])
    up_one = up_w.one(attn_two)
    attn_w = attn_w.halves(up_z)
    down_z = down_w.along_z(attn_two)

    rows, start, normed_one, across_one, bias_mine, bias_other, bias_up = start_rows(
        place, tokens, absorbed, attn_w, fixed, up_cols, table_cols, small_cols, chips, hidden_part
    )
    up_two = up_w.two(normed_one)
    qkv_mine, context_mine = attention(after(normed_one, up_one), attn_w[0], bias_mine, seq_length)
    down_one = down_w.one(up_two, context_mine)
    up_w = up_w.halves(context_mine)
    qkv_other, context_other = attention(after(normed_one, up_two), attn_w[1], bias_other, seq_length)
    down_two = down_w.two()
    contexts = (context_mine, context_other)
    middle, normed_two, across_two = middle_rows(place, contexts, attn_w, after(start, down_one), rows)
    hidden, slope = [None, None], [None, None]
    hidden[0], slope[0] = feed(normed_two, up_w[0], bias_up, 0)
    down_w = down_w.halves(hidden[0])
    hidden[1], slope[1] = feed(normed_two, up_w[1], bias_up, 1)

    grad_branch = (cotangent * absorbed).astype(BF)
    down_sum = reduction(hidden_part)
    down_sum.add(left_product(hidden[0], grad_branch), left_product(hidden[1], grad_branch))
    up_sum = reduction(2 * part)
    grad_pre, grad_b_up, grad_up = [None, None], [None, None], [None, None]
    if fast:
        down_sum.one()
    grad_pre[1], grad_b_up[1], grad_up[1] = feed_back(
        grad_branch, down_w[1], slope[1], across_two, BF
    )
    grad_pre[0], grad_b_up[0], grad_up[0] = feed_back(grad_branch, down_w[0], slope[0], across_two, F32)
    up_sum.add(grad_up[0], grad_up[1])
    if fast:
        down_sum.two(grad_pre[1])
    grad_pre = after(grad_pre, down_sum.sent)
    grad_middle, *grad_context, grad_out_mine, grad_out_other, middle_sums = middle_back(
        place, grad_pre, up_w, middle, cotangent, absorbed, rows, contexts, attn_w
    )

    attn_sum = reduction(2 * part)
    up_sum.add(grad_out_mine, grad_out_other)
    if fast:
        up_sum.one(down_sum.got)
        down_sum.along_z()
    grads = [None, None]
    grads[1] = attention_back(
        qkv_other, after(grad_context[1], down_sum.sent, up_sum.sent), across_one, seq_length, BF
    )
    if fast:
        up_sum.two(down_sum.got, grads[1])
    grads[0] = attention_back(qkv_mine, after(grad_context[0], up_sum.sent), across_one, seq_length, F32)
    grad_qkv, grad_weights, sums = zip(*grads)
    attn_sum.add(grad_weights[0], grad_weights[1])
    if fast:
        attn_sum.one()
        up_sum.along_z()
    grad_qkv = after(grad_qkv, up_sum.sent, attn_sum.sent)
    grad_b_up = paired(core, *[item.reshape(chips, hidden_part) for item in grad_b_up], 1).reshape(count, hidden_part)
    grad_b_up = jnp.pad(grad_b_up[:, None], ((0, 0), (0, part - 1), (LANES - hidden_part, 0)))
    seqs = count * seq_count
    grad_tokens, *blocks = start_back(
        place, grad_qkv, attn_w, start, grad_middle, absorbed, rows, middle_sums, sums,
        grad_b_up.reshape(width, LANES), seqs, seq_length, fast,
    )
    if fast:
        attn_sum.two()
        extra_sum = reduction(2 * part)
        extra_sum.add(*blocks)
        extra_sum.one()
        extra_sum.two(attn_sum.sent, up_sum.got)
        attn_sum.along_z(extra_sum)
        hidden, rows = after((hidden, rows), attn_sum.sent)
    output = middle + (product(hidden[0], down_w[0]) + product(hidden[1], down_w[1]) + rows[seq_count + 3])
    if fast:
        attn_grad = attn_sum.columns(output)
        small, seq_sums = attn_grad[:, 0, 3 * half :], attn_grad[:, 1, 3 * half :]
    else:
        attn_grad = attn_sum.columns()
        small, seq_sums = [
            lax.psum_scatter(item.astype(BF), AXES, scatter_dimension=0, tiled=True).astype(F32) for item in blocks
        ]
    steps = rows[seq_count + fixed + up_cols : seq_count + small_cols]
    steps = steps.reshape(seq_cols, count, part).transpose(1, 0, 2).reshape(count, -1).astype(jnp.int32)
    steps = (steps[:, :seq_count] * 256 + steps[:, seq_count : 2 * seq_count]).reshape(-1)
    grad_b_up = small[0, LANES - hidden_part :]
    small = small[:, :fixed].T
    onehot = (steps[:, None] == lax.broadcasted_iota(jnp.int32, (seqs, table_cols), 1)).astype(F32)
    grad_time_table = jnp.dot(seq_sums, onehot, precision=lax.Precision.HIGHEST)
    grad_w_qkv = attn_grad[:, :, : 3 * half].reshape(part, 2, 3, half).transpose(0, 2, 1, 3).reshape(part, 3 * width)
    up_grad = up_sum.columns(extra_sum.sent if fast else ())
    grad_w_out = up_grad[:, :, hidden_width // 2 :].reshape(part, width)
    grad_w_up = up_grad[:, :, : hidden_width // 2].reshape(part, 2, chips, hidden_part).transpose(0, 2, 1, 3)
    grad_w_up = grad_w_up.reshape(part, hidden_width)
    return (
        output,
        grad_tokens,
        grad_w_qkv,
        grad_w_out,
        grad_w_up,
        down_sum.sums(extra_sum.sent if fast else ()),
        grad_time_table,
        small[0],
        small[1],
        small[2],
        grad_b_up,
        small[3],
        small[4],
        small[5],
        small[6],
        small[7],
        small[8],
    )


def solution(mesh):
    matrix, vector = P(AXES, None), P(AXES)
    fast = dict(mesh.shape) == {"fsdp": 8, "rep": 4}
    return jax.shard_map(
        functools.partial(body, fast),
        mesh=mesh,
        in_specs=(matrix, vector, vector) + (matrix,) * 6 + (vector,) * 10,
        out_specs=(matrix,) * 7 + (vector,) * 10,
        check_vma=False,
    )
```
